32 devices in a mesh: seq: 16 (over z, y, x), head: 2 (over core).
Axes of the slice: x: 2, y: 2, z: 4, core: 2. Of those that a mesh axis runs over, the one named last changes fastest.
Arguments:
- tokens: bfloat16 [2, 4096, 2048], P(None, 'seq'), may hold values from -6 to 6
- grad_out: bfloat16 [2, 4096, 2048], P(None, 'seq'), may hold values from -6 to 6
- query_weight: bfloat16 [2048, 2048], P('seq', 'head'), may hold values from -0.5 to 0.5
- key_weight: bfloat16 [2048, 2048], P('seq', 'head'), may hold values from -0.5 to 0.5
- value_weight: bfloat16 [2048, 2048], P('seq', 'head'), may hold values from -0.125 to 0.125
- forget_weight: bfloat16 [2048, 256], P('seq', 'head'), may hold values from -0.125 to 0.125
- forget_bias: bfloat16 [4, 64], P('head', 'seq'), as said below
- outgate_weight: bfloat16 [2048, 2048], P('seq', 'head'), may hold values from -0.125 to 0.125
- output_weight: bfloat16 [2048, 2048], P('head', 'seq'), may hold values from -0.125 to 0.125
- slot_gain: bfloat16 [512], P('seq'), may hold values from 0.5 to 1.5
- first_gain: bfloat16 [2048], P('seq'), may hold values from 0.5 to 1.5
- second_gain: bfloat16 [2048], P('seq'), may hold values from 0.5 to 1.5
- gate_weight: bfloat16 [2048, 5632], P('seq', 'head'), may hold values from -0.125 to 0.125
- up_weight: bfloat16 [2048, 5632], P('seq', 'head'), may hold values from -0.125 to 0.125
- down_weight: bfloat16 [5632, 2048], P('head', 'seq'), may hold values from -0.078125 to 0.078125
Outputs:
- output: bfloat16 [2, 4096, 2048], P(None, 'seq')
- input_grad: float32 [2, 4096, 2048], P(None, 'seq')
- query_grad: float32 [2048, 2048], P('seq', 'head')
- key_grad: float32 [2048, 2048], P('seq', 'head')
- value_grad: float32 [2048, 2048], P('seq', 'head')
- forget_grad: float32 [2048, 256], P('seq', 'head')
- forget_bias_grad: float32 [4, 64], P('head', 'seq')
- outgate_grad: float32 [2048, 2048], P('seq', 'head')
- output_grad: float32 [2048, 2048], P('head', 'seq')
- slot_gain_grad: float32 [512], P('seq')
- first_gain_grad: float32 [2048], P('seq')
- second_gain_grad: float32 [2048], P('seq')
- gate_grad: float32 [2048, 5632], P('seq', 'head')
- up_grad: float32 [2048, 5632], P('seq', 'head')
- down_grad: float32 [5632, 2048], P('head', 'seq')
The draws below stay inside these ranges and needn't reach their ends.
Inputs may be any that keep to these rules, and one draw needn't show every extreme that they name: `forget_bias`: forget gate offsets of the heads and slots, those of per-token decay rates between 0.25 / 4096 and 1 / 30, so about 1 to 9.
All inputs are finite; a program needn't handle non-finite values.
Results may differ from the reference program's by a relative error of at most 0.01655.
Values may be sent and summed in bfloat16 or wider, within the bound.
A program may use at most 320 MiB of HBM per device.

```python
import math
import jax
import jax.numpy as jnp
from jax import lax

D = 2048
H = 4
K = 512
M = 64
FF = 5632
TOK_DEV = 256
SEQS = 2
LEN = 4096


decay_scale = 8.0


def draw_forget_bias(key, part):
    streams = jax.random.split(key, 3)
    chooser = jax.random.uniform(streams[0], (H, M))
    slow_rate = jnp.exp(jax.random.uniform(streams[1], (H, M), minval=math.log(0.25 / LEN), maxval=math.log(1.0 / LEN)))
    fast_rate = jnp.exp(jax.random.uniform(streams[2], (H, M), minval=math.log(1.0 / 50.0), maxval=math.log(1.0 / 30.0)))
    share = 0.5
    rate = jnp.where(chooser < share, slow_rate, fast_rate)
    return (-jnp.log(jnp.expm1(decay_scale * rate))).astype(jnp.bfloat16)


def levels(stream_key, shape, cuts, smallest, high):
    def one(axis_at, blocks):
        steps = jax.random.uniform(jax.random.fold_in(jax.random.fold_in(stream_key, 6), axis_at), (blocks,), jnp.float32, smallest / len(cuts), high / len(cuts))
        return jnp.repeat(jnp.exp(steps), shape[axis_at] // blocks).reshape((-1,) + (1,) * (len(shape) - axis_at - 1))

    loudness = one(*cuts[0])
    for cut in cuts[1:]:
        loudness = loudness * one(*cut)
    return loudness


def bell_draw(stream_key, dims, deviation, most, pieces=(), dtype=jnp.bfloat16):
    values = jax.random.normal(stream_key, dims, jnp.float32) * deviation
    if len(pieces) > 0:
        values = levels(stream_key, dims, pieces, -0.22, 0.18) * values
    return jnp.clip(values, min=-most, max=most).astype(dtype)


def setup_inputs(seed: int = 0) -> dict:
    arg_keys = jax.random.split(jax.random.key(seed), 16)
    tokens = bell_draw(arg_keys[0], (SEQS, LEN, D), 1.0, 6.0, ((1, 16),))
    grad_out = bell_draw(arg_keys[1], (SEQS, LEN, D), 1.0, 6.0, ((1, 16),))
    query_weight = bell_draw(arg_keys[2], (D, H * K), (D // 16) ** -0.5, 0.5, ((0, 16), (1, 2)))
    key_weight = bell_draw(arg_keys[3], (D, H * K), (D // 16) ** -0.5, 0.5, ((0, 16), (1, 2)))
    value_weight = bell_draw(arg_keys[4], (D, H * K), D ** -0.5, 0.125, ((0, 16), (1, 2)))
    forget_weight = bell_draw(arg_keys[5], (D, H * M), D ** -0.5, 0.125, ((0, 16), (1, 2)))
    forget_bias = draw_forget_bias(jax.random.fold_in(arg_keys[15], 71), 0)
    outgate_weight = bell_draw(arg_keys[7], (D, H * K), D ** -0.5, 0.125, ((0, 16), (1, 2)))
    output_weight = bell_draw(arg_keys[8], (H * K, D), (H * K) ** -0.5, 0.125, ((0, 2), (1, 16)))
    slot_gain = jnp.clip(1.0 + 0.1 * jax.random.normal(arg_keys[9], (K,), jnp.float32), 0.5, 1.5).astype(jnp.bfloat16)
    first_gain = jnp.clip(1.0 + 0.1 * jax.random.normal(arg_keys[10], (D,), jnp.float32), 0.5, 1.5).astype(jnp.bfloat16)
    second_gain = jnp.clip(1.0 + 0.1 * jax.random.normal(arg_keys[11], (D,), jnp.float32), 0.5, 1.5).astype(jnp.bfloat16)
    gate_weight = bell_draw(arg_keys[12], (D, FF), D ** -0.5, 0.125, ((0, 16), (1, 2)))
    up_weight = bell_draw(arg_keys[13], (D, FF), D ** -0.5, 0.125, ((0, 16), (1, 2)))
    down_weight = bell_draw(arg_keys[14], (FF, D), FF ** -0.5, 0.078125, ((0, 2), (1, 16)))
    return dict(tokens=tokens, grad_out=grad_out, query_weight=query_weight, key_weight=key_weight, value_weight=value_weight, forget_weight=forget_weight, forget_bias=forget_bias, outgate_weight=outgate_weight, output_weight=output_weight, slot_gain=slot_gain, first_gain=first_gain, second_gain=second_gain, gate_weight=gate_weight, up_weight=up_weight, down_weight=down_weight)


HIGH = lax.Precision.HIGHEST
TAU = 8.0
EPS = 1e-06

@jax.custom_vjp
def low(v):
    return lax.optimization_barrier(v.astype(jnp.bfloat16)).astype(jnp.float32)

@jax.custom_vjp
def low_back(v):
    return v

def low_keep(v):
    return (low(v), None)

def low_pass(kept, grad):
    return (grad,)

def back_keep(v):
    return (v, None)

def back_low(kept, grad):
    return (low(grad),)
low.defvjp(low_keep, low_pass)
low_back.defvjp(back_keep, back_low)

def rms_scale(values, gain):
    return values * lax.rsqrt(lax.optimization_barrier(jnp.mean(values * values, axis=-1, keepdims=True)) + EPS) * gain

def out_gate(attended, gate, gain):
    return rms_scale(attended, gain) * jax.nn.silu(gate)

def slot_single(query, keys, values, log_decay, keys_in, values_in):
    count = query.shape[0]
    keep = -jnp.expm1(log_decay)
    total = jnp.cumsum(log_decay, axis=0)
    causal = (jnp.arange(count)[:, None] >= jnp.arange(count)[None, :])[:, :, None]
    spread = jnp.where(causal, total[:, None, :] - total[None, :, :], 0.0)
    mixing = jnp.where(causal, jnp.exp(spread), 0.0) * keep[None, :, :]
    scaled = query * query.shape[1] ** (-0.5)
    paired = jnp.dot(scaled, keys.T, precision=HIGH)
    growth = jnp.exp(total)
    scores = jnp.einsum('ts,tsi->ti', paired, mixing, precision=HIGH) + growth * jnp.dot(scaled, keys_in.T, precision=HIGH)
    probs = jax.nn.softmax(scores, axis=-1)
    weights = jnp.einsum('ti,tsi->ts', probs, mixing, precision=HIGH)
    return jnp.dot(weights, values, precision=HIGH) + jnp.dot(probs * growth, values_in, precision=HIGH)

def slot_end(keys, values, log_decay):
    total = jnp.cumsum(log_decay, axis=0)
    last = total[-1]
    weight = jnp.exp(last[None, :] - total) * -jnp.expm1(log_decay)
    return (jnp.exp(last), jnp.dot(weight.T, keys, precision=HIGH), jnp.dot(weight.T, values, precision=HIGH))

def heads_attend(query, keys, values, log_decay, keys_in, values_in):

    def one_head(parts):
        return jax.vmap(slot_single)(parts[0], parts[1], parts[2], parts[3], parts[4], parts[5])
    stacked = (jnp.moveaxis(query, 2, 0), jnp.moveaxis(keys, 2, 0), jnp.moveaxis(values, 2, 0), jnp.moveaxis(log_decay, 2, 0), jnp.moveaxis(keys_in, 1, 0), jnp.moveaxis(values_in, 1, 0))
    return jnp.moveaxis(lax.map(jax.checkpoint(one_head), stacked), 0, 2)

def heads_end(keys, values, log_decay):
    inner = jax.vmap(slot_end, in_axes=(1, 1, 1), out_axes=0)
    return jax.vmap(inner, in_axes=(0, 0, 0), out_axes=0)(keys, values, log_decay)

def sequence_attend(query, keys, values, log_decay):
    seqs = query.shape[0]
    length = query.shape[1]
    heads = query.shape[2]
    blocks = length // TOK_DEV

    def split(array):
        return jnp.moveaxis(array.reshape(seqs, blocks, TOK_DEV, heads, array.shape[3]), 1, 0)

    def advance(state, parts):
        keys_in, values_in = state
        attended = heads_attend(parts[0], parts[1], parts[2], parts[3], keys_in, values_in)
        decay, local_keys, local_values = heads_end(parts[1], parts[2], parts[3])
        fresh = (decay[..., None] * keys_in + local_keys, decay[..., None] * values_in + local_values)
        return (fresh, attended)
    start = jnp.zeros((seqs, heads, log_decay.shape[3], query.shape[3]), jnp.float32)
    final, outs = lax.scan(jax.checkpoint(advance), (start, start), (split(query), split(keys), split(values), split(log_decay)))
    return jnp.moveaxis(outs, 0, 1).reshape(seqs, length, heads, query.shape[3])

def project(left, right):
    return jnp.dot(left, right, precision=HIGH)

def forward(tokens, query_weight, key_weight, value_weight, forget_weight, forget_bias, outgate_weight, output_weight, slot_gain, first_gain, second_gain, gate_weight, up_weight, down_weight):
    seqs = tokens.shape[0]
    length = tokens.shape[1]
    heads = forget_bias.shape[0]
    slots = forget_bias.shape[1]
    head_dim = slot_gain.shape[0]
    normed_one = low(rms_scale(tokens, first_gain))
    query = jax.nn.silu(low(low_back(project(normed_one, query_weight)))).reshape(seqs, length, heads, head_dim)
    keys = jax.nn.silu(low(low_back(project(normed_one, key_weight)))).reshape(seqs, length, heads, head_dim)
    values = low(low_back(project(normed_one, value_weight))).reshape(seqs, length, heads, head_dim)
    logit = low_back(project(normed_one, forget_weight) + forget_bias.reshape(heads * slots))
    log_decay = (-jax.nn.softplus(-logit) / TAU).reshape(seqs, length, heads, slots)
    attended = sequence_attend(query, keys, values, log_decay)
    gate = low_back(project(normed_one, outgate_weight)).reshape(seqs, length, heads, head_dim)
    gated = low(out_gate(attended, gate, slot_gain)).reshape(seqs, length, heads * head_dim)
    residual = tokens + low_back(project(gated, output_weight))
    normed_two = low(rms_scale(residual, second_gain))
    ff_gate = low_back(project(normed_two, gate_weight))
    ff_up = low_back(project(normed_two, up_weight))
    activated = low(jax.nn.silu(ff_gate) * ff_up)
    return residual + low_back(project(activated, down_weight))

def reference(tokens, grad_out, query_weight, key_weight, value_weight, forget_weight, forget_bias, outgate_weight, output_weight, slot_gain, first_gain, second_gain, gate_weight, up_weight, down_weight):
    inputs = (tokens, query_weight, key_weight, value_weight, forget_weight, forget_bias, outgate_weight, output_weight, slot_gain, first_gain, second_gain, gate_weight, up_weight, down_weight)
    wide = tuple((item.astype(jnp.float32) for item in inputs))
    result, pullback = jax.vjp(forward, *wide)
    grads = pullback(grad_out.astype(jnp.float32))
    return (result.astype(jnp.bfloat16), grads[0], grads[1], grads[2], grads[3], grads[4], grads[5], grads[6], grads[7], grads[8], grads[9], grads[10], grads[11], grads[12], grads[13])
```

```python
import functools

import jax
import jax.numpy as jnp
import numpy as np
from jax import lax
from jax.experimental import pallas as pl
from jax.experimental.pallas import tpu as pltpu
from jax.sharding import PartitionSpec as P

F32, BF16 = jnp.float32, jnp.bfloat16
MESH = pl.DeviceIdType.MESH
HBM = pltpu.HBM
EPS = 1e-06
TAU = 8.0


CHUNK = 256
NT = (((1,), (1,)), ((), ()))
NN = (((1,), (0,)), ((), ()))
TN = (((0,), (0,)), ((), ()))


def decay_tables(count):
    at = np.arange(count)
    paths, masks = [], []
    half = count // 2
    while half >= 1:
        block, second = at // (2 * half), (at // half) % 2 == 1
        edge = block * 2 * half + half - 1
        r, t = at[None, :], at[:, None]
        fore = second[:, None] & (r > edge[:, None]) & (r <= t)
        back = ~second[:, None] & (r > t) & (r <= edge[:, None])
        paths.append(fore | back)
        masks.append((block[:, None] == block[None, :]) & second[:, None] & ~second[None, :])
        half //= 2
    paths.append(at[None, :] <= at[:, None])
    paths.append(at[None, :] > at[:, None])
    return np.concatenate(paths, 0), np.stack(masks)


def bf(x):
    return x.astype(BF16)


def halves(x):
    hi = bf(x)
    return hi, bf(x - hi.astype(F32))


def mm(a, b, dims):
    return lax.dot_general(a, b, dims, preferred_element_type=F32)


def dot3(a, b, dims):
    return mm(a[0], b[0], dims) + (mm(a[0], b[1], dims) + mm(a[1], b[0], dims))


def exact_sums(table, x):
    hi, mid = halves(x)
    low = bf(x - hi.astype(F32) - mid.astype(F32))
    n = x.shape[1]
    both = mm(table, jnp.concatenate([hi, mid, low, jnp.zeros_like(low)], axis=1), NN)
    return both[:, :n] + (both[:, n : 2 * n] + both[:, 2 * n : 3 * n])


def silu(v):
    return v / (1.0 + jnp.exp(-v))


def sigmoid(v):
    return 1.0 / (1.0 + jnp.exp(-v))


def silu_slope(v):
    s = sigmoid(v)
    return s + v * s * (1.0 - s)


def columns_total(x):
    ones = jnp.ones((x.shape[0], 128), BF16)
    hi, mid = halves(x)
    low = bf(x - hi.astype(F32) - mid.astype(F32))
    return mm(hi, ones, TN) + (mm(mid, ones, TN) + mm(low, ones, TN))


def spread(column, width):
    return jnp.concatenate([column] * (width // 128), axis=1)


def ends_kernel(levels, k_ref, v_ref, decay_ref, keep_ref, table_ref, unit_ref, dec_ref, all_ref, alldec_ref):
    count = table_ref.shape[1]
    chunks = k_ref.shape[0] // count
    head = k_ref.shape[1]
    total, total_dec = None, None
    for j in range(chunks):
        rows = pl.ds(j * count, count)
        decay = decay_ref[rows, :]
        weight = jnp.exp(exact_sums(table_ref[...], decay)) * keep_ref[rows, :]
        weight = halves(weight)
        keys = halves(silu(k_ref[rows, :].astype(F32)))
        values = v_ref[rows, :]
        unit_k = dot3(weight, keys, TN)
        unit_v = mm(weight[0], values, TN) + mm(weight[1], values, TN)
        unit = jnp.concatenate([unit_k, unit_v], axis=1)
        dec = jnp.exp(columns_total(decay))
        unit_ref[j] = unit
        dec_ref[j] = dec
        if j == 0:
            total, total_dec = unit, dec
        else:
            total = spread(dec, 2 * head) * total + unit
            total_dec = total_dec * dec
    all_ref[0] = total
    alldec_ref[0] = total_dec


def mix(pair, ratios, keep, masks_ref, own):
    out = own * keep
    for l, ratio in enumerate(ratios):
        left = pair * masks_ref[l].astype(F32)
        out += ratio * dot3(halves(left), halves(ratio * keep), NN)
    return out


def unmix(probs, ratios, keep, masks_ref, diag):
    out = diag * jnp.sum(probs * keep, axis=1, keepdims=True)
    for l, ratio in enumerate(ratios):
        part = dot3(halves(probs * ratio), halves(ratio * keep), NT)
        out += masks_ref[l].astype(F32) * part
    return out


def on_diagonal(count):
    return (
        lax.broadcasted_iota(jnp.int32, (count, count), 0) == lax.broadcasted_iota(jnp.int32, (count, count), 1)
    ).astype(F32)


def attend_kernel(
    levels, q_ref, k_ref, v_ref, gate_ref, decay_ref, keep_ref, start_ref, unit_ref, dec_ref, gain_ref, table_ref, masks_ref,
    gated_ref, attended_ref, probs_ref, scores_ref, weights_ref, states_ref,
):
    count = table_ref.shape[1]
    chunks = k_ref.shape[0] // count
    head = k_ref.shape[1]
    diag = on_diagonal(count)
    states_ref[0] = start_ref[0]

    def chunk(j, carry):
        rows = pl.ds(pl.multiple_of(j * count, count), count)
        keep = keep_ref[rows, :]
        powers = jnp.exp(exact_sums(table_ref[: (levels + 1) * count, :], decay_ref[rows, :]))
        ratios = [powers[l * count : (l + 1) * count] for l in range(levels)]
        growth = powers[levels * count : (levels + 1) * count]
        query = halves(silu(q_ref[rows, :].astype(F32)) * head ** (-0.5))
        keys = halves(silu(k_ref[rows, :].astype(F32)))
        state = states_ref[j]
        pair = dot3(query, keys, NT)
        scores = mix(pair, ratios, keep, masks_ref, jnp.sum(pair * diag, axis=1, keepdims=True))
        scores += growth * dot3(query, halves(state[:, :head]), NT)
        top = jnp.max(scores, axis=1, keepdims=True)
        raised = jnp.exp(scores - top)
        probs = raised / jnp.sum(raised, axis=1, keepdims=True)
        weights = unmix(probs, ratios, keep, masks_ref, diag)
        values = v_ref[rows, :]
        whi, wlo = halves(weights)
        attended = mm(whi, values, NN) + mm(wlo, values, NN)
        attended += dot3(halves(probs * growth), halves(state[:, head:]), NN)
        scale = lax.rsqrt(jnp.mean(attended * attended, axis=1, keepdims=True) + EPS)
        gated = attended * scale * gain_ref[...] * silu(gate_ref[rows, :])
        gated_ref[rows, :] = bf(gated)
        attended_ref[rows, :] = attended
        probs_ref[rows, :] = probs
        scores_ref[rows, :] = scores
        weights_ref[rows, :] = weights
        states_ref[j + 1] = spread(dec_ref[j], 2 * head) * state + unit_ref[j]
        return carry

    lax.fori_loop(0, chunks, chunk, 0)


def back_one_kernel(
    levels, q_ref, v_ref, gate_ref, decay_ref, keep_ref, grad_ref, attended_ref, probs_ref, states_ref, dec_ref, gain_ref,
    table_ref, masks_ref,
    gate_term_ref, gain_grad_ref, attended_grad_ref, dprobs_ref, dscores_ref, unit_ref, all_ref,
):
    count = table_ref.shape[1]
    chunks = q_ref.shape[0] // count
    head = q_ref.shape[1]
    diag = on_diagonal(count)
    gain = gain_ref[...]

    def chunk(n, carry):
        j = chunks - 1 - n
        rows = pl.ds(pl.multiple_of(j * count, count), count)
        gate = gate_ref[rows, :]
        attended = attended_ref[rows, :]
        grad = grad_ref[rows, :]
        scale = lax.rsqrt(jnp.mean(attended * attended, axis=1, keepdims=True) + EPS)
        normed = attended * scale
        weighted = grad * silu(gate)
        gate_term_ref[rows, :] = bf(grad * normed * gain * silu_slope(gate))
        part = jnp.sum(weighted * normed, axis=0, keepdims=True)
        c = weighted * gain
        att_grad = scale * c - attended * (scale * scale * scale) * jnp.mean(c * attended, axis=1, keepdims=True)
        attended_grad_ref[rows, :] = att_grad
        keep = keep_ref[rows, :]
        powers = jnp.exp(exact_sums(table_ref[: (levels + 1) * count, :], decay_ref[rows, :]))
        ratios = [powers[l * count : (l + 1) * count] for l in range(levels)]
        growth = powers[levels * count : (levels + 1) * count]
        ahalf = halves(att_grad)
        values = v_ref[rows, :]
        pair = mm(ahalf[0], values, NT) + mm(ahalf[1], values, NT)
        state = states_ref[j]
        dprobs = mix(pair, ratios, keep, masks_ref, jnp.sum(pair * diag, axis=1, keepdims=True))
        dprobs += growth * dot3(ahalf, halves(state[:, head:]), NT)
        probs = probs_ref[rows, :]
        dscores = probs * (dprobs - jnp.sum(probs * dprobs, axis=1, keepdims=True))
        query = halves(silu(q_ref[rows, :].astype(F32)) * head ** (-0.5))
        unit_k = dot3(halves(growth * dscores), query, TN)
        unit_v = dot3(halves(growth * probs), ahalf, TN)
        unit = jnp.concatenate([unit_k, unit_v], axis=1)
        dprobs_ref[rows, :] = dprobs
        dscores_ref[rows, :] = dscores
        unit_ref[j] = unit
        gsum, total = carry
        return gsum + part, spread(dec_ref[j], 2 * head) * total + unit

    gsum, total = lax.fori_loop(
        0, chunks, chunk, (jnp.zeros((1, head), F32), jnp.zeros((unit_ref.shape[1], 2 * head), F32))
    )
    gain_grad_ref[0] = jnp.broadcast_to(gsum, (8, head))
    all_ref[0] = total


def back_two_kernel(
    levels, q_ref, k_ref, v_ref, decay_ref, keep_ref, probs_ref, scores_ref, weights_ref, states_ref, dec_ref, unit_ref,
    attended_grad_ref, dprobs_ref, dscores_ref, end_ref, table_ref, later_ref, masks_ref,
    term_ref, decay_term_ref,
):
    count = table_ref.shape[1]
    chunks = q_ref.shape[0] // count
    head = q_ref.shape[1]
    diag = on_diagonal(count)
    last = (lax.broadcasted_iota(jnp.int32, (count, 1), 0) == count - 1).astype(F32)

    def chunk(n, adj):
        j = chunks - 1 - n
        rows = pl.ds(pl.multiple_of(j * count, count), count)
        keep = keep_ref[rows, :]
        decay = decay_ref[rows, :]
        powers = jnp.exp(exact_sums(table_ref[...], decay))
        ratios = [powers[l * count : (l + 1) * count] for l in range(levels)]
        growth = powers[levels * count : (levels + 1) * count]
        rest = powers[(levels + 1) * count :]
        qraw = q_ref[rows, :].astype(F32)
        kraw = k_ref[rows, :].astype(F32)
        query = halves(silu(qraw) * head ** (-0.5))
        keys = halves(silu(kraw))
        values = v_ref[rows, :]
        att_grad = halves(attended_grad_ref[rows, :])
        probs, dscores = probs_ref[rows, :], dscores_ref[rows, :]
        state = halves(states_ref[j][:, :head])
        ahalf = halves(adj)
        adj_k, adj_v = (ahalf[0][:, :head], ahalf[1][:, :head]), (ahalf[0][:, head:], ahalf[1][:, head:])
        dweights = halves(unmix(dscores, ratios, keep, masks_ref, diag))
        dquery = dot3(dweights, keys, NN) + dot3(halves(dscores * growth), state, NN)
        term_ref[rows, :head] = bf(silu_slope(qraw) * dquery * head ** (-0.5))
        ending = halves(rest * keep)
        dkey = dot3(dweights, query, TN) + dot3(ending, adj_k, NN)
        term_ref[rows, head : 2 * head] = bf(silu_slope(kraw) * dkey)
        dvalue = dot3(halves(weights_ref[rows, :]), att_grad, TN) + dot3(ending, adj_v, NN)
        term_ref[rows, 2 * head :] = bf(dvalue)
        pair_k = dot3(query, keys, NT)
        pair_v = mm(att_grad[0], values, NT) + mm(att_grad[1], values, NT)
        dkeep = jnp.sum(pair_k * diag, axis=1, keepdims=True) * dscores
        dkeep += jnp.sum(pair_v * diag, axis=1, keepdims=True) * probs
        dkeep += rest * (dot3(keys, adj_k, NT) + mm(values, adj_v[0], NT) + mm(values, adj_v[1], NT))
        for l, ratio in enumerate(ratios):
            mask = masks_ref[l].astype(F32)
            part = dot3(halves(pair_k * mask), halves(dscores * ratio), TN)
            part += dot3(halves(pair_v * mask), halves(probs * ratio), TN)
            dkeep += ratio * part
        dsum = dscores * scores_ref[rows, :] + probs * dprobs_ref[rows, :] - keep * dkeep
        at_end = jnp.sum(adj * states_ref[j + 1], axis=1, keepdims=True)
        at_end = jnp.sum(at_end * on_diagonal(adj.shape[0]), axis=0, keepdims=True)
        dsum += last * at_end
        ddecay = exact_sums(later_ref[...], dsum) - (1.0 - keep) * dkeep
        decay_term_ref[rows, :] = ddecay
        return spread(dec_ref[j], 2 * head) * adj + unit_ref[j]

    lax.fori_loop(0, chunks, chunk, end_ref[0])


def params():
    return pltpu.CompilerParams(vmem_limit_bytes=56 * 2**20)


def call(kernel, grid, ins, outs, name, flops=0):
    return pl.pallas_call(
        kernel,
        grid=grid,
        in_specs=[pl.BlockSpec(block, where) for _, block, where in ins],
        out_specs=[pl.BlockSpec(block, where) for _, _, block, where in outs],
        out_shape=[jax.ShapeDtypeStruct(shape, dtype) for shape, dtype, _, _ in outs],
        compiler_params=params(),
        name=name,
    )(*[array for array, _, _ in ins])


class Slots:
    def __init__(self, seqs, rows, head, slots, chunk):
        self.seqs, self.rows, self.head, self.slots, self.chunk = seqs, rows, head, slots, chunk
        self.chunks = rows // chunk
        paths, masks = decay_tables(chunk)
        self.levels = masks.shape[0]
        self.paths = jnp.asarray(paths, BF16)
        self.masks = jnp.asarray(masks, BF16)

    def row(self, array, width=None, place=0):
        width = array.shape[1] if width is None else width
        return (array, (self.rows, width), lambda b: (b, place))

    def whole(self, array):
        return (array, array.shape, lambda b: (0,) * array.ndim)

    def per(self, array, count):
        return (array, (count,) + array.shape[1:], lambda b: (b,) + (0,) * (array.ndim - 1))

    def out_row(self, width, dtype):
        return ((self.seqs * self.rows, width), dtype, (self.rows, width), lambda b: (b, 0))

    def out_per(self, count, shape, dtype=F32):
        return ((self.seqs * count,) + shape, dtype, (count,) + shape, lambda b: (b,) + (0,) * len(shape))

    def ends(self, qkv, decay, keep):
        m, w = self.slots, 2 * self.head
        tail = self.paths[-self.chunk :]
        return call(
            functools.partial(ends_kernel, self.levels), (self.seqs,),
            [self.row(qkv, self.head, 1), self.row(qkv, self.head, 2), self.row(decay), self.row(keep), self.whole(tail)],
            [self.out_per(self.chunks, (m, w)), self.out_per(self.chunks, (m, 128)), self.out_per(1, (m, w)), self.out_per(1, (m, 128))],
            "slot_ends",
        )

    def attend(self, qkv, gate, decay, keep, start, unit, dec, gain):
        h, m = self.head, self.slots
        return call(
            functools.partial(attend_kernel, self.levels), (self.seqs,),
            [self.row(qkv, h, 0), self.row(qkv, h, 1), self.row(qkv, h, 2), self.row(gate, h, 0), self.row(decay), self.row(keep),
             self.per(start, 1), self.per(unit, self.chunks), self.per(dec, self.chunks), self.whole(gain), self.whole(self.paths),
             self.whole(self.masks)],
            [self.out_row(h, BF16), self.out_row(h, F32), self.out_row(m, F32), self.out_row(m, F32), self.out_row(self.chunk, F32),
             self.out_per(self.chunks + 1, (m, 2 * h))],
            "slot_attend",
        )

    def back_one(self, qkv, gate, decay, keep, grad, attended, probs, states, dec, gain):
        h, m = self.head, self.slots
        return call(
            functools.partial(back_one_kernel, self.levels), (self.seqs,),
            [self.row(qkv, h, 0), self.row(qkv, h, 2), self.row(gate, h, 0), self.row(decay), self.row(keep), self.row(grad),
             self.row(attended), self.row(probs), self.per(states, self.chunks + 1), self.per(dec, self.chunks), self.whole(gain),
             self.whole(self.paths), self.whole(self.masks)],
            [self.out_row(h, BF16), self.out_per(1, (8, h)), self.out_row(h, F32), self.out_row(m, F32), self.out_row(m, F32),
             self.out_per(self.chunks, (m, 2 * h)), self.out_per(1, (m, 2 * h))],
            "slot_back_one",
        )

    def back_two(self, qkv, decay, keep, probs, scores, weights, states, dec, unit, attended_grad, dprobs, dscores, end):
        h, m = self.head, self.slots
        later = self.paths[-2 * self.chunk : -self.chunk].T
        return call(
            functools.partial(back_two_kernel, self.levels), (self.seqs,),
            [self.row(qkv, h, 0), self.row(qkv, h, 1), self.row(qkv, h, 2), self.row(decay), self.row(keep), self.row(probs),
             self.row(scores), self.row(weights), self.per(states, self.chunks + 1), self.per(dec, self.chunks),
             self.per(unit, self.chunks), self.row(attended_grad), self.row(dprobs), self.row(dscores), self.per(end, 1),
             self.whole(self.paths), self.whole(later), self.whole(self.masks)],
            [self.out_row(3 * h, BF16), self.out_row(m, F32)],
            "slot_back_two",
        )

class Place:
    def __init__(self, size):
        self.size = size
        self.line = size // 4
        s = lax.axis_index("seq")
        self.c = lax.axis_index("head")
        self.s = s
        self.x = lax.rem(s, 2)
        self.b = lax.rem(s // 2, 2)
        self.a = s // 4

    def at(self, a, b, x):
        return (a * 2 + b) * 2 + x

    def partner(self):
        return (self.at(self.a, self.b, 1 - self.x), self.c)

    def across(self):
        return (self.at(self.a, 1 - self.b, self.x), self.c)

    def up(self):
        return (self.at(jnp.minimum(self.a + 1, self.line - 1), self.b, self.x), self.c)

    def down(self):
        return (self.at(jnp.maximum(self.a - 1, 0), self.b, self.x), self.c)

    def sibling(self):
        return (self.s, 1 - self.c)

    def has_up(self):
        return self.a < self.line - 1

    def has_down(self):
        return self.a > 0


def signal(sem, device):
    pl.semaphore_signal(sem, inc=1, device_id=device, device_id_type=MESH)


def greet(place, partner=True, across=True, line=True, sibling=False):
    barrier = pltpu.get_barrier_semaphore()
    count = jnp.int32(0)
    if partner:
        signal(barrier, place.partner())
        count = count + 1
    if sibling:
        signal(barrier, place.sibling())
        count = count + 1
    if across:
        signal(barrier, place.across())
        count = count + 1
    if line:
        pl.when(place.has_up())(lambda: signal(barrier, place.up()))
        pl.when(place.has_down())(lambda: signal(barrier, place.down()))
        count = count + place.has_up().astype(jnp.int32) + place.has_down().astype(jnp.int32)
    pl.semaphore_wait(barrier, count)


def remote(src, dst, send, recv, device):
    return pltpu.make_async_remote_copy(
        src_ref=src, dst_ref=dst, send_sem=send, recv_sem=recv, device_id=device, device_id_type=MESH
    )


class Gather:
    def __init__(self, place, shard, full, unit, offset, width, sems, late):
        self.pl, self.shard, self.full = place, shard, full
        self.unit, self.offset, self.width, self.late = unit, offset, width, late
        self.x_sem, self.b_sem, self.up_sem, self.down_sem = sems

    def part(self, start, count):
        rows = pl.ds(start * self.unit, count * self.unit)
        if self.width == self.full.shape[1]:
            return self.full.at[rows]
        return self.full.at[rows, pl.ds(self.offset, self.width)]

    def mine(self, x):
        if self.shard.shape[1] == self.width:
            return self.shard
        return self.shard.at[:, pl.ds(x * self.width, self.width)]

    def x_copy(self):
        p = self.pl
        return remote(self.mine(1 - p.x), self.part(p.s, 1), self.x_sem.at[0], self.x_sem.at[1], p.partner())

    def own_copy(self):
        return pltpu.make_async_copy(self.mine(self.pl.x), self.part(self.pl.s, 1), self.x_sem.at[2])

    def block(self, a):
        p = self.pl
        if self.late:
            return self.part(4 * a, 4)
        return self.part(4 * a + 2 * p.b, 2)

    def b_copy(self, i, a):
        p = self.pl
        return remote(
            self.part(4 * a + 2 * p.b, 2), self.part(4 * a + 2 * p.b, 2),
            self.b_sem.at[0, i], self.b_sem.at[1, i], p.across(),
        )

    def line_copy(self, way, h):
        p = self.pl
        if way == "up":
            blk = self.block(jnp.maximum(p.a - (h - 1), 0))
            return remote(blk, blk, self.up_sem.at[0, h - 1], self.up_sem.at[1, h - 1], p.up())
        blk = self.block(jnp.minimum(p.a + (h - 1), p.line - 1))
        return remote(blk, blk, self.down_sem.at[0, h - 1], self.down_sem.at[1, h - 1], p.down())

    def sends(self, way, h):
        p = self.pl
        if way == "up":
            return jnp.logical_and(p.has_up(), p.a - (h - 1) >= 0)
        return jnp.logical_and(p.has_down(), p.a + (h - 1) <= p.line - 1)

    def gets(self, way, h):
        p = self.pl
        if way == "up":
            return p.a - h >= 0
        return p.a + h <= p.line - 1

    def got(self, way, h):
        p = self.pl
        if way == "up":
            return jnp.maximum(p.a - h, 0)
        return jnp.minimum(p.a + h, p.line - 1)

    def slot(self, way, h):
        return h if way == "up" else self.pl.line - 1 + h

    def start_x(self):
        self.x_copy().start()
        self.own_copy().start()

    def stage(self, h):
        p = self.pl
        if h == 0:
            self.own_copy().wait()
            self.x_copy().wait_recv()
            if self.late:
                self.b_copy(0, p.a).start()
            else:
                for way in ("up", "down"):
                    pl.when(self.sends(way, 1))(lambda way=way: self.line_copy(way, 1).start())
                self.b_copy(0, p.a).start()
            return
        if self.late:
            if h == 1:
                self.b_copy(0, p.a).wait_recv()
                for way in ("up", "down"):
                    pl.when(self.sends(way, 1))(lambda way=way: self.line_copy(way, 1).start())
                return
            h = h - 1
        for way in ("up", "down"):

            def go(way=way):
                self.line_copy(way, h).wait_recv()
                if not self.late:
                    self.b_copy(self.slot(way, h), self.got(way, h)).start()

            def on(way=way):
                self.line_copy(way, h + 1).start()

            pl.when(self.gets(way, h))(go)
            if h + 1 <= p.line - 1:
                pl.when(self.sends(way, h + 1))(on)

    def stages(self):
        return self.pl.line + (1 if self.late else 0)

    def finish(self):
        p = self.pl
        self.x_copy().wait_send()
        self.b_copy(0, p.a).wait_send()
        if not self.late:
            self.b_copy(0, p.a).wait_recv()
        for way in ("up", "down"):
            for h in range(1, p.line):
                pl.when(self.sends(way, h))(lambda way=way, h=h: self.line_copy(way, h).wait_send())
                if not self.late:

                    def both(way=way, h=h):
                        cp = self.b_copy(self.slot(way, h), self.got(way, h))
                        cp.wait_send()
                        cp.wait_recv()

                    pl.when(self.gets(way, h))(both)


def gather_sems(line):
    return [
        pltpu.SemaphoreType.DMA((3,)),
        pltpu.SemaphoreType.DMA((2, 2 * line - 1)),
        pltpu.SemaphoreType.DMA((2, line - 1)),
        pltpu.SemaphoreType.DMA((2, line - 1)),
    ]


def gather_ops(gathers, ahead):
    steps = []
    n = len(gathers)
    for k in range(min(ahead, n)):
        steps.append(gathers[k].start_x)
    steps.append(functools.partial(gathers[0].stage, 0))
    for k in range(n):
        if k + ahead < n:
            steps.append(gathers[k + ahead].start_x)
        if k + 1 < n:
            steps.append(functools.partial(gathers[k + 1].stage, 0))
        for h in range(1, gathers[k].stages()):
            steps.append(functools.partial(gathers[k].stage, h))
    for g in gathers:
        steps.append(g.finish)
    return steps

def prefix_kernel(size, back, own_ref, dec_ref, start_ref, peer, peer_dec, line, out, p_sem, d_sem, l_sem):
    p = Place(size)
    greet(p, partner=False)
    seqs, slots, width = own_ref.shape
    half = width // 2
    pieces = [(b, h) for b in range(seqs) for h in range(2)]

    def cut(ref, piece):
        return ref.at[piece[0], :, pl.ds(piece[1] * half, half)]

    def peer_copy(i, piece):
        return remote(cut(own_ref, piece), cut(peer, piece), p_sem.at[0, i], p_sem.at[1, i], p.across())

    if back:
        has_prev, has_next, after = p.has_up(), p.has_down(), p.down()
    else:
        has_prev, has_next, after = p.has_down(), p.has_up(), p.up()

    def line_copy(i, piece):
        return remote(cut(out, piece), cut(line, piece), l_sem.at[0, i], l_sem.at[1, i], after)

    dec_copy = remote(dec_ref, peer_dec, d_sem.at[0], d_sem.at[1], p.across())
    dec_copy.start()
    for i, piece in enumerate(pieces):
        peer_copy(i, piece).start()
    own_first = (p.b == 1) if back else (p.b == 0)
    first = own_first.astype(F32)
    dec_copy.wait_recv()
    for i, piece in enumerate(pieces):
        peer_copy(i, piece).wait_recv()
        dec_own = spread(dec_ref[piece[0]], half)
        dec_peer = spread(peer_dec[piece[0]], half)
        own, other = cut(own_ref, piece)[...], cut(peer, piece)[...]
        both = first * (dec_peer * own + other) + (1.0 - first) * (dec_own * other + own)
        here = cut(out, piece)

        def go_on():
            line_copy(i, piece).wait_recv()
            came = cut(line, piece)[...]
            here[...] = dec_own * dec_peer * came + both
            cut(start_ref, piece)[...] = first * came + (1.0 - first) * (dec_peer * came + other)

        def begin():
            here[...] = both
            cut(start_ref, piece)[...] = (1.0 - first) * other

        pl.when(has_prev)(go_on)
        pl.when(jnp.logical_not(has_prev))(begin)
        pl.when(has_next)(lambda i=i, piece=piece: line_copy(i, piece).start())
    dec_copy.wait_send()
    for i, piece in enumerate(pieces):
        peer_copy(i, piece).wait_send()
        pl.when(has_next)(lambda i=i, piece=piece: line_copy(i, piece).wait_send())


VM = pl.BlockSpec(memory_space=pltpu.VMEM)
ANY = pl.BlockSpec(memory_space=HBM)


def remote_params(number, mib=56):
    return pltpu.CompilerParams(collective_id=number, has_side_effects=True, vmem_limit_bytes=mib * 2**20)


def prefix(size, number, own, dec, back):
    shape = own.shape
    count = 2 * shape[0]
    return pl.pallas_call(
        functools.partial(prefix_kernel, size, back),
        out_shape=jax.ShapeDtypeStruct(shape, F32),
        in_specs=[VM, VM],
        out_specs=VM,
        scratch_shapes=[
            pltpu.VMEM(shape, F32), pltpu.VMEM(dec.shape, F32), pltpu.VMEM(shape, F32), pltpu.VMEM(shape, F32),
            pltpu.SemaphoreType.DMA((2, count)), pltpu.SemaphoreType.DMA((2,)), pltpu.SemaphoreType.DMA((2, count)),
        ],
        compiler_params=remote_params(number),
        name="slot_suffix" if back else "slot_prefix",
    )(own, dec)


STRIPS = 4


class Fold:
    def __init__(self, place, part, sib, sent, came, sems):
        self.p, self.part, self.sib, self.sent, self.came = place, part, sib, sent, came
        self.s_sem, self.x_sem = sems
        self.rows = part.shape[2] // STRIPS

    def strip(self, r):
        return pl.ds(r * self.rows, self.rows)

    def sib_copy(self, far, r):
        p = self.p
        x = 1 - p.x if far else p.x
        i = (0 if far else STRIPS) + r
        return remote(
            self.part.at[1 - p.c, x, self.strip(r)], self.sib.at[1 if far else 0, self.strip(r)],
            self.s_sem.at[0, i], self.s_sem.at[1, i], p.sibling(),
        )

    def x_copy(self, r):
        return remote(
            self.sent.at[self.strip(r)], self.came.at[self.strip(r)], self.x_sem.at[0, r], self.x_sem.at[1, r], self.p.partner()
        )

    def start(self):
        for r in range(STRIPS):
            self.sib_copy(True, r).start()
        for r in range(STRIPS):
            self.sib_copy(False, r).start()

    def cross(self, r):
        p = self.p
        self.sib_copy(True, r).wait_recv()
        own = self.part[p.c, 1 - p.x, self.strip(r)].astype(F32)
        self.sent[self.strip(r)] = bf(own + self.sib[1, self.strip(r)].astype(F32))
        self.x_copy(r).start()

    def total(self, r):
        p = self.p
        self.sib_copy(False, r).wait_recv()
        self.x_copy(r).wait_recv()
        own = self.part[p.c, p.x, self.strip(r)].astype(F32) + self.sib[0, self.strip(r)].astype(F32)
        return own + self.came[self.strip(r)].astype(F32)

    def finish(self):
        for r in range(STRIPS):
            self.sib_copy(True, r).wait_send()
            self.sib_copy(False, r).wait_send()
            self.x_copy(r).wait_send()


def fold_scratch(rows, width):
    return [
        pltpu.VMEM((2, rows, width), BF16), pltpu.VMEM((rows, width), BF16), pltpu.VMEM((rows, width), BF16),
        pltpu.SemaphoreType.DMA((2, 2 * STRIPS)), pltpu.SemaphoreType.DMA((2, STRIPS)),
    ]


class Share:
    def __init__(self, place, out, sems):
        self.p, self.out = place, out
        self.x_sem, self.s_sem = sems
        self.rows = out.shape[2] // STRIPS

    def strip(self, r):
        return pl.ds(r * self.rows, self.rows)

    def x_copy(self, r):
        p = self.p
        block = self.out.at[p.c, p.x, self.strip(r)]
        return remote(block, block, self.x_sem.at[0, r], self.x_sem.at[1, r], p.partner())

    def s_copy(self, far, r):
        p = self.p
        block = self.out.at[p.c, 1 - p.x if far else p.x, self.strip(r)]
        i = (0 if far else STRIPS) + r
        return remote(block, block, self.s_sem.at[0, i], self.s_sem.at[1, i], p.sibling())

    def put(self, r, value):
        self.out[self.p.c, self.p.x, self.strip(r)] = value
        self.x_copy(r).start()
        self.s_copy(False, r).start()

    def forward(self, r):
        self.x_copy(r).wait_recv()
        self.s_copy(True, r).start()

    def finish(self):
        for r in range(STRIPS):
            self.x_copy(r).wait_send()
            for far in (False, True):
                self.s_copy(far, r).wait_send()
                self.s_copy(far, r).wait_recv()


SHARE_SEMS = [pltpu.SemaphoreType.DMA((2, STRIPS)), pltpu.SemaphoreType.DMA((2, 2 * STRIPS))]


def inverse_rms(values):
    return lax.rsqrt(jnp.mean(values * values, axis=-1, keepdims=True) + EPS)


def norm_back(grad, values, gain):
    scale = inverse_rms(values)
    u = grad * gain
    down = scale * u - values * (scale * scale * scale) * jnp.mean(u * values, axis=-1, keepdims=True)
    return down, jnp.sum(grad * values * scale, axis=0, keepdims=True)


def blend_kernel(size, part, tokens, gain, residual, normed, sib, sent, came, s1, s2, s3, s4):
    p = Place(size)
    greet(p, across=False, line=False, sibling=True)
    fold = Fold(p, part, sib, sent, came, (s1, s2))
    share = Share(p, normed, (s3, s4))
    fold.start()
    for r in range(STRIPS):
        fold.cross(r)
    for r in range(STRIPS):
        value = tokens[p.c, fold.strip(r)].astype(F32) + fold.total(r)
        residual[fold.strip(r)] = value
        share.put(r, bf(value * inverse_rms(value) * gain[...]))
    for r in range(STRIPS):
        share.forward(r)
    share.finish()
    fold.finish()


def blend(size, number, part, tokens, gain):
    _, _, rows, width = part.shape
    return pl.pallas_call(
        functools.partial(blend_kernel, size),
        out_shape=[jax.ShapeDtypeStruct((rows, width), F32), jax.ShapeDtypeStruct(part.shape, BF16)],
        in_specs=[VM] * 3,
        out_specs=[VM] * 2,
        scratch_shapes=fold_scratch(rows, width) + SHARE_SEMS,
        compiler_params=remote_params(number),
        name="blend",
    )(part, tokens, gain)


def blend_back_kernel(size, part, grad_out, residual, gain, residual_grad, low, gain_grad, sib, sent, came, s1, s2, s3, s4):
    p = Place(size)
    greet(p, across=False, line=False, sibling=True)
    fold = Fold(p, part, sib, sent, came, (s1, s2))
    share = Share(p, low, (s3, s4))
    fold.start()
    for r in range(STRIPS):
        fold.cross(r)
    gains = jnp.zeros((1, part.shape[3]), F32)
    for r in range(STRIPS):
        down, more = norm_back(fold.total(r), residual[fold.strip(r)], gain[...])
        value = grad_out[p.c, fold.strip(r)].astype(F32) + down
        gains += more
        residual_grad[fold.strip(r)] = value
        share.put(r, bf(value))
    gain_grad[...] = gains
    for r in range(STRIPS):
        share.forward(r)
    share.finish()
    fold.finish()


def blend_back(size, number, part, grad_out, residual, gain):
    _, _, rows, width = part.shape
    return pl.pallas_call(
        functools.partial(blend_back_kernel, size),
        out_shape=[
            jax.ShapeDtypeStruct((rows, width), F32), jax.ShapeDtypeStruct(part.shape, BF16), jax.ShapeDtypeStruct((1, width), F32)
        ],
        in_specs=[VM] * 4,
        out_specs=[VM] * 3,
        scratch_shapes=fold_scratch(rows, width) + SHARE_SEMS,
        compiler_params=remote_params(number),
        name="blend_back",
    )(part, grad_out, residual, gain)


def finish_kernel(
    size, part, ff_part, tokens, residual, residual_grad, gain, input_grad, output, gain_grad,
    sib, sent, came, s1, s2, sib2, sent2, came2, t1, t2, out_sem,
):
    p = Place(size)
    greet(p, across=False, line=False, sibling=True)
    fold = Fold(p, part, sib, sent, came, (s1, s2))
    ff = Fold(p, ff_part, sib2, sent2, came2, (t1, t2))
    ff.start()
    fold.start()
    for r in range(STRIPS):
        ff.cross(r)
        fold.cross(r)
    gains = jnp.zeros((1, part.shape[3]), F32)

    def out_copy(ref, k, r):
        block = ref.at[p.c, fold.strip(r)]
        return remote(block, block, out_sem.at[0, k * STRIPS + r], out_sem.at[1, k * STRIPS + r], p.sibling())

    for r in range(STRIPS):
        output[p.c, fold.strip(r)] = bf(residual[fold.strip(r)] + ff.total(r))
        out_copy(output, 0, r).start()
        down, more = norm_back(fold.total(r), tokens[p.c, fold.strip(r)].astype(F32), gain[...])
        gains += more
        input_grad[p.c, fold.strip(r)] = residual_grad[fold.strip(r)] + down
        out_copy(input_grad, 1, r).start()
    gain_grad[...] = gains
    for r in range(STRIPS):
        out_copy(output, 0, r).wait()
        out_copy(input_grad, 1, r).wait()
    ff.finish()
    fold.finish()


def finish(size, number, part, ff_part, tokens, residual, residual_grad, gain):
    _, _, rows, width = part.shape
    return pl.pallas_call(
        functools.partial(finish_kernel, size),
        out_shape=[
            jax.ShapeDtypeStruct((2, rows, width), F32), jax.ShapeDtypeStruct((2, rows, width), BF16),
            jax.ShapeDtypeStruct((1, width), F32),
        ],
        in_specs=[VM] * 6,
        out_specs=[VM] * 3,
        scratch_shapes=fold_scratch(rows, width) * 2 + [pltpu.SemaphoreType.DMA((2, 2 * STRIPS))],
        compiler_params=remote_params(number),
        name="finish",
    )(part, ff_part, tokens, residual, residual_grad, gain)


class Scatter:
    def __init__(self, place, grad, out, unit, offset, width, bufs, sems):
        self.p, self.grad, self.out = place, grad, out
        self.unit, self.offset, self.width = unit, offset, width
        self.whole = out.shape[-1] == width
        self.own, self.peer, self.line, self.total = bufs
        self.o_sem, self.b_sem, self.l_sem, self.x_sem = sems

    def block(self, a, b):
        rows = pl.ds((4 * a + 2 * b) * self.unit, 2 * self.unit)
        if self.width == self.grad.shape[1]:
            return self.grad.at[rows]
        return self.grad.at[rows, pl.ds(self.offset, self.width)]

    def own_copy(self, a):
        return pltpu.make_async_copy(self.block(a, self.p.b), self.own.at[a], self.o_sem.at[a])

    def b_copy(self, a):
        return remote(self.block(a, 1 - self.p.b), self.peer.at[a], self.b_sem.at[0, a], self.b_sem.at[1, a], self.p.across())

    def send_line(self, d, way):
        p = self.p
        if way == "up":
            return remote(self.own.at[d], self.line.at[d], self.l_sem.at[0, d], self.l_sem.at[1, d], p.up())
        slot = jnp.where(p.a - 1 == d, p.line, d)
        return remote(self.own.at[d], self.line.at[slot], self.l_sem.at[0, d], self.l_sem.at[1, slot], p.down())

    def wait_line(self, d, slot):
        p = self.p
        remote(self.own.at[d], self.line.at[slot], self.l_sem.at[0, d], self.l_sem.at[1, slot], p.across()).wait_recv()

    def start(self):
        lines = self.p.line
        for a in sorted(range(lines), key=lambda a: -abs(2 * a - lines + 1)):
            self.b_copy(a).start()
            self.own_copy(a).start()

    def strips(self, do):
        rows, width = self.own.shape[1], self.own.shape[2]
        step = max(r for r in (16, 32, 64, 128) if rows % r == 0 and (r == 16 or r * width <= 64 * 1024))

        def one(i, carry):
            do(pl.ds(pl.multiple_of(i * step, step), step))
            return carry

        lax.fori_loop(0, rows // step, one, 0)

    def ready(self, d):
        self.own_copy(d).wait()
        self.b_copy(d).wait_recv()

    def add(self, d, lines):
        def do(rows):
            value = self.own[d, rows].astype(F32) + self.peer[d, rows].astype(F32)
            for slot in lines:
                value += self.line[slot, rows].astype(F32)
            self.own[d, rows] = bf(value)

        self.strips(do)

    def hop(self, j):
        p = self.p

        def go(d, way, has_prev):
            self.ready(d)

            def more():
                self.wait_line(d, d)
                self.add(d, [d])

            pl.when(has_prev)(more)
            pl.when(jnp.logical_not(has_prev))(lambda: self.add(d, []))
            self.send_line(d, way).start()

        up = p.line - 1 - j
        pl.when(up > p.a)(lambda: go(up, "up", p.has_down()))
        pl.when(j < p.a)(lambda: go(j, "down", p.has_up()))

    def last(self):
        p = self.p
        lines = p.line
        for a in range(lines):

            def here(a=a):
                self.ready(a)
                slots = []
                if a > 0:
                    self.wait_line(a, a)
                    slots.append(a)
                if a < lines - 1:
                    self.wait_line(a, lines)
                    slots.append(lines)

                def do(rows):
                    value = self.own[a, rows].astype(F32) + self.peer[a, rows].astype(F32)
                    for slot in slots:
                        value += self.line[slot, rows].astype(F32)
                    self.total[rows] = value

                self.strips(do)

            pl.when(p.a == a)(here)
        self.x_copy().start()
        if not self.whole:
            self.out_copy().start()

    def half(self, x):
        return self.total.at[pl.ds(x * self.unit, self.unit)]

    def place(self):
        return self.out.at[:, pl.ds(self.p.x * self.width, self.width)]

    def x_copy(self):
        p = self.p
        where = self.out.at[1] if self.whole else self.place()
        return remote(self.half(1 - p.x), where, self.x_sem.at[0], self.x_sem.at[1], p.partner())

    def out_copy(self):
        return pltpu.make_async_copy(self.half(self.p.x), self.place(), self.x_sem.at[2])

    def finish(self):
        p = self.p
        self.x_copy().wait()
        if self.whole:
            self.out[0] = self.out[1] + self.half(p.x)[...]
        else:
            self.out_copy().wait()
        for a in range(p.line):
            self.b_copy(a).wait_send()
            pl.when(a > p.a)(lambda a=a: self.send_line(a, "up").wait_send())
            pl.when(a < p.a)(lambda a=a: self.send_line(a, "down").wait_send())


def scatter_scratch(line, block):
    return [
        pltpu.VMEM((line,) + block, BF16), pltpu.VMEM((line,) + block, BF16), pltpu.VMEM((line + 1,) + block, BF16),
        pltpu.VMEM(block, F32),
        pltpu.SemaphoreType.DMA((line,)), pltpu.SemaphoreType.DMA((2, line)), pltpu.SemaphoreType.DMA((2, line + 1)),
        pltpu.SemaphoreType.DMA((3,)),
    ]


def greet_all(place):
    barrier = pltpu.get_barrier_semaphore()

    def one(i, carry):
        signal(barrier, (lax.rem(place.s + i // 2, place.size), lax.rem(place.c + lax.rem(i, 2), 2)))
        return carry

    lax.fori_loop(1, 2 * place.size, one, 0)
    pl.semaphore_wait(barrier, 2 * place.size - 1)


class Smalls:
    def __init__(self, place, pack, out, came, sems):
        self.p, self.pack, self.out, self.came, self.sems = place, pack, out, came, sems

    def copy(self, i):
        p = self.p
        s = lax.rem(p.s + i // 2, p.size)
        return remote(
            self.pack.at[s], self.came.at[i], self.sems.at[0, i], self.sems.at[1, i], (s, lax.rem(p.c + lax.rem(i, 2), 2))
        )

    def start(self):
        lax.fori_loop(1, 2 * self.p.size, lambda i, c: (self.copy(i).start(), c)[1], 0)

    def finish(self):
        def one(i, total):
            self.copy(i).wait()
            return total + self.came[i]

        self.out[...] = lax.fori_loop(1, 2 * self.p.size, one, self.pack[self.p.s])


def scatter_kernel(size, plan, *refs):
    p = Place(size)
    grads = max(i for i, _, _, _ in plan) + 1
    outs = len(plan)
    ins, refs = refs[: grads + 1], refs[grads + 1 :]
    out_refs, refs = refs[: outs + 1], refs[outs + 1 :]
    came, s_sem = refs[:2]
    refs = refs[2:]
    greet_all(p)
    smalls = Smalls(p, ins[grads], out_refs[outs], came, s_sem)
    work = []
    for n, (i, unit, offset, width) in enumerate(plan):
        mine = refs[8 * n : 8 * n + 8]
        work.append(Scatter(p, ins[i], out_refs[n], unit, offset, width, mine[:4], mine[4:]))
    work[0].start()
    smalls.start()
    for n, chunk in enumerate(work):
        if n + 1 < len(work):
            work[n + 1].start()
        for j in range(p.line - 1):
            chunk.hop(j)
        chunk.last()
    smalls.finish()
    for chunk in work:
        chunk.finish()


def scatter(size, number, plan, grads, pack):
    line = size // 4
    shapes, specs, scratch = [], [], []
    for i, unit, offset, width, whole in plan:
        shapes.append(jax.ShapeDtypeStruct((2, unit, width) if whole else (unit, 2 * width), F32))
        specs.append(VM if whole else ANY)
        scratch += scatter_scratch(line, (2 * unit, width))
    return pl.pallas_call(
        functools.partial(scatter_kernel, size, [entry[:4] for entry in plan]),
        out_shape=shapes + [jax.ShapeDtypeStruct(pack.shape[1:], F32)],
        in_specs=[ANY] * len(grads) + [VM],
        out_specs=specs + [VM],
        scratch_shapes=[pltpu.VMEM((2 * size,) + pack.shape[1:], F32), pltpu.SemaphoreType.DMA((2, 2 * size))] + scratch,
        compiler_params=remote_params(number, 60),
        name="scatter",
    )(*grads, pack)


class Swap:
    def __init__(self, place, own, both, sems):
        self.p, self.own, self.both, self.sems = place, own, both, sems

    def start(self):
        p = self.p
        self.cross = remote(self.own, self.both.at[:, p.x], self.sems.at[0], self.sems.at[1], p.partner())
        self.keep = pltpu.make_async_copy(self.own, self.both.at[:, p.x], self.sems.at[2])
        self.cross.start()
        self.keep.start()

    def finish(self):
        self.keep.wait()
        self.cross.wait()


def gather_kernel(size, plan, swaps, *refs):
    p = Place(size)
    shards = len(plan)
    fulls = max(i for i, _, _, _, _ in plan) + 1
    ins, refs = refs[: shards + swaps], refs[shards + swaps :]
    outs, refs = refs[: fulls + swaps], refs[fulls + swaps :]
    greet(p)
    work = []
    for n, (i, unit, offset, width, late) in enumerate(plan):
        work.append(Gather(p, ins[n], outs[i], unit, offset, width, refs[4 * n : 4 * n + 4], late))
    moves = [Swap(p, ins[shards + n], outs[fulls + n], refs[4 * shards + n]) for n in range(swaps)]
    steps = gather_ops(work, 3)
    for step in steps[: -len(work)]:
        step()
    for move in moves:
        move.start()
    for step in steps[-len(work) :]:
        step()
    for move in moves:
        move.finish()


def gather(size, number, plan, shards, fulls, tokens):
    line = size // 4
    scratch = []
    for _ in plan:
        scratch += gather_sems(line)
    shapes = [jax.ShapeDtypeStruct(shape, BF16) for shape in fulls]
    for array in tokens:
        shapes.append(jax.ShapeDtypeStruct((array.shape[0], 2) + array.shape[1:], BF16))
        scratch.append(pltpu.SemaphoreType.DMA((3,)))
    return pl.pallas_call(
        functools.partial(gather_kernel, size, plan, len(tokens)),
        out_shape=shapes,
        in_specs=[ANY] * (len(shards) + len(tokens)),
        out_specs=[ANY] * len(shapes),
        scratch_shapes=scratch,
        compiler_params=remote_params(number, 16),
        name="gather",
    )(*shards, *tokens)


def dot(left, right, dims, dtype=F32):
    return lax.dot_general(left, right, dims, preferred_element_type=F32).astype(dtype)


def lanes(row):
    return jnp.pad(row.reshape(-1), (0, 128 - row.size))


def shards(
    tokens, grad_out, query_weight, key_weight, value_weight, forget_weight, forget_bias, outgate_weight, output_weight,
    slot_gain, first_gain, second_gain, gate_weight, up_weight, down_weight,
):
    size = lax.axis_size("seq")
    x = lax.rem(lax.axis_index("seq"), 2)
    c = lax.axis_index("head")
    seqs, block, width = tokens.shape
    heads_here, slot_part = forget_bias.shape
    slots = slot_part * size
    head = slot_gain.shape[0] * size
    unit = first_gain.shape[0]
    hidden = gate_weight.shape[1] // 2
    rows = seqs * 2 * block
    pack = jnp.stack([lanes(first_gain), lanes(second_gain), lanes(slot_gain), lanes(forget_bias)] + [jnp.zeros(128, BF16)] * 12)
    plan = [
        (0, unit, 0, head, False), (0, unit, head, head, False), (0, unit, 2 * head, head, False),
        (1, unit, 0, head, False), (1, unit, head, 2 * slots, False), (2, unit, 0, head, False),
        (3, 16, 0, 128, False),
        (4, unit, 0, hidden, False), (4, unit, hidden, hidden, False), (5, unit, 0, hidden, False),
    ]
    fulls = [
        (width, 3 * head), (width, head + 2 * slots), (width, head), (16 * size, 128), (width, 2 * hidden), (width, hidden),
    ]
    qkv_full, gate_full, out_full, small_full, ff_full, down_full, tok, gout = gather(
        size, 0, plan,
        (query_weight, key_weight, value_weight, outgate_weight, forget_weight, output_weight.T, pack, gate_weight, up_weight,
         down_weight.T),
        fulls, (tokens, grad_out),
    )
    small = small_full.reshape(size, 16, 128).astype(F32)
    first_full = small[:, 0, :unit].reshape(1, width)
    second_full = small[:, 1, :unit].reshape(1, width)
    slot_full = small[:, 2, : head // size].reshape(1, head)
    bias_full = small[:, 3, : heads_here * slot_part].reshape(size, heads_here, slot_part)
    bias_full = jnp.moveaxis(bias_full, 1, 0).reshape(heads_here, slots)

    def own_head(array, axis):
        return jnp.where(x == 0, *jnp.split(array, 2, axis=axis))

    inputs = tok.reshape(rows, width).astype(F32)
    normed_one = (inputs * inverse_rms(inputs) * first_full).astype(BF16)
    qkv = dot(normed_one, qkv_full, NN, BF16)
    gates = dot(normed_one, gate_full, NN)
    logit = own_head(gates[:, head:], 1) + own_head(bias_full, 0)
    decay = -jax.nn.softplus(-logit) / TAU
    keep = -jnp.expm1(decay)
    chunk = min(CHUNK, 2 * block)
    slot = Slots(seqs, 2 * block, head, slots, chunk)
    units, decs, ends, end_decs = slot.ends(qkv, decay, keep)
    start = prefix(size, 1, ends, end_decs, False)
    gated, attended, probs, scores, weights, states = slot.attend(qkv, gates, decay, keep, start, units, decs, slot_full)
    shape = (seqs, 2, block, width)
    mixed = dot(gated, out_full, NT, BF16).reshape(shape)
    residual, normed_two = blend(size, 2, mixed, tokens, second_full)
    normed_two = normed_two.reshape(rows, width)
    ff = dot(normed_two, ff_full, NN)
    ff_gate, ff_up = ff[:, :hidden], ff[:, hidden:]
    sig = jax.nn.sigmoid(ff_gate)
    activated = (ff_gate * sig * ff_up).astype(BF16)
    ff_part = dot(activated, down_full, NT, BF16).reshape(shape)
    gout = gout.reshape(rows, width)
    act_grad = dot(gout, down_full, NN)
    ff_term = jnp.concatenate(
        [act_grad * ff_up * (sig + ff_gate * sig * (1.0 - sig)), act_grad * ff_gate * sig], axis=1
    ).astype(BF16)
    down_grad = dot(gout, activated, TN, BF16)
    ff_grad = dot(normed_two, ff_term, TN, BF16)
    normed_two_grad = dot(ff_term, ff_full, NT, BF16).reshape(shape)
    residual_grad, low, second_part = blend_back(size, 3, normed_two_grad, grad_out, residual, second_full)
    low = low.reshape(rows, width)
    gated_grad = dot(low, out_full, NN)
    out_grad = dot(low, gated, TN, BF16)
    gate_term, slot_part_grad, att_grad, dprobs, dscores, back_units, back_ends = slot.back_one(
        qkv, gates, decay, keep, gated_grad, attended, probs, states, decs, slot_full
    )
    finals = prefix(size, 4, back_ends, end_decs, True)
    qkv_term, decay_term = slot.back_two(
        qkv, decay, keep, probs, scores, weights, states, decs, back_units, att_grad, dprobs, dscores, finals
    )
    forget_term = (decay_term * jax.nn.sigmoid(-logit) / TAU).astype(BF16)
    none = jnp.zeros_like(forget_term)
    gates_term = jnp.concatenate(
        [gate_term, jnp.where(x == 0, forget_term, none), jnp.where(x == 0, none, forget_term)], axis=1
    )
    qkv_grad = dot(normed_one, qkv_term, TN, BF16)
    gates_grad = dot(normed_one, gates_term, TN, BF16)
    normed_one_grad = (dot(qkv_term, qkv_full, NT) + dot(gates_term, gate_full, NT)).astype(BF16).reshape(shape)
    input_grad, output, first_part = finish(size, 5, normed_one_grad, ff_part, tokens, residual, residual_grad, first_full)
    bias_part = jnp.sum(forget_term.astype(F32), axis=0)
    which = jnp.arange(2 * heads_here) == heads_here * c + x
    bias_part = jnp.where(which[:, None], bias_part[None, :], 0.0).reshape(2 * heads_here, size, slot_part)
    slot_part_sum = jnp.sum(slot_part_grad[:, 0], axis=0)

    def rows_of(array):
        array = array.reshape(size, -1)
        return jnp.pad(array, ((0, 0), (0, 128 - array.shape[1])))

    zero = jnp.zeros((size, 128), F32)
    packed = jnp.stack(
        [rows_of(first_part), rows_of(second_part), rows_of(slot_part_sum), rows_of(jnp.moveaxis(bias_part, 1, 0))] + [zero] * 4, axis=1
    )
    grads = (ff_grad, down_grad, out_grad, qkv_grad, gates_grad)
    plan = [
        (0, unit, 0, hidden, False), (0, unit, hidden, hidden, False), (1, unit, 0, hidden, False), (2, unit, 0, head, False),
        (3, unit, 0, head, False), (3, unit, head, head, False), (3, unit, 2 * head, head, False), (4, unit, 0, head, False),
        (4, unit, head, 2 * slots, True),
    ]
    gate_grad, up_grad, down_grad, output_grad, query_grad, key_grad, value_grad, outgate_grad, forget_grad, sums = scatter(
        size, 6, plan, grads, packed
    )
    bias_grad = sums[3, : 2 * heads_here * slot_part].reshape(2, heads_here, slot_part)
    bias_grad = jnp.where(c == 0, bias_grad[0], bias_grad[1])
    return (
        output, input_grad, query_grad, key_grad, value_grad, forget_grad[0], bias_grad, outgate_grad, output_grad.T,
        sums[2, : head // size], sums[0, :unit], sums[1, :unit], gate_grad, up_grad, down_grad.T,
    )


def solution(mesh):
    row, column, vector, token = P("seq", "head"), P("head", "seq"), P("seq"), P(None, "seq", None)
    return jax.shard_map(
        shards,
        mesh=mesh,
        in_specs=(token, token, row, row, row, row, column, row, column, vector, vector, vector, row, row, column),
        out_specs=(token, token, row, row, row, row, column, row, column, vector, vector, vector, row, row, column),
        check_vma=False,
    )
```

```python
import functools

import jax
import jax.numpy as jnp
import numpy as np
from jax import lax
from jax.experimental import pallas as pl
from jax.experimental.pallas import tpu as pltpu
from jax.sharding import PartitionSpec as P

F32, BF16 = jnp.float32, jnp.bfloat16
MESH = pl.DeviceIdType.MESH
HBM = pltpu.HBM
EPS = 1e-06
TAU = 8.0


CHUNK = 256
NT = (((1,), (1,)), ((), ()))
NN = (((1,), (0,)), ((), ()))
TN = (((0,), (0,)), ((), ()))


def decay_tables(count):
    at = np.arange(count)
    paths, masks = [], []
    half = count // 2
    while half >= 1:
        block, second = at // (2 * half), (at // half) % 2 == 1
        edge = block * 2 * half + half - 1
        r, t = at[None, :], at[:, None]
        fore = second[:, None] & (r > edge[:, None]) & (r <= t)
        back = ~second[:, None] & (r > t) & (r <= edge[:, None])
        paths.append(fore | back)
        masks.append((block[:, None] == block[None, :]) & second[:, None] & ~second[None, :])
        half //= 2
    paths.append(at[None, :] <= at[:, None])
    paths.append(at[None, :] > at[:, None])
    return np.concatenate(paths, 0), np.stack(masks)


def bf(x):
    return x.astype(BF16)


def halves(x):
    hi = bf(x)
    return hi, bf(x - hi.astype(F32))


def mm(a, b, dims):
    return lax.dot_general(a, b, dims, preferred_element_type=F32)


def dot3(a, b, dims):
    return mm(a[0], b[0], dims) + (mm(a[0], b[1], dims) + mm(a[1], b[0], dims))


def exact_sums(table, x):
    hi, mid = halves(x)
    low = bf(x - hi.astype(F32) - mid.astype(F32))
    n = x.shape[1]
    both = mm(table, jnp.concatenate([hi, mid, low, jnp.zeros_like(low)], axis=1), NN)
    return both[:, :n] + (both[:, n : 2 * n] + both[:, 2 * n : 3 * n])


def silu(v):
    return v / (1.0 + jnp.exp(-v))


def sigmoid(v):
    return 1.0 / (1.0 + jnp.exp(-v))


def silu_slope(v):
    s = sigmoid(v)
    return s + v * s * (1.0 - s)


def columns_total(x):
    ones = jnp.ones((x.shape[0], 128), BF16)
    hi, mid = halves(x)
    low = bf(x - hi.astype(F32) - mid.astype(F32))
    return mm(hi, ones, TN) + (mm(mid, ones, TN) + mm(low, ones, TN))


def spread(column, width):
    return jnp.concatenate([column] * (width // 128), axis=1)


def ends_kernel(levels, k_ref, v_ref, decay_ref, keep_ref, table_ref, unit_ref, dec_ref, all_ref, alldec_ref):
    count = table_ref.shape[1]
    chunks = k_ref.shape[0] // count
    head = k_ref.shape[1]
    total, total_dec = None, None
    for j in range(chunks):
        rows = pl.ds(j * count, count)
        decay = decay_ref[rows, :]
        weight = jnp.exp(exact_sums(table_ref[...], decay)) * keep_ref[rows, :]
        weight = halves(weight)
        keys = halves(silu(k_ref[rows, :].astype(F32)))
        values = v_ref[rows, :]
        unit_k = dot3(weight, keys, TN)
        unit_v = mm(weight[0], values, TN) + mm(weight[1], values, TN)
        unit = jnp.concatenate([unit_k, unit_v], axis=1)
        dec = jnp.exp(columns_total(decay))
        unit_ref[j] = unit
        dec_ref[j] = dec
        if j == 0:
            total, total_dec = unit, dec
        else:
            total = spread(dec, 2 * head) * total + unit
            total_dec = total_dec * dec
    all_ref[0] = total
    alldec_ref[0] = total_dec


def mix(pair, ratios, keep, masks_ref, own):
    out = own * keep
    for l, ratio in enumerate(ratios):
        left = pair * masks_ref[l].astype(F32)
        out += ratio * dot3(halves(left), halves(ratio * keep), NN)
    return out


def unmix(probs, ratios, keep, masks_ref, diag):
    out = diag * jnp.sum(probs * keep, axis=1, keepdims=True)
    for l, ratio in enumerate(ratios):
        part = dot3(halves(probs * ratio), halves(ratio * keep), NT)
        out += masks_ref[l].astype(F32) * part
    return out


def on_diagonal(count):
    return (
        lax.broadcasted_iota(jnp.int32, (count, count), 0) == lax.broadcasted_iota(jnp.int32, (count, count), 1)
    ).astype(F32)


def attend_kernel(
    levels, q_ref, k_ref, v_ref, gate_ref, decay_ref, keep_ref, start_ref, unit_ref, dec_ref, gain_ref, table_ref, masks_ref,
    gated_ref, attended_ref, probs_ref, scores_ref, weights_ref, states_ref,
):
    count = table_ref.shape[1]
    chunks = k_ref.shape[0] // count
    head = k_ref.shape[1]
    diag = on_diagonal(count)
    states_ref[0] = start_ref[0]

    def chunk(j, carry):
        rows = pl.ds(pl.multiple_of(j * count, count), count)
        keep = keep_ref[rows, :]
        powers = jnp.exp(exact_sums(table_ref[: (levels + 1) * count, :], decay_ref[rows, :]))
        ratios = [powers[l * count : (l + 1) * count] for l in range(levels)]
        growth = powers[levels * count : (levels + 1) * count]
        query = halves(silu(q_ref[rows, :].astype(F32)) * head ** (-0.5))
        keys = halves(silu(k_ref[rows, :].astype(F32)))
        state = states_ref[j]
        pair = dot3(query, keys, NT)
        scores = mix(pair, ratios, keep, masks_ref, jnp.sum(pair * diag, axis=1, keepdims=True))
        scores += growth * dot3(query, halves(state[:, :head]), NT)
        top = jnp.max(scores, axis=1, keepdims=True)
        raised = jnp.exp(scores - top)
        probs = raised / jnp.sum(raised, axis=1, keepdims=True)
        weights = unmix(probs, ratios, keep, masks_ref, diag)
        values = v_ref[rows, :]
        whi, wlo = halves(weights)
        attended = mm(whi, values, NN) + mm(wlo, values, NN)
        attended += dot3(halves(probs * growth), halves(state[:, head:]), NN)
        scale = lax.rsqrt(jnp.mean(attended * attended, axis=1, keepdims=True) + EPS)
        gated = attended * scale * gain_ref[...] * silu(gate_ref[rows, :])
        gated_ref[rows, :] = bf(gated)
        attended_ref[rows, :] = attended
        probs_ref[rows, :] = probs
        scores_ref[rows, :] = scores
        weights_ref[rows, :] = weights
        states_ref[j + 1] = spread(dec_ref[j], 2 * head) * state + unit_ref[j]
        return carry

    lax.fori_loop(0, chunks, chunk, 0)


def back_one_kernel(
    levels, q_ref, v_ref, gate_ref, decay_ref, keep_ref, grad_ref, attended_ref, probs_ref, states_ref, dec_ref, gain_ref,
    table_ref, masks_ref,
    gate_term_ref, gain_grad_ref, attended_grad_ref, dprobs_ref, dscores_ref, unit_ref, all_ref,
):
    count = table_ref.shape[1]
    chunks = q_ref.shape[0] // count
    head = q_ref.shape[1]
    diag = on_diagonal(count)
    gain = gain_ref[...]

    def chunk(n, carry):
        j = chunks - 1 - n
        rows = pl.ds(pl.multiple_of(j * count, count), count)
        gate = gate_ref[rows, :]
        attended = attended_ref[rows, :]
        grad = grad_ref[rows, :]
        scale = lax.rsqrt(jnp.mean(attended * attended, axis=1, keepdims=True) + EPS)
        normed = attended * scale
        weighted = grad * silu(gate)
        gate_term_ref[rows, :] = bf(grad * normed * gain * silu_slope(gate))
        part = jnp.sum(weighted * normed, axis=0, keepdims=True)
        c = weighted * gain
        att_grad = scale * c - attended * (scale * scale * scale) * jnp.mean(c * attended, axis=1, keepdims=True)
        attended_grad_ref[rows, :] = att_grad
        keep = keep_ref[rows, :]
        powers = jnp.exp(exact_sums(table_ref[: (levels + 1) * count, :], decay_ref[rows, :]))
        ratios = [powers[l * count : (l + 1) * count] for l in range(levels)]
        growth = powers[levels * count : (levels + 1) * count]
        ahalf = halves(att_grad)
        values = v_ref[rows, :]
        pair = mm(ahalf[0], values, NT) + mm(ahalf[1], values, NT)
        state = states_ref[j]
        dprobs = mix(pair, ratios, keep, masks_ref, jnp.sum(pair * diag, axis=1, keepdims=True))
        dprobs += growth * dot3(ahalf, halves(state[:, head:]), NT)
        probs = probs_ref[rows, :]
        dscores = probs * (dprobs - jnp.sum(probs * dprobs, axis=1, keepdims=True))
        query = halves(silu(q_ref[rows, :].astype(F32)) * head ** (-0.5))
        unit_k = dot3(halves(growth * dscores), query, TN)
        unit_v = dot3(halves(growth * probs), ahalf, TN)
        unit = jnp.concatenate([unit_k, unit_v], axis=1)
        dprobs_ref[rows, :] = dprobs
        dscores_ref[rows, :] = dscores
        unit_ref[j] = unit
        gsum, total = carry
        return gsum + part, spread(dec_ref[j], 2 * head) * total + unit

    gsum, total = lax.fori_loop(
        0, chunks, chunk, (jnp.zeros((1, head), F32), jnp.zeros((unit_ref.shape[1], 2 * head), F32))
    )
    gain_grad_ref[0] = jnp.broadcast_to(gsum, (8, head))
    all_ref[0] = total


def back_two_kernel(
    levels, q_ref, k_ref, v_ref, decay_ref, keep_ref, probs_ref, scores_ref, weights_ref, states_ref, dec_ref, unit_ref,
    attended_grad_ref, dprobs_ref, dscores_ref, end_ref, table_ref, later_ref, masks_ref,
    term_ref, decay_term_ref,
):
    count = table_ref.shape[1]
    chunks = q_ref.shape[0] // count
    head = q_ref.shape[1]
    diag = on_diagonal(count)
    last = (lax.broadcasted_iota(jnp.int32, (count, 1), 0) == count - 1).astype(F32)

    def chunk(n, adj):
        j = chunks - 1 - n
        rows = pl.ds(pl.multiple_of(j * count, count), count)
        keep = keep_ref[rows, :]
        decay = decay_ref[rows, :]
        powers = jnp.exp(exact_sums(table_ref[...], decay))
        ratios = [powers[l * count : (l + 1) * count] for l in range(levels)]
        growth = powers[levels * count : (levels + 1) * count]
        rest = powers[(levels + 1) * count :]
        qraw = q_ref[rows, :].astype(F32)
        kraw = k_ref[rows, :].astype(F32)
        query = halves(silu(qraw) * head ** (-0.5))
        keys = halves(silu(kraw))
        values = v_ref[rows, :]
        att_grad = halves(attended_grad_ref[rows, :])
        probs, dscores = probs_ref[rows, :], dscores_ref[rows, :]
        state = halves(states_ref[j][:, :head])
        ahalf = halves(adj)
        adj_k, adj_v = (ahalf[0][:, :head], ahalf[1][:, :head]), (ahalf[0][:, head:], ahalf[1][:, head:])
        dweights = halves(unmix(dscores, ratios, keep, masks_ref, diag))
        dquery = dot3(dweights, keys, NN) + dot3(halves(dscores * growth), state, NN)
        term_ref[rows, :head] = bf(silu_slope(qraw) * dquery * head ** (-0.5))
        ending = halves(rest * keep)
        dkey = dot3(dweights, query, TN) + dot3(ending, adj_k, NN)
        term_ref[rows, head : 2 * head] = bf(silu_slope(kraw) * dkey)
        dvalue = dot3(halves(weights_ref[rows, :]), att_grad, TN) + dot3(ending, adj_v, NN)
        term_ref[rows, 2 * head :] = bf(dvalue)
        pair_k = dot3(query, keys, NT)
        pair_v = mm(att_grad[0], values, NT) + mm(att_grad[1], values, NT)
        dkeep = jnp.sum(pair_k * diag, axis=1, keepdims=True) * dscores
        dkeep += jnp.sum(pair_v * diag, axis=1, keepdims=True) * probs
        dkeep += rest * (dot3(keys, adj_k, NT) + mm(values, adj_v[0], NT) + mm(values, adj_v[1], NT))
        for l, ratio in enumerate(ratios):
            mask = masks_ref[l].astype(F32)
            part = dot3(halves(pair_k * mask), halves(dscores * ratio), TN)
            part += dot3(halves(pair_v * mask), halves(probs * ratio), TN)
            dkeep += ratio * part
        dsum = dscores * scores_ref[rows, :] + probs * dprobs_ref[rows, :] - keep * dkeep
        at_end = jnp.sum(adj * states_ref[j + 1], axis=1, keepdims=True)
        at_end = jnp.sum(at_end * on_diagonal(adj.shape[0]), axis=0, keepdims=True)
        dsum += last * at_end
        ddecay = exact_sums(later_ref[...], dsum) - (1.0 - keep) * dkeep
        decay_term_ref[rows, :] = ddecay
        return spread(dec_ref[j], 2 * head) * adj + unit_ref[j]

    lax.fori_loop(0, chunks, chunk, end_ref[0])


def params():
    return pltpu.CompilerParams(vmem_limit_bytes=56 * 2**20)


def call(kernel, grid, ins, outs, name, flops=0):
    return pl.pallas_call(
        kernel,
        grid=grid,
        in_specs=[pl.BlockSpec(block, where) for _, block, where in ins],
        out_specs=[pl.BlockSpec(block, where) for _, _, block, where in outs],
        out_shape=[jax.ShapeDtypeStruct(shape, dtype) for shape, dtype, _, _ in outs],
        compiler_params=params(),
        name=name,
    )(*[array for array, _, _ in ins])


class Slots:
    def __init__(self, seqs, rows, head, slots, chunk):
        self.seqs, self.rows, self.head, self.slots, self.chunk = seqs, rows, head, slots, chunk
        self.chunks = rows // chunk
        paths, masks = decay_tables(chunk)
        self.levels = masks.shape[0]
        self.paths = jnp.asarray(paths, BF16)
        self.masks = jnp.asarray(masks, BF16)

    def row(self, array, width=None, place=0):
        width = array.shape[1] if width is None else width
        return (array, (self.rows, width), lambda b: (b, place))

    def whole(self, array):
        return (array, array.shape, lambda b: (0,) * array.ndim)

    def per(self, array, count):
        return (array, (count,) + array.shape[1:], lambda b: (b,) + (0,) * (array.ndim - 1))

    def out_row(self, width, dtype):
        return ((self.seqs * self.rows, width), dtype, (self.rows, width), lambda b: (b, 0))

    def out_per(self, count, shape, dtype=F32):
        return ((self.seqs * count,) + shape, dtype, (count,) + shape, lambda b: (b,) + (0,) * len(shape))

    def ends(self, qkv, decay, keep):
        m, w = self.slots, 2 * self.head
        tail = self.paths[-self.chunk :]
        return call(
            functools.partial(ends_kernel, self.levels), (self.seqs,),
            [self.row(qkv, self.head, 1), self.row(qkv, self.head, 2), self.row(decay), self.row(keep), self.whole(tail)],
            [self.out_per(self.chunks, (m, w)), self.out_per(self.chunks, (m, 128)), self.out_per(1, (m, w)), self.out_per(1, (m, 128))],
            "slot_ends",
        )

    def attend(self, qkv, gate, decay, keep, start, unit, dec, gain):
        h, m = self.head, self.slots
        return call(
            functools.partial(attend_kernel, self.levels), (self.seqs,),
            [self.row(qkv, h, 0), self.row(qkv, h, 1), self.row(qkv, h, 2), self.row(gate, h, 0), self.row(decay), self.row(keep),
             self.per(start, 1), self.per(unit, self.chunks), self.per(dec, self.chunks), self.whole(gain), self.whole(self.paths),
             self.whole(self.masks)],
            [self.out_row(h, BF16), self.out_row(h, F32), self.out_row(m, F32), self.out_row(m, F32), self.out_row(self.chunk, F32),
             self.out_per(self.chunks + 1, (m, 2 * h))],
            "slot_attend",
        )

    def back_one(self, qkv, gate, decay, keep, grad, attended, probs, states, dec, gain):
        h, m = self.head, self.slots
        return call(
            functools.partial(back_one_kernel, self.levels), (self.seqs,),
            [self.row(qkv, h, 0), self.row(qkv, h, 2), self.row(gate, h, 0), self.row(decay), self.row(keep), self.row(grad),
             self.row(attended), self.row(probs), self.per(states, self.chunks + 1), self.per(dec, self.chunks), self.whole(gain),
             self.whole(self.paths), self.whole(self.masks)],
            [self.out_row(h, BF16), self.out_per(1, (8, h)), self.out_row(h, F32), self.out_row(m, F32), self.out_row(m, F32),
             self.out_per(self.chunks, (m, 2 * h)), self.out_per(1, (m, 2 * h))],
            "slot_back_one",
        )

    def back_two(self, qkv, decay, keep, probs, scores, weights, states, dec, unit, attended_grad, dprobs, dscores, end):
        h, m = self.head, self.slots
        later = self.paths[-2 * self.chunk : -self.chunk].T
        return call(
            functools.partial(back_two_kernel, self.levels), (self.seqs,),
            [self.row(qkv, h, 0), self.row(qkv, h, 1), self.row(qkv, h, 2), self.row(decay), self.row(keep), self.row(probs),
             self.row(scores), self.row(weights), self.per(states, self.chunks + 1), self.per(dec, self.chunks),
             self.per(unit, self.chunks), self.row(attended_grad), self.row(dprobs), self.row(dscores), self.per(end, 1),
             self.whole(self.paths), self.whole(later), self.whole(self.masks)],
            [self.out_row(3 * h, BF16), self.out_row(m, F32)],
            "slot_back_two",
        )

class Place:
    def __init__(self, size):
        self.size = size
        self.line = size // 4
        s = lax.axis_index("seq")
        self.c = lax.axis_index("head")
        self.s = s
        self.x = lax.rem(s, 2)
        self.b = lax.rem(s // 2, 2)
        self.a = s // 4

    def at(self, a, b, x):
        return (a * 2 + b) * 2 + x

    def partner(self):
        return (self.at(self.a, self.b, 1 - self.x), self.c)

    def across(self):
        return (self.at(self.a, 1 - self.b, self.x), self.c)

    def up(self):
        return (self.at(jnp.minimum(self.a + 1, self.line - 1), self.b, self.x), self.c)

    def down(self):
        return (self.at(jnp.maximum(self.a - 1, 0), self.b, self.x), self.c)

    def sibling(self):
        return (self.s, 1 - self.c)

    def has_up(self):
        return self.a < self.line - 1

    def has_down(self):
        return self.a > 0


def signal(sem, device):
    pl.semaphore_signal(sem, inc=1, device_id=device, device_id_type=MESH)


def greet(place, partner=True, across=True, line=True, sibling=False):
    barrier = pltpu.get_barrier_semaphore()
    count = jnp.int32(0)
    if partner:
        signal(barrier, place.partner())
        count = count + 1
    if sibling:
        signal(barrier, place.sibling())
        count = count + 1
    if across:
        signal(barrier, place.across())
        count = count + 1
    if line:
        pl.when(place.has_up())(lambda: signal(barrier, place.up()))
        pl.when(place.has_down())(lambda: signal(barrier, place.down()))
        count = count + place.has_up().astype(jnp.int32) + place.has_down().astype(jnp.int32)
    pl.semaphore_wait(barrier, count)


def remote(src, dst, send, recv, device):
    return pltpu.make_async_remote_copy(
        src_ref=src, dst_ref=dst, send_sem=send, recv_sem=recv, device_id=device, device_id_type=MESH
    )


class Gather:
    def __init__(self, place, shard, full, unit, offset, width, sems, late):
        self.pl, self.shard, self.full = place, shard, full
        self.unit, self.offset, self.width, self.late = unit, offset, width, late
        self.x_sem, self.b_sem, self.up_sem, self.down_sem = sems

    def part(self, start, count):
        rows = pl.ds(start * self.unit, count * self.unit)
        if self.width == self.full.shape[1]:
            return self.full.at[rows]
        return self.full.at[rows, pl.ds(self.offset, self.width)]

    def mine(self, x):
        if self.shard.shape[1] == self.width:
            return self.shard
        return self.shard.at[:, pl.ds(x * self.width, self.width)]

    def x_copy(self):
        p = self.pl
        return remote(self.mine(1 - p.x), self.part(p.s, 1), self.x_sem.at[0], self.x_sem.at[1], p.partner())

    def own_copy(self):
        return pltpu.make_async_copy(self.mine(self.pl.x), self.part(self.pl.s, 1), self.x_sem.at[2])

    def block(self, a):
        p = self.pl
        if self.late:
            return self.part(4 * a, 4)
        return self.part(4 * a + 2 * p.b, 2)

    def b_copy(self, i, a):
        p = self.pl
        return remote(
            self.part(4 * a + 2 * p.b, 2), self.part(4 * a + 2 * p.b, 2),
            self.b_sem.at[0, i], self.b_sem.at[1, i], p.across(),
        )

    def line_copy(self, way, h):
        p = self.pl
        if way == "up":
            blk = self.block(jnp.maximum(p.a - (h - 1), 0))
            return remote(blk, blk, self.up_sem.at[0, h - 1], self.up_sem.at[1, h - 1], p.up())
        blk = self.block(jnp.minimum(p.a + (h - 1), p.line - 1))
        return remote(blk, blk, self.down_sem.at[0, h - 1], self.down_sem.at[1, h - 1], p.down())

    def sends(self, way, h):
        p = self.pl
        if way == "up":
            return jnp.logical_and(p.has_up(), p.a - (h - 1) >= 0)
        return jnp.logical_and(p.has_down(), p.a + (h - 1) <= p.line - 1)

    def gets(self, way, h):
        p = self.pl
        if way == "up":
            return p.a - h >= 0
        return p.a + h <= p.line - 1

    def got(self, way, h):
        p = self.pl
        if way == "up":
            return jnp.maximum(p.a - h, 0)
        return jnp.minimum(p.a + h, p.line - 1)

    def slot(self, way, h):
        return h if way == "up" else self.pl.line - 1 + h

    def start_x(self):
        self.x_copy().start()
        self.own_copy().start()

    def stage(self, h):
        p = self.pl
        if h == 0:
            self.own_copy().wait()
            self.x_copy().wait_recv()
            if self.late:
                self.b_copy(0, p.a).start()
            else:
                for way in ("up", "down"):
                    pl.when(self.sends(way, 1))(lambda way=way: self.line_copy(way, 1).start())
                self.b_copy(0, p.a).start()
            return
        if self.late:
            if h == 1:
                self.b_copy(0, p.a).wait_recv()
                for way in ("up", "down"):
                    pl.when(self.sends(way, 1))(lambda way=way: self.line_copy(way, 1).start())
                return
            h = h - 1
        for way in ("up", "down"):

            def go(way=way):
                self.line_copy(way, h).wait_recv()
                if not self.late:
                    self.b_copy(self.slot(way, h), self.got(way, h)).start()

            def on(way=way):
                self.line_copy(way, h + 1).start()

            pl.when(self.gets(way, h))(go)
            if h + 1 <= p.line - 1:
                pl.when(self.sends(way, h + 1))(on)

    def stages(self):
        return self.pl.line + (1 if self.late else 0)

    def finish(self):
        p = self.pl
        self.x_copy().wait_send()
        self.b_copy(0, p.a).wait_send()
        if not self.late:
            self.b_copy(0, p.a).wait_recv()
        for way in ("up", "down"):
            for h in range(1, p.line):
                pl.when(self.sends(way, h))(lambda way=way, h=h: self.line_copy(way, h).wait_send())
                if not self.late:

                    def both(way=way, h=h):
                        cp = self.b_copy(self.slot(way, h), self.got(way, h))
                        cp.wait_send()
                        cp.wait_recv()

                    pl.when(self.gets(way, h))(both)


def gather_sems(line):
    return [
        pltpu.SemaphoreType.DMA((3,)),
        pltpu.SemaphoreType.DMA((2, 2 * line - 1)),
        pltpu.SemaphoreType.DMA((2, line - 1)),
        pltpu.SemaphoreType.DMA((2, line - 1)),
    ]


def gather_ops(gathers, ahead):
    steps = []
    n = len(gathers)
    for k in range(min(ahead, n)):
        steps.append(gathers[k].start_x)
    steps.append(functools.partial(gathers[0].stage, 0))
    for k in range(n):
        if k + ahead < n:
            steps.append(gathers[k + ahead].start_x)
        if k + 1 < n:
            steps.append(functools.partial(gathers[k + 1].stage, 0))
        for h in range(1, gathers[k].stages()):
            steps.append(functools.partial(gathers[k].stage, h))
    for g in gathers:
        steps.append(g.finish)
    return steps

def prefix_kernel(size, back, own_ref, dec_ref, start_ref, peer, peer_dec, line, out, p_sem, d_sem, l_sem):
    p = Place(size)
    greet(p, partner=False)
    seqs, slots, width = own_ref.shape
    half = width // 2
    pieces = [(b, h) for b in range(seqs) for h in range(2)]

    def cut(ref, piece):
        return ref.at[piece[0], :, pl.ds(piece[1] * half, half)]

    def peer_copy(i, piece):
        return remote(cut(own_ref, piece), cut(peer, piece), p_sem.at[0, i], p_sem.at[1, i], p.across())

    if back:
        has_prev, has_next, after = p.has_up(), p.has_down(), p.down()
    else:
        has_prev, has_next, after = p.has_down(), p.has_up(), p.up()

    def line_copy(i, piece):
        return remote(cut(out, piece), cut(line, piece), l_sem.at[0, i], l_sem.at[1, i], after)

    dec_copy = remote(dec_ref, peer_dec, d_sem.at[0], d_sem.at[1], p.across())
    dec_copy.start()
    for i, piece in enumerate(pieces):
        peer_copy(i, piece).start()
    own_first = (p.b == 1) if back else (p.b == 0)
    first = own_first.astype(F32)
    dec_copy.wait_recv()
    for i, piece in enumerate(pieces):
        peer_copy(i, piece).wait_recv()
        dec_own = spread(dec_ref[piece[0]], half)
        dec_peer = spread(peer_dec[piece[0]], half)
        own, other = cut(own_ref, piece)[...], cut(peer, piece)[...]
        both = first * (dec_peer * own + other) + (1.0 - first) * (dec_own * other + own)
        here = cut(out, piece)

        def go_on():
            line_copy(i, piece).wait_recv()
            came = cut(line, piece)[...]
            here[...] = dec_own * dec_peer * came + both
            cut(start_ref, piece)[...] = first * came + (1.0 - first) * (dec_peer * came + other)

        def begin():
            here[...] = both
            cut(start_ref, piece)[...] = (1.0 - first) * other

        pl.when(has_prev)(go_on)
        pl.when(jnp.logical_not(has_prev))(begin)
        pl.when(has_next)(lambda i=i, piece=piece: line_copy(i, piece).start())
    dec_copy.wait_send()
    for i, piece in enumerate(pieces):
        peer_copy(i, piece).wait_send()
        pl.when(has_next)(lambda i=i, piece=piece: line_copy(i, piece).wait_send())


VM = pl.BlockSpec(memory_space=pltpu.VMEM)
ANY = pl.BlockSpec(memory_space=HBM)


def remote_params(number, mib=56):
    return pltpu.CompilerParams(collective_id=number, has_side_effects=True, vmem_limit_bytes=mib * 2**20)


def prefix(size, number, own, dec, back):
    shape = own.shape
    count = 2 * shape[0]
    return pl.pallas_call(
        functools.partial(prefix_kernel, size, back),
        out_shape=jax.ShapeDtypeStruct(shape, F32),
        in_specs=[VM, VM],
        out_specs=VM,
        scratch_shapes=[
            pltpu.VMEM(shape, F32), pltpu.VMEM(dec.shape, F32), pltpu.VMEM(shape, F32), pltpu.VMEM(shape, F32),
            pltpu.SemaphoreType.DMA((2, count)), pltpu.SemaphoreType.DMA((2,)), pltpu.SemaphoreType.DMA((2, count)),
        ],
        compiler_params=remote_params(number),
        name="slot_suffix" if back else "slot_prefix",
    )(own, dec)


STRIPS = 4


class Fold:
    def __init__(self, place, part, sib, sent, came, sems):
        self.p, self.part, self.sib, self.sent, self.came = place, part, sib, sent, came
        self.s_sem, self.x_sem = sems
        self.rows = part.shape[2] // STRIPS

    def strip(self, r):
        return pl.ds(r * self.rows, self.rows)

    def sib_copy(self, far, r):
        p = self.p
        x = 1 - p.x if far else p.x
        i = (0 if far else STRIPS) + r
        return remote(
            self.part.at[1 - p.c, x, self.strip(r)], self.sib.at[1 if far else 0, self.strip(r)],
            self.s_sem.at[0, i], self.s_sem.at[1, i], p.sibling(),
        )

    def x_copy(self, r):
        return remote(
            self.sent.at[self.strip(r)], self.came.at[self.strip(r)], self.x_sem.at[0, r], self.x_sem.at[1, r], self.p.partner()
        )

    def start(self):
        for r in range(STRIPS):
            self.sib_copy(True, r).start()
        for r in range(STRIPS):
            self.sib_copy(False, r).start()

    def sib_all(self, far):
        for r in range(STRIPS):
            self.sib_copy(far, r).start()

    def cross(self, r):
        p = self.p
        self.sib_copy(True, r).wait_recv()
        own = self.part[p.c, 1 - p.x, self.strip(r)].astype(F32)
        self.sent[self.strip(r)] = bf(own + self.sib[1, self.strip(r)].astype(F32))
        self.x_copy(r).start()

    def total(self, r):
        p = self.p
        self.sib_copy(False, r).wait_recv()
        self.x_copy(r).wait_recv()
        own = self.part[p.c, p.x, self.strip(r)].astype(F32) + self.sib[0, self.strip(r)].astype(F32)
        return own + self.came[self.strip(r)].astype(F32)

    def finish(self):
        for r in range(STRIPS):
            self.sib_copy(True, r).wait_send()
            self.sib_copy(False, r).wait_send()
            self.x_copy(r).wait_send()


def fold_scratch(rows, width):
    return [
        pltpu.VMEM((2, rows, width), BF16), pltpu.VMEM((rows, width), BF16), pltpu.VMEM((rows, width), BF16),
        pltpu.SemaphoreType.DMA((2, 2 * STRIPS)), pltpu.SemaphoreType.DMA((2, STRIPS)),
    ]


class Share:
    def __init__(self, place, out, sems):
        self.p, self.out = place, out
        self.x_sem, self.s_sem = sems
        self.rows = out.shape[2] // STRIPS

    def strip(self, r):
        return pl.ds(r * self.rows, self.rows)

    def x_copy(self, r):
        p = self.p
        block = self.out.at[p.c, p.x, self.strip(r)]
        return remote(block, block, self.x_sem.at[0, r], self.x_sem.at[1, r], p.partner())

    def s_copy(self, far, r):
        p = self.p
        block = self.out.at[p.c, 1 - p.x if far else p.x, self.strip(r)]
        i = (0 if far else STRIPS) + r
        return remote(block, block, self.s_sem.at[0, i], self.s_sem.at[1, i], p.sibling())

    def put(self, r, value):
        self.out[self.p.c, self.p.x, self.strip(r)] = value
        self.x_copy(r).start()
        self.s_copy(False, r).start()

    def forward(self, r):
        self.x_copy(r).wait_recv()
        self.s_copy(True, r).start()

    def finish(self):
        for r in range(STRIPS):
            self.x_copy(r).wait_send()
            for far in (False, True):
                self.s_copy(far, r).wait_send()
                self.s_copy(far, r).wait_recv()


SHARE_SEMS = [pltpu.SemaphoreType.DMA((2, STRIPS)), pltpu.SemaphoreType.DMA((2, 2 * STRIPS))]


def inverse_rms(values):
    return lax.rsqrt(jnp.mean(values * values, axis=-1, keepdims=True) + EPS)


def norm_back(grad, values, gain):
    scale = inverse_rms(values)
    u = grad * gain
    down = scale * u - values * (scale * scale * scale) * jnp.mean(u * values, axis=-1, keepdims=True)
    return down, jnp.sum(grad * values * scale, axis=0, keepdims=True)


def blend_kernel(size, part, tokens, gain, residual, normed, sib, sent, came, s1, s2, s3, s4):
    p = Place(size)
    greet(p, across=False, line=False, sibling=True)
    fold = Fold(p, part, sib, sent, came, (s1, s2))
    share = Share(p, normed, (s3, s4))
    fold.start()
    for r in range(STRIPS):
        fold.cross(r)
    for r in range(STRIPS):
        value = tokens[p.c, fold.strip(r)].astype(F32) + fold.total(r)
        residual[fold.strip(r)] = value
        share.put(r, bf(value * inverse_rms(value) * gain[...]))
    for r in range(STRIPS):
        share.forward(r)
    share.finish()
    fold.finish()


def blend(size, number, part, tokens, gain):
    _, _, rows, width = part.shape
    return pl.pallas_call(
        functools.partial(blend_kernel, size),
        out_shape=[jax.ShapeDtypeStruct((rows, width), F32), jax.ShapeDtypeStruct(part.shape, BF16)],
        in_specs=[VM] * 3,
        out_specs=[VM] * 2,
        scratch_shapes=fold_scratch(rows, width) + SHARE_SEMS,
        compiler_params=remote_params(number),
        name="blend",
    )(part, tokens, gain)


def blend_back_kernel(size, part, grad_out, residual, gain, residual_grad, low, gain_grad, sib, sent, came, s1, s2, s3, s4):
    p = Place(size)
    greet(p, across=False, line=False, sibling=True)
    fold = Fold(p, part, sib, sent, came, (s1, s2))
    share = Share(p, low, (s3, s4))
    fold.start()
    for r in range(STRIPS):
        fold.cross(r)
    gains = jnp.zeros((1, part.shape[3]), F32)
    for r in range(STRIPS):
        down, more = norm_back(fold.total(r), residual[fold.strip(r)], gain[...])
        value = grad_out[p.c, fold.strip(r)].astype(F32) + down
        gains += more
        residual_grad[fold.strip(r)] = value
        share.put(r, bf(value))
    gain_grad[...] = gains
    for r in range(STRIPS):
        share.forward(r)
    share.finish()
    fold.finish()


def blend_back(size, number, part, grad_out, residual, gain):
    _, _, rows, width = part.shape
    return pl.pallas_call(
        functools.partial(blend_back_kernel, size),
        out_shape=[
            jax.ShapeDtypeStruct((rows, width), F32), jax.ShapeDtypeStruct(part.shape, BF16), jax.ShapeDtypeStruct((1, width), F32)
        ],
        in_specs=[VM] * 4,
        out_specs=[VM] * 3,
        scratch_shapes=fold_scratch(rows, width) + SHARE_SEMS,
        compiler_params=remote_params(number),
        name="blend_back",
    )(part, grad_out, residual, gain)


def finish_kernel(
    size, part, ff_part, tokens, residual, residual_grad, gain, input_grad, output, gain_grad,
    sib, sent, came, s1, s2, sib2, sent2, came2, t1, t2, out_sem,
):
    p = Place(size)
    greet(p, across=False, line=False, sibling=True)
    fold = Fold(p, part, sib, sent, came, (s1, s2))
    ff = Fold(p, ff_part, sib2, sent2, came2, (t1, t2))
    ff.start()
    fold.start()
    for r in range(STRIPS):
        ff.cross(r)
        fold.cross(r)
    gains = jnp.zeros((1, part.shape[3]), F32)

    def out_copy(ref, k, r):
        block = ref.at[p.c, fold.strip(r)]
        return remote(block, block, out_sem.at[0, k * STRIPS + r], out_sem.at[1, k * STRIPS + r], p.sibling())

    for r in range(STRIPS):
        output[p.c, fold.strip(r)] = bf(residual[fold.strip(r)] + ff.total(r))
        out_copy(output, 0, r).start()
        down, more = norm_back(fold.total(r), tokens[p.c, fold.strip(r)].astype(F32), gain[...])
        gains += more
        input_grad[p.c, fold.strip(r)] = residual_grad[fold.strip(r)] + down
        out_copy(input_grad, 1, r).start()
    gain_grad[...] = gains
    for r in range(STRIPS):
        out_copy(output, 0, r).wait()
        out_copy(input_grad, 1, r).wait()
    ff.finish()
    fold.finish()


def finish(size, number, part, ff_part, tokens, residual, residual_grad, gain):
    _, _, rows, width = part.shape
    return pl.pallas_call(
        functools.partial(finish_kernel, size),
        out_shape=[
            jax.ShapeDtypeStruct((2, rows, width), F32), jax.ShapeDtypeStruct((2, rows, width), BF16),
            jax.ShapeDtypeStruct((1, width), F32),
        ],
        in_specs=[VM] * 6,
        out_specs=[VM] * 3,
        scratch_shapes=fold_scratch(rows, width) * 2 + [pltpu.SemaphoreType.DMA((2, 2 * STRIPS))],
        compiler_params=remote_params(number),
        name="finish",
    )(part, ff_part, tokens, residual, residual_grad, gain)


def ends_chunk(k, v, decay, keep, tail):
    weight = halves(jnp.exp(exact_sums(tail, decay)) * keep)
    unit_k = dot3(weight, halves(silu(k.astype(F32))), TN)
    unit_v = mm(weight[0], v, TN) + mm(weight[1], v, TN)
    return jnp.concatenate([unit_k, unit_v], axis=1), jnp.exp(columns_total(decay))


def powers_of(table, count, levels, decay):
    powers = jnp.exp(exact_sums(table, decay))
    return [powers[l * count : (l + 1) * count] for l in range(levels)], [
        powers[l * count : (l + 1) * count] for l in range(levels, table.shape[0] // count)
    ]


class Prefix:
    def __init__(self, place, back, own, dec, start, peer, peer_dec, line, out, sems):
        p = self.p = place
        self.own, self.dec, self.start_ref, self.peer, self.peer_dec = own, dec, start, peer, peer_dec
        self.line, self.out = line, out
        self.p_sem, self.d_sem, self.l_sem = sems
        seqs, slots, width = own.shape
        self.half = width // 2
        self.pieces = [(b, h) for b in range(seqs) for h in range(2)]
        if back:
            self.has_prev, self.has_next, self.after = p.has_up(), p.has_down(), p.down()
        else:
            self.has_prev, self.has_next, self.after = p.has_down(), p.has_up(), p.up()
        self.first = ((p.b == 1) if back else (p.b == 0)).astype(F32)

    def cut(self, ref, i):
        b, h = self.pieces[i]
        return ref.at[b, :, pl.ds(h * self.half, self.half)]

    def peer_copy(self, i):
        return remote(self.cut(self.own, i), self.cut(self.peer, i), self.p_sem.at[0, i], self.p_sem.at[1, i], self.p.across())

    def line_copy(self, i):
        return remote(self.cut(self.out, i), self.cut(self.line, i), self.l_sem.at[0, i], self.l_sem.at[1, i], self.after)

    def dec_copy(self):
        return remote(self.dec, self.peer_dec, self.d_sem.at[0], self.d_sem.at[1], self.p.across())

    def start(self):
        self.dec_copy().start()
        for i in range(len(self.pieces)):
            self.peer_copy(i).start()

    def run(self):
        self.dec_copy().wait_recv()
        for i, (b, _) in enumerate(self.pieces):
            self.peer_copy(i).wait_recv()
            dec_own = spread(self.dec[b], self.half)
            dec_peer = spread(self.peer_dec[b], self.half)
            own, other = self.cut(self.own, i)[...], self.cut(self.peer, i)[...]
            first = self.first
            both = first * (dec_peer * own + other) + (1.0 - first) * (dec_own * other + own)
            here, result = self.cut(self.out, i), self.cut(self.start_ref, i)

            def go_on(i=i):
                self.line_copy(i).wait_recv()
                came = self.cut(self.line, i)[...]
                here[...] = dec_own * dec_peer * came + both
                result[...] = first * came + (1.0 - first) * (dec_peer * came + other)

            def begin():
                here[...] = both
                result[...] = (1.0 - first) * other

            pl.when(self.has_prev)(go_on)
            pl.when(jnp.logical_not(self.has_prev))(begin)
            pl.when(self.has_next)(lambda i=i: self.line_copy(i).start())

    def finish(self):
        self.dec_copy().wait_send()
        for i in range(len(self.pieces)):
            self.peer_copy(i).wait_send()
            pl.when(self.has_next)(lambda i=i: self.line_copy(i).wait_send())


def prefix_scratch(seqs, slots, width):
    count = 2 * seqs
    return [
        pltpu.VMEM((seqs, slots, width), F32), pltpu.VMEM((seqs, slots, width), F32), pltpu.VMEM((seqs, slots, 128), F32),
        pltpu.VMEM((seqs, slots, width), F32), pltpu.VMEM((seqs, slots, width), F32),
        pltpu.SemaphoreType.DMA((2, count)), pltpu.SemaphoreType.DMA((2,)), pltpu.SemaphoreType.DMA((2, count)),
    ]


def take(refs, count):
    return refs[:count], refs[count:]


class Weave:
    def __init__(self, steps):
        self.steps = list(steps)

    def run(self, count):
        for step in self.steps[:count]:
            step()
        self.steps = self.steps[count:]

    def rest(self):
        self.run(len(self.steps))


def blocks_in_order(p, seqs):
    def block(i):
        b = jnp.where(i < 2, 1 - p.c, p.c)
        x = jnp.where(lax.rem(i, 2) == 0, 1 - p.x, p.x)
        return b, x

    return block


def forward_kernel(size, plan, levels, *refs):
    p = Place(size)
    (qkv, gates, decay, keep, gain, out_w, tokens, gain2, paths, masks), refs = take(refs, 10)
    shard_refs, refs = take(refs, len(plan))
    (gated, attended, probs, scores, weights, states, decs, end_dec, residual, normed), refs = take(refs, 10)
    fulls, refs = take(refs, max(i for i, _, _, _, _ in plan) + 1)
    (units, part, total), refs = take(refs, 3)
    (start, *prefix_refs), refs = take(refs, 8)
    fold_refs, refs = take(refs, 5)
    share_sems, refs = take(refs, 2)
    count = paths.shape[1]
    head = gated.shape[1]
    seqs = tokens.shape[0]
    slots = keep.shape[1]
    greet(p, sibling=True)
    work = []
    for n, (i, unit, offset, width, late) in enumerate(plan):
        work.append(Gather(p, shard_refs[n], fulls[i], unit, offset, width, refs[4 * n : 4 * n + 4], late))
    weave = Weave(gather_ops(work, 3))
    weave.run(3)
    tail = paths[(levels + 1) * count :, :]

    def ends(b):
        for j in range(2):
            rows = pl.ds((b * 2 + j) * count, count)
            unit, dec = ends_chunk(
                qkv[rows, head : 2 * head], qkv[rows, 2 * head :], decay[rows, :], keep[rows, :], tail
            )
            units[b, j] = unit
            decs[b, j] = dec
        total[b] = spread(dec, 2 * head) * units[b, 0] + unit
        end_dec[b] = decs[b, 0] * dec

    for b in range(seqs):
        ends(b)
    carry = Prefix(p, False, total, end_dec, start, *prefix_refs[:4], prefix_refs[4:])
    carry.start()
    weave.run(1)
    carry.run()
    for b in range(seqs):
        states[3 * b] = start[b]
        for j in range(2):
            states[3 * b + j + 1] = spread(decs[b, j], 2 * head) * states[3 * b + j] + units[b, j]
    weave.run(1)
    diag = on_diagonal(count)
    order = blocks_in_order(p, seqs)
    fold = Fold(p, part, *fold_refs[:3], fold_refs[3:])
    share = Share(p, normed, share_sems)

    def attend(i, nothing):
        b, j = order(i)
        rows = pl.ds(pl.multiple_of((b * 2 + j) * count, count), count)
        here = keep[rows, :]
        ratios, (growth,) = powers_of(paths[: (levels + 1) * count, :], count, levels, decay[rows, :])
        query = halves(silu(qkv[rows, :head].astype(F32)) * head ** (-0.5))
        keys = halves(silu(qkv[rows, head : 2 * head].astype(F32)))
        state = states[3 * b + j]
        pair = dot3(query, keys, NT)
        score = mix(pair, ratios, here, masks, jnp.sum(pair * diag, axis=1, keepdims=True))
        score += growth * dot3(query, halves(state[:, :head]), NT)
        raised = jnp.exp(score - jnp.max(score, axis=1, keepdims=True))
        prob = raised / jnp.sum(raised, axis=1, keepdims=True)
        weight = unmix(prob, ratios, here, masks, diag)
        values = qkv[rows, 2 * head :]
        whi, wlo = halves(weight)
        result = mm(whi, values, NN) + mm(wlo, values, NN)
        result += dot3(halves(prob * growth), halves(state[:, head:]), NN)
        scale = lax.rsqrt(jnp.mean(result * result, axis=1, keepdims=True) + EPS)
        low = bf(result * scale * gain[...] * silu(gates[rows, :head]))
        gated[rows, :] = low
        attended[rows, :] = result
        probs[rows, :] = prob
        scores[rows, :] = score
        weights[rows, :] = weight
        part[b, j] = bf(mm(low, out_w[...], NT))
        pl.when(i == 0)(lambda: fold.sib_all(True))
        pl.when(i == 1)(lambda: fold.sib_all(False))
        return nothing

    lax.fori_loop(0, 2, attend, 0)
    weave.run(1)
    lax.fori_loop(2, 3, attend, 0)
    for r in range(STRIPS):
        fold.cross(r)
    lax.fori_loop(3, 4, attend, 0)
    weave.run(1)
    for r in range(STRIPS):
        value = tokens[p.c, fold.strip(r)].astype(F32) + fold.total(r)
        residual[fold.strip(r)] = value
        share.put(r, bf(value * inverse_rms(value) * gain2[...]))
    weave.run(2)
    for r in range(STRIPS):
        share.forward(r)
    weave.rest()
    share.finish()
    fold.finish()
    carry.finish()


def forward(size, number, slot, plan, fulls, qkv, gates, decay, keep, gain, out_w, tokens, gain2, shards):
    seqs, block, width = tokens.shape
    h, m, n, rows = slot.head, slot.slots, slot.chunks, slot.seqs * slot.rows
    shape = jax.ShapeDtypeStruct
    outs = [
        shape((rows, h), BF16), shape((rows, h), F32), shape((rows, m), F32), shape((rows, m), F32), shape((rows, slot.chunk), F32),
        shape((seqs * (n + 1), m, 2 * h), F32), shape((seqs, n, m, 128), F32), shape((seqs, m, 128), F32),
        shape((block, width), F32), shape((seqs, 2, block, width), BF16),
    ]
    scratch = [
        pltpu.VMEM((seqs, n, m, 2 * h), F32), pltpu.VMEM((seqs, 2, block, width), BF16), pltpu.VMEM((seqs, m, 2 * h), F32),
    ]
    scratch += prefix_scratch(seqs, m, 2 * h) + fold_scratch(block, width) + SHARE_SEMS
    for _ in plan:
        scratch += gather_sems(size // 4)
    return pl.pallas_call(
        functools.partial(forward_kernel, size, plan, slot.levels),
        out_shape=outs + [shape(full, BF16) for full in fulls],
        in_specs=[VM] * 10 + [ANY] * len(shards),
        out_specs=[VM] * 10 + [ANY] * len(fulls),
        scratch_shapes=scratch,
        compiler_params=remote_params(number, 60),
        name="attend_forward",
    )(qkv, gates, decay, keep, gain, out_w, tokens, gain2, slot.paths, slot.masks, *shards)

class Scatter:
    def __init__(self, place, grad, out, unit, offset, width, bufs, sems):
        self.p, self.grad, self.out = place, grad, out
        self.unit, self.offset, self.width = unit, offset, width
        self.whole = out.shape[-1] == width
        self.own, self.peer, self.line, self.total = bufs
        self.o_sem, self.b_sem, self.l_sem, self.x_sem = sems

    def block(self, a, b):
        rows = pl.ds((4 * a + 2 * b) * self.unit, 2 * self.unit)
        if self.width == self.grad.shape[1]:
            return self.grad.at[rows]
        return self.grad.at[rows, pl.ds(self.offset, self.width)]

    def own_copy(self, a):
        return pltpu.make_async_copy(self.block(a, self.p.b), self.own.at[a], self.o_sem.at[a])

    def b_copy(self, a):
        return remote(self.block(a, 1 - self.p.b), self.peer.at[a], self.b_sem.at[0, a], self.b_sem.at[1, a], self.p.across())

    def send_line(self, d, way):
        p = self.p
        if way == "up":
            return remote(self.own.at[d], self.line.at[d], self.l_sem.at[0, d], self.l_sem.at[1, d], p.up())
        slot = jnp.where(p.a - 1 == d, p.line, d)
        return remote(self.own.at[d], self.line.at[slot], self.l_sem.at[0, d], self.l_sem.at[1, slot], p.down())

    def wait_line(self, d, slot):
        p = self.p
        remote(self.own.at[d], self.line.at[slot], self.l_sem.at[0, d], self.l_sem.at[1, slot], p.across()).wait_recv()

    def start(self):
        lines = self.p.line
        for a in sorted(range(lines), key=lambda a: -abs(2 * a - lines + 1)):
            self.b_copy(a).start()
            self.own_copy(a).start()

    def strips(self, do):
        rows, width = self.own.shape[1], self.own.shape[2]
        step = max(r for r in (16, 32, 64, 128) if rows % r == 0 and (r == 16 or r * width <= 64 * 1024))

        def one(i, carry):
            do(pl.ds(pl.multiple_of(i * step, step), step))
            return carry

        lax.fori_loop(0, rows // step, one, 0)

    def ready(self, d):
        self.own_copy(d).wait()
        self.b_copy(d).wait_recv()

    def add(self, d, lines):
        def do(rows):
            value = self.own[d, rows].astype(F32) + self.peer[d, rows].astype(F32)
            for slot in lines:
                value += self.line[slot, rows].astype(F32)
            self.own[d, rows] = bf(value)

        self.strips(do)

    def hop(self, j):
        p = self.p

        def go(d, way, has_prev):
            self.ready(d)

            def more():
                self.wait_line(d, d)
                self.add(d, [d])

            pl.when(has_prev)(more)
            pl.when(jnp.logical_not(has_prev))(lambda: self.add(d, []))
            self.send_line(d, way).start()

        up = p.line - 1 - j
        pl.when(up > p.a)(lambda: go(up, "up", p.has_down()))
        pl.when(j < p.a)(lambda: go(j, "down", p.has_up()))

    def last(self):
        p = self.p
        lines = p.line
        for a in range(lines):

            def here(a=a):
                self.ready(a)
                slots = []
                if a > 0:
                    self.wait_line(a, a)
                    slots.append(a)
                if a < lines - 1:
                    self.wait_line(a, lines)
                    slots.append(lines)

                def do(rows):
                    value = self.own[a, rows].astype(F32) + self.peer[a, rows].astype(F32)
                    for slot in slots:
                        value += self.line[slot, rows].astype(F32)
                    self.total[rows] = value

                self.strips(do)

            pl.when(p.a == a)(here)
        self.x_copy().start()
        if not self.whole:
            self.out_copy().start()

    def half(self, x):
        return self.total.at[pl.ds(x * self.unit, self.unit)]

    def place(self):
        return self.out.at[:, pl.ds(self.p.x * self.width, self.width)]

    def x_copy(self):
        p = self.p
        where = self.out.at[1] if self.whole else self.place()
        return remote(self.half(1 - p.x), where, self.x_sem.at[0], self.x_sem.at[1], p.partner())

    def out_copy(self):
        return pltpu.make_async_copy(self.half(self.p.x), self.place(), self.x_sem.at[2])

    def finish(self):
        p = self.p
        self.x_copy().wait()
        if self.whole:
            self.out[0] = self.out[1] + self.half(p.x)[...]
        else:
            self.out_copy().wait()
        for a in range(p.line):
            self.b_copy(a).wait_send()
            pl.when(a > p.a)(lambda a=a: self.send_line(a, "up").wait_send())
            pl.when(a < p.a)(lambda a=a: self.send_line(a, "down").wait_send())


def scatter_scratch(line, block):
    return [
        pltpu.VMEM((line,) + block, BF16), pltpu.VMEM((line,) + block, BF16), pltpu.VMEM((line + 1,) + block, BF16),
        pltpu.VMEM(block, F32),
        pltpu.SemaphoreType.DMA((line,)), pltpu.SemaphoreType.DMA((2, line)), pltpu.SemaphoreType.DMA((2, line + 1)),
        pltpu.SemaphoreType.DMA((3,)),
    ]


def greet_all(place):
    barrier = pltpu.get_barrier_semaphore()

    def one(i, carry):
        signal(barrier, (lax.rem(place.s + i // 2, place.size), lax.rem(place.c + lax.rem(i, 2), 2)))
        return carry

    lax.fori_loop(1, 2 * place.size, one, 0)
    pl.semaphore_wait(barrier, 2 * place.size - 1)


class Smalls:
    def __init__(self, place, pack, out, came, sems):
        self.p, self.pack, self.out, self.came, self.sems = place, pack, out, came, sems

    def copy(self, i):
        p = self.p
        s = lax.rem(p.s + i // 2, p.size)
        return remote(
            self.pack.at[s], self.came.at[i], self.sems.at[0, i], self.sems.at[1, i], (s, lax.rem(p.c + lax.rem(i, 2), 2))
        )

    def start(self):
        lax.fori_loop(1, 2 * self.p.size, lambda i, c: (self.copy(i).start(), c)[1], 0)

    def finish(self):
        def one(i, total):
            self.copy(i).wait()
            return total + self.came[i]

        self.out[...] = lax.fori_loop(1, 2 * self.p.size, one, self.pack[self.p.s])


def scatter_kernel(size, plan, *refs):
    p = Place(size)
    grads = max(i for i, _, _, _ in plan) + 1
    outs = len(plan)
    ins, refs = refs[: grads + 1], refs[grads + 1 :]
    out_refs, refs = refs[: outs + 1], refs[outs + 1 :]
    came, s_sem = refs[:2]
    refs = refs[2:]
    greet_all(p)
    smalls = Smalls(p, ins[grads], out_refs[outs], came, s_sem)
    work = []
    for n, (i, unit, offset, width) in enumerate(plan):
        mine = refs[8 * n : 8 * n + 8]
        work.append(Scatter(p, ins[i], out_refs[n], unit, offset, width, mine[:4], mine[4:]))
    work[0].start()
    smalls.start()
    for n, chunk in enumerate(work):
        if n + 1 < len(work):
            work[n + 1].start()
        for j in range(p.line - 1):
            chunk.hop(j)
        chunk.last()
    smalls.finish()
    for chunk in work:
        chunk.finish()


def scatter(size, number, plan, grads, pack):
    line = size // 4
    shapes, specs, scratch = [], [], []
    for i, unit, offset, width, whole in plan:
        shapes.append(jax.ShapeDtypeStruct((2, unit, width) if whole else (unit, 2 * width), F32))
        specs.append(VM if whole else ANY)
        scratch += scatter_scratch(line, (2 * unit, width))
    return pl.pallas_call(
        functools.partial(scatter_kernel, size, [entry[:4] for entry in plan]),
        out_shape=shapes + [jax.ShapeDtypeStruct(pack.shape[1:], F32)],
        in_specs=[ANY] * len(grads) + [VM],
        out_specs=specs + [VM],
        scratch_shapes=[pltpu.VMEM((2 * size,) + pack.shape[1:], F32), pltpu.SemaphoreType.DMA((2, 2 * size))] + scratch,
        compiler_params=remote_params(number, 60),
        name="scatter",
    )(*grads, pack)


class Swap:
    def __init__(self, place, own, both, sems):
        p = self.p = place
        self.keep = pltpu.make_async_copy(own, both.at[:, p.x], sems.at[0])
        self.cross = remote(own.at[p.c], both.at[p.c, p.x], sems.at[1], sems.at[2], p.partner())
        came = both.at[p.c, 1 - p.x]
        self.hand = remote(came, came, sems.at[3], sems.at[4], p.sibling())

    def start(self):
        self.cross.start()
        self.keep.start()

    def forward(self):
        self.cross.wait_recv()
        self.hand.start()

    def finish(self):
        self.keep.wait()
        self.cross.wait_send()
        self.hand.wait()


def gather_kernel(size, plan, swaps, *refs):
    p = Place(size)
    shards = len(plan)
    fulls = max(i for i, _, _, _, _ in plan) + 1
    ins, refs = refs[: shards + swaps], refs[shards + swaps :]
    outs, refs = refs[: fulls + swaps], refs[fulls + swaps :]
    greet(p, sibling=True)
    work = []
    for n, (i, unit, offset, width, late) in enumerate(plan):
        work.append(Gather(p, ins[n], outs[i], unit, offset, width, refs[4 * n : 4 * n + 4], late))
    moves = [Swap(p, ins[shards + n], outs[fulls + n], refs[4 * shards + n]) for n in range(swaps)]
    weave = Weave(gather_ops(work, len(work)))
    weave.run(len(work))
    for move in moves:
        move.start()
    weave.run(len(weave.steps) - len(work))
    for move in moves:
        move.forward()
    weave.rest()
    for move in moves:
        move.finish()


def gather(size, number, plan, shards, fulls, tokens):
    line = size // 4
    scratch = []
    for _ in plan:
        scratch += gather_sems(line)
    shapes = [jax.ShapeDtypeStruct(shape, BF16) for shape in fulls]
    for array in tokens:
        shapes.append(jax.ShapeDtypeStruct((array.shape[0], 2) + array.shape[1:], BF16))
        scratch.append(pltpu.SemaphoreType.DMA((5,)))
    return pl.pallas_call(
        functools.partial(gather_kernel, size, plan, len(tokens)),
        out_shape=shapes,
        in_specs=[ANY] * (len(shards) + len(tokens)),
        out_specs=[ANY] * len(shapes),
        scratch_shapes=scratch,
        compiler_params=remote_params(number, 60),
        name="gather",
    )(*shards, *tokens)


def dot(left, right, dims, dtype=F32):
    return lax.dot_general(left, right, dims, preferred_element_type=F32).astype(dtype)


def lanes(row):
    return jnp.pad(row.reshape(-1), (0, 128 - row.size))


def shards(
    tokens, grad_out, query_weight, key_weight, value_weight, forget_weight, forget_bias, outgate_weight, output_weight,
    slot_gain, first_gain, second_gain, gate_weight, up_weight, down_weight,
):
    size = lax.axis_size("seq")
    x = lax.rem(lax.axis_index("seq"), 2)
    c = lax.axis_index("head")
    seqs, block, width = tokens.shape
    heads_here, slot_part = forget_bias.shape
    slots = slot_part * size
    head = slot_gain.shape[0] * size
    unit = first_gain.shape[0]
    hidden = gate_weight.shape[1] // 2
    rows = seqs * 2 * block
    pack = jnp.stack([lanes(first_gain), lanes(second_gain), lanes(slot_gain), lanes(forget_bias)] + [jnp.zeros(128, BF16)] * 12)
    plan = [
        (0, unit, 0, head, False), (0, unit, head, head, False), (0, unit, 2 * head, head, False),
        (1, unit, 0, head, False), (1, unit, head, 2 * slots, False), (2, unit, 0, head, False),
        (3, 16, 0, 128, False),
    ]
    fulls = [(width, 3 * head), (width, head + 2 * slots), (width, head), (16 * size, 128)]
    qkv_full, gate_full, out_full, small_full, tok, gout = gather(
        size, 0, plan,
        (query_weight, key_weight, value_weight, outgate_weight, forget_weight, output_weight.T, pack),
        fulls, (tokens, grad_out),
    )
    small = small_full.reshape(size, 16, 128).astype(F32)
    first_full = small[:, 0, :unit].reshape(1, width)
    second_full = small[:, 1, :unit].reshape(1, width)
    slot_full = small[:, 2, : head // size].reshape(1, head)
    bias_full = small[:, 3, : heads_here * slot_part].reshape(size, heads_here, slot_part)
    bias_full = jnp.moveaxis(bias_full, 1, 0).reshape(heads_here, slots)

    def own_head(array, axis):
        return jnp.where(x == 0, *jnp.split(array, 2, axis=axis))

    inputs = tok.reshape(rows, width).astype(F32)
    normed_one = (inputs * inverse_rms(inputs) * first_full).astype(BF16)
    qkv = dot(normed_one, qkv_full, NN, BF16)
    gates = dot(normed_one, gate_full, NN)
    logit = own_head(gates[:, head:], 1) + own_head(bias_full, 0)
    decay = -jax.nn.softplus(-logit) / TAU
    keep = -jnp.expm1(decay)
    chunk = min(CHUNK, 2 * block)
    slot = Slots(seqs, 2 * block, head, slots, chunk)
    ff_plan = [(0, unit, 0, hidden, False), (0, unit, hidden, hidden, False), (1, unit, 0, hidden, False)]
    (gated, attended, probs, scores, weights, states, decs, end_decs, residual, normed_two, ff_full, down_full) = forward(
        size, 1, slot, ff_plan, [(width, 2 * hidden), (width, hidden)], qkv, gates, decay, keep, slot_full, out_full, tokens,
        second_full, (gate_weight, up_weight, down_weight.T),
    )
    decs = decs.reshape(seqs * slot.chunks, slots, 128)
    shape = (seqs, 2, block, width)
    normed_two = normed_two.reshape(rows, width)
    ff = dot(normed_two, ff_full, NN)
    ff_gate, ff_up = ff[:, :hidden], ff[:, hidden:]
    sig = jax.nn.sigmoid(ff_gate)
    activated = (ff_gate * sig * ff_up).astype(BF16)
    ff_part = dot(activated, down_full, NT, BF16).reshape(shape)
    gout = gout.reshape(rows, width)
    act_grad = dot(gout, down_full, NN)
    ff_term = jnp.concatenate(
        [act_grad * ff_up * (sig + ff_gate * sig * (1.0 - sig)), act_grad * ff_gate * sig], axis=1
    ).astype(BF16)
    down_grad = dot(gout, activated, TN, BF16)
    ff_grad = dot(normed_two, ff_term, TN, BF16)
    normed_two_grad = dot(ff_term, ff_full, NT, BF16).reshape(shape)
    residual_grad, low, second_part = blend_back(size, 3, normed_two_grad, grad_out, residual, second_full)
    low = low.reshape(rows, width)
    gated_grad = dot(low, out_full, NN)
    out_grad = dot(low, gated, TN, BF16)
    gate_term, slot_part_grad, att_grad, dprobs, dscores, back_units, back_ends = slot.back_one(
        qkv, gates, decay, keep, gated_grad, attended, probs, states, decs, slot_full
    )
    finals = prefix(size, 4, back_ends, end_decs, True)
    qkv_term, decay_term = slot.back_two(
        qkv, decay, keep, probs, scores, weights, states, decs, back_units, att_grad, dprobs, dscores, finals
    )
    forget_term = (decay_term * jax.nn.sigmoid(-logit) / TAU).astype(BF16)
    none = jnp.zeros_like(forget_term)
    gates_term = jnp.concatenate(
        [gate_term, jnp.where(x == 0, forget_term, none), jnp.where(x == 0, none, forget_term)], axis=1
    )
    qkv_grad = dot(normed_one, qkv_term, TN, BF16)
    gates_grad = dot(normed_one, gates_term, TN, BF16)
    normed_one_grad = (dot(qkv_term, qkv_full, NT) + dot(gates_term, gate_full, NT)).astype(BF16).reshape(shape)
    input_grad, output, first_part = finish(size, 5, normed_one_grad, ff_part, tokens, residual, residual_grad, first_full)
    bias_part = jnp.sum(forget_term.astype(F32), axis=0)
    which = jnp.arange(2 * heads_here) == heads_here * c + x
    bias_part = jnp.where(which[:, None], bias_part[None, :], 0.0).reshape(2 * heads_here, size, slot_part)
    slot_part_sum = jnp.sum(slot_part_grad[:, 0], axis=0)

    def rows_of(array):
        array = array.reshape(size, -1)
        return jnp.pad(array, ((0, 0), (0, 128 - array.shape[1])))

    zero = jnp.zeros((size, 128), F32)
    packed = jnp.stack(
        [rows_of(first_part), rows_of(second_part), rows_of(slot_part_sum), rows_of(jnp.moveaxis(bias_part, 1, 0))] + [zero] * 4, axis=1
    )
    grads = (ff_grad, down_grad, out_grad, qkv_grad, gates_grad)
    plan = [
        (0, unit, 0, hidden, False), (0, unit, hidden, hidden, False), (1, unit, 0, hidden, False), (2, unit, 0, head, False),
        (3, unit, 0, head, False), (3, unit, head, head, False), (3, unit, 2 * head, head, False), (4, unit, 0, head, False),
        (4, unit, head, 2 * slots, True),
    ]
    gate_grad, up_grad, down_grad, output_grad, query_grad, key_grad, value_grad, outgate_grad, forget_grad, sums = scatter(
        size, 6, plan, grads, packed
    )
    bias_grad = sums[3, : 2 * heads_here * slot_part].reshape(2, heads_here, slot_part)
    bias_grad = jnp.where(c == 0, bias_grad[0], bias_grad[1])
    return (
        output, input_grad, query_grad, key_grad, value_grad, forget_grad[0], bias_grad, outgate_grad, output_grad.T,
        sums[2, : head // size], sums[0, :unit], sums[1, :unit], gate_grad, up_grad, down_grad.T,
    )


def solution(mesh):
    row, column, vector, token = P("seq", "head"), P("head", "seq"), P("seq"), P(None, "seq", None)
    return jax.shard_map(
        shards,
        mesh=mesh,
        in_specs=(token, token, row, row, row, row, column, row, column, vector, vector, vector, row, row, column),
        out_specs=(token, token, row, row, row, row, column, row, column, vector, vector, vector, row, row, column),
        check_vma=False,
    )
```

```python
import functools

import jax
import jax.numpy as jnp
import numpy as np
from jax import lax
from jax.experimental import pallas as pl
from jax.experimental.pallas import tpu as pltpu
from jax.sharding import PartitionSpec as P

F32, BF16 = jnp.float32, jnp.bfloat16
MESH = pl.DeviceIdType.MESH
HBM = pltpu.HBM
EPS = 1e-06
TAU = 8.0


CHUNK = 256
NT = (((1,), (1,)), ((), ()))
NN = (((1,), (0,)), ((), ()))
TN = (((0,), (0,)), ((), ()))


def decay_tables(count):
    at = np.arange(count)
    paths, masks = [], []
    half = count // 2
    while half >= 1:
        block, second = at // (2 * half), (at // half) % 2 == 1
        edge = block * 2 * half + half - 1
        r, t = at[None, :], at[:, None]
        fore = second[:, None] & (r > edge[:, None]) & (r <= t)
        back = ~second[:, None] & (r > t) & (r <= edge[:, None])
        paths.append(fore | back)
        masks.append((block[:, None] == block[None, :]) & second[:, None] & ~second[None, :])
        half //= 2
    paths.append(at[None, :] <= at[:, None])
    paths.append(at[None, :] > at[:, None])
    return np.concatenate(paths, 0), np.stack(masks)


def bf(x):
    return x.astype(BF16)


def halves(x):
    hi = bf(x)
    return hi, bf(x - hi.astype(F32))


def mm(a, b, dims):
    return lax.dot_general(a, b, dims, preferred_element_type=F32)


def dot3(a, b, dims):
    return mm(a[0], b[0], dims) + (mm(a[0], b[1], dims) + mm(a[1], b[0], dims))


def exact_sums(table, x):
    hi, mid = halves(x)
    low = bf(x - hi.astype(F32) - mid.astype(F32))
    n = x.shape[1]
    both = mm(table, jnp.concatenate([hi, mid, low, jnp.zeros_like(low)], axis=1), NN)
    return both[:, :n] + (both[:, n : 2 * n] + both[:, 2 * n : 3 * n])


def silu(v):
    return v / (1.0 + jnp.exp(-v))


def sigmoid(v):
    return 1.0 / (1.0 + jnp.exp(-v))


def silu_slope(v):
    s = sigmoid(v)
    return s + v * s * (1.0 - s)


def columns_total(x):
    ones = jnp.ones((x.shape[0], 128), BF16)
    hi, mid = halves(x)
    low = bf(x - hi.astype(F32) - mid.astype(F32))
    return mm(hi, ones, TN) + (mm(mid, ones, TN) + mm(low, ones, TN))


def spread(column, width):
    return jnp.concatenate([column] * (width // 128), axis=1)


def mix(pair, ratios, keep, masks_ref, own):
    out = own * keep
    for l, ratio in enumerate(ratios):
        left = pair * masks_ref[l].astype(F32)
        out += ratio * dot3(halves(left), halves(ratio * keep), NN)
    return out


def unmix(probs, ratios, keep, masks_ref, diag):
    out = diag * jnp.sum(probs * keep, axis=1, keepdims=True)
    for l, ratio in enumerate(ratios):
        part = dot3(halves(probs * ratio), halves(ratio * keep), NT)
        out += masks_ref[l].astype(F32) * part
    return out


def on_diagonal(count):
    return (
        lax.broadcasted_iota(jnp.int32, (count, count), 0) == lax.broadcasted_iota(jnp.int32, (count, count), 1)
    ).astype(F32)


class Slots:
    def __init__(self, seqs, rows, head, slots, chunk):
        self.seqs, self.rows, self.head, self.slots, self.chunk = seqs, rows, head, slots, chunk
        self.chunks = rows // chunk
        paths, masks = decay_tables(chunk)
        self.levels = masks.shape[0]
        self.paths = jnp.asarray(paths, BF16)
        self.masks = jnp.asarray(masks, BF16)

class Place:
    def __init__(self, size):
        self.size = size
        self.line = size // 4
        s = lax.axis_index("seq")
        self.c = lax.axis_index("head")
        self.s = s
        self.x = lax.rem(s, 2)
        self.b = lax.rem(s // 2, 2)
        self.a = s // 4

    def at(self, a, b, x):
        return (a * 2 + b) * 2 + x

    def partner(self):
        return (self.at(self.a, self.b, 1 - self.x), self.c)

    def across(self):
        return (self.at(self.a, 1 - self.b, self.x), self.c)

    def up(self):
        return (self.at(jnp.minimum(self.a + 1, self.line - 1), self.b, self.x), self.c)

    def down(self):
        return (self.at(jnp.maximum(self.a - 1, 0), self.b, self.x), self.c)

    def sibling(self):
        return (self.s, 1 - self.c)

    def has_up(self):
        return self.a < self.line - 1

    def has_down(self):
        return self.a > 0


def signal(sem, device):
    pl.semaphore_signal(sem, inc=1, device_id=device, device_id_type=MESH)


def greet(place, partner=True, across=True, line=True, sibling=False):
    barrier = pltpu.get_barrier_semaphore()
    count = jnp.int32(0)
    if partner:
        signal(barrier, place.partner())
        count = count + 1
    if sibling:
        signal(barrier, place.sibling())
        count = count + 1
    if across:
        signal(barrier, place.across())
        count = count + 1
    if line:
        pl.when(place.has_up())(lambda: signal(barrier, place.up()))
        pl.when(place.has_down())(lambda: signal(barrier, place.down()))
        count = count + place.has_up().astype(jnp.int32) + place.has_down().astype(jnp.int32)
    pl.semaphore_wait(barrier, count)


def remote(src, dst, send, recv, device):
    return pltpu.make_async_remote_copy(
        src_ref=src, dst_ref=dst, send_sem=send, recv_sem=recv, device_id=device, device_id_type=MESH
    )


class Gather:
    def __init__(self, place, shard, full, unit, offset, width, sems, late):
        self.pl, self.shard, self.full = place, shard, full
        self.unit, self.offset, self.width, self.late = unit, offset, width, late
        self.x_sem, self.b_sem, self.up_sem, self.down_sem = sems

    def part(self, start, count):
        rows = pl.ds(start * self.unit, count * self.unit)
        if self.width == self.full.shape[1]:
            return self.full.at[rows]
        return self.full.at[rows, pl.ds(self.offset, self.width)]

    def mine(self, x):
        if self.shard.shape[1] == self.width:
            return self.shard
        return self.shard.at[:, pl.ds(x * self.width, self.width)]

    def x_copy(self):
        p = self.pl
        return remote(self.mine(1 - p.x), self.part(p.s, 1), self.x_sem.at[0], self.x_sem.at[1], p.partner())

    def own_copy(self):
        return pltpu.make_async_copy(self.mine(self.pl.x), self.part(self.pl.s, 1), self.x_sem.at[2])

    def block(self, a):
        p = self.pl
        if self.late:
            return self.part(4 * a, 4)
        return self.part(4 * a + 2 * p.b, 2)

    def b_copy(self, i, a):
        p = self.pl
        return remote(
            self.part(4 * a + 2 * p.b, 2), self.part(4 * a + 2 * p.b, 2),
            self.b_sem.at[0, i], self.b_sem.at[1, i], p.across(),
        )

    def line_copy(self, way, h):
        p = self.pl
        if way == "up":
            blk = self.block(jnp.maximum(p.a - (h - 1), 0))
            return remote(blk, blk, self.up_sem.at[0, h - 1], self.up_sem.at[1, h - 1], p.up())
        blk = self.block(jnp.minimum(p.a + (h - 1), p.line - 1))
        return remote(blk, blk, self.down_sem.at[0, h - 1], self.down_sem.at[1, h - 1], p.down())

    def sends(self, way, h):
        p = self.pl
        if way == "up":
            return jnp.logical_and(p.has_up(), p.a - (h - 1) >= 0)
        return jnp.logical_and(p.has_down(), p.a + (h - 1) <= p.line - 1)

    def gets(self, way, h):
        p = self.pl
        if way == "up":
            return p.a - h >= 0
        return p.a + h <= p.line - 1

    def got(self, way, h):
        p = self.pl
        if way == "up":
            return jnp.maximum(p.a - h, 0)
        return jnp.minimum(p.a + h, p.line - 1)

    def slot(self, way, h):
        return h if way == "up" else self.pl.line - 1 + h

    def start_x(self):
        self.x_copy().start()
        self.own_copy().start()

    def stage(self, h):
        p = self.pl
        if h == 0:
            self.own_copy().wait()
            self.x_copy().wait_recv()
            if self.late:
                self.b_copy(0, p.a).start()
            else:
                for way in ("up", "down"):
                    pl.when(self.sends(way, 1))(lambda way=way: self.line_copy(way, 1).start())
                self.b_copy(0, p.a).start()
            return
        if self.late:
            if h == 1:
                self.b_copy(0, p.a).wait_recv()
                for way in ("up", "down"):
                    pl.when(self.sends(way, 1))(lambda way=way: self.line_copy(way, 1).start())
                return
            h = h - 1
        for way in ("up", "down"):

            def go(way=way):
                self.line_copy(way, h).wait_recv()
                if not self.late:
                    self.b_copy(self.slot(way, h), self.got(way, h)).start()

            def on(way=way):
                self.line_copy(way, h + 1).start()

            pl.when(self.gets(way, h))(go)
            if h + 1 <= p.line - 1:
                pl.when(self.sends(way, h + 1))(on)

    def stages(self):
        return self.pl.line + (1 if self.late else 0)

    def finish(self):
        p = self.pl
        self.x_copy().wait_send()
        self.b_copy(0, p.a).wait_send()
        if not self.late:
            self.b_copy(0, p.a).wait_recv()
        for way in ("up", "down"):
            for h in range(1, p.line):
                pl.when(self.sends(way, h))(lambda way=way, h=h: self.line_copy(way, h).wait_send())
                if not self.late:

                    def both(way=way, h=h):
                        cp = self.b_copy(self.slot(way, h), self.got(way, h))
                        cp.wait_send()
                        cp.wait_recv()

                    pl.when(self.gets(way, h))(both)


def gather_sems(line):
    return [
        pltpu.SemaphoreType.DMA((3,)),
        pltpu.SemaphoreType.DMA((2, 2 * line - 1)),
        pltpu.SemaphoreType.DMA((2, line - 1)),
        pltpu.SemaphoreType.DMA((2, line - 1)),
    ]


def gather_ops(gathers, ahead):
    steps = []
    n = len(gathers)
    for k in range(min(ahead, n)):
        steps.append(gathers[k].start_x)
    steps.append(functools.partial(gathers[0].stage, 0))
    for k in range(n):
        if k + ahead < n:
            steps.append(gathers[k + ahead].start_x)
        if k + 1 < n:
            steps.append(functools.partial(gathers[k + 1].stage, 0))
        for h in range(1, gathers[k].stages()):
            steps.append(functools.partial(gathers[k].stage, h))
    for g in gathers:
        steps.append(g.finish)
    return steps

VM = pl.BlockSpec(memory_space=pltpu.VMEM)
ANY = pl.BlockSpec(memory_space=HBM)


def remote_params(number, mib=56):
    return pltpu.CompilerParams(collective_id=number, has_side_effects=True, vmem_limit_bytes=mib * 2**20)


STRIPS = 4


class Fold:
    def __init__(self, place, part, sib, sent, came, sems, own=None):
        self.p, self.part, self.sib, self.sent, self.came = place, part, sib, sent, came
        self.own = part.at[place.c] if own is None else own
        self.s_sem, self.x_sem = sems
        self.rows = part.shape[2] // STRIPS

    def strip(self, r):
        return pl.ds(r * self.rows, self.rows)

    def sib_copy(self, far, r):
        p = self.p
        x = 1 - p.x if far else p.x
        i = (0 if far else STRIPS) + r
        return remote(
            self.part.at[1 - p.c, x, self.strip(r)], self.sib.at[1 if far else 0, self.strip(r)],
            self.s_sem.at[0, i], self.s_sem.at[1, i], p.sibling(),
        )

    def x_copy(self, r):
        return remote(
            self.sent.at[self.strip(r)], self.came.at[self.strip(r)], self.x_sem.at[0, r], self.x_sem.at[1, r], self.p.partner()
        )

    def start(self):
        for r in range(STRIPS):
            self.sib_copy(True, r).start()
        for r in range(STRIPS):
            self.sib_copy(False, r).start()

    def sib_all(self, far):
        for r in range(STRIPS):
            self.sib_copy(far, r).start()

    def cross(self, r):
        p = self.p
        self.sib_copy(True, r).wait_recv()
        own = self.own[1 - p.x, self.strip(r)].astype(F32)
        self.sent[self.strip(r)] = bf(own + self.sib[1, self.strip(r)].astype(F32))
        self.x_copy(r).start()

    def total(self, r):
        p = self.p
        self.sib_copy(False, r).wait_recv()
        self.x_copy(r).wait_recv()
        own = self.own[p.x, self.strip(r)].astype(F32) + self.sib[0, self.strip(r)].astype(F32)
        return own + self.came[self.strip(r)].astype(F32)

    def finish(self):
        for r in range(STRIPS):
            self.sib_copy(True, r).wait_send()
            self.sib_copy(False, r).wait_send()
            self.x_copy(r).wait_send()


def fold_scratch(rows, width):
    return [
        pltpu.VMEM((2, rows, width), BF16), pltpu.VMEM((rows, width), BF16), pltpu.VMEM((rows, width), BF16),
        pltpu.SemaphoreType.DMA((2, 2 * STRIPS)), pltpu.SemaphoreType.DMA((2, STRIPS)),
    ]


class Share:
    def __init__(self, place, out, sems):
        self.p, self.out = place, out
        self.x_sem, self.s_sem = sems
        self.rows = out.shape[2] // STRIPS

    def strip(self, r):
        return pl.ds(r * self.rows, self.rows)

    def x_copy(self, r):
        p = self.p
        block = self.out.at[p.c, p.x, self.strip(r)]
        return remote(block, block, self.x_sem.at[0, r], self.x_sem.at[1, r], p.partner())

    def s_copy(self, far, r):
        p = self.p
        block = self.out.at[p.c, 1 - p.x if far else p.x, self.strip(r)]
        i = (0 if far else STRIPS) + r
        return remote(block, block, self.s_sem.at[0, i], self.s_sem.at[1, i], p.sibling())

    def put(self, r, value):
        self.out[self.p.c, self.p.x, self.strip(r)] = value
        self.x_copy(r).start()
        self.s_copy(False, r).start()

    def forward(self, r):
        self.x_copy(r).wait_recv()
        self.s_copy(True, r).start()

    def wait_sibling(self, far):
        for r in range(STRIPS):
            self.s_copy(far, r).wait_recv()

    def finish(self, receive=True):
        for r in range(STRIPS):
            self.x_copy(r).wait_send()
            for far in (False, True):
                self.s_copy(far, r).wait_send()
                if receive:
                    self.s_copy(far, r).wait_recv()


SHARE_SEMS = [pltpu.SemaphoreType.DMA((2, STRIPS)), pltpu.SemaphoreType.DMA((2, 2 * STRIPS))]


def inverse_rms(values):
    return lax.rsqrt(jnp.mean(values * values, axis=-1, keepdims=True) + EPS)


def norm_back(grad, values, gain):
    scale = inverse_rms(values)
    u = grad * gain
    down = scale * u - values * (scale * scale * scale) * jnp.mean(u * values, axis=-1, keepdims=True)
    return down, jnp.sum(grad * values * scale, axis=0, keepdims=True)


def ends_chunk(k, v, decay, keep, tail):
    weight = halves(jnp.exp(exact_sums(tail, decay)) * keep)
    unit_k = dot3(weight, halves(silu(k.astype(F32))), TN)
    unit_v = mm(weight[0], v, TN) + mm(weight[1], v, TN)
    return jnp.concatenate([unit_k, unit_v], axis=1), jnp.exp(columns_total(decay))


def powers_of(table, count, levels, decay):
    powers = jnp.exp(exact_sums(table, decay))
    return [powers[l * count : (l + 1) * count] for l in range(levels)], [
        powers[l * count : (l + 1) * count] for l in range(levels, table.shape[0] // count)
    ]


class Prefix:
    def __init__(self, place, back, own, dec, start, peer, peer_dec, line, out, sems):
        p = self.p = place
        self.own, self.dec, self.start_ref, self.peer, self.peer_dec = own, dec, start, peer, peer_dec
        self.line, self.out = line, out
        self.p_sem, self.d_sem, self.l_sem = sems
        seqs, slots, width = own.shape
        self.half = width // 2
        self.pieces = [(b, h) for b in range(seqs) for h in range(2)]
        if back:
            self.has_prev, self.has_next, self.after = p.has_up(), p.has_down(), p.down()
        else:
            self.has_prev, self.has_next, self.after = p.has_down(), p.has_up(), p.up()
        self.first = ((p.b == 1) if back else (p.b == 0)).astype(F32)

    def cut(self, ref, i):
        b, h = self.pieces[i]
        return ref.at[b, :, pl.ds(h * self.half, self.half)]

    def peer_copy(self, i):
        return remote(self.cut(self.own, i), self.cut(self.peer, i), self.p_sem.at[0, i], self.p_sem.at[1, i], self.p.across())

    def line_copy(self, i):
        return remote(self.cut(self.out, i), self.cut(self.line, i), self.l_sem.at[0, i], self.l_sem.at[1, i], self.after)

    def dec_copy(self):
        return remote(self.dec, self.peer_dec, self.d_sem.at[0], self.d_sem.at[1], self.p.across())

    def start(self):
        self.dec_copy().start()
        for i in range(len(self.pieces)):
            self.peer_copy(i).start()

    def run(self):
        self.dec_copy().wait_recv()
        for i, (b, _) in enumerate(self.pieces):
            self.peer_copy(i).wait_recv()
            dec_own = spread(self.dec[b], self.half)
            dec_peer = spread(self.peer_dec[b], self.half)
            own, other = self.cut(self.own, i)[...], self.cut(self.peer, i)[...]
            first = self.first
            both = first * (dec_peer * own + other) + (1.0 - first) * (dec_own * other + own)
            here, result = self.cut(self.out, i), self.cut(self.start_ref, i)

            def go_on(i=i):
                self.line_copy(i).wait_recv()
                came = self.cut(self.line, i)[...]
                here[...] = dec_own * dec_peer * came + both
                result[...] = first * came + (1.0 - first) * (dec_peer * came + other)

            def begin():
                here[...] = both
                result[...] = (1.0 - first) * other

            pl.when(self.has_prev)(go_on)
            pl.when(jnp.logical_not(self.has_prev))(begin)
            pl.when(self.has_next)(lambda i=i: self.line_copy(i).start())

    def finish(self):
        self.dec_copy().wait_send()
        for i in range(len(self.pieces)):
            self.peer_copy(i).wait_send()
            pl.when(self.has_next)(lambda i=i: self.line_copy(i).wait_send())


def prefix_scratch(seqs, slots, width):
    count = 2 * seqs
    return [
        pltpu.VMEM((seqs, slots, width), F32), pltpu.VMEM((seqs, slots, width), F32), pltpu.VMEM((seqs, slots, 128), F32),
        pltpu.VMEM((seqs, slots, width), F32), pltpu.VMEM((seqs, slots, width), F32),
        pltpu.SemaphoreType.DMA((2, count)), pltpu.SemaphoreType.DMA((2,)), pltpu.SemaphoreType.DMA((2, count)),
    ]


def take(refs, count):
    return refs[:count], refs[count:]


class Weave:
    def __init__(self, steps):
        self.steps = list(steps)

    def run(self, count):
        for step in self.steps[:count]:
            step()
        self.steps = self.steps[count:]

    def rest(self):
        self.run(len(self.steps))


def blocks_in_order(p, seqs):
    def block(i):
        b = jnp.where(i < 2, 1 - p.c, p.c)
        x = jnp.where(lax.rem(i, 2) == 0, 1 - p.x, p.x)
        return b, x

    return block


def forward_kernel(size, plan, levels, *refs):
    p = Place(size)
    (qkv, gates, decay, keep, gain, out_w, tokens, gain2, paths, masks), refs = take(refs, 10)
    shard_refs, refs = take(refs, len(plan))
    (gated, attended, probs, scores, weights, states, decs, end_dec, residual, normed), refs = take(refs, 10)
    fulls, refs = take(refs, max(i for i, _, _, _, _ in plan) + 1)
    (units, part, total), refs = take(refs, 3)
    (start, *prefix_refs), refs = take(refs, 8)
    fold_refs, refs = take(refs, 5)
    share_sems, refs = take(refs, 2)
    count = paths.shape[1]
    head = gated.shape[1]
    seqs = tokens.shape[0]
    slots = keep.shape[1]
    greet(p, sibling=True)
    work = []
    for n, (i, unit, offset, width, late) in enumerate(plan):
        work.append(Gather(p, shard_refs[n], fulls[i], unit, offset, width, refs[4 * n : 4 * n + 4], late))
    weave = Weave(gather_ops(work, 3))
    weave.run(3)
    tail = paths[(levels + 1) * count :, :]

    def ends(b):
        for j in range(2):
            rows = pl.ds((b * 2 + j) * count, count)
            unit, dec = ends_chunk(
                qkv[rows, head : 2 * head], qkv[rows, 2 * head :], decay[rows, :], keep[rows, :], tail
            )
            units[b, j] = unit
            decs[b, j] = dec
        total[b] = spread(dec, 2 * head) * units[b, 0] + unit
        end_dec[b] = decs[b, 0] * dec

    for b in range(seqs):
        ends(b)
    carry = Prefix(p, False, total, end_dec, start, *prefix_refs[:4], prefix_refs[4:])
    carry.start()
    weave.run(1)
    carry.run()
    for b in range(seqs):
        states[3 * b] = start[b]
        for j in range(2):
            states[3 * b + j + 1] = spread(decs[b, j], 2 * head) * states[3 * b + j] + units[b, j]
    weave.run(1)
    diag = on_diagonal(count)
    order = blocks_in_order(p, seqs)
    fold = Fold(p, part, *fold_refs[:3], fold_refs[3:])
    share = Share(p, normed, share_sems)

    def attend(i, nothing):
        b, j = order(i)
        rows = pl.ds(pl.multiple_of((b * 2 + j) * count, count), count)
        here = keep[rows, :]
        ratios, (growth,) = powers_of(paths[: (levels + 1) * count, :], count, levels, decay[rows, :])
        query = halves(silu(qkv[rows, :head].astype(F32)) * head ** (-0.5))
        keys = halves(silu(qkv[rows, head : 2 * head].astype(F32)))
        state = states[3 * b + j]
        pair = dot3(query, keys, NT)
        score = mix(pair, ratios, here, masks, jnp.sum(pair * diag, axis=1, keepdims=True))
        score += growth * dot3(query, halves(state[:, :head]), NT)
        raised = jnp.exp(score - jnp.max(score, axis=1, keepdims=True))
        prob = raised / jnp.sum(raised, axis=1, keepdims=True)
        weight = unmix(prob, ratios, here, masks, diag)
        values = qkv[rows, 2 * head :]
        whi, wlo = halves(weight)
        result = mm(whi, values, NN) + mm(wlo, values, NN)
        result += dot3(halves(prob * growth), halves(state[:, head:]), NN)
        scale = lax.rsqrt(jnp.mean(result * result, axis=1, keepdims=True) + EPS)
        low = bf(result * scale * gain[...] * silu(gates[rows, :head]))
        gated[rows, :] = low
        attended[rows, :] = result
        probs[rows, :] = prob
        scores[rows, :] = score
        weights[rows, :] = weight
        part[b, j] = bf(mm(low, out_w[...], NT))
        pl.when(i == 0)(lambda: fold.sib_all(True))
        pl.when(i == 1)(lambda: fold.sib_all(False))
        return nothing

    lax.fori_loop(0, 2, attend, 0)
    weave.run(1)
    lax.fori_loop(2, 3, attend, 0)
    for r in range(STRIPS):
        fold.cross(r)
    lax.fori_loop(3, 4, attend, 0)
    weave.run(1)
    for r in range(STRIPS):
        value = tokens[p.c, fold.strip(r)].astype(F32) + fold.total(r)
        residual[fold.strip(r)] = value
        share.put(r, bf(value * inverse_rms(value) * gain2[...]))
    weave.run(2)
    for r in range(STRIPS):
        share.forward(r)
    weave.rest()
    share.finish()
    fold.finish()
    carry.finish()


def forward(size, number, slot, plan, fulls, qkv, gates, decay, keep, gain, out_w, tokens, gain2, shards):
    seqs, block, width = tokens.shape
    h, m, n, rows = slot.head, slot.slots, slot.chunks, slot.seqs * slot.rows
    shape = jax.ShapeDtypeStruct
    outs = [
        shape((rows, h), BF16), shape((rows, h), F32), shape((rows, m), F32), shape((rows, m), F32), shape((rows, slot.chunk), F32),
        shape((seqs * (n + 1), m, 2 * h), F32), shape((seqs, n, m, 128), F32), shape((seqs, m, 128), F32),
        shape((block, width), F32), shape((seqs, 2, block, width), BF16),
    ]
    scratch = [
        pltpu.VMEM((seqs, n, m, 2 * h), F32), pltpu.VMEM((seqs, 2, block, width), BF16), pltpu.VMEM((seqs, m, 2 * h), F32),
    ]
    scratch += prefix_scratch(seqs, m, 2 * h) + fold_scratch(block, width) + SHARE_SEMS
    for _ in plan:
        scratch += gather_sems(size // 4)
    return pl.pallas_call(
        functools.partial(forward_kernel, size, plan, slot.levels),
        out_shape=outs + [shape(full, BF16) for full in fulls],
        in_specs=[VM] * 10 + [ANY] * len(shards),
        out_specs=[VM] * 10 + [ANY] * len(fulls),
        scratch_shapes=scratch,
        compiler_params=remote_params(number, 60),
        name="attend_forward",
    )(qkv, gates, decay, keep, gain, out_w, tokens, gain2, slot.paths, slot.masks, *shards)

class Pool:
    def __init__(self, refs):
        self.loads, self.extra, self.sends, self.totals, self.sems = refs

    def slot(self, which, slot):
        return self.extra if slot == 3 else self.loads.at[which, slot]


POOL_SENDS = 2


def pool_scratch(rows, width):
    return [
        pltpu.VMEM((2, 3, rows, width), BF16), pltpu.VMEM((rows, width), BF16), pltpu.VMEM((POOL_SENDS, rows, width), BF16),
        pltpu.VMEM((rows, width), F32),
        pltpu.SemaphoreType.DMA((2, 4)),
    ]


class Scatter:
    def __init__(self, place, grad, out, peer, line, unit, offset, width, sems):
        self.p, self.grad, self.out, self.peer, self.line = place, grad, out, peer, line
        self.unit, self.offset, self.width = unit, offset, width
        self.whole = out.shape[-1] == width
        self.b_sem, self.l_sem, self.x_sem = sems

    def goal(self, n):
        p = self.p
        low, high = p.a, p.line - 1 - p.a
        more, less = jnp.maximum(low, high), jnp.minimum(low, high)
        alone = more - less
        up_more = jnp.where(high >= low, 1, -1)
        m = n - alone
        early = n < alone
        reach = jnp.where(early, more - n, less - m // 2)
        side = jnp.where(early, up_more, jnp.where(lax.rem(jnp.maximum(m, 0), 2) == 0, 1, -1))
        return p.a + side * reach

    def block(self, a, b):
        rows = pl.ds((4 * a + 2 * b) * self.unit, 2 * self.unit)
        if self.width == self.grad.shape[1]:
            return self.grad.at[rows]
        return self.grad.at[rows, pl.ds(self.offset, self.width)]

    def b_copy(self, a):
        return remote(self.block(a, 1 - self.p.b), self.peer.at[a], self.b_sem.at[0, a], self.b_sem.at[1, a], self.p.across())

    def start(self):
        for n in range(self.p.line):
            self.b_copy(self.goal(n)).start()

    def cut(self, ref):
        return ref if self.width == ref.shape[1] else ref.at[:, pl.ds(0, self.width)]

    def load(self, pool, which, slot, source):
        return pltpu.make_async_copy(source, self.cut(pool.slot(which, slot)), pool.sems.at[which, slot])

    def prepare(self, pool, which, n):
        d = self.goal(n)
        self.b_copy(d).wait_recv()
        self.load(pool, which, 0, self.block(d, self.p.b)).start()
        self.load(pool, which, 1, self.peer.at[d]).start()

    def loaded(self, pool, which, n):
        d = self.goal(n)
        self.load(pool, which, 0, self.block(d, self.p.b)).wait()
        self.load(pool, which, 1, self.peer.at[d]).wait()

    def strips(self, do):
        rows = 2 * self.unit
        step = max(r for r in (16, 32, 64, 128) if rows % r == 0 and (r == 16 or r * self.width <= 64 * 1024))

        def one(i, carry):
            do(pl.ds(pl.multiple_of(i * step, step), step))
            return carry

        lax.fori_loop(0, rows // step, one, 0)

    def bring(self, pool, which, slot, place):
        remote(self.line.at[place], self.line.at[place], self.l_sem.at[0, 0], self.l_sem.at[1, place], self.p.across()).wait_recv()
        self.load(pool, which, slot, self.line.at[place]).start()

    def send(self, pool, out, n):
        p = self.p
        d = self.goal(n)
        up = d > p.a
        to = jnp.clip(p.a + jnp.where(up, 1, -1), 0, p.line - 1)
        slot = jnp.where(jnp.logical_and(jnp.logical_not(up), d == p.a - 1), p.line, d)
        return remote(
            self.cut(pool.sends.at[out]), self.line.at[slot], self.l_sem.at[0, n], self.l_sem.at[1, slot], (p.at(to, p.b, p.x), p.c)
        )

    def hop(self, pool, which, n, out):
        p = self.p
        d = self.goal(n)
        behind = jnp.logical_or(jnp.logical_and(d > p.a, p.has_down()), jnp.logical_and(d < p.a, p.has_up()))
        pl.when(behind)(lambda: self.bring(pool, which, 2, d))
        self.loaded(pool, which, n)
        a, b, c = (self.cut(pool.slot(which, i)) for i in range(3))
        to = self.cut(pool.sends.at[out])

        def with_line():
            self.load(pool, which, 2, self.line.at[d]).wait()

            def do(rows):
                to[rows] = bf(a[rows].astype(F32) + b[rows].astype(F32) + c[rows].astype(F32))

            self.strips(do)

        def without():
            def do(rows):
                to[rows] = bf(a[rows].astype(F32) + b[rows].astype(F32))

            self.strips(do)

        pl.when(behind)(with_line)
        pl.when(jnp.logical_not(behind))(without)
        self.send(pool, out, n).start()

    def last(self, pool, which):
        p = self.p
        n = p.line - 1
        pl.when(p.has_down())(lambda: self.bring(pool, which, 2, p.a))
        pl.when(p.has_up())(lambda: self.bring(pool, which, 3, p.line))
        self.loaded(pool, which, n)
        a, b, c, d = (self.cut(pool.slot(which, i)) for i in range(4))
        to = self.total = self.cut(pool.totals)

        def first(rows):
            to[rows] = a[rows].astype(F32) + b[rows].astype(F32)

        self.strips(first)

        def more(slot, place, ref):
            def go():
                self.load(pool, which, slot, self.line.at[place]).wait()

                def do(rows):
                    to[rows] = to[rows] + ref[rows].astype(F32)

                self.strips(do)

            return go

        pl.when(p.has_down())(more(2, p.a, c))
        pl.when(p.has_up())(more(3, p.line, d))
        self.x_copy().start()
        if not self.whole:
            self.out_copy().start()

    def half(self, x):
        return self.total.at[pl.ds(x * self.unit, self.unit)]

    def place(self):
        return self.out.at[:, pl.ds(self.p.x * self.width, self.width)]

    def x_copy(self):
        p = self.p
        where = self.out.at[1] if self.whole else self.place()
        return remote(self.half(1 - p.x), where, self.x_sem.at[0], self.x_sem.at[1], p.partner())

    def out_copy(self):
        return pltpu.make_async_copy(self.half(self.p.x), self.place(), self.x_sem.at[2])

    def sent(self):
        self.x_copy().wait_send()
        if not self.whole:
            self.out_copy().wait()

    def finish(self):
        p = self.p
        self.x_copy().wait_recv()
        if self.whole:
            self.out[0] = self.out[1] + self.half(p.x)[...]
        for n in range(p.line):
            self.b_copy(self.goal(n)).wait_send()


def scatter_sems(line):
    return [pltpu.SemaphoreType.DMA((2, line)), pltpu.SemaphoreType.DMA((2, line + 1)), pltpu.SemaphoreType.DMA((3,))]


def scatter_ops(work, pool):
    lines = work[0].p.line
    jobs = [(k, n) for k in range(len(work)) for n in range(lines)]
    steps = [work[0].start]
    if len(work) > 1:
        steps.append(work[1].start)
    sends, totals = [], []

    def job(i):
        k, n = jobs[i]

        def step():
            work[k].prepare(pool, i % 2, n)
            if n == 0 and 0 < k < len(work) - 1:
                work[k + 1].start()
            if n < lines - 1:
                out = len(sends) % POOL_SENDS
                if len(sends) >= POOL_SENDS:
                    ok, on, oo = sends[-POOL_SENDS]
                    work[ok].send(pool, oo, on).wait_send()
                work[k].hop(pool, i % 2, n, out)
                sends.append((k, n, out))
            else:
                if totals:
                    work[totals[-1]].sent()
                work[k].last(pool, i % 2)
                totals.append(k)

        return step

    steps += [job(i) for i in range(len(jobs))]

    def finish():
        for ok, on, oo in sends[-POOL_SENDS:]:
            work[ok].send(pool, oo, on).wait_send()
        work[totals[-1]].sent()
        for chunk in work:
            chunk.finish()

    steps.append(finish)
    return steps

SECOND_JOBS = ((0, 1), (1, 1), (2, 1), (3, 1))


def backward_kernel(size, plan, levels, *refs):
    p = Place(size)
    (grad_out_all, gates_all, attended, grad_part), refs = take(refs, 4)
    (residual, gain2, out_w, qkv, decay, keep, gain, probs, scores, weights, states, decs,
     end_dec, paths, later, masks), refs = take(refs, 16)
    grads = max(i for i, _, _, _, _ in plan) + 1
    grad_refs, refs = take(refs, grads)
    (residual_grad, low, second_part, gate_term, gain_part, term, decay_term), refs = take(refs, 7)
    outs, refs = take(refs, len(plan))
    spaces, refs = take(refs, 2 * len(plan))
    (grad_out, gates, own_part, own_sem, att_grad, dprobs, dscores, units, adjoints, total), refs = take(refs, 10)
    (ending, *prefix_refs), refs = take(refs, 8)
    fold_refs, refs = take(refs, 5)
    share_sems, refs = take(refs, 2)
    pool_refs, refs = take(refs, 5)
    count = paths.shape[1]
    head = gate_term.shape[1]
    seqs = grad_out_all.shape[0]
    own = [
        pltpu.make_async_copy(grad_out_all.at[p.c], grad_out, own_sem.at[0]),
        pltpu.make_async_copy(gates_all.at[:, pl.ds(0, head)], gates, own_sem.at[1]),
        pltpu.make_async_copy(attended, att_grad, own_sem.at[2]),
        pltpu.make_async_copy(grad_part.at[p.c], own_part, own_sem.at[3]),
    ]
    for copy in own:
        copy.start()
    greet(p, sibling=True)
    pool = Pool(pool_refs)
    work = []
    for n, (i, unit, offset, width, _) in enumerate(plan):
        work.append(
            Scatter(p, grad_refs[i], outs[n], spaces[2 * n], spaces[2 * n + 1], unit, offset, width, refs[3 * n : 3 * n + 3])
        )
    weave = Weave(scatter_ops(work, pool))
    fold = Fold(p, grad_part, *fold_refs[:3], fold_refs[3:], own_part)
    share = Share(p, low, share_sems)
    fold.start()
    weave.run(2)
    own[3].wait()
    for r in range(STRIPS):
        fold.cross(r)
    own[0].wait()
    gains = jnp.zeros((1, grad_part.shape[3]), F32)
    for r in range(STRIPS):
        down, more = norm_back(fold.total(r), residual[fold.strip(r)], gain2[...])
        value = grad_out[fold.strip(r)].astype(F32) + down
        gains += more
        residual_grad[fold.strip(r)] = value
        share.put(r, bf(value))
        if r == 1:
            weave.run(1)
    second_part[...] = gains
    weave.run(1)
    diag = on_diagonal(count)
    gain_part[...] = jnp.zeros_like(gain_part)

    def place(i):
        b = jnp.where(lax.rem(i, 2) == 0, p.c, 1 - p.c)
        x = jnp.where(i < 2, p.x, 1 - p.x)
        return b, x

    def first(i, nothing):
        b, j = place(i)
        rows = pl.ds(pl.multiple_of((b * 2 + j) * count, count), count)
        grad = mm(low[b, j], out_w[...], NN)
        gate = gates[rows, :]
        value = att_grad[rows, :]
        scale = lax.rsqrt(jnp.mean(value * value, axis=1, keepdims=True) + EPS)
        normed = value * scale
        weighted = grad * silu(gate)
        gate_term[rows, :] = bf(grad * normed * gain[...] * silu_slope(gate))
        gain_part[...] += jnp.sum(weighted * normed, axis=0, keepdims=True)
        c = weighted * gain[...]
        agrad = scale * c - value * (scale * scale * scale) * jnp.mean(c * value, axis=1, keepdims=True)
        att_grad[rows, :] = agrad
        here = keep[rows, :]
        ratios, (growth,) = powers_of(paths[: (levels + 1) * count, :], count, levels, decay[rows, :])
        ahalf = halves(agrad)
        values = qkv[rows, 2 * head :]
        pair = mm(ahalf[0], values, NT) + mm(ahalf[1], values, NT)
        state = states[3 * b + j]
        dprob = mix(pair, ratios, here, masks, jnp.sum(pair * diag, axis=1, keepdims=True))
        dprob += growth * dot3(ahalf, halves(state[:, head:]), NT)
        prob = probs[rows, :]
        dscore = prob * (dprob - jnp.sum(prob * dprob, axis=1, keepdims=True))
        query = halves(silu(qkv[rows, :head].astype(F32)) * head ** (-0.5))
        dprobs[rows, :] = dprob
        dscores[rows, :] = dscore
        unit_k = dot3(halves(growth * dscore), query, TN)
        unit_v = dot3(halves(growth * prob), ahalf, TN)
        units[b, j] = jnp.concatenate([unit_k, unit_v], axis=1)
        return nothing

    own[1].wait()
    own[2].wait()
    lax.fori_loop(0, 1, first, 0)
    for r in range(STRIPS):
        share.forward(r)
    share.wait_sibling(False)
    lax.fori_loop(1, 3, first, 0)
    weave.run(1)
    share.wait_sibling(True)
    lax.fori_loop(3, 4, first, 0)
    weave.run(1)
    for b in range(seqs):
        total[b] = spread(decs[b, 0], 2 * head) * units[b, 1] + units[b, 0]
    carry = Prefix(p, True, total, end_dec, ending, *prefix_refs[:4], prefix_refs[4:])
    carry.start()
    weave.run(1)
    carry.run()
    weave.run(1)
    for b in range(seqs):
        adjoints[b, 1] = ending[b]
        adjoints[b, 0] = spread(decs[b, 1], 2 * head) * ending[b] + units[b, 1]
    is_last = (lax.broadcasted_iota(jnp.int32, (count, 1), 0) == count - 1).astype(F32)

    def second(i, nothing):
        b, j = place(i)
        rows = pl.ds(pl.multiple_of((b * 2 + j) * count, count), count)
        here = keep[rows, :]
        ratios, (growth, rest) = powers_of(paths[...], count, levels, decay[rows, :])
        qraw = qkv[rows, :head].astype(F32)
        kraw = qkv[rows, head : 2 * head].astype(F32)
        query = halves(silu(qraw) * head ** (-0.5))
        keys = halves(silu(kraw))
        values = qkv[rows, 2 * head :]
        agrad = halves(att_grad[rows, :])
        prob, dscore = probs[rows, :], dscores[rows, :]
        state = halves(states[3 * b + j][:, :head])
        adj = adjoints[b, j]
        ahalf = halves(adj)
        adj_k, adj_v = (ahalf[0][:, :head], ahalf[1][:, :head]), (ahalf[0][:, head:], ahalf[1][:, head:])
        dweights = halves(unmix(dscore, ratios, here, masks, diag))
        dquery = dot3(dweights, keys, NN) + dot3(halves(dscore * growth), state, NN)
        term[rows, :head] = bf(silu_slope(qraw) * dquery * head ** (-0.5))
        left = halves(rest * here)
        dkey = dot3(dweights, query, TN) + dot3(left, adj_k, NN)
        term[rows, head : 2 * head] = bf(silu_slope(kraw) * dkey)
        dvalue = dot3(halves(weights[rows, :]), agrad, TN) + dot3(left, adj_v, NN)
        term[rows, 2 * head :] = bf(dvalue)
        pair_k = dot3(query, keys, NT)
        pair_v = mm(agrad[0], values, NT) + mm(agrad[1], values, NT)
        dkeep = jnp.sum(pair_k * diag, axis=1, keepdims=True) * dscore
        dkeep += jnp.sum(pair_v * diag, axis=1, keepdims=True) * prob
        dkeep += rest * (dot3(keys, adj_k, NT) + mm(values, adj_v[0], NT) + mm(values, adj_v[1], NT))
        for l, ratio in enumerate(ratios):
            mask = masks[l].astype(F32)
            more = dot3(halves(pair_k * mask), halves(dscore * ratio), TN)
            more += dot3(halves(pair_v * mask), halves(prob * ratio), TN)
            dkeep += ratio * more
        dsum = dscore * scores[rows, :] + prob * dprobs[rows, :] - here * dkeep
        at_end = jnp.sum(adj * states[3 * b + j + 1], axis=1, keepdims=True)
        at_end = jnp.sum(at_end * on_diagonal(adj.shape[0]), axis=0, keepdims=True)
        dsum += is_last * at_end
        decay_term[rows, :] = exact_sums(later[...], dsum) - (1.0 - here) * dkeep
        for k, jobs in SECOND_JOBS:
            pl.when(i == k)(functools.partial(weave.run, jobs))
        return nothing

    lax.fori_loop(0, 4, second, 0)
    weave.rest()
    share.finish(False)
    fold.finish()
    carry.finish()


def backward(size, number, slot, plan, hbm_ins, vmem_ins, grads):
    seqs, block, width = hbm_ins[0].shape
    h, m, n, rows = slot.head, slot.slots, slot.chunks, slot.seqs * slot.rows
    line = size // 4
    shape = jax.ShapeDtypeStruct
    outs = [
        shape((block, width), F32), shape((seqs, 2, block, width), BF16), shape((1, width), F32), shape((rows, h), BF16),
        shape((1, h), F32), shape((rows, 3 * h), BF16), shape((rows, m), F32),
    ]
    results, spaces, sems = [], [], []
    for i, unit, offset, columns, whole in plan:
        results.append(shape((2, unit, columns) if whole else (unit, 2 * columns), F32))
        spaces += [shape((line, 2 * unit, columns), BF16), shape((line + 1, 2 * unit, columns), BF16)]
        sems += scatter_sems(line)
    widest = max(entry[3] for entry in plan)
    scratch = [
        pltpu.VMEM((block, width), BF16), pltpu.VMEM((rows, h), F32),
        pltpu.VMEM((2, block, width), BF16), pltpu.SemaphoreType.DMA((4,)),
        pltpu.VMEM((rows, h), F32), pltpu.VMEM((rows, m), F32), pltpu.VMEM((rows, m), F32), pltpu.VMEM((seqs, n, m, 2 * h), F32),
        pltpu.VMEM((seqs, n, m, 2 * h), F32), pltpu.VMEM((seqs, m, 2 * h), F32),
    ]
    scratch += prefix_scratch(seqs, m, 2 * h) + fold_scratch(block, width) + SHARE_SEMS
    scratch += pool_scratch(2 * plan[0][1], widest) + sems
    later = slot.paths[-2 * slot.chunk : -slot.chunk].T
    result = pl.pallas_call(
        functools.partial(backward_kernel, size, plan, slot.levels),
        out_shape=outs + results + spaces,
        in_specs=[ANY] * 4 + [VM] * 16 + [ANY] * len(grads),
        out_specs=[VM] * 7 + [ANY] * (len(results) + len(spaces)),
        scratch_shapes=scratch,
        compiler_params=remote_params(number, 62),
        name="attend_backward",
    )(*hbm_ins, *vmem_ins, slot.paths, later, slot.masks, *grads)
    return result[: 7 + len(results)]


def last_kernel(size, plan, *refs):
    p = Place(size)
    (part, ff_part, tokens, residual, residual_grad, gain, pack), refs = take(refs, 7)
    grads = max(i for i, _, _, _, _ in plan) + 1
    grad_refs, refs = take(refs, grads)
    (input_grad, output, sums), refs = take(refs, 3)
    outs, refs = take(refs, len(plan))
    spaces, refs = take(refs, 2 * len(plan))
    fold_refs, refs = take(refs, 5)
    ff_refs, refs = take(refs, 5)
    (out_sem, mine, came, s_sem), refs = take(refs, 4)
    pool_refs, refs = take(refs, 5)
    greet_all(p)
    pool = Pool(pool_refs)
    work = []
    for n, (i, unit, offset, width, _) in enumerate(plan):
        work.append(
            Scatter(p, grad_refs[i], outs[n], spaces[2 * n], spaces[2 * n + 1], unit, offset, width, refs[3 * n : 3 * n + 3])
        )
    weave = Weave(scatter_ops(work, pool))
    fold = Fold(p, part, *fold_refs[:3], fold_refs[3:])
    ff = Fold(p, ff_part, *ff_refs[:3], ff_refs[3:])
    weave.run(2)
    fold.start()
    ff.start()
    for r in range(STRIPS):
        fold.cross(r)
    weave.run(1)
    gains = jnp.zeros((1, part.shape[3]), F32)

    def out_copy(ref, k, r):
        block = ref.at[p.c, fold.strip(r)]
        return remote(block, block, out_sem.at[0, k * STRIPS + r], out_sem.at[1, k * STRIPS + r], p.sibling())

    for r in range(STRIPS):
        ff.cross(r)
    weave.run(2)
    for r in range(STRIPS):
        down, more = norm_back(fold.total(r), tokens[p.c, fold.strip(r)].astype(F32), gain[...])
        gains += more
        input_grad[p.c, fold.strip(r)] = residual_grad[fold.strip(r)] + down
        out_copy(input_grad, 1, r).start()
        if r % 2 == 1:
            weave.run(1)
    unit = plan[0][1]
    mine[...] = pack[...]
    for s in range(size):
        mine[s, 0:1, pl.ds(0, unit)] = gains[:, s * unit : (s + 1) * unit]
    smalls = Smalls(p, mine, sums, came, s_sem)
    smalls.start()
    weave.run(2)
    for r in range(STRIPS):
        output[p.c, fold.strip(r)] = bf(residual[fold.strip(r)] + ff.total(r))
        out_copy(output, 0, r).start()
        if r % 2 == 1:
            weave.run(1)
    weave.rest()
    smalls.finish()
    for r in range(STRIPS):
        out_copy(output, 0, r).wait()
        out_copy(input_grad, 1, r).wait()
    ff.finish()
    fold.finish()


def last(size, number, plan, vmem_ins, grads):
    seqs, _, block, width = vmem_ins[0].shape
    pack = vmem_ins[-1]
    line = size // 4
    shape = jax.ShapeDtypeStruct
    outs = [shape((seqs, block, width), F32), shape((seqs, block, width), BF16), shape(pack.shape[1:], F32)]
    results, specs, spaces, sems = [], [], [], []
    for i, unit, offset, columns, whole in plan:
        results.append(shape((2, unit, columns) if whole else (unit, 2 * columns), F32))
        specs.append(VM if whole else ANY)
        spaces += [shape((line, 2 * unit, columns), BF16), shape((line + 1, 2 * unit, columns), BF16)]
        sems += scatter_sems(line)
    widest = max(entry[3] for entry in plan)
    scratch = fold_scratch(block, width) * 2 + [
        pltpu.SemaphoreType.DMA((2, 2 * STRIPS)), pltpu.VMEM(pack.shape, F32), pltpu.VMEM((2 * size,) + pack.shape[1:], F32),
        pltpu.SemaphoreType.DMA((2, 2 * size)),
    ]
    scratch += pool_scratch(2 * plan[0][1], widest) + sems
    result = pl.pallas_call(
        functools.partial(last_kernel, size, plan),
        out_shape=outs + results + spaces,
        in_specs=[VM] * 7 + [ANY] * len(grads),
        out_specs=[VM] * 3 + specs + [ANY] * len(spaces),
        scratch_shapes=scratch,
        compiler_params=remote_params(number, 60),
        name="last",
    )(*vmem_ins, *grads)
    return result[: 3 + len(results)]

def greet_all(place):
    barrier = pltpu.get_barrier_semaphore()

    def one(i, carry):
        signal(barrier, (lax.rem(place.s + i // 2, place.size), lax.rem(place.c + lax.rem(i, 2), 2)))
        return carry

    lax.fori_loop(1, 2 * place.size, one, 0)
    pl.semaphore_wait(barrier, 2 * place.size - 1)


class Smalls:
    def __init__(self, place, pack, out, came, sems):
        self.p, self.pack, self.out, self.came, self.sems = place, pack, out, came, sems

    def copy(self, i):
        p = self.p
        s = lax.rem(p.s + i // 2, p.size)
        return remote(
            self.pack.at[s], self.came.at[i], self.sems.at[0, i], self.sems.at[1, i], (s, lax.rem(p.c + lax.rem(i, 2), 2))
        )

    def start(self):
        lax.fori_loop(1, 2 * self.p.size, lambda i, c: (self.copy(i).start(), c)[1], 0)

    def finish(self):
        def one(i, total):
            self.copy(i).wait()
            return total + self.came[i]

        self.out[...] = lax.fori_loop(1, 2 * self.p.size, one, self.pack[self.p.s])


class Swap:
    def __init__(self, place, own, both, sems):
        p = self.p = place
        self.keep = pltpu.make_async_copy(own, both.at[:, p.x], sems.at[0])
        self.cross = remote(own.at[p.c], both.at[p.c, p.x], sems.at[1], sems.at[2], p.partner())
        came = both.at[p.c, 1 - p.x]
        self.hand = remote(came, came, sems.at[3], sems.at[4], p.sibling())

    def start(self):
        self.cross.start()
        self.keep.start()

    def forward(self):
        self.cross.wait_recv()
        self.hand.start()

    def finish(self):
        self.keep.wait()
        self.cross.wait_send()
        self.hand.wait()


def gather_kernel(size, plan, swaps, *refs):
    p = Place(size)
    shards = len(plan)
    fulls = max(i for i, _, _, _, _ in plan) + 1
    ins, refs = refs[: shards + swaps], refs[shards + swaps :]
    outs, refs = refs[: fulls + swaps], refs[fulls + swaps :]
    greet(p, sibling=True)
    work = []
    for n, (i, unit, offset, width, late) in enumerate(plan):
        work.append(Gather(p, ins[n], outs[i], unit, offset, width, refs[4 * n : 4 * n + 4], late))
    moves = [Swap(p, ins[shards + n], outs[fulls + n], refs[4 * shards + n]) for n in range(swaps)]
    weave = Weave(gather_ops(work, len(work)))
    weave.run(len(work))
    for move in moves:
        move.start()
    weave.run(len(weave.steps) - len(work))
    for move in moves:
        move.forward()
    weave.rest()
    for move in moves:
        move.finish()


def gather(size, number, plan, shards, fulls, tokens):
    line = size // 4
    scratch = []
    for _ in plan:
        scratch += gather_sems(line)
    shapes = [jax.ShapeDtypeStruct(shape, BF16) for shape in fulls]
    for array in tokens:
        shapes.append(jax.ShapeDtypeStruct((array.shape[0], 2) + array.shape[1:], BF16))
        scratch.append(pltpu.SemaphoreType.DMA((5,)))
    return pl.pallas_call(
        functools.partial(gather_kernel, size, plan, len(tokens)),
        out_shape=shapes,
        in_specs=[ANY] * (len(shards) + len(tokens)),
        out_specs=[ANY] * len(shapes),
        scratch_shapes=scratch,
        compiler_params=remote_params(number, 60),
        name="gather",
    )(*shards, *tokens)


def dot(left, right, dims, dtype=F32):
    return lax.dot_general(left, right, dims, preferred_element_type=F32).astype(dtype)


def lanes(row):
    return jnp.pad(row.reshape(-1), (0, 128 - row.size))


def shards(
    tokens, grad_out, query_weight, key_weight, value_weight, forget_weight, forget_bias, outgate_weight, output_weight,
    slot_gain, first_gain, second_gain, gate_weight, up_weight, down_weight,
):
    size = lax.axis_size("seq")
    x = lax.rem(lax.axis_index("seq"), 2)
    c = lax.axis_index("head")
    seqs, block, width = tokens.shape
    heads_here, slot_part = forget_bias.shape
    slots = slot_part * size
    head = slot_gain.shape[0] * size
    unit = first_gain.shape[0]
    hidden = gate_weight.shape[1] // 2
    rows = seqs * 2 * block
    pack = jnp.stack([lanes(first_gain), lanes(second_gain), lanes(slot_gain), lanes(forget_bias)] + [jnp.zeros(128, BF16)] * 12)
    plan = [
        (0, unit, 0, head, False), (0, unit, head, head, False), (0, unit, 2 * head, head, False),
        (1, unit, 0, head, False), (1, unit, head, 2 * slots, False), (2, unit, 0, head, False),
        (3, 16, 0, 128, False),
    ]
    fulls = [(width, 3 * head), (width, head + 2 * slots), (width, head), (16 * size, 128)]
    qkv_full, gate_full, out_full, small_full, tok, gout = gather(
        size, 0, plan,
        (query_weight, key_weight, value_weight, outgate_weight, forget_weight, output_weight.T, pack),
        fulls, (tokens, grad_out),
    )
    small = small_full.reshape(size, 16, 128).astype(F32)
    first_full = small[:, 0, :unit].reshape(1, width)
    second_full = small[:, 1, :unit].reshape(1, width)
    slot_full = small[:, 2, : head // size].reshape(1, head)
    bias_full = small[:, 3, : heads_here * slot_part].reshape(size, heads_here, slot_part)
    bias_full = jnp.moveaxis(bias_full, 1, 0).reshape(heads_here, slots)

    def own_head(array, axis):
        return jnp.where(x == 0, *jnp.split(array, 2, axis=axis))

    inputs = tok.reshape(rows, width).astype(F32)
    normed_one = (inputs * inverse_rms(inputs) * first_full).astype(BF16)
    qkv = dot(normed_one, qkv_full, NN, BF16)
    gates = dot(normed_one, gate_full, NN)
    logit = own_head(gates[:, head:], 1) + own_head(bias_full, 0)
    decay = -jax.nn.softplus(-logit) / TAU
    keep = -jnp.expm1(decay)
    slot = Slots(seqs, 2 * block, head, slots, block)
    ff_plan = [(0, unit, 0, hidden, False), (0, unit, hidden, hidden, False), (1, unit, 0, hidden, False)]
    (gated, attended, probs, scores, weights, states, decs, end_decs, residual, normed_two, ff_full, down_full) = forward(
        size, 1, slot, ff_plan, [(width, 2 * hidden), (width, hidden)], qkv, gates, decay, keep, slot_full, out_full, tokens,
        second_full, (gate_weight, up_weight, down_weight.T),
    )
    shape = (seqs, 2, block, width)
    normed_two = normed_two.reshape(rows, width)
    ff = dot(normed_two, ff_full, NN)
    ff_gate, ff_up = ff[:, :hidden], ff[:, hidden:]
    sig = jax.nn.sigmoid(ff_gate)
    activated = (ff_gate * sig * ff_up).astype(BF16)
    ff_part = dot(activated, down_full, NT, BF16).reshape(shape)
    gout = gout.reshape(rows, width)
    act_grad = dot(gout, down_full, NN)
    ff_term = jnp.concatenate(
        [act_grad * ff_up * (sig + ff_gate * sig * (1.0 - sig)), act_grad * ff_gate * sig], axis=1
    ).astype(BF16)
    down_grad = dot(gout, activated, TN, BF16)
    ff_grad = dot(normed_two, ff_term, TN, BF16)
    normed_two_grad = dot(ff_term, ff_full, NT, BF16).reshape(shape)
    ff_plan = [(0, unit, 0, hidden, False), (0, unit, hidden, hidden, False), (1, unit, 0, hidden, False)]
    residual_grad, low, second_part, gate_term, slot_part_grad, qkv_term, decay_term, gate_grad, up_grad, down_grad = backward(
        size, 2, slot, ff_plan,
        (grad_out, gates, attended, normed_two_grad),
        (residual, second_full, out_full, qkv, decay, keep, slot_full, probs, scores, weights, states, decs,
         end_decs),
        (ff_grad, down_grad),
    )
    low = low.reshape(rows, width)
    out_grad = dot(low, gated, TN, BF16)
    forget_term = (decay_term * jax.nn.sigmoid(-logit) / TAU).astype(BF16)
    none = jnp.zeros_like(forget_term)
    gates_term = jnp.concatenate(
        [gate_term, jnp.where(x == 0, forget_term, none), jnp.where(x == 0, none, forget_term)], axis=1
    )
    qkv_grad = dot(normed_one, qkv_term, TN, BF16)
    gates_grad = dot(normed_one, gates_term, TN, BF16)
    normed_one_grad = (dot(qkv_term, qkv_full, NT) + dot(gates_term, gate_full, NT)).astype(BF16).reshape(shape)
    bias_part = jnp.sum(forget_term.astype(F32), axis=0)
    which = jnp.arange(2 * heads_here) == heads_here * c + x
    bias_part = jnp.where(which[:, None], bias_part[None, :], 0.0).reshape(2 * heads_here, size, slot_part)

    def rows_of(array):
        array = array.reshape(size, -1)
        return jnp.pad(array, ((0, 0), (0, 128 - array.shape[1])))

    zero = jnp.zeros((size, 128), F32)
    packed = jnp.stack(
        [zero, rows_of(second_part), rows_of(slot_part_grad), rows_of(jnp.moveaxis(bias_part, 1, 0))] + [zero] * 4, axis=1
    )
    plan = [
        (0, unit, 0, head, False), (1, unit, 0, head, False), (1, unit, head, head, False), (1, unit, 2 * head, head, False),
        (2, unit, 0, head, False), (2, unit, head, 2 * slots, True),
    ]
    input_grad, output, sums, output_grad, query_grad, key_grad, value_grad, outgate_grad, forget_grad = last(
        size, 3, plan, (normed_one_grad, ff_part, tokens, residual, residual_grad, first_full, packed),
        (out_grad, qkv_grad, gates_grad),
    )
    bias_grad = sums[3, : 2 * heads_here * slot_part].reshape(2, heads_here, slot_part)
    bias_grad = jnp.where(c == 0, bias_grad[0], bias_grad[1])
    return (
        output, input_grad, query_grad, key_grad, value_grad, forget_grad[0], bias_grad, outgate_grad, output_grad.T,
        sums[2, : head // size], sums[0, :unit], sums[1, :unit], gate_grad, up_grad, down_grad.T,
    )


def solution(mesh):
    row, column, vector, token = P("seq", "head"), P("head", "seq"), P("seq"), P(None, "seq", None)
    return jax.shard_map(
        shards,
        mesh=mesh,
        in_specs=(token, token, row, row, row, row, column, row, column, vector, vector, vector, row, row, column),
        out_specs=(token, token, row, row, row, row, column, row, column, vector, vector, vector, row, row, column),
        check_vma=False,
    )
```

```python
import functools

import jax
import jax.numpy as jnp
import numpy as np
from jax import lax
from jax.experimental import pallas as pl
from jax.experimental.pallas import tpu as pltpu
from jax.sharding import PartitionSpec as P

F32, BF16 = jnp.float32, jnp.bfloat16
MESH = pl.DeviceIdType.MESH
HBM = pltpu.HBM
EPS = 1e-06
TAU = 8.0


CHUNK = 256
NT = (((1,), (1,)), ((), ()))
NN = (((1,), (0,)), ((), ()))
TN = (((0,), (0,)), ((), ()))


def decay_tables(count):
    at = np.arange(count)
    paths, masks = [], []
    half = count // 2
    while half >= 1:
        block, second = at // (2 * half), (at // half) % 2 == 1
        edge = block * 2 * half + half - 1
        r, t = at[None, :], at[:, None]
        fore = second[:, None] & (r > edge[:, None]) & (r <= t)
        back = ~second[:, None] & (r > t) & (r <= edge[:, None])
        paths.append(fore | back)
        masks.append((block[:, None] == block[None, :]) & second[:, None] & ~second[None, :])
        half //= 2
    paths.append(at[None, :] <= at[:, None])
    paths.append(at[None, :] > at[:, None])
    return np.concatenate(paths, 0), np.stack(masks)


def bf(x):
    return x.astype(BF16)


def halves(x):
    hi = bf(x)
    return hi, bf(x - hi.astype(F32))


def mm(a, b, dims):
    return lax.dot_general(a, b, dims, preferred_element_type=F32)


def dot3(a, b, dims):
    return mm(a[0], b[0], dims) + (mm(a[0], b[1], dims) + mm(a[1], b[0], dims))


def exact_sums(table, x):
    hi, mid = halves(x)
    low = bf(x - hi.astype(F32) - mid.astype(F32))
    n = x.shape[1]
    both = mm(table, jnp.concatenate([hi, mid, low, jnp.zeros_like(low)], axis=1), NN)
    return both[:, :n] + (both[:, n : 2 * n] + both[:, 2 * n : 3 * n])


def silu(v):
    return v / (1.0 + jnp.exp(-v))


def sigmoid(v):
    return 1.0 / (1.0 + jnp.exp(-v))


def silu_slope(v):
    s = sigmoid(v)
    return s + v * s * (1.0 - s)


def columns_total(x):
    ones = jnp.ones((x.shape[0], 128), BF16)
    hi, mid = halves(x)
    low = bf(x - hi.astype(F32) - mid.astype(F32))
    return mm(hi, ones, TN) + (mm(mid, ones, TN) + mm(low, ones, TN))


def spread(column, width):
    return jnp.concatenate([column] * (width // 128), axis=1)


def mix(pair, ratios, keep, masks_ref, own):
    out = own * keep
    for l, ratio in enumerate(ratios):
        left = pair * masks_ref[l].astype(F32)
        out += ratio * dot3(halves(left), halves(ratio * keep), NN)
    return out


def unmix(probs, ratios, keep, masks_ref, diag):
    out = diag * jnp.sum(probs * keep, axis=1, keepdims=True)
    for l, ratio in enumerate(ratios):
        part = dot3(halves(probs * ratio), halves(ratio * keep), NT)
        out += masks_ref[l].astype(F32) * part
    return out


def on_diagonal(count):
    return (
        lax.broadcasted_iota(jnp.int32, (count, count), 0) == lax.broadcasted_iota(jnp.int32, (count, count), 1)
    ).astype(F32)


class Slots:
    def __init__(self, seqs, rows, head, slots, chunk):
        self.seqs, self.rows, self.head, self.slots, self.chunk = seqs, rows, head, slots, chunk
        self.chunks = rows // chunk
        paths, masks = decay_tables(chunk)
        self.levels = masks.shape[0]
        self.paths = jnp.asarray(paths, BF16)
        self.masks = jnp.asarray(masks, BF16)

class Place:
    def __init__(self, size):
        self.size = size
        self.line = size // 4
        s = lax.axis_index("seq")
        self.c = lax.axis_index("head")
        self.s = s
        self.x = lax.rem(s, 2)
        self.b = lax.rem(s // 2, 2)
        self.a = s // 4

    def at(self, a, b, x):
        return (a * 2 + b) * 2 + x

    def partner(self):
        return (self.at(self.a, self.b, 1 - self.x), self.c)

    def across(self):
        return (self.at(self.a, 1 - self.b, self.x), self.c)

    def up(self):
        return (self.at(jnp.minimum(self.a + 1, self.line - 1), self.b, self.x), self.c)

    def down(self):
        return (self.at(jnp.maximum(self.a - 1, 0), self.b, self.x), self.c)

    def sibling(self):
        return (self.s, 1 - self.c)

    def has_up(self):
        return self.a < self.line - 1

    def has_down(self):
        return self.a > 0


def signal(sem, device):
    pl.semaphore_signal(sem, inc=1, device_id=device, device_id_type=MESH)


def greet(place, partner=True, across=True, line=True, sibling=False):
    barrier = pltpu.get_barrier_semaphore()
    count = jnp.int32(0)
    if partner:
        signal(barrier, place.partner())
        count = count + 1
    if sibling:
        signal(barrier, place.sibling())
        count = count + 1
    if across:
        signal(barrier, place.across())
        count = count + 1
    if line:
        pl.when(place.has_up())(lambda: signal(barrier, place.up()))
        pl.when(place.has_down())(lambda: signal(barrier, place.down()))
        count = count + place.has_up().astype(jnp.int32) + place.has_down().astype(jnp.int32)
    pl.semaphore_wait(barrier, count)


def remote(src, dst, send, recv, device):
    return pltpu.make_async_remote_copy(
        src_ref=src, dst_ref=dst, send_sem=send, recv_sem=recv, device_id=device, device_id_type=MESH
    )


class Gather:
    def __init__(self, place, shard, full, unit, offset, width, sems, late):
        self.pl, self.shard, self.full = place, shard, full
        self.unit, self.offset, self.width, self.late = unit, offset, width, late
        self.x_sem, self.b_sem, self.up_sem, self.down_sem = sems

    def part(self, start, count):
        rows = pl.ds(start * self.unit, count * self.unit)
        if self.width == self.full.shape[1]:
            return self.full.at[rows]
        return self.full.at[rows, pl.ds(self.offset, self.width)]

    def mine(self, x):
        if self.shard.shape[1] == self.width:
            return self.shard
        return self.shard.at[:, pl.ds(x * self.width, self.width)]

    def x_copy(self):
        p = self.pl
        return remote(self.mine(1 - p.x), self.part(p.s, 1), self.x_sem.at[0], self.x_sem.at[1], p.partner())

    def own_copy(self):
        return pltpu.make_async_copy(self.mine(self.pl.x), self.part(self.pl.s, 1), self.x_sem.at[2])

    def block(self, a):
        p = self.pl
        if self.late:
            return self.part(4 * a, 4)
        return self.part(4 * a + 2 * p.b, 2)

    def b_copy(self, i, a):
        p = self.pl
        return remote(
            self.part(4 * a + 2 * p.b, 2), self.part(4 * a + 2 * p.b, 2),
            self.b_sem.at[0, i], self.b_sem.at[1, i], p.across(),
        )

    def line_copy(self, way, h):
        p = self.pl
        if way == "up":
            blk = self.block(jnp.maximum(p.a - (h - 1), 0))
            return remote(blk, blk, self.up_sem.at[0, h - 1], self.up_sem.at[1, h - 1], p.up())
        blk = self.block(jnp.minimum(p.a + (h - 1), p.line - 1))
        return remote(blk, blk, self.down_sem.at[0, h - 1], self.down_sem.at[1, h - 1], p.down())

    def sends(self, way, h):
        p = self.pl
        if way == "up":
            return jnp.logical_and(p.has_up(), p.a - (h - 1) >= 0)
        return jnp.logical_and(p.has_down(), p.a + (h - 1) <= p.line - 1)

    def gets(self, way, h):
        p = self.pl
        if way == "up":
            return p.a - h >= 0
        return p.a + h <= p.line - 1

    def got(self, way, h):
        p = self.pl
        if way == "up":
            return jnp.maximum(p.a - h, 0)
        return jnp.minimum(p.a + h, p.line - 1)

    def slot(self, way, h):
        return h if way == "up" else self.pl.line - 1 + h

    def start_x(self):
        self.x_copy().start()
        self.own_copy().start()

    def stage(self, h):
        p = self.pl
        if h == 0:
            self.own_copy().wait()
            self.x_copy().wait_recv()
            if self.late:
                self.b_copy(0, p.a).start()
            else:
                for way in ("up", "down"):
                    pl.when(self.sends(way, 1))(lambda way=way: self.line_copy(way, 1).start())
                self.b_copy(0, p.a).start()
            return
        if self.late:
            if h == 1:
                self.b_copy(0, p.a).wait_recv()
                for way in ("up", "down"):
                    pl.when(self.sends(way, 1))(lambda way=way: self.line_copy(way, 1).start())
                return
            h = h - 1
        for way in ("up", "down"):

            def go(way=way):
                self.line_copy(way, h).wait_recv()
                if not self.late:
                    self.b_copy(self.slot(way, h), self.got(way, h)).start()

            def on(way=way):
                self.line_copy(way, h + 1).start()

            pl.when(self.gets(way, h))(go)
            if h + 1 <= p.line - 1:
                pl.when(self.sends(way, h + 1))(on)

    def stages(self):
        return self.pl.line + (1 if self.late else 0)

    def finish(self):
        p = self.pl
        self.x_copy().wait_send()
        self.b_copy(0, p.a).wait_send()
        if not self.late:
            self.b_copy(0, p.a).wait_recv()
        for way in ("up", "down"):
            for h in range(1, p.line):
                pl.when(self.sends(way, h))(lambda way=way, h=h: self.line_copy(way, h).wait_send())
                if not self.late:

                    def both(way=way, h=h):
                        cp = self.b_copy(self.slot(way, h), self.got(way, h))
                        cp.wait_send()
                        cp.wait_recv()

                    pl.when(self.gets(way, h))(both)


def gather_sems(line):
    return [
        pltpu.SemaphoreType.DMA((3,)),
        pltpu.SemaphoreType.DMA((2, 2 * line - 1)),
        pltpu.SemaphoreType.DMA((2, line - 1)),
        pltpu.SemaphoreType.DMA((2, line - 1)),
    ]


def gather_ops(gathers, ahead):
    steps = []
    n = len(gathers)
    for k in range(min(ahead, n)):
        steps.append(gathers[k].start_x)
    steps.append(functools.partial(gathers[0].stage, 0))
    for k in range(n):
        if k + ahead < n:
            steps.append(gathers[k + ahead].start_x)
        if k + 1 < n:
            steps.append(functools.partial(gathers[k + 1].stage, 0))
        for h in range(1, gathers[k].stages()):
            steps.append(functools.partial(gathers[k].stage, h))
    for g in gathers:
        steps.append(g.finish)
    return steps

VM = pl.BlockSpec(memory_space=pltpu.VMEM)
ANY = pl.BlockSpec(memory_space=HBM)


def remote_params(number, mib=56):
    return pltpu.CompilerParams(collective_id=number, has_side_effects=True, vmem_limit_bytes=mib * 2**20)


STRIPS = 4


class Fold:
    def __init__(self, place, part, sib, sent, came, sems, own=None):
        self.p, self.part, self.sib, self.sent, self.came = place, part, sib, sent, came
        self.own = part.at[place.c] if own is None else own
        self.s_sem, self.x_sem = sems
        self.rows = part.shape[2] // STRIPS

    def strip(self, r):
        return pl.ds(r * self.rows, self.rows)

    def sib_copy(self, far, r):
        p = self.p
        x = 1 - p.x if far else p.x
        i = (0 if far else STRIPS) + r
        return remote(
            self.part.at[1 - p.c, x, self.strip(r)], self.sib.at[1 if far else 0, self.strip(r)],
            self.s_sem.at[0, i], self.s_sem.at[1, i], p.sibling(),
        )

    def x_copy(self, r):
        return remote(
            self.sent.at[self.strip(r)], self.came.at[self.strip(r)], self.x_sem.at[0, r], self.x_sem.at[1, r], self.p.partner()
        )

    def start(self):
        for r in range(STRIPS):
            self.sib_copy(True, r).start()
        for r in range(STRIPS):
            self.sib_copy(False, r).start()

    def sib_all(self, far):
        for r in range(STRIPS):
            self.sib_copy(far, r).start()

    def cross(self, r):
        p = self.p
        self.sib_copy(True, r).wait_recv()
        own = self.own[1 - p.x, self.strip(r)].astype(F32)
        self.sent[self.strip(r)] = bf(own + self.sib[1, self.strip(r)].astype(F32))
        self.x_copy(r).start()

    def total(self, r):
        p = self.p
        self.sib_copy(False, r).wait_recv()
        self.x_copy(r).wait_recv()
        own = self.own[p.x, self.strip(r)].astype(F32) + self.sib[0, self.strip(r)].astype(F32)
        return own + self.came[self.strip(r)].astype(F32)

    def finish(self):
        for r in range(STRIPS):
            self.sib_copy(True, r).wait_send()
            self.sib_copy(False, r).wait_send()
            self.x_copy(r).wait_send()


def fold_scratch(rows, width):
    return [
        pltpu.VMEM((2, rows, width), BF16), pltpu.VMEM((rows, width), BF16), pltpu.VMEM((rows, width), BF16),
        pltpu.SemaphoreType.DMA((2, 2 * STRIPS)), pltpu.SemaphoreType.DMA((2, STRIPS)),
    ]


class Share:
    def __init__(self, place, out, sems):
        self.p, self.out = place, out
        self.x_sem, self.s_sem = sems
        self.rows = out.shape[2] // STRIPS

    def strip(self, r):
        return pl.ds(r * self.rows, self.rows)

    def x_copy(self, r):
        p = self.p
        block = self.out.at[p.c, p.x, self.strip(r)]
        return remote(block, block, self.x_sem.at[0, r], self.x_sem.at[1, r], p.partner())

    def s_copy(self, far, r):
        p = self.p
        block = self.out.at[p.c, 1 - p.x if far else p.x, self.strip(r)]
        i = (0 if far else STRIPS) + r
        return remote(block, block, self.s_sem.at[0, i], self.s_sem.at[1, i], p.sibling())

    def put(self, r, value):
        self.out[self.p.c, self.p.x, self.strip(r)] = value
        self.x_copy(r).start()
        self.s_copy(False, r).start()

    def forward(self, r):
        self.x_copy(r).wait_recv()
        self.s_copy(True, r).start()

    def wait_sibling(self, far):
        for r in range(STRIPS):
            self.s_copy(far, r).wait_recv()

    def finish(self, receive=True):
        for r in range(STRIPS):
            self.x_copy(r).wait_send()
            for far in (False, True):
                self.s_copy(far, r).wait_send()
                if receive:
                    self.s_copy(far, r).wait_recv()


SHARE_SEMS = [pltpu.SemaphoreType.DMA((2, STRIPS)), pltpu.SemaphoreType.DMA((2, 2 * STRIPS))]


def inverse_rms(values):
    return lax.rsqrt(jnp.mean(values * values, axis=-1, keepdims=True) + EPS)


def norm_back(grad, values, gain):
    scale = inverse_rms(values)
    u = grad * gain
    down = scale * u - values * (scale * scale * scale) * jnp.mean(u * values, axis=-1, keepdims=True)
    return down, jnp.sum(grad * values * scale, axis=0, keepdims=True)


def ends_chunk(k, v, decay, keep, tail):
    weight = halves(jnp.exp(exact_sums(tail, decay)) * keep)
    unit_k = dot3(weight, halves(silu(k.astype(F32))), TN)
    unit_v = mm(weight[0], v, TN) + mm(weight[1], v, TN)
    return jnp.concatenate([unit_k, unit_v], axis=1), jnp.exp(columns_total(decay))


def powers_of(table, count, levels, decay):
    powers = jnp.exp(exact_sums(table, decay))
    return [powers[l * count : (l + 1) * count] for l in range(levels)], [
        powers[l * count : (l + 1) * count] for l in range(levels, table.shape[0] // count)
    ]


class Prefix:
    def __init__(self, place, back, own, dec, start, peer, peer_dec, line, out, sems):
        p = self.p = place
        self.own, self.dec, self.start_ref, self.peer, self.peer_dec = own, dec, start, peer, peer_dec
        self.line, self.out = line, out
        self.p_sem, self.d_sem, self.l_sem = sems
        seqs, slots, width = own.shape
        self.half = width // 2
        self.pieces = [(b, h) for b in range(seqs) for h in range(2)]
        if back:
            self.has_prev, self.has_next, self.after = p.has_up(), p.has_down(), p.down()
        else:
            self.has_prev, self.has_next, self.after = p.has_down(), p.has_up(), p.up()
        self.first = ((p.b == 1) if back else (p.b == 0)).astype(F32)

    def cut(self, ref, i):
        b, h = self.pieces[i]
        return ref.at[b, :, pl.ds(h * self.half, self.half)]

    def peer_copy(self, i):
        return remote(self.cut(self.own, i), self.cut(self.peer, i), self.p_sem.at[0, i], self.p_sem.at[1, i], self.p.across())

    def line_copy(self, i):
        return remote(self.cut(self.out, i), self.cut(self.line, i), self.l_sem.at[0, i], self.l_sem.at[1, i], self.after)

    def dec_copy(self):
        return remote(self.dec, self.peer_dec, self.d_sem.at[0], self.d_sem.at[1], self.p.across())

    def start(self):
        self.dec_copy().start()
        for i in range(len(self.pieces)):
            self.peer_copy(i).start()

    def run(self):
        self.dec_copy().wait_recv()
        for i, (b, _) in enumerate(self.pieces):
            self.peer_copy(i).wait_recv()
            dec_own = spread(self.dec[b], self.half)
            dec_peer = spread(self.peer_dec[b], self.half)
            own, other = self.cut(self.own, i)[...], self.cut(self.peer, i)[...]
            first = self.first
            both = first * (dec_peer * own + other) + (1.0 - first) * (dec_own * other + own)
            here, result = self.cut(self.out, i), self.cut(self.start_ref, i)

            def go_on(i=i):
                self.line_copy(i).wait_recv()
                came = self.cut(self.line, i)[...]
                here[...] = dec_own * dec_peer * came + both
                result[...] = first * came + (1.0 - first) * (dec_peer * came + other)

            def begin():
                here[...] = both
                result[...] = (1.0 - first) * other

            pl.when(self.has_prev)(go_on)
            pl.when(jnp.logical_not(self.has_prev))(begin)
            pl.when(self.has_next)(lambda i=i: self.line_copy(i).start())

    def finish(self):
        self.dec_copy().wait_send()
        for i in range(len(self.pieces)):
            self.peer_copy(i).wait_send()
            pl.when(self.has_next)(lambda i=i: self.line_copy(i).wait_send())


def prefix_scratch(seqs, slots, width):
    count = 2 * seqs
    return [
        pltpu.VMEM((seqs, slots, width), F32), pltpu.VMEM((seqs, slots, width), F32), pltpu.VMEM((seqs, slots, 128), F32),
        pltpu.VMEM((seqs, slots, width), F32), pltpu.VMEM((seqs, slots, width), F32),
        pltpu.SemaphoreType.DMA((2, count)), pltpu.SemaphoreType.DMA((2,)), pltpu.SemaphoreType.DMA((2, count)),
    ]


def take(refs, count):
    return refs[:count], refs[count:]


class Weave:
    def __init__(self, steps):
        self.steps = list(steps)

    def run(self, count):
        for step in self.steps[:count]:
            step()
        self.steps = self.steps[count:]

    def rest(self):
        self.run(len(self.steps))


def blocks_in_order(p, seqs):
    def block(i):
        b = jnp.where(i < 2, 1 - p.c, p.c)
        x = jnp.where(lax.rem(i, 2) == 0, 1 - p.x, p.x)
        return b, x

    return block


def forward_kernel(size, plan, levels, *refs):
    p = Place(size)
    (qkv, gates, decay, keep, gain, out_w, tokens, gain2, paths, masks), refs = take(refs, 10)
    shard_refs, refs = take(refs, len(plan))
    (gated, attended, probs, scores, weights, states, decs, end_dec, residual, normed), refs = take(refs, 10)
    fulls, refs = take(refs, max(i for i, _, _, _, _ in plan) + 1)
    (units, part, total), refs = take(refs, 3)
    (start, *prefix_refs), refs = take(refs, 8)
    fold_refs, refs = take(refs, 5)
    share_sems, refs = take(refs, 2)
    count = paths.shape[1]
    head = gated.shape[1]
    seqs = tokens.shape[0]
    slots = keep.shape[1]
    greet(p, sibling=True)
    work = []
    for n, (i, unit, offset, width, late) in enumerate(plan):
        work.append(Gather(p, shard_refs[n], fulls[i], unit, offset, width, refs[4 * n : 4 * n + 4], late))
    weave = Weave(gather_ops(work, 3))
    weave.run(3)
    tail = paths[(levels + 1) * count :, :]

    def ends(b):
        for j in range(2):
            rows = pl.ds((b * 2 + j) * count, count)
            unit, dec = ends_chunk(
                qkv[rows, head : 2 * head], qkv[rows, 2 * head :], decay[rows, :], keep[rows, :], tail
            )
            units[b, j] = unit
            decs[b, j] = dec
        total[b] = spread(dec, 2 * head) * units[b, 0] + unit
        end_dec[b] = decs[b, 0] * dec

    for b in range(seqs):
        ends(b)
    carry = Prefix(p, False, total, end_dec, start, *prefix_refs[:4], prefix_refs[4:])
    carry.start()
    weave.run(1)
    carry.run()
    for b in range(seqs):
        states[3 * b] = start[b]
        for j in range(2):
            states[3 * b + j + 1] = spread(decs[b, j], 2 * head) * states[3 * b + j] + units[b, j]
    weave.run(1)
    diag = on_diagonal(count)
    order = blocks_in_order(p, seqs)
    fold = Fold(p, part, *fold_refs[:3], fold_refs[3:])
    share = Share(p, normed, share_sems)

    def attend(i, nothing):
        b, j = order(i)
        rows = pl.ds(pl.multiple_of((b * 2 + j) * count, count), count)
        here = keep[rows, :]
        ratios, (growth,) = powers_of(paths[: (levels + 1) * count, :], count, levels, decay[rows, :])
        query = halves(silu(qkv[rows, :head].astype(F32)) * head ** (-0.5))
        keys = halves(silu(qkv[rows, head : 2 * head].astype(F32)))
        state = states[3 * b + j]
        pair = dot3(query, keys, NT)
        score = mix(pair, ratios, here, masks, jnp.sum(pair * diag, axis=1, keepdims=True))
        score += growth * dot3(query, halves(state[:, :head]), NT)
        raised = jnp.exp(score - jnp.max(score, axis=1, keepdims=True))
        prob = raised / jnp.sum(raised, axis=1, keepdims=True)
        weight = unmix(prob, ratios, here, masks, diag)
        values = qkv[rows, 2 * head :]
        whi, wlo = halves(weight)
        result = mm(whi, values, NN) + mm(wlo, values, NN)
        result += dot3(halves(prob * growth), halves(state[:, head:]), NN)
        scale = lax.rsqrt(jnp.mean(result * result, axis=1, keepdims=True) + EPS)
        low = bf(result * scale * gain[...] * silu(gates[rows, :head]))
        gated[rows, :] = low
        attended[rows, :] = result
        probs[rows, :] = prob
        scores[rows, :] = score
        weights[rows, :] = weight
        part[b, j] = bf(mm(low, out_w[...], NT))
        pl.when(i == 0)(lambda: fold.sib_all(True))
        pl.when(i == 1)(lambda: fold.sib_all(False))
        return nothing

    lax.fori_loop(0, 2, attend, 0)
    weave.run(1)
    lax.fori_loop(2, 3, attend, 0)
    for r in range(STRIPS):
        fold.cross(r)
    lax.fori_loop(3, 4, attend, 0)
    weave.run(1)
    for r in range(STRIPS):
        value = tokens[p.c, fold.strip(r)].astype(F32) + fold.total(r)
        residual[fold.strip(r)] = value
        share.put(r, bf(value * inverse_rms(value) * gain2[...]))
    weave.run(2)
    for r in range(STRIPS):
        share.forward(r)
    weave.rest()
    share.finish()
    fold.finish()
    carry.finish()


def forward(size, number, slot, plan, fulls, qkv, gates, decay, keep, gain, out_w, tokens, gain2, shards):
    seqs, block, width = tokens.shape
    h, m, n, rows = slot.head, slot.slots, slot.chunks, slot.seqs * slot.rows
    shape = jax.ShapeDtypeStruct
    outs = [
        shape((rows, h), BF16), shape((rows, h), F32), shape((rows, m), F32), shape((rows, m), F32), shape((rows, slot.chunk), F32),
        shape((seqs * (n + 1), m, 2 * h), F32), shape((seqs, n, m, 128), F32), shape((seqs, m, 128), F32),
        shape((block, width), F32), shape((seqs, 2, block, width), BF16),
    ]
    scratch = [
        pltpu.VMEM((seqs, n, m, 2 * h), F32), pltpu.VMEM((seqs, 2, block, width), BF16), pltpu.VMEM((seqs, m, 2 * h), F32),
    ]
    scratch += prefix_scratch(seqs, m, 2 * h) + fold_scratch(block, width) + SHARE_SEMS
    for _ in plan:
        scratch += gather_sems(size // 4)
    return pl.pallas_call(
        functools.partial(forward_kernel, size, plan, slot.levels),
        out_shape=outs + [shape(full, BF16) for full in fulls],
        in_specs=[VM] * 10 + [ANY] * len(shards),
        out_specs=[VM] * 10 + [ANY] * len(fulls),
        scratch_shapes=scratch,
        compiler_params=remote_params(number, 60),
        name="attend_forward",
    )(qkv, gates, decay, keep, gain, out_w, tokens, gain2, slot.paths, slot.masks, *shards)

class Pool:
    def __init__(self, refs):
        self.loads, self.extra, self.sends, self.totals, self.sems = refs

    def slot(self, which, slot):
        return self.extra if slot == 3 else self.loads.at[which, slot]


POOL_SENDS = 2
AHEAD = 3
LAG = 1


def pool_scratch(rows, width):
    return [
        pltpu.VMEM((2, 3, rows, width), BF16), pltpu.VMEM((rows, width), BF16), pltpu.VMEM((POOL_SENDS, rows, width), BF16),
        pltpu.VMEM((rows, width), F32),
        pltpu.SemaphoreType.DMA((2, 4)),
    ]


class Scatter:
    def __init__(self, place, grad, out, peer, line, unit, offset, width, sems):
        self.p, self.grad, self.out, self.peer, self.line = place, grad, out, peer, line
        self.unit, self.offset, self.width = unit, offset, width
        self.whole = out.shape[-1] == width
        self.b_sem, self.l_sem, self.x_sem = sems

    def goal(self, n):
        p = self.p
        low, high = p.a, p.line - 1 - p.a
        more, less = jnp.maximum(low, high), jnp.minimum(low, high)
        alone = more - less
        up_more = jnp.where(high >= low, 1, -1)
        m = n - alone
        early = n < alone
        reach = jnp.where(early, more - n, less - m // 2)
        side = jnp.where(early, up_more, jnp.where(lax.rem(jnp.maximum(m, 0), 2) == 0, 1, -1))
        return p.a + side * reach

    def block(self, a, b):
        rows = pl.ds((4 * a + 2 * b) * self.unit, 2 * self.unit)
        if self.width == self.grad.shape[1]:
            return self.grad.at[rows]
        return self.grad.at[rows, pl.ds(self.offset, self.width)]

    def b_copy(self, a):
        return remote(self.block(a, 1 - self.p.b), self.peer.at[a], self.b_sem.at[0, a], self.b_sem.at[1, a], self.p.across())

    def start(self, n):
        self.b_copy(self.goal(n)).start()

    def cut(self, ref):
        return ref if self.width == ref.shape[1] else ref.at[:, pl.ds(0, self.width)]

    def load(self, pool, which, slot, source):
        return pltpu.make_async_copy(source, self.cut(pool.slot(which, slot)), pool.sems.at[which, slot])

    def prepare(self, pool, which, n):
        d = self.goal(n)
        self.b_copy(d).wait_recv()
        self.load(pool, which, 0, self.block(d, self.p.b)).start()
        self.load(pool, which, 1, self.peer.at[d]).start()

    def loaded(self, pool, which, n):
        d = self.goal(n)
        self.load(pool, which, 0, self.block(d, self.p.b)).wait()
        self.load(pool, which, 1, self.peer.at[d]).wait()

    def strips(self, do):
        rows = 2 * self.unit
        step = max(r for r in (16, 32, 64, 128) if rows % r == 0 and (r == 16 or r * self.width <= 64 * 1024))

        def one(i, carry):
            do(pl.ds(pl.multiple_of(i * step, step), step))
            return carry

        lax.fori_loop(0, rows // step, one, 0)

    def bring(self, pool, which, slot, place):
        remote(self.line.at[place], self.line.at[place], self.l_sem.at[0, 0], self.l_sem.at[1, place], self.p.across()).wait_recv()
        self.load(pool, which, slot, self.line.at[place]).start()

    def send(self, pool, out, n):
        p = self.p
        d = self.goal(n)
        up = d > p.a
        to = jnp.clip(p.a + jnp.where(up, 1, -1), 0, p.line - 1)
        slot = jnp.where(jnp.logical_and(jnp.logical_not(up), d == p.a - 1), p.line, d)
        return remote(
            self.cut(pool.sends.at[out]), self.line.at[slot], self.l_sem.at[0, n], self.l_sem.at[1, slot], (p.at(to, p.b, p.x), p.c)
        )

    def hop(self, pool, which, n, out):
        p = self.p
        d = self.goal(n)
        behind = jnp.logical_or(jnp.logical_and(d > p.a, p.has_down()), jnp.logical_and(d < p.a, p.has_up()))
        pl.when(behind)(lambda: self.bring(pool, which, 2, d))
        self.loaded(pool, which, n)
        a, b, c = (self.cut(pool.slot(which, i)) for i in range(3))
        to = self.cut(pool.sends.at[out])

        def with_line():
            self.load(pool, which, 2, self.line.at[d]).wait()

            def do(rows):
                to[rows] = bf(a[rows].astype(F32) + b[rows].astype(F32) + c[rows].astype(F32))

            self.strips(do)

        def without():
            def do(rows):
                to[rows] = bf(a[rows].astype(F32) + b[rows].astype(F32))

            self.strips(do)

        pl.when(behind)(with_line)
        pl.when(jnp.logical_not(behind))(without)
        self.send(pool, out, n).start()

    def last(self, pool, which):
        p = self.p
        n = p.line - 1
        pl.when(p.has_down())(lambda: self.bring(pool, which, 2, p.a))
        pl.when(p.has_up())(lambda: self.bring(pool, which, 3, p.line))
        self.loaded(pool, which, n)
        a, b, c, d = (self.cut(pool.slot(which, i)) for i in range(4))
        to = self.total = self.cut(pool.totals)

        def first(rows):
            to[rows] = a[rows].astype(F32) + b[rows].astype(F32)

        self.strips(first)

        def more(slot, place, ref):
            def go():
                self.load(pool, which, slot, self.line.at[place]).wait()

                def do(rows):
                    to[rows] = to[rows] + ref[rows].astype(F32)

                self.strips(do)

            return go

        pl.when(p.has_down())(more(2, p.a, c))
        pl.when(p.has_up())(more(3, p.line, d))
        self.x_copy().start()
        if not self.whole:
            self.out_copy().start()

    def half(self, x):
        return self.total.at[pl.ds(x * self.unit, self.unit)]

    def place(self):
        return self.out.at[:, pl.ds(self.p.x * self.width, self.width)]

    def x_copy(self):
        p = self.p
        where = self.out.at[1] if self.whole else self.place()
        return remote(self.half(1 - p.x), where, self.x_sem.at[0], self.x_sem.at[1], p.partner())

    def out_copy(self):
        return pltpu.make_async_copy(self.half(self.p.x), self.place(), self.x_sem.at[2])

    def sent(self):
        self.x_copy().wait_send()
        if not self.whole:
            self.out_copy().wait()

    def finish(self):
        p = self.p
        self.x_copy().wait_recv()
        if self.whole:
            self.out[0] = self.out[1] + self.half(p.x)[...]
        for n in range(p.line):
            self.b_copy(self.goal(n)).wait_send()


def scatter_sems(line):
    return [pltpu.SemaphoreType.DMA((2, line)), pltpu.SemaphoreType.DMA((2, line + 1)), pltpu.SemaphoreType.DMA((3,))]


def scatter_ops(work, pool):
    lines = work[0].p.line
    jobs = [(k * (lines - 1) + n, k, n) for k in range(len(work)) for n in range(lines - 1)]
    jobs += [((k + 1) * (lines - 1) - 0.5 + LAG, k, lines - 1) for k in range(len(work))]
    jobs = [(k, n) for _, k, n in sorted(jobs)]
    sends, totals = [], []

    def begin():
        for k, n in jobs[:AHEAD]:
            work[k].start(n)


    def job(i):
        k, n = jobs[i]

        def step():
            work[k].prepare(pool, i % 2, n)
            if i + AHEAD < len(jobs):
                work[jobs[i + AHEAD][0]].start(jobs[i + AHEAD][1])
            if n < lines - 1:
                out = len(sends) % POOL_SENDS
                if len(sends) >= POOL_SENDS:
                    ok, on, oo = sends[-POOL_SENDS]
                    work[ok].send(pool, oo, on).wait_send()
                work[k].hop(pool, i % 2, n, out)
                sends.append((k, n, out))
            else:
                if totals:
                    work[totals[-1]].sent()
                work[k].last(pool, i % 2)
                totals.append(k)

        return step

    steps = [begin] + [job(i) for i in range(len(jobs))]

    def finish():
        for ok, on, oo in sends[-POOL_SENDS:]:
            work[ok].send(pool, oo, on).wait_send()
        work[totals[-1]].sent()
        for chunk in work:
            chunk.finish()

    steps.append(finish)
    return steps

BACK_STEPS = (0, 1, 1, 0, 1, 1, 0, 2, 3, 2, 0, 1)


def backward_kernel(size, plan, levels, *refs):
    p = Place(size)
    (grad_out_all, gates_all, attended, grad_part), refs = take(refs, 4)
    (residual, gain2, out_w, qkv, decay, keep, gain, probs, scores, weights, states, decs,
     end_dec, paths, later, masks), refs = take(refs, 16)
    grads = max(i for i, _, _, _, _ in plan) + 1
    grad_refs, refs = take(refs, grads)
    (residual_grad, low, second_part, gate_term, gain_part, term, decay_term), refs = take(refs, 7)
    outs, refs = take(refs, len(plan))
    spaces, refs = take(refs, 2 * len(plan))
    (grad_out, gates, own_part, own_sem, att_grad, dprobs, dscores, units, adjoints, total), refs = take(refs, 10)
    (ending, *prefix_refs), refs = take(refs, 8)
    fold_refs, refs = take(refs, 5)
    share_sems, refs = take(refs, 2)
    pool_refs, refs = take(refs, 5)
    count = paths.shape[1]
    head = gate_term.shape[1]
    seqs = grad_out_all.shape[0]
    own = [
        pltpu.make_async_copy(grad_out_all.at[p.c], grad_out, own_sem.at[0]),
        pltpu.make_async_copy(gates_all.at[:, pl.ds(0, head)], gates, own_sem.at[1]),
        pltpu.make_async_copy(attended, att_grad, own_sem.at[2]),
        pltpu.make_async_copy(grad_part.at[p.c], own_part, own_sem.at[3]),
    ]
    for copy in own:
        copy.start()
    greet(p, sibling=True)
    pool = Pool(pool_refs)
    work = []
    for n, (i, unit, offset, width, _) in enumerate(plan):
        work.append(
            Scatter(p, grad_refs[i], outs[n], spaces[2 * n], spaces[2 * n + 1], unit, offset, width, refs[3 * n : 3 * n + 3])
        )
    weave = Weave(scatter_ops(work, pool))
    fold = Fold(p, grad_part, *fold_refs[:3], fold_refs[3:], own_part)
    share = Share(p, low, share_sems)
    fold.start()
    weave.run(1 + BACK_STEPS[0])
    own[3].wait()
    for r in range(STRIPS):
        fold.cross(r)
    weave.run(BACK_STEPS[1])
    own[0].wait()
    gains = jnp.zeros((1, grad_part.shape[3]), F32)
    for r in range(STRIPS):
        down, more = norm_back(fold.total(r), residual[fold.strip(r)], gain2[...])
        value = grad_out[fold.strip(r)].astype(F32) + down
        gains += more
        residual_grad[fold.strip(r)] = value
        share.put(r, bf(value))
        if r == 1:
            weave.run(BACK_STEPS[2])
    second_part[...] = gains
    weave.run(BACK_STEPS[3])
    diag = on_diagonal(count)
    gain_part[...] = jnp.zeros_like(gain_part)

    def place(i):
        b = jnp.where(lax.rem(i, 2) == 0, p.c, 1 - p.c)
        x = jnp.where(i < 2, p.x, 1 - p.x)
        return b, x

    def first(i, nothing):
        b, j = place(i)
        rows = pl.ds(pl.multiple_of((b * 2 + j) * count, count), count)
        grad = mm(low[b, j], out_w[...], NN)
        gate = gates[rows, :]
        value = att_grad[rows, :]
        scale = lax.rsqrt(jnp.mean(value * value, axis=1, keepdims=True) + EPS)
        normed = value * scale
        weighted = grad * silu(gate)
        gate_term[rows, :] = bf(grad * normed * gain[...] * silu_slope(gate))
        gain_part[...] += jnp.sum(weighted * normed, axis=0, keepdims=True)
        c = weighted * gain[...]
        agrad = scale * c - value * (scale * scale * scale) * jnp.mean(c * value, axis=1, keepdims=True)
        att_grad[rows, :] = agrad
        here = keep[rows, :]
        ratios, (growth,) = powers_of(paths[: (levels + 1) * count, :], count, levels, decay[rows, :])
        ahalf = halves(agrad)
        values = qkv[rows, 2 * head :]
        pair = mm(ahalf[0], values, NT) + mm(ahalf[1], values, NT)
        state = states[3 * b + j]
        dprob = mix(pair, ratios, here, masks, jnp.sum(pair * diag, axis=1, keepdims=True))
        dprob += growth * dot3(ahalf, halves(state[:, head:]), NT)
        prob = probs[rows, :]
        dscore = prob * (dprob - jnp.sum(prob * dprob, axis=1, keepdims=True))
        query = halves(silu(qkv[rows, :head].astype(F32)) * head ** (-0.5))
        dprobs[rows, :] = dprob
        dscores[rows, :] = dscore
        unit_k = dot3(halves(growth * dscore), query, TN)
        unit_v = dot3(halves(growth * prob), ahalf, TN)
        units[b, j] = jnp.concatenate([unit_k, unit_v], axis=1)
        return nothing

    own[1].wait()
    own[2].wait()
    lax.fori_loop(0, 1, first, 0)
    weave.run(BACK_STEPS[4])
    for r in range(STRIPS):
        share.forward(r)
    share.wait_sibling(False)
    lax.fori_loop(1, 3, first, 0)
    weave.run(BACK_STEPS[5])
    share.wait_sibling(True)
    lax.fori_loop(3, 4, first, 0)
    weave.run(BACK_STEPS[6])
    for b in range(seqs):
        total[b] = spread(decs[b, 0], 2 * head) * units[b, 1] + units[b, 0]
    carry = Prefix(p, True, total, end_dec, ending, *prefix_refs[:4], prefix_refs[4:])
    carry.start()
    weave.run(BACK_STEPS[7])
    carry.run()
    for b in range(seqs):
        adjoints[b, 1] = ending[b]
        adjoints[b, 0] = spread(decs[b, 1], 2 * head) * ending[b] + units[b, 1]
    is_last = (lax.broadcasted_iota(jnp.int32, (count, 1), 0) == count - 1).astype(F32)

    def second(i, nothing):
        for k in range(4):
            pl.when(i == k)(functools.partial(weave.run, BACK_STEPS[8 + k]))
        b, j = place(i)
        rows = pl.ds(pl.multiple_of((b * 2 + j) * count, count), count)
        here = keep[rows, :]
        ratios, (growth, rest) = powers_of(paths[...], count, levels, decay[rows, :])
        qraw = qkv[rows, :head].astype(F32)
        kraw = qkv[rows, head : 2 * head].astype(F32)
        query = halves(silu(qraw) * head ** (-0.5))
        keys = halves(silu(kraw))
        values = qkv[rows, 2 * head :]
        agrad = halves(att_grad[rows, :])
        prob, dscore = probs[rows, :], dscores[rows, :]
        state = halves(states[3 * b + j][:, :head])
        adj = adjoints[b, j]
        ahalf = halves(adj)
        adj_k, adj_v = (ahalf[0][:, :head], ahalf[1][:, :head]), (ahalf[0][:, head:], ahalf[1][:, head:])
        dweights = halves(unmix(dscore, ratios, here, masks, diag))
        dquery = dot3(dweights, keys, NN) + dot3(halves(dscore * growth), state, NN)
        term[rows, :head] = bf(silu_slope(qraw) * dquery * head ** (-0.5))
        left = halves(rest * here)
        dkey = dot3(dweights, query, TN) + dot3(left, adj_k, NN)
        term[rows, head : 2 * head] = bf(silu_slope(kraw) * dkey)
        dvalue = dot3(halves(weights[rows, :]), agrad, TN) + dot3(left, adj_v, NN)
        term[rows, 2 * head :] = bf(dvalue)
        pair_k = dot3(query, keys, NT)
        pair_v = mm(agrad[0], values, NT) + mm(agrad[1], values, NT)
        dkeep = jnp.sum(pair_k * diag, axis=1, keepdims=True) * dscore
        dkeep += jnp.sum(pair_v * diag, axis=1, keepdims=True) * prob
        dkeep += rest * (dot3(keys, adj_k, NT) + mm(values, adj_v[0], NT) + mm(values, adj_v[1], NT))
        for l, ratio in enumerate(ratios):
            mask = masks[l].astype(F32)
            more = dot3(halves(pair_k * mask), halves(dscore * ratio), TN)
            more += dot3(halves(pair_v * mask), halves(prob * ratio), TN)
            dkeep += ratio * more
        dsum = dscore * scores[rows, :] + prob * dprobs[rows, :] - here * dkeep
        at_end = jnp.sum(adj * states[3 * b + j + 1], axis=1, keepdims=True)
        at_end = jnp.sum(at_end * on_diagonal(adj.shape[0]), axis=0, keepdims=True)
        dsum += is_last * at_end
        decay_term[rows, :] = exact_sums(later[...], dsum) - (1.0 - here) * dkeep
        return nothing

    lax.fori_loop(0, 4, second, 0)
    weave.rest()
    share.finish(False)
    fold.finish()
    carry.finish()


def backward(size, number, slot, plan, hbm_ins, vmem_ins, grads):
    seqs, block, width = hbm_ins[0].shape
    h, m, n, rows = slot.head, slot.slots, slot.chunks, slot.seqs * slot.rows
    line = size // 4
    shape = jax.ShapeDtypeStruct
    outs = [
        shape((block, width), F32), shape((seqs, 2, block, width), BF16), shape((1, width), F32), shape((rows, h), BF16),
        shape((1, h), F32), shape((rows, 3 * h), BF16), shape((rows, m), F32),
    ]
    results, spaces, sems = [], [], []
    for i, unit, offset, columns, whole in plan:
        results.append(shape((2, unit, columns) if whole else (unit, 2 * columns), F32))
        spaces += [shape((line, 2 * unit, columns), BF16), shape((line + 1, 2 * unit, columns), BF16)]
        sems += scatter_sems(line)
    widest = max(entry[3] for entry in plan)
    scratch = [
        pltpu.VMEM((block, width), BF16), pltpu.VMEM((rows, h), F32),
        pltpu.VMEM((2, block, width), BF16), pltpu.SemaphoreType.DMA((4,)),
        pltpu.VMEM((rows, h), F32), pltpu.VMEM((rows, m), F32), pltpu.VMEM((rows, m), F32), pltpu.VMEM((seqs, n, m, 2 * h), F32),
        pltpu.VMEM((seqs, n, m, 2 * h), F32), pltpu.VMEM((seqs, m, 2 * h), F32),
    ]
    scratch += prefix_scratch(seqs, m, 2 * h) + fold_scratch(block, width) + SHARE_SEMS
    scratch += pool_scratch(2 * plan[0][1], widest) + sems
    later = slot.paths[-2 * slot.chunk : -slot.chunk].T
    result = pl.pallas_call(
        functools.partial(backward_kernel, size, plan, slot.levels),
        out_shape=outs + results + spaces,
        in_specs=[ANY] * 4 + [VM] * 16 + [ANY] * len(grads),
        out_specs=[VM] * 7 + [ANY] * (len(results) + len(spaces)),
        scratch_shapes=scratch,
        compiler_params=remote_params(number, 62),
        name="attend_backward",
    )(*hbm_ins, *vmem_ins, slot.paths, later, slot.masks, *grads)
    return result[: 7 + len(results)]


def last_kernel(size, plan, *refs):
    p = Place(size)
    (part, ff_part, tokens, residual, residual_grad, gain, pack), refs = take(refs, 7)
    grads = max(i for i, _, _, _, _ in plan) + 1
    grad_refs, refs = take(refs, grads)
    (input_grad, output, sums), refs = take(refs, 3)
    outs, refs = take(refs, len(plan))
    spaces, refs = take(refs, 2 * len(plan))
    fold_refs, refs = take(refs, 5)
    ff_refs, refs = take(refs, 5)
    (out_sem, mine, came, s_sem), refs = take(refs, 4)
    pool_refs, refs = take(refs, 5)
    greet_all(p)
    pool = Pool(pool_refs)
    work = []
    for n, (i, unit, offset, width, _) in enumerate(plan):
        work.append(
            Scatter(p, grad_refs[i], outs[n], spaces[2 * n], spaces[2 * n + 1], unit, offset, width, refs[3 * n : 3 * n + 3])
        )
    weave = Weave(scatter_ops(work, pool))
    fold = Fold(p, part, *fold_refs[:3], fold_refs[3:])
    ff = Fold(p, ff_part, *ff_refs[:3], ff_refs[3:])
    weave.run(1)
    fold.start()
    ff.start()
    for r in range(STRIPS):
        fold.cross(r)
    weave.run(1)
    gains = jnp.zeros((1, part.shape[3]), F32)

    def out_copy(ref, k, r):
        block = ref.at[p.c, fold.strip(r)]
        return remote(block, block, out_sem.at[0, k * STRIPS + r], out_sem.at[1, k * STRIPS + r], p.sibling())

    for r in range(STRIPS):
        ff.cross(r)
    weave.run(2)
    for r in range(STRIPS):
        down, more = norm_back(fold.total(r), tokens[p.c, fold.strip(r)].astype(F32), gain[...])
        gains += more
        input_grad[p.c, fold.strip(r)] = residual_grad[fold.strip(r)] + down
        out_copy(input_grad, 1, r).start()
        if r % 2 == 1:
            weave.run(1)
    unit = plan[0][1]
    mine[...] = pack[...]
    for s in range(size):
        mine[s, 0:1, pl.ds(0, unit)] = gains[:, s * unit : (s + 1) * unit]
    smalls = Smalls(p, mine, sums, came, s_sem)
    smalls.start()
    weave.run(2)
    for r in range(STRIPS):
        output[p.c, fold.strip(r)] = bf(residual[fold.strip(r)] + ff.total(r))
        out_copy(output, 0, r).start()
        if r % 2 == 1:
            weave.run(1)
    weave.rest()
    smalls.finish()
    for r in range(STRIPS):
        out_copy(output, 0, r).wait()
        out_copy(input_grad, 1, r).wait()
    ff.finish()
    fold.finish()


def last(size, number, plan, vmem_ins, grads):
    seqs, _, block, width = vmem_ins[0].shape
    pack = vmem_ins[-1]
    line = size // 4
    shape = jax.ShapeDtypeStruct
    outs = [shape((seqs, block, width), F32), shape((seqs, block, width), BF16), shape(pack.shape[1:], F32)]
    results, specs, spaces, sems = [], [], [], []
    for i, unit, offset, columns, whole in plan:
        results.append(shape((2, unit, columns) if whole else (unit, 2 * columns), F32))
        specs.append(VM if whole else ANY)
        spaces += [shape((line, 2 * unit, columns), BF16), shape((line + 1, 2 * unit, columns), BF16)]
        sems += scatter_sems(line)
    widest = max(entry[3] for entry in plan)
    scratch = fold_scratch(block, width) * 2 + [
        pltpu.SemaphoreType.DMA((2, 2 * STRIPS)), pltpu.VMEM(pack.shape, F32), pltpu.VMEM((2 * size,) + pack.shape[1:], F32),
        pltpu.SemaphoreType.DMA((2, 2 * size)),
    ]
    scratch += pool_scratch(2 * plan[0][1], widest) + sems
    result = pl.pallas_call(
        functools.partial(last_kernel, size, plan),
        out_shape=outs + results + spaces,
        in_specs=[VM] * 7 + [ANY] * len(grads),
        out_specs=[VM] * 3 + specs + [ANY] * len(spaces),
        scratch_shapes=scratch,
        compiler_params=remote_params(number, 60),
        name="last",
    )(*vmem_ins, *grads)
    return result[: 3 + len(results)]

def greet_all(place):
    barrier = pltpu.get_barrier_semaphore()

    def one(i, carry):
        signal(barrier, (lax.rem(place.s + i // 2, place.size), lax.rem(place.c + lax.rem(i, 2), 2)))
        return carry

    lax.fori_loop(1, 2 * place.size, one, 0)
    pl.semaphore_wait(barrier, 2 * place.size - 1)


class Smalls:
    def __init__(self, place, pack, out, came, sems):
        self.p, self.pack, self.out, self.came, self.sems = place, pack, out, came, sems

    def copy(self, i):
        p = self.p
        s = lax.rem(p.s + i // 2, p.size)
        return remote(
            self.pack.at[s], self.came.at[i], self.sems.at[0, i], self.sems.at[1, i], (s, lax.rem(p.c + lax.rem(i, 2), 2))
        )

    def start(self):
        lax.fori_loop(1, 2 * self.p.size, lambda i, c: (self.copy(i).start(), c)[1], 0)

    def finish(self):
        def one(i, total):
            self.copy(i).wait()
            return total + self.came[i]

        self.out[...] = lax.fori_loop(1, 2 * self.p.size, one, self.pack[self.p.s])


class Swap:
    def __init__(self, place, own, both, sems):
        p = self.p = place
        self.keep = pltpu.make_async_copy(own, both.at[:, p.x], sems.at[0])
        self.cross = remote(own.at[p.c], both.at[p.c, p.x], sems.at[1], sems.at[2], p.partner())
        came = both.at[p.c, 1 - p.x]
        self.hand = remote(came, came, sems.at[3], sems.at[4], p.sibling())

    def start(self):
        self.cross.start()
        self.keep.start()

    def forward(self):
        self.cross.wait_recv()
        self.hand.start()

    def finish(self):
        self.keep.wait()
        self.cross.wait_send()
        self.hand.wait()


def gather_kernel(size, plan, swaps, *refs):
    p = Place(size)
    shards = len(plan)
    fulls = max(i for i, _, _, _, _ in plan) + 1
    ins, refs = refs[: shards + swaps], refs[shards + swaps :]
    outs, refs = refs[: fulls + swaps], refs[fulls + swaps :]
    greet(p, sibling=True)
    work = []
    for n, (i, unit, offset, width, late) in enumerate(plan):
        work.append(Gather(p, ins[n], outs[i], unit, offset, width, refs[4 * n : 4 * n + 4], late))
    moves = [Swap(p, ins[shards + n], outs[fulls + n], refs[4 * shards + n]) for n in range(swaps)]
    weave = Weave(gather_ops(work, len(work)))
    weave.run(len(work))
    for move in moves:
        move.start()
    weave.run(len(weave.steps) - len(work))
    for move in moves:
        move.forward()
    weave.rest()
    for move in moves:
        move.finish()


def gather(size, number, plan, shards, fulls, tokens):
    line = size // 4
    scratch = []
    for _ in plan:
        scratch += gather_sems(line)
    shapes = [jax.ShapeDtypeStruct(shape, BF16) for shape in fulls]
    for array in tokens:
        shapes.append(jax.ShapeDtypeStruct((array.shape[0], 2) + array.shape[1:], BF16))
        scratch.append(pltpu.SemaphoreType.DMA((5,)))
    return pl.pallas_call(
        functools.partial(gather_kernel, size, plan, len(tokens)),
        out_shape=shapes,
        in_specs=[ANY] * (len(shards) + len(tokens)),
        out_specs=[ANY] * len(shapes),
        scratch_shapes=scratch,
        compiler_params=remote_params(number, 60),
        name="gather",
    )(*shards, *tokens)


def dot(left, right, dims, dtype=F32):
    return lax.dot_general(left, right, dims, preferred_element_type=F32).astype(dtype)


def lanes(row):
    return jnp.pad(row.reshape(-1), (0, 128 - row.size))


def shards(
    tokens, grad_out, query_weight, key_weight, value_weight, forget_weight, forget_bias, outgate_weight, output_weight,
    slot_gain, first_gain, second_gain, gate_weight, up_weight, down_weight,
):
    size = lax.axis_size("seq")
    x = lax.rem(lax.axis_index("seq"), 2)
    c = lax.axis_index("head")
    seqs, block, width = tokens.shape
    heads_here, slot_part = forget_bias.shape
    slots = slot_part * size
    head = slot_gain.shape[0] * size
    unit = first_gain.shape[0]
    hidden = gate_weight.shape[1] // 2
    rows = seqs * 2 * block
    pack = jnp.stack([lanes(first_gain), lanes(second_gain), lanes(slot_gain), lanes(forget_bias)] + [jnp.zeros(128, BF16)] * 12)
    plan = [
        (0, unit, 0, head, False), (0, unit, head, head, False), (0, unit, 2 * head, head, False),
        (1, unit, 0, head, False), (1, unit, head, 2 * slots, False), (2, unit, 0, head, False),
        (3, 16, 0, 128, False),
    ]
    fulls = [(width, 3 * head), (width, head + 2 * slots), (width, head), (16 * size, 128)]
    qkv_full, gate_full, out_full, small_full, tok, gout = gather(
        size, 0, plan,
        (query_weight, key_weight, value_weight, outgate_weight, forget_weight, output_weight.T, pack),
        fulls, (tokens, grad_out),
    )
    small = small_full.reshape(size, 16, 128).astype(F32)
    first_full = small[:, 0, :unit].reshape(1, width)
    second_full = small[:, 1, :unit].reshape(1, width)
    slot_full = small[:, 2, : head // size].reshape(1, head)
    bias_full = small[:, 3, : heads_here * slot_part].reshape(size, heads_here, slot_part)
    bias_full = jnp.moveaxis(bias_full, 1, 0).reshape(heads_here, slots)

    def own_head(array, axis):
        return jnp.where(x == 0, *jnp.split(array, 2, axis=axis))

    inputs = tok.reshape(rows, width).astype(F32)
    normed_one = (inputs * inverse_rms(inputs) * first_full).astype(BF16)
    qkv = dot(normed_one, qkv_full, NN, BF16)
    gates = dot(normed_one, gate_full, NN)
    logit = own_head(gates[:, head:], 1) + own_head(bias_full, 0)
    decay = -jax.nn.softplus(-logit) / TAU
    keep = -jnp.expm1(decay)
    slot = Slots(seqs, 2 * block, head, slots, block)
    ff_plan = [(0, unit, 0, hidden, False), (0, unit, hidden, hidden, False), (1, unit, 0, hidden, False)]
    (gated, attended, probs, scores, weights, states, decs, end_decs, residual, normed_two, ff_full, down_full) = forward(
        size, 1, slot, ff_plan, [(width, 2 * hidden), (width, hidden)], qkv, gates, decay, keep, slot_full, out_full, tokens,
        second_full, (gate_weight, up_weight, down_weight.T),
    )
    shape = (seqs, 2, block, width)
    normed_two = normed_two.reshape(rows, width)
    ff = dot(normed_two, ff_full, NN)
    ff_gate, ff_up = ff[:, :hidden], ff[:, hidden:]
    sig = jax.nn.sigmoid(ff_gate)
    activated = (ff_gate * sig * ff_up).astype(BF16)
    ff_part = dot(activated, down_full, NT, BF16).reshape(shape)
    gout = gout.reshape(rows, width)
    act_grad = dot(gout, down_full, NN)
    ff_term = jnp.concatenate(
        [act_grad * ff_up * (sig + ff_gate * sig * (1.0 - sig)), act_grad * ff_gate * sig], axis=1
    ).astype(BF16)
    down_grad = dot(gout, activated, TN, BF16)
    ff_grad = dot(normed_two, ff_term, TN, BF16)
    normed_two_grad = dot(ff_term, ff_full, NT, BF16).reshape(shape)
    ff_plan = [(0, unit, 0, hidden, False), (0, unit, hidden, hidden, False), (1, unit, 0, hidden, False)]
    residual_grad, low, second_part, gate_term, slot_part_grad, qkv_term, decay_term, gate_grad, up_grad, down_grad = backward(
        size, 2, slot, ff_plan,
        (grad_out, gates, attended, normed_two_grad),
        (residual, second_full, out_full, qkv, decay, keep, slot_full, probs, scores, weights, states, decs,
         end_decs),
        (ff_grad, down_grad),
    )
    low = low.reshape(rows, width)
    out_grad = dot(low, gated, TN, BF16)
    forget_term = (decay_term * jax.nn.sigmoid(-logit) / TAU).astype(BF16)
    none = jnp.zeros_like(forget_term)
    gates_term = jnp.concatenate(
        [gate_term, jnp.where(x == 0, forget_term, none), jnp.where(x == 0, none, forget_term)], axis=1
    )
    qkv_grad = dot(normed_one, qkv_term, TN, BF16)
    gates_grad = dot(normed_one, gates_term, TN, BF16)
    normed_one_grad = (dot(qkv_term, qkv_full, NT) + dot(gates_term, gate_full, NT)).astype(BF16).reshape(shape)
    bias_part = jnp.sum(forget_term.astype(F32), axis=0)
    which = jnp.arange(2 * heads_here) == heads_here * c + x
    bias_part = jnp.where(which[:, None], bias_part[None, :], 0.0).reshape(2 * heads_here, size, slot_part)

    def rows_of(array):
        array = array.reshape(size, -1)
        return jnp.pad(array, ((0, 0), (0, 128 - array.shape[1])))

    zero = jnp.zeros((size, 128), F32)
    packed = jnp.stack(
        [zero, rows_of(second_part), rows_of(slot_part_grad), rows_of(jnp.moveaxis(bias_part, 1, 0))] + [zero] * 4, axis=1
    )
    plan = [
        (0, unit, 0, head, False), (1, unit, 0, head, False), (1, unit, head, head, False), (1, unit, 2 * head, head, False),
        (2, unit, 0, head, False), (2, unit, head, 2 * slots, True),
    ]
    input_grad, output, sums, output_grad, query_grad, key_grad, value_grad, outgate_grad, forget_grad = last(
        size, 3, plan, (normed_one_grad, ff_part, tokens, residual, residual_grad, first_full, packed),
        (out_grad, qkv_grad, gates_grad),
    )
    bias_grad = sums[3, : 2 * heads_here * slot_part].reshape(2, heads_here, slot_part)
    bias_grad = jnp.where(c == 0, bias_grad[0], bias_grad[1])
    return (
        output, input_grad, query_grad, key_grad, value_grad, forget_grad[0], bias_grad, outgate_grad, output_grad.T,
        sums[2, : head // size], sums[0, :unit], sums[1, :unit], gate_grad, up_grad, down_grad.T,
    )


def solution(mesh):
    row, column, vector, token = P("seq", "head"), P("head", "seq"), P("seq"), P(None, "seq", None)
    return jax.shard_map(
        shards,
        mesh=mesh,
        in_specs=(token, token, row, row, row, row, column, row, column, vector, vector, vector, row, row, column),
        out_specs=(token, token, row, row, row, row, column, row, column, vector, vector, vector, row, row, column),
        check_vma=False,
    )
```

```python
import functools

import jax
import jax.numpy as jnp
import numpy as np
from jax import lax
from jax.experimental import pallas as pl
from jax.experimental.pallas import tpu as pltpu
from jax.sharding import PartitionSpec as P

F32, BF16 = jnp.float32, jnp.bfloat16
MESH = pl.DeviceIdType.MESH
HBM = pltpu.HBM
EPS = 1e-06
TAU = 8.0


CHUNK = 256
NT = (((1,), (1,)), ((), ()))
NN = (((1,), (0,)), ((), ()))
TN = (((0,), (0,)), ((), ()))


def decay_tables(count):
    at = np.arange(count)
    paths, masks = [], []
    half = count // 2
    while half >= 1:
        block, second = at // (2 * half), (at // half) % 2 == 1
        edge = block * 2 * half + half - 1
        r, t = at[None, :], at[:, None]
        fore = second[:, None] & (r > edge[:, None]) & (r <= t)
        back = ~second[:, None] & (r > t) & (r <= edge[:, None])
        paths.append(fore | back)
        masks.append((block[:, None] == block[None, :]) & second[:, None] & ~second[None, :])
        half //= 2
    paths.append(at[None, :] <= at[:, None])
    paths.append(at[None, :] > at[:, None])
    return np.concatenate(paths, 0), np.stack(masks)


def bf(x):
    return x.astype(BF16)


def halves(x):
    hi = bf(x)
    return hi, bf(x - hi.astype(F32))


def mm(a, b, dims):
    return lax.dot_general(a, b, dims, preferred_element_type=F32)


def dot3(a, b, dims):
    return mm(a[0], b[0], dims) + (mm(a[0], b[1], dims) + mm(a[1], b[0], dims))


def exact_sums(table, x):
    hi, mid = halves(x)
    low = bf(x - hi.astype(F32) - mid.astype(F32))
    n = x.shape[1]
    both = mm(table, jnp.concatenate([hi, mid, low, jnp.zeros_like(low)], axis=1), NN)
    return both[:, :n] + (both[:, n : 2 * n] + both[:, 2 * n : 3 * n])


def silu(v):
    return v / (1.0 + jnp.exp(-v))


def sigmoid(v):
    return 1.0 / (1.0 + jnp.exp(-v))


def silu_slope(v):
    s = sigmoid(v)
    return s + v * s * (1.0 - s)


def columns_total(x):
    ones = jnp.ones((x.shape[0], 128), BF16)
    hi, mid = halves(x)
    low = bf(x - hi.astype(F32) - mid.astype(F32))
    return mm(hi, ones, TN) + (mm(mid, ones, TN) + mm(low, ones, TN))


def spread(column, width):
    return jnp.concatenate([column] * (width // 128), axis=1)


def mix(pair, ratios, keep, masks_ref, own):
    out = own * keep
    for l, ratio in enumerate(ratios):
        left = pair * masks_ref[l].astype(F32)
        out += ratio * dot3(halves(left), halves(ratio * keep), NN)
    return out


def unmix(probs, ratios, keep, masks_ref, diag):
    out = diag * jnp.sum(probs * keep, axis=1, keepdims=True)
    for l, ratio in enumerate(ratios):
        part = dot3(halves(probs * ratio), halves(ratio * keep), NT)
        out += masks_ref[l].astype(F32) * part
    return out


def on_diagonal(count):
    return (
        lax.broadcasted_iota(jnp.int32, (count, count), 0) == lax.broadcasted_iota(jnp.int32, (count, count), 1)
    ).astype(F32)


class Slots:
    def __init__(self, seqs, rows, head, slots, chunk):
        self.seqs, self.rows, self.head, self.slots, self.chunk = seqs, rows, head, slots, chunk
        self.chunks = rows // chunk
        paths, masks = decay_tables(chunk)
        self.levels = masks.shape[0]
        self.paths = jnp.asarray(paths, BF16)
        self.masks = jnp.asarray(masks, BF16)

class Place:
    def __init__(self, size):
        self.size = size
        self.line = size // 4
        s = lax.axis_index("seq")
        self.c = lax.axis_index("head")
        self.s = s
        self.x = lax.rem(s, 2)
        self.b = lax.rem(s // 2, 2)
        self.a = s // 4

    def at(self, a, b, x):
        return (a * 2 + b) * 2 + x

    def partner(self):
        return (self.at(self.a, self.b, 1 - self.x), self.c)

    def across(self):
        return (self.at(self.a, 1 - self.b, self.x), self.c)

    def up(self):
        return (self.at(jnp.minimum(self.a + 1, self.line - 1), self.b, self.x), self.c)

    def down(self):
        return (self.at(jnp.maximum(self.a - 1, 0), self.b, self.x), self.c)

    def sibling(self):
        return (self.s, 1 - self.c)

    def has_up(self):
        return self.a < self.line - 1

    def has_down(self):
        return self.a > 0


def signal(sem, device):
    pl.semaphore_signal(sem, inc=1, device_id=device, device_id_type=MESH)


def greet(place, partner=True, across=True, line=True, sibling=False):
    barrier = pltpu.get_barrier_semaphore()
    count = jnp.int32(0)
    if partner:
        signal(barrier, place.partner())
        count = count + 1
    if sibling:
        signal(barrier, place.sibling())
        count = count + 1
    if across:
        signal(barrier, place.across())
        count = count + 1
    if line:
        pl.when(place.has_up())(lambda: signal(barrier, place.up()))
        pl.when(place.has_down())(lambda: signal(barrier, place.down()))
        count = count + place.has_up().astype(jnp.int32) + place.has_down().astype(jnp.int32)
    pl.semaphore_wait(barrier, count)


def remote(src, dst, send, recv, device):
    return pltpu.make_async_remote_copy(
        src_ref=src, dst_ref=dst, send_sem=send, recv_sem=recv, device_id=device, device_id_type=MESH
    )


class Gather:
    def __init__(self, place, full, unit, pieces, sems, late=False):
        self.pl, self.full, self.unit, self.pieces, self.late = place, full, unit, pieces, late
        self.offset = min(offset for _, offset, _ in pieces)
        self.width = sum(width for _, _, width in pieces)
        self.x_sem, self.b_sem, self.up_sem, self.down_sem = sems

    def part(self, start, count, offset=None, width=None):
        offset, width = (self.offset, self.width) if width is None else (offset, width)
        rows = pl.ds(start * self.unit, count * self.unit)
        if width == self.full.shape[1]:
            return self.full.at[rows]
        return self.full.at[rows, pl.ds(offset, width)]

    def mine(self, i, x):
        shard, _, width = self.pieces[i]
        if shard.shape[1] == width:
            return shard
        return shard.at[:, pl.ds(x * width, width)]

    def x_copy(self, i):
        p = self.pl
        _, offset, width = self.pieces[i]
        here = self.part(p.s, 1, offset, width)
        return remote(self.mine(i, 1 - p.x), here, self.x_sem.at[0, i], self.x_sem.at[1, i], p.partner())

    def own_copy(self, i):
        _, offset, width = self.pieces[i]
        return pltpu.make_async_copy(self.mine(i, self.pl.x), self.part(self.pl.s, 1, offset, width), self.x_sem.at[2, i])

    def block(self, a):
        p = self.pl
        if self.late:
            return self.part(4 * a, 4)
        return self.part(4 * a + 2 * p.b, 2)

    def b_copy(self, i, a):
        p = self.pl
        return remote(
            self.part(4 * a + 2 * p.b, 2), self.part(4 * a + 2 * p.b, 2),
            self.b_sem.at[0, i], self.b_sem.at[1, i], p.across(),
        )

    def line_copy(self, way, h):
        p = self.pl
        if way == "up":
            blk = self.block(jnp.maximum(p.a - (h - 1), 0))
            return remote(blk, blk, self.up_sem.at[0, h - 1], self.up_sem.at[1, h - 1], p.up())
        blk = self.block(jnp.minimum(p.a + (h - 1), p.line - 1))
        return remote(blk, blk, self.down_sem.at[0, h - 1], self.down_sem.at[1, h - 1], p.down())

    def sends(self, way, h):
        p = self.pl
        if way == "up":
            return jnp.logical_and(p.has_up(), p.a - (h - 1) >= 0)
        return jnp.logical_and(p.has_down(), p.a + (h - 1) <= p.line - 1)

    def gets(self, way, h):
        p = self.pl
        if way == "up":
            return p.a - h >= 0
        return p.a + h <= p.line - 1

    def got(self, way, h):
        p = self.pl
        if way == "up":
            return jnp.maximum(p.a - h, 0)
        return jnp.minimum(p.a + h, p.line - 1)

    def slot(self, way, h):
        return h if way == "up" else self.pl.line - 1 + h

    def start_x(self):
        for i in range(len(self.pieces)):
            self.x_copy(i).start()
            self.own_copy(i).start()

    def stage(self, h):
        p = self.pl
        if h == 0:
            for i in range(len(self.pieces)):
                self.own_copy(i).wait()
                self.x_copy(i).wait_recv()
            if self.late:
                self.b_copy(0, p.a).start()
            else:
                for way in ("up", "down"):
                    pl.when(self.sends(way, 1))(lambda way=way: self.line_copy(way, 1).start())
                self.b_copy(0, p.a).start()
            return
        if self.late:
            if h == 1:
                self.b_copy(0, p.a).wait_recv()
                for way in ("up", "down"):
                    pl.when(self.sends(way, 1))(lambda way=way: self.line_copy(way, 1).start())
                return
            h = h - 1
        for way in ("up", "down"):

            def go(way=way):
                self.line_copy(way, h).wait_recv()
                if not self.late:
                    self.b_copy(self.slot(way, h), self.got(way, h)).start()

            def on(way=way):
                self.line_copy(way, h + 1).start()

            pl.when(self.gets(way, h))(go)
            if h + 1 <= p.line - 1:
                pl.when(self.sends(way, h + 1))(on)

    def stages(self):
        return self.pl.line + (1 if self.late else 0)

    def finish(self):
        p = self.pl
        for i in range(len(self.pieces)):
            self.x_copy(i).wait_send()
        self.b_copy(0, p.a).wait_send()
        if not self.late:
            self.b_copy(0, p.a).wait_recv()
        for way in ("up", "down"):
            for h in range(1, p.line):
                pl.when(self.sends(way, h))(lambda way=way, h=h: self.line_copy(way, h).wait_send())
                if not self.late:

                    def both(way=way, h=h):
                        cp = self.b_copy(self.slot(way, h), self.got(way, h))
                        cp.wait_send()
                        cp.wait_recv()

                    pl.when(self.gets(way, h))(both)


def gather_sems(line, pieces):
    return [
        pltpu.SemaphoreType.DMA((3, pieces)),
        pltpu.SemaphoreType.DMA((2, 2 * line - 1)),
        pltpu.SemaphoreType.DMA((2, line - 1)),
        pltpu.SemaphoreType.DMA((2, line - 1)),
    ]


def gathers_of(place, plan, shards, fulls, sems):
    work, at = [], 0
    for n, (i, unit, columns) in enumerate(plan):
        pieces = [(shards[at + m], offset, width) for m, (offset, width) in enumerate(columns)]
        at += len(columns)
        work.append(Gather(place, fulls[i], unit, pieces, sems[4 * n : 4 * n + 4]))
    return work


def gather_ops(gathers, pace):
    order = sorted((k * pace + h, k, h) for k, g in enumerate(gathers) for h in range(g.stages()))
    steps = [functools.partial(gathers[k].stage, h) for _, k, h in order]
    return steps + [g.finish for g in gathers]

VM = pl.BlockSpec(memory_space=pltpu.VMEM)
ANY = pl.BlockSpec(memory_space=HBM)


def remote_params(number, mib=56):
    return pltpu.CompilerParams(collective_id=number, has_side_effects=True, vmem_limit_bytes=mib * 2**20)


STRIPS = 4


class Fold:
    def __init__(self, place, part, sib, sent, came, sems, own=None):
        self.p, self.part, self.sib, self.sent, self.came = place, part, sib, sent, came
        self.own = part.at[place.c] if own is None else own
        self.s_sem, self.x_sem = sems
        self.rows = part.shape[2] // STRIPS

    def strip(self, r):
        return pl.ds(r * self.rows, self.rows)

    def sib_copy(self, far, r):
        p = self.p
        x = 1 - p.x if far else p.x
        i = (0 if far else STRIPS) + r
        return remote(
            self.part.at[1 - p.c, x, self.strip(r)], self.sib.at[1 if far else 0, self.strip(r)],
            self.s_sem.at[0, i], self.s_sem.at[1, i], p.sibling(),
        )

    def x_copy(self, r):
        return remote(
            self.sent.at[self.strip(r)], self.came.at[self.strip(r)], self.x_sem.at[0, r], self.x_sem.at[1, r], self.p.partner()
        )

    def start(self):
        for r in range(STRIPS):
            self.sib_copy(True, r).start()
        for r in range(STRIPS):
            self.sib_copy(False, r).start()

    def sib_all(self, far):
        for r in range(STRIPS):
            self.sib_copy(far, r).start()

    def cross(self, r):
        p = self.p
        self.sib_copy(True, r).wait_recv()
        own = self.own[1 - p.x, self.strip(r)].astype(F32)
        self.sent[self.strip(r)] = bf(own + self.sib[1, self.strip(r)].astype(F32))
        self.x_copy(r).start()

    def total(self, r):
        p = self.p
        self.sib_copy(False, r).wait_recv()
        self.x_copy(r).wait_recv()
        own = self.own[p.x, self.strip(r)].astype(F32) + self.sib[0, self.strip(r)].astype(F32)
        return own + self.came[self.strip(r)].astype(F32)

    def finish(self):
        for r in range(STRIPS):
            self.sib_copy(True, r).wait_send()
            self.sib_copy(False, r).wait_send()
            self.x_copy(r).wait_send()


def fold_scratch(rows, width):
    return [
        pltpu.VMEM((2, rows, width), BF16), pltpu.VMEM((rows, width), BF16), pltpu.VMEM((rows, width), BF16),
        pltpu.SemaphoreType.DMA((2, 2 * STRIPS)), pltpu.SemaphoreType.DMA((2, STRIPS)),
    ]


class Share:
    def __init__(self, place, out, sems):
        self.p, self.out = place, out
        self.x_sem, self.s_sem = sems
        self.rows = out.shape[2] // STRIPS

    def strip(self, r):
        return pl.ds(r * self.rows, self.rows)

    def x_copy(self, r):
        p = self.p
        block = self.out.at[p.c, p.x, self.strip(r)]
        return remote(block, block, self.x_sem.at[0, r], self.x_sem.at[1, r], p.partner())

    def s_copy(self, far, r):
        p = self.p
        block = self.out.at[p.c, 1 - p.x if far else p.x, self.strip(r)]
        i = (0 if far else STRIPS) + r
        return remote(block, block, self.s_sem.at[0, i], self.s_sem.at[1, i], p.sibling())

    def put(self, r, value):
        self.out[self.p.c, self.p.x, self.strip(r)] = value
        self.x_copy(r).start()
        self.s_copy(False, r).start()

    def forward(self, r):
        self.x_copy(r).wait_recv()
        self.s_copy(True, r).start()

    def wait_sibling(self, far):
        for r in range(STRIPS):
            self.s_copy(far, r).wait_recv()

    def finish(self, receive=True):
        for r in range(STRIPS):
            self.x_copy(r).wait_send()
            for far in (False, True):
                self.s_copy(far, r).wait_send()
                if receive:
                    self.s_copy(far, r).wait_recv()


SHARE_SEMS = [pltpu.SemaphoreType.DMA((2, STRIPS)), pltpu.SemaphoreType.DMA((2, 2 * STRIPS))]


def inverse_rms(values):
    return lax.rsqrt(jnp.mean(values * values, axis=-1, keepdims=True) + EPS)


def norm_back(grad, values, gain):
    scale = inverse_rms(values)
    u = grad * gain
    down = scale * u - values * (scale * scale * scale) * jnp.mean(u * values, axis=-1, keepdims=True)
    return down, jnp.sum(grad * values * scale, axis=0, keepdims=True)


def ends_chunk(k, v, decay, keep, tail):
    weight = halves(jnp.exp(exact_sums(tail, decay)) * keep)
    unit_k = dot3(weight, halves(silu(k.astype(F32))), TN)
    unit_v = mm(weight[0], v, TN) + mm(weight[1], v, TN)
    return jnp.concatenate([unit_k, unit_v], axis=1), jnp.exp(columns_total(decay))


def powers_of(table, count, levels, decay):
    powers = jnp.exp(exact_sums(table, decay))
    return [powers[l * count : (l + 1) * count] for l in range(levels)], [
        powers[l * count : (l + 1) * count] for l in range(levels, table.shape[0] // count)
    ]


class Prefix:
    def __init__(self, place, back, own, dec, start, peer, peer_dec, line, out, sems):
        p = self.p = place
        self.own, self.dec, self.start_ref, self.peer, self.peer_dec = own, dec, start, peer, peer_dec
        self.line, self.out = line, out
        self.p_sem, self.d_sem, self.l_sem = sems
        seqs, slots, width = own.shape
        self.half = width // 2
        self.pieces = [(b, h) for b in range(seqs) for h in range(2)]
        if back:
            self.has_prev, self.has_next, self.after = p.has_up(), p.has_down(), p.down()
        else:
            self.has_prev, self.has_next, self.after = p.has_down(), p.has_up(), p.up()
        self.first = ((p.b == 1) if back else (p.b == 0)).astype(F32)

    def cut(self, ref, i):
        b, h = self.pieces[i]
        return ref.at[b, :, pl.ds(h * self.half, self.half)]

    def peer_copy(self, i):
        return remote(self.cut(self.own, i), self.cut(self.peer, i), self.p_sem.at[0, i], self.p_sem.at[1, i], self.p.across())

    def line_copy(self, i):
        return remote(self.cut(self.out, i), self.cut(self.line, i), self.l_sem.at[0, i], self.l_sem.at[1, i], self.after)

    def dec_copy(self):
        return remote(self.dec, self.peer_dec, self.d_sem.at[0], self.d_sem.at[1], self.p.across())

    def start(self):
        self.dec_copy().start()
        for i in range(len(self.pieces)):
            self.peer_copy(i).start()

    def run(self):
        self.dec_copy().wait_recv()
        for i, (b, _) in enumerate(self.pieces):
            self.peer_copy(i).wait_recv()
            dec_own = spread(self.dec[b], self.half)
            dec_peer = spread(self.peer_dec[b], self.half)
            own, other = self.cut(self.own, i)[...], self.cut(self.peer, i)[...]
            first = self.first
            both = first * (dec_peer * own + other) + (1.0 - first) * (dec_own * other + own)
            here, result = self.cut(self.out, i), self.cut(self.start_ref, i)

            def go_on(i=i):
                self.line_copy(i).wait_recv()
                came = self.cut(self.line, i)[...]
                here[...] = dec_own * dec_peer * came + both
                result[...] = first * came + (1.0 - first) * (dec_peer * came + other)

            def begin():
                here[...] = both
                result[...] = (1.0 - first) * other

            pl.when(self.has_prev)(go_on)
            pl.when(jnp.logical_not(self.has_prev))(begin)
            pl.when(self.has_next)(lambda i=i: self.line_copy(i).start())

    def finish(self):
        self.dec_copy().wait_send()
        for i in range(len(self.pieces)):
            self.peer_copy(i).wait_send()
            pl.when(self.has_next)(lambda i=i: self.line_copy(i).wait_send())


def prefix_scratch(seqs, slots, width):
    count = 2 * seqs
    return [
        pltpu.VMEM((seqs, slots, width), F32), pltpu.VMEM((seqs, slots, width), F32), pltpu.VMEM((seqs, slots, 128), F32),
        pltpu.VMEM((seqs, slots, width), F32), pltpu.VMEM((seqs, slots, width), F32),
        pltpu.SemaphoreType.DMA((2, count)), pltpu.SemaphoreType.DMA((2,)), pltpu.SemaphoreType.DMA((2, count)),
    ]


def take(refs, count):
    return refs[:count], refs[count:]


class Weave:
    def __init__(self, steps):
        self.steps = list(steps)

    def run(self, count):
        for step in self.steps[:count]:
            step()
        self.steps = self.steps[count:]

    def rest(self):
        self.run(len(self.steps))


def blocks_in_order(p, seqs):
    def block(i):
        b = jnp.where(i < 2, 1 - p.c, p.c)
        x = jnp.where(lax.rem(i, 2) == 0, 1 - p.x, p.x)
        return b, x

    return block


PACE = 1.5
FORE_STEPS = (0, 6, 0, 4, 0, 2, 0, 0)


def forward_kernel(size, plan, levels, *refs):
    p = Place(size)
    (qkv, gates, decay, keep, gain, out_w, tokens, gain2, paths, masks, grad_out), refs = take(refs, 11)
    shard_refs, refs = take(refs, sum(len(columns) for _, _, columns in plan))
    (gated, attended, probs, scores, weights, states, decs, end_dec, residual, normed, grads), refs = take(refs, 11)
    fulls, refs = take(refs, max(i for i, _, _ in plan) + 1)
    (units, part, total), refs = take(refs, 3)
    (start, *prefix_refs), refs = take(refs, 8)
    fold_refs, refs = take(refs, 5)
    share_sems, refs = take(refs, 2)
    (swap_sem,), refs = take(refs, 1)
    count = paths.shape[1]
    head = gated.shape[1]
    seqs = tokens.shape[0]
    slots = keep.shape[1]
    greet(p, sibling=True)
    work = gathers_of(p, plan, shard_refs, fulls, refs)
    for gathered in work:
        gathered.start_x()
    weave = Weave(gather_ops(work, PACE))
    weave.run(FORE_STEPS[0])
    tail = paths[(levels + 1) * count :, :]

    def ends(b):
        for j in range(2):
            rows = pl.ds((b * 2 + j) * count, count)
            unit, dec = ends_chunk(
                qkv[rows, head : 2 * head], qkv[rows, 2 * head :], decay[rows, :], keep[rows, :], tail
            )
            units[b, j] = unit
            decs[b, j] = dec
        total[b] = spread(dec, 2 * head) * units[b, 0] + unit
        end_dec[b] = decs[b, 0] * dec

    for b in range(seqs):
        ends(b)
    carry = Prefix(p, False, total, end_dec, start, *prefix_refs[:4], prefix_refs[4:])
    carry.start()
    weave.run(FORE_STEPS[1])
    move = Swap(p, grad_out, grads, swap_sem)
    move.start()
    carry.run()
    for b in range(seqs):
        states[3 * b] = start[b]
        for j in range(2):
            states[3 * b + j + 1] = spread(decs[b, j], 2 * head) * states[3 * b + j] + units[b, j]
    weave.run(FORE_STEPS[2])
    diag = on_diagonal(count)
    order = blocks_in_order(p, seqs)
    fold = Fold(p, part, *fold_refs[:3], fold_refs[3:])
    share = Share(p, normed, share_sems)

    def attend(i, nothing):
        b, j = order(i)
        rows = pl.ds(pl.multiple_of((b * 2 + j) * count, count), count)
        here = keep[rows, :]
        ratios, (growth,) = powers_of(paths[: (levels + 1) * count, :], count, levels, decay[rows, :])
        query = halves(silu(qkv[rows, :head].astype(F32)) * head ** (-0.5))
        keys = halves(silu(qkv[rows, head : 2 * head].astype(F32)))
        state = states[3 * b + j]
        pair = dot3(query, keys, NT)
        score = mix(pair, ratios, here, masks, jnp.sum(pair * diag, axis=1, keepdims=True))
        score += growth * dot3(query, halves(state[:, :head]), NT)
        raised = jnp.exp(score - jnp.max(score, axis=1, keepdims=True))
        prob = raised / jnp.sum(raised, axis=1, keepdims=True)
        weight = unmix(prob, ratios, here, masks, diag)
        values = qkv[rows, 2 * head :]
        whi, wlo = halves(weight)
        result = mm(whi, values, NN) + mm(wlo, values, NN)
        result += dot3(halves(prob * growth), halves(state[:, head:]), NN)
        scale = lax.rsqrt(jnp.mean(result * result, axis=1, keepdims=True) + EPS)
        low = bf(result * scale * gain[...] * silu(gates[rows, :head]))
        gated[rows, :] = low
        attended[rows, :] = result
        probs[rows, :] = prob
        scores[rows, :] = score
        weights[rows, :] = weight
        part[b, j] = bf(mm(low, out_w[...], NT))
        pl.when(i == 0)(lambda: fold.sib_all(True))
        pl.when(i == 1)(lambda: fold.sib_all(False))
        return nothing

    lax.fori_loop(0, 2, attend, 0)
    weave.run(FORE_STEPS[3])
    lax.fori_loop(2, 3, attend, 0)
    for r in range(STRIPS):
        fold.cross(r)
    weave.run(FORE_STEPS[4])
    move.forward()
    lax.fori_loop(3, 4, attend, 0)
    weave.run(FORE_STEPS[5])
    for r in range(STRIPS):
        value = tokens[p.c, fold.strip(r)].astype(F32) + fold.total(r)
        residual[fold.strip(r)] = value
        share.put(r, bf(value * inverse_rms(value) * gain2[...]))
        if r == 1:
            weave.run(FORE_STEPS[6])
    weave.run(FORE_STEPS[7])
    for r in range(STRIPS):
        share.forward(r)
    weave.rest()
    share.finish()
    fold.finish()
    carry.finish()
    move.finish()


def forward(size, number, slot, plan, fulls, qkv, gates, decay, keep, gain, out_w, tokens, gain2, grad_out, shards):
    seqs, block, width = tokens.shape
    h, m, n, rows = slot.head, slot.slots, slot.chunks, slot.seqs * slot.rows
    shape = jax.ShapeDtypeStruct
    outs = [
        shape((rows, h), BF16), shape((rows, h), F32), shape((rows, m), F32), shape((rows, m), F32), shape((rows, slot.chunk), F32),
        shape((seqs * (n + 1), m, 2 * h), F32), shape((seqs, n, m, 128), F32), shape((seqs, m, 128), F32),
        shape((block, width), F32), shape((seqs, 2, block, width), BF16), shape((seqs, 2, block, width), BF16),
    ]
    scratch = [
        pltpu.VMEM((seqs, n, m, 2 * h), F32), pltpu.VMEM((seqs, 2, block, width), BF16), pltpu.VMEM((seqs, m, 2 * h), F32),
    ]
    scratch += prefix_scratch(seqs, m, 2 * h) + fold_scratch(block, width) + SHARE_SEMS + [pltpu.SemaphoreType.DMA((5,))]
    for _, _, columns in plan:
        scratch += gather_sems(size // 4, len(columns))
    return pl.pallas_call(
        functools.partial(forward_kernel, size, plan, slot.levels),
        out_shape=outs + [shape(full, BF16) for full in fulls],
        in_specs=[VM] * 10 + [ANY] * (1 + len(shards)),
        out_specs=[VM] * 10 + [ANY] * (1 + len(fulls)),
        scratch_shapes=scratch,
        compiler_params=remote_params(number, 60),
        name="attend_forward",
    )(qkv, gates, decay, keep, gain, out_w, tokens, gain2, slot.paths, slot.masks, grad_out, *shards)

class Pool:
    def __init__(self, refs):
        self.loads, self.extra, self.sends, self.totals, self.sems = refs

    def slot(self, which, slot):
        return self.extra if slot == 3 else self.loads.at[which, slot]


POOL_SENDS = 2
AHEAD = 3
LAG = 1


def pool_scratch(rows, width):
    return [
        pltpu.VMEM((2, 3, rows, width), BF16), pltpu.VMEM((rows, width), BF16), pltpu.VMEM((POOL_SENDS, rows, width), BF16),
        pltpu.VMEM((rows, width), F32),
        pltpu.SemaphoreType.DMA((2, 4)),
    ]


class Scatter:
    def __init__(self, place, grad, out, peer, line, unit, offset, width, sems):
        self.p, self.grad, self.out, self.peer, self.line = place, grad, out, peer, line
        self.unit, self.offset, self.width = unit, offset, width
        self.whole = out.shape[-1] == width
        self.b_sem, self.l_sem, self.x_sem = sems

    def goal(self, n):
        p = self.p
        low, high = p.a, p.line - 1 - p.a
        more, less = jnp.maximum(low, high), jnp.minimum(low, high)
        alone = more - less
        up_more = jnp.where(high >= low, 1, -1)
        m = n - alone
        early = n < alone
        reach = jnp.where(early, more - n, less - m // 2)
        side = jnp.where(early, up_more, jnp.where(lax.rem(jnp.maximum(m, 0), 2) == 0, 1, -1))
        return p.a + side * reach

    def block(self, a, b):
        rows = pl.ds((4 * a + 2 * b) * self.unit, 2 * self.unit)
        if self.width == self.grad.shape[1]:
            return self.grad.at[rows]
        return self.grad.at[rows, pl.ds(self.offset, self.width)]

    def b_copy(self, a):
        return remote(self.block(a, 1 - self.p.b), self.peer.at[a], self.b_sem.at[0, a], self.b_sem.at[1, a], self.p.across())

    def start(self, n):
        self.b_copy(self.goal(n)).start()

    def cut(self, ref):
        return ref if self.width == ref.shape[1] else ref.at[:, pl.ds(0, self.width)]

    def load(self, pool, which, slot, source):
        return pltpu.make_async_copy(source, self.cut(pool.slot(which, slot)), pool.sems.at[which, slot])

    def prepare(self, pool, which, n):
        d = self.goal(n)
        self.b_copy(d).wait_recv()
        self.load(pool, which, 0, self.block(d, self.p.b)).start()
        self.load(pool, which, 1, self.peer.at[d]).start()

    def loaded(self, pool, which, n):
        d = self.goal(n)
        self.load(pool, which, 0, self.block(d, self.p.b)).wait()
        self.load(pool, which, 1, self.peer.at[d]).wait()

    def strips(self, do):
        rows = 2 * self.unit
        step = max(r for r in (16, 32, 64, 128) if rows % r == 0 and (r == 16 or r * self.width <= 64 * 1024))

        def one(i, carry):
            do(pl.ds(pl.multiple_of(i * step, step), step))
            return carry

        lax.fori_loop(0, rows // step, one, 0)

    def bring(self, pool, which, slot, place):
        remote(self.line.at[place], self.line.at[place], self.l_sem.at[0, 0], self.l_sem.at[1, place], self.p.across()).wait_recv()
        self.load(pool, which, slot, self.line.at[place]).start()

    def send(self, pool, out, n):
        p = self.p
        d = self.goal(n)
        up = d > p.a
        to = jnp.clip(p.a + jnp.where(up, 1, -1), 0, p.line - 1)
        slot = jnp.where(jnp.logical_and(jnp.logical_not(up), d == p.a - 1), p.line, d)
        return remote(
            self.cut(pool.sends.at[out]), self.line.at[slot], self.l_sem.at[0, n], self.l_sem.at[1, slot], (p.at(to, p.b, p.x), p.c)
        )

    def hop(self, pool, which, n, out):
        p = self.p
        d = self.goal(n)
        behind = jnp.logical_or(jnp.logical_and(d > p.a, p.has_down()), jnp.logical_and(d < p.a, p.has_up()))
        pl.when(behind)(lambda: self.bring(pool, which, 2, d))
        self.loaded(pool, which, n)
        a, b, c = (self.cut(pool.slot(which, i)) for i in range(3))
        to = self.cut(pool.sends.at[out])

        def with_line():
            self.load(pool, which, 2, self.line.at[d]).wait()

            def do(rows):
                to[rows] = bf(a[rows].astype(F32) + b[rows].astype(F32) + c[rows].astype(F32))

            self.strips(do)

        def without():
            def do(rows):
                to[rows] = bf(a[rows].astype(F32) + b[rows].astype(F32))

            self.strips(do)

        pl.when(behind)(with_line)
        pl.when(jnp.logical_not(behind))(without)
        self.send(pool, out, n).start()

    def last(self, pool, which):
        p = self.p
        n = p.line - 1
        pl.when(p.has_down())(lambda: self.bring(pool, which, 2, p.a))
        pl.when(p.has_up())(lambda: self.bring(pool, which, 3, p.line))
        self.loaded(pool, which, n)
        a, b, c, d = (self.cut(pool.slot(which, i)) for i in range(4))
        to = self.total = self.cut(pool.totals)

        def first(rows):
            to[rows] = a[rows].astype(F32) + b[rows].astype(F32)

        self.strips(first)

        def more(slot, place, ref):
            def go():
                self.load(pool, which, slot, self.line.at[place]).wait()

                def do(rows):
                    to[rows] = to[rows] + ref[rows].astype(F32)

                self.strips(do)

            return go

        pl.when(p.has_down())(more(2, p.a, c))
        pl.when(p.has_up())(more(3, p.line, d))
        self.x_copy().start()
        if not self.whole:
            self.out_copy().start()

    def half(self, x):
        return self.total.at[pl.ds(x * self.unit, self.unit)]

    def place(self):
        return self.out.at[:, pl.ds(self.p.x * self.width, self.width)]

    def x_copy(self):
        p = self.p
        where = self.out.at[1] if self.whole else self.place()
        return remote(self.half(1 - p.x), where, self.x_sem.at[0], self.x_sem.at[1], p.partner())

    def out_copy(self):
        return pltpu.make_async_copy(self.half(self.p.x), self.place(), self.x_sem.at[2])

    def sent(self):
        self.x_copy().wait_send()
        if not self.whole:
            self.out_copy().wait()

    def finish(self):
        p = self.p
        self.x_copy().wait_recv()
        if self.whole:
            self.out[0] = self.out[1] + self.half(p.x)[...]
        for n in range(p.line):
            self.b_copy(self.goal(n)).wait_send()


def scatter_sems(line):
    return [pltpu.SemaphoreType.DMA((2, line)), pltpu.SemaphoreType.DMA((2, line + 1)), pltpu.SemaphoreType.DMA((3,))]


def scatter_ops(work, pool):
    lines = work[0].p.line
    jobs = [(k * (lines - 1) + n, k, n) for k in range(len(work)) for n in range(lines - 1)]
    jobs += [((k + 1) * (lines - 1) - 0.5 + LAG, k, lines - 1) for k in range(len(work))]
    jobs = [(k, n) for _, k, n in sorted(jobs)]
    sends, totals = [], []

    def begin():
        for k, n in jobs[:AHEAD]:
            work[k].start(n)


    def job(i):
        k, n = jobs[i]

        def step():
            work[k].prepare(pool, i % 2, n)
            if i + AHEAD < len(jobs):
                work[jobs[i + AHEAD][0]].start(jobs[i + AHEAD][1])
            if n < lines - 1:
                out = len(sends) % POOL_SENDS
                if len(sends) >= POOL_SENDS:
                    ok, on, oo = sends[-POOL_SENDS]
                    work[ok].send(pool, oo, on).wait_send()
                work[k].hop(pool, i % 2, n, out)
                sends.append((k, n, out))
            else:
                if totals:
                    work[totals[-1]].sent()
                work[k].last(pool, i % 2)
                totals.append(k)

        return step

    steps = [begin] + [job(i) for i in range(len(jobs))]

    def finish():
        for ok, on, oo in sends[-POOL_SENDS:]:
            work[ok].send(pool, oo, on).wait_send()
        work[totals[-1]].sent()
        for chunk in work:
            chunk.finish()

    steps.append(finish)
    return steps

BACK_STEPS = (0, 1, 1, 0, 1, 1, 0, 2, 3, 2, 0, 1)


def backward_kernel(size, plan, levels, *refs):
    p = Place(size)
    (grad_out_all, gates_all, attended, grad_part), refs = take(refs, 4)
    (residual, gain2, out_w, qkv, decay, keep, gain, probs, scores, weights, states, decs,
     end_dec, paths, later, masks), refs = take(refs, 16)
    grads = max(i for i, _, _, _, _ in plan) + 1
    grad_refs, refs = take(refs, grads)
    (residual_grad, low, second_part, gate_term, gain_part, term, decay_term), refs = take(refs, 7)
    outs, refs = take(refs, len(plan))
    spaces, refs = take(refs, 2 * len(plan))
    (grad_out, gates, own_part, own_sem, att_grad, dprobs, dscores, units, adjoints, total), refs = take(refs, 10)
    (ending, *prefix_refs), refs = take(refs, 8)
    fold_refs, refs = take(refs, 5)
    share_sems, refs = take(refs, 2)
    pool_refs, refs = take(refs, 5)
    count = paths.shape[1]
    head = gate_term.shape[1]
    seqs = grad_out_all.shape[0]
    own = [
        pltpu.make_async_copy(grad_out_all.at[p.c], grad_out, own_sem.at[0]),
        pltpu.make_async_copy(gates_all.at[:, pl.ds(0, head)], gates, own_sem.at[1]),
        pltpu.make_async_copy(attended, att_grad, own_sem.at[2]),
        pltpu.make_async_copy(grad_part.at[p.c], own_part, own_sem.at[3]),
    ]
    for copy in own:
        copy.start()
    greet(p, sibling=True)
    pool = Pool(pool_refs)
    work = []
    for n, (i, unit, offset, width, _) in enumerate(plan):
        work.append(
            Scatter(p, grad_refs[i], outs[n], spaces[2 * n], spaces[2 * n + 1], unit, offset, width, refs[3 * n : 3 * n + 3])
        )
    weave = Weave(scatter_ops(work, pool))
    fold = Fold(p, grad_part, *fold_refs[:3], fold_refs[3:], own_part)
    share = Share(p, low, share_sems)
    fold.start()
    weave.run(1 + BACK_STEPS[0])
    own[3].wait()
    for r in range(STRIPS):
        fold.cross(r)
    weave.run(BACK_STEPS[1])
    own[0].wait()
    gains = jnp.zeros((1, grad_part.shape[3]), F32)
    for r in range(STRIPS):
        down, more = norm_back(fold.total(r), residual[fold.strip(r)], gain2[...])
        value = grad_out[fold.strip(r)].astype(F32) + down
        gains += more
        residual_grad[fold.strip(r)] = value
        share.put(r, bf(value))
        if r == 1:
            weave.run(BACK_STEPS[2])
    second_part[...] = gains
    weave.run(BACK_STEPS[3])
    diag = on_diagonal(count)
    gain_part[...] = jnp.zeros_like(gain_part)

    def place(i):
        b = jnp.where(lax.rem(i, 2) == 0, p.c, 1 - p.c)
        x = jnp.where(i < 2, p.x, 1 - p.x)
        return b, x

    def first(i, nothing):
        b, j = place(i)
        rows = pl.ds(pl.multiple_of((b * 2 + j) * count, count), count)
        grad = mm(low[b, j], out_w[...], NN)
        gate = gates[rows, :]
        value = att_grad[rows, :]
        scale = lax.rsqrt(jnp.mean(value * value, axis=1, keepdims=True) + EPS)
        normed = value * scale
        weighted = grad * silu(gate)
        gate_term[rows, :] = bf(grad * normed * gain[...] * silu_slope(gate))
        gain_part[...] += jnp.sum(weighted * normed, axis=0, keepdims=True)
        c = weighted * gain[...]
        agrad = scale * c - value * (scale * scale * scale) * jnp.mean(c * value, axis=1, keepdims=True)
        att_grad[rows, :] = agrad
        here = keep[rows, :]
        ratios, (growth,) = powers_of(paths[: (levels + 1) * count, :], count, levels, decay[rows, :])
        ahalf = halves(agrad)
        values = qkv[rows, 2 * head :]
        pair = mm(ahalf[0], values, NT) + mm(ahalf[1], values, NT)
        state = states[3 * b + j]
        dprob = mix(pair, ratios, here, masks, jnp.sum(pair * diag, axis=1, keepdims=True))
        dprob += growth * dot3(ahalf, halves(state[:, head:]), NT)
        prob = probs[rows, :]
        dscore = prob * (dprob - jnp.sum(prob * dprob, axis=1, keepdims=True))
        query = halves(silu(qkv[rows, :head].astype(F32)) * head ** (-0.5))
        dprobs[rows, :] = dprob
        dscores[rows, :] = dscore
        unit_k = dot3(halves(growth * dscore), query, TN)
        unit_v = dot3(halves(growth * prob), ahalf, TN)
        units[b, j] = jnp.concatenate([unit_k, unit_v], axis=1)
        return nothing

    own[1].wait()
    own[2].wait()
    lax.fori_loop(0, 1, first, 0)
    weave.run(BACK_STEPS[4])
    for r in range(STRIPS):
        share.forward(r)
    share.wait_sibling(False)
    lax.fori_loop(1, 3, first, 0)
    weave.run(BACK_STEPS[5])
    share.wait_sibling(True)
    lax.fori_loop(3, 4, first, 0)
    weave.run(BACK_STEPS[6])
    for b in range(seqs):
        total[b] = spread(decs[b, 0], 2 * head) * units[b, 1] + units[b, 0]
    carry = Prefix(p, True, total, end_dec, ending, *prefix_refs[:4], prefix_refs[4:])
    carry.start()
    weave.run(BACK_STEPS[7])
    carry.run()
    for b in range(seqs):
        adjoints[b, 1] = ending[b]
        adjoints[b, 0] = spread(decs[b, 1], 2 * head) * ending[b] + units[b, 1]
    is_last = (lax.broadcasted_iota(jnp.int32, (count, 1), 0) == count - 1).astype(F32)

    def second(i, nothing):
        for k in range(4):
            pl.when(i == k)(functools.partial(weave.run, BACK_STEPS[8 + k]))
        b, j = place(i)
        rows = pl.ds(pl.multiple_of((b * 2 + j) * count, count), count)
        here = keep[rows, :]
        ratios, (growth, rest) = powers_of(paths[...], count, levels, decay[rows, :])
        qraw = qkv[rows, :head].astype(F32)
        kraw = qkv[rows, head : 2 * head].astype(F32)
        query = halves(silu(qraw) * head ** (-0.5))
        keys = halves(silu(kraw))
        values = qkv[rows, 2 * head :]
        agrad = halves(att_grad[rows, :])
        prob, dscore = probs[rows, :], dscores[rows, :]
        state = halves(states[3 * b + j][:, :head])
        adj = adjoints[b, j]
        ahalf = halves(adj)
        adj_k, adj_v = (ahalf[0][:, :head], ahalf[1][:, :head]), (ahalf[0][:, head:], ahalf[1][:, head:])
        dweights = halves(unmix(dscore, ratios, here, masks, diag))
        dquery = dot3(dweights, keys, NN) + dot3(halves(dscore * growth), state, NN)
        term[rows, :head] = bf(silu_slope(qraw) * dquery * head ** (-0.5))
        left = halves(rest * here)
        dkey = dot3(dweights, query, TN) + dot3(left, adj_k, NN)
        term[rows, head : 2 * head] = bf(silu_slope(kraw) * dkey)
        dvalue = dot3(halves(weights[rows, :]), agrad, TN) + dot3(left, adj_v, NN)
        term[rows, 2 * head :] = bf(dvalue)
        pair_k = dot3(query, keys, NT)
        pair_v = mm(agrad[0], values, NT) + mm(agrad[1], values, NT)
        dkeep = jnp.sum(pair_k * diag, axis=1, keepdims=True) * dscore
        dkeep += jnp.sum(pair_v * diag, axis=1, keepdims=True) * prob
        dkeep += rest * (dot3(keys, adj_k, NT) + mm(values, adj_v[0], NT) + mm(values, adj_v[1], NT))
        for l, ratio in enumerate(ratios):
            mask = masks[l].astype(F32)
            more = dot3(halves(pair_k * mask), halves(dscore * ratio), TN)
            more += dot3(halves(pair_v * mask), halves(prob * ratio), TN)
            dkeep += ratio * more
        dsum = dscore * scores[rows, :] + prob * dprobs[rows, :] - here * dkeep
        at_end = jnp.sum(adj * states[3 * b + j + 1], axis=1, keepdims=True)
        at_end = jnp.sum(at_end * on_diagonal(adj.shape[0]), axis=0, keepdims=True)
        dsum += is_last * at_end
        decay_term[rows, :] = exact_sums(later[...], dsum) - (1.0 - here) * dkeep
        return nothing

    lax.fori_loop(0, 4, second, 0)
    weave.rest()
    share.finish(False)
    fold.finish()
    carry.finish()


def backward(size, number, slot, plan, hbm_ins, vmem_ins, grads):
    seqs, block, width = hbm_ins[0].shape
    h, m, n, rows = slot.head, slot.slots, slot.chunks, slot.seqs * slot.rows
    line = size // 4
    shape = jax.ShapeDtypeStruct
    outs = [
        shape((block, width), F32), shape((seqs, 2, block, width), BF16), shape((1, width), F32), shape((rows, h), BF16),
        shape((1, h), F32), shape((rows, 3 * h), BF16), shape((rows, m), F32),
    ]
    results, spaces, sems = [], [], []
    for i, unit, offset, columns, whole in plan:
        results.append(shape((2, unit, columns) if whole else (unit, 2 * columns), F32))
        spaces += [shape((line, 2 * unit, columns), BF16), shape((line + 1, 2 * unit, columns), BF16)]
        sems += scatter_sems(line)
    widest = max(entry[3] for entry in plan)
    scratch = [
        pltpu.VMEM((block, width), BF16), pltpu.VMEM((rows, h), F32),
        pltpu.VMEM((2, block, width), BF16), pltpu.SemaphoreType.DMA((4,)),
        pltpu.VMEM((rows, h), F32), pltpu.VMEM((rows, m), F32), pltpu.VMEM((rows, m), F32), pltpu.VMEM((seqs, n, m, 2 * h), F32),
        pltpu.VMEM((seqs, n, m, 2 * h), F32), pltpu.VMEM((seqs, m, 2 * h), F32),
    ]
    scratch += prefix_scratch(seqs, m, 2 * h) + fold_scratch(block, width) + SHARE_SEMS
    scratch += pool_scratch(2 * plan[0][1], widest) + sems
    later = slot.paths[-2 * slot.chunk : -slot.chunk].T
    result = pl.pallas_call(
        functools.partial(backward_kernel, size, plan, slot.levels),
        out_shape=outs + results + spaces,
        in_specs=[ANY] * 4 + [VM] * 16 + [ANY] * len(grads),
        out_specs=[VM] * 7 + [ANY] * (len(results) + len(spaces)),
        scratch_shapes=scratch,
        compiler_params=remote_params(number, 62),
        name="attend_backward",
    )(*hbm_ins, *vmem_ins, slot.paths, later, slot.masks, *grads)
    return result[: 7 + len(results)]


def products(p, part, fold, terms, i):
    count, width = part.shape[2], part.shape[3]
    stripe = min(512, width)
    b, x = blocks_in_order(p, part.shape[0])(i)
    rows = pl.ds(pl.multiple_of((b * 2 + x) * count, count), count)

    def one(t, nothing):
        columns = pl.ds(pl.multiple_of(t * stripe, stripe), stripe)
        value = None
        for left, right in terms:
            more = mm(left[rows, :], right[columns, :], NT)
            value = more if value is None else value + more
        part[b, x, :, columns] = bf(value)
        return nothing

    lax.fori_loop(0, width // stripe, one, 0)
    if i < 2:
        fold.sib_all(i == 0)


LAST_STEPS = (0, 1, 1, 1, 1, 1, 1, 2, 1)


def last_kernel(size, plan, *refs):
    p = Place(size)
    (qkv_full, gate_full, down_full), refs = take(refs, 3)
    (qkv_term, gates_term, activated, tokens, residual, residual_grad, gain, pack), refs = take(refs, 8)
    grads = max(i for i, _, _, _, _ in plan) + 1
    grad_refs, refs = take(refs, grads)
    (input_grad, output, sums), refs = take(refs, 3)
    outs, refs = take(refs, len(plan))
    spaces, refs = take(refs, 2 * len(plan))
    (part, ff_part, qkv_w, gate_w, down_w, load_sem), refs = take(refs, 6)
    fold_refs, refs = take(refs, 5)
    ff_refs, refs = take(refs, 5)
    (out_sem, mine, came, s_sem), refs = take(refs, 4)
    pool_refs, refs = take(refs, 5)
    loads = [
        pltpu.make_async_copy(source, to, load_sem.at[n])
        for n, (source, to) in enumerate(((qkv_full, qkv_w), (gate_full, gate_w), (down_full, down_w)))
    ]
    for load in loads:
        load.start()
    greet_all(p)
    pool = Pool(pool_refs)
    work = []
    for n, (i, unit, offset, width, _) in enumerate(plan):
        work.append(
            Scatter(p, grad_refs[i], outs[n], spaces[2 * n], spaces[2 * n + 1], unit, offset, width, refs[3 * n : 3 * n + 3])
        )
    weave = Weave(scatter_ops(work, pool))
    fold = Fold(p, part, *fold_refs[:3], fold_refs[3:])
    ff = Fold(p, ff_part, *ff_refs[:3], ff_refs[3:])
    weave.run(1 + LAST_STEPS[0])
    loads[0].wait()
    loads[1].wait()
    terms = [(qkv_term, qkv_w), (gates_term, gate_w)]
    for i in range(3):
        products(p, part, fold, terms, i)
    for r in range(STRIPS):
        fold.cross(r)
    weave.run(LAST_STEPS[1])
    products(p, part, fold, terms, 3)
    loads[2].wait()
    products(p, ff_part, ff, [(activated, down_w)], 0)
    weave.run(LAST_STEPS[2])
    products(p, ff_part, ff, [(activated, down_w)], 1)
    products(p, ff_part, ff, [(activated, down_w)], 2)
    weave.run(LAST_STEPS[3])
    for r in range(STRIPS):
        ff.cross(r)
    products(p, ff_part, ff, [(activated, down_w)], 3)
    weave.run(LAST_STEPS[4])
    gains = jnp.zeros((1, part.shape[3]), F32)

    def out_copy(ref, k, r):
        block = ref.at[p.c, fold.strip(r)]
        return remote(block, block, out_sem.at[0, k * STRIPS + r], out_sem.at[1, k * STRIPS + r], p.sibling())

    for r in range(STRIPS):
        down, more = norm_back(fold.total(r), tokens[p.c, fold.strip(r)].astype(F32), gain[...])
        gains += more
        input_grad[p.c, fold.strip(r)] = residual_grad[fold.strip(r)] + down
        out_copy(input_grad, 1, r).start()
        if r % 2 == 1:
            weave.run(LAST_STEPS[5 + r // 2])
    unit = plan[0][1]
    mine[...] = pack[...]
    for s in range(size):
        mine[s, 0:1, pl.ds(0, unit)] = gains[:, s * unit : (s + 1) * unit]
    smalls = Smalls(p, mine, sums, came, s_sem)
    smalls.start()
    weave.run(LAST_STEPS[7])
    for r in range(STRIPS):
        output[p.c, fold.strip(r)] = bf(residual[fold.strip(r)] + ff.total(r))
        out_copy(output, 0, r).start()
        if r % 2 == 1:
            weave.run(LAST_STEPS[8])
    weave.rest()
    smalls.finish()
    for r in range(STRIPS):
        out_copy(output, 0, r).wait()
        out_copy(input_grad, 1, r).wait()
    ff.finish()
    fold.finish()


def last(size, number, plan, hbm_ins, vmem_ins, grads):
    qkv_term, _, _, tokens = vmem_ins[:4]
    seqs, block, width = tokens.shape
    pack = vmem_ins[-1]
    line = size // 4
    shape = jax.ShapeDtypeStruct
    outs = [shape((seqs, block, width), F32), shape((seqs, block, width), BF16), shape(pack.shape[1:], F32)]
    results, specs, spaces, sems = [], [], [], []
    for i, unit, offset, columns, whole in plan:
        results.append(shape((2, unit, columns) if whole else (unit, 2 * columns), F32))
        specs.append(VM if whole else ANY)
        spaces += [shape((line, 2 * unit, columns), BF16), shape((line + 1, 2 * unit, columns), BF16)]
        sems += scatter_sems(line)
    widest = max(entry[3] for entry in plan)
    scratch = [pltpu.VMEM((seqs, 2, block, width), BF16)] * 2 + [pltpu.VMEM(w.shape, BF16) for w in hbm_ins]
    scratch += [pltpu.SemaphoreType.DMA((3,))] + fold_scratch(block, width) * 2 + [
        pltpu.SemaphoreType.DMA((2, 2 * STRIPS)), pltpu.VMEM(pack.shape, F32), pltpu.VMEM((2 * size,) + pack.shape[1:], F32),
        pltpu.SemaphoreType.DMA((2, 2 * size)),
    ]
    scratch += pool_scratch(2 * plan[0][1], widest) + sems
    result = pl.pallas_call(
        functools.partial(last_kernel, size, plan),
        out_shape=outs + results + spaces,
        in_specs=[ANY] * 3 + [VM] * 8 + [ANY] * len(grads),
        out_specs=[VM] * 3 + specs + [ANY] * len(spaces),
        scratch_shapes=scratch,
        compiler_params=remote_params(number, 62),
        name="last",
    )(*hbm_ins, *vmem_ins, *grads)
    return result[: 3 + len(results)]

def greet_all(place):
    barrier = pltpu.get_barrier_semaphore()

    def one(i, carry):
        signal(barrier, (lax.rem(place.s + i // 2, place.size), lax.rem(place.c + lax.rem(i, 2), 2)))
        return carry

    lax.fori_loop(1, 2 * place.size, one, 0)
    pl.semaphore_wait(barrier, 2 * place.size - 1)


class Smalls:
    def __init__(self, place, pack, out, came, sems):
        self.p, self.pack, self.out, self.came, self.sems = place, pack, out, came, sems

    def copy(self, i):
        p = self.p
        s = lax.rem(p.s + i // 2, p.size)
        return remote(
            self.pack.at[s], self.came.at[i], self.sems.at[0, i], self.sems.at[1, i], (s, lax.rem(p.c + lax.rem(i, 2), 2))
        )

    def start(self):
        lax.fori_loop(1, 2 * self.p.size, lambda i, c: (self.copy(i).start(), c)[1], 0)

    def finish(self):
        def one(i, total):
            self.copy(i).wait()
            return total + self.came[i]

        self.out[...] = lax.fori_loop(1, 2 * self.p.size, one, self.pack[self.p.s])


class Swap:
    def __init__(self, place, own, both, sems):
        p = self.p = place
        self.keep = pltpu.make_async_copy(own, both.at[:, p.x], sems.at[0])
        self.cross = remote(own.at[p.c], both.at[p.c, p.x], sems.at[1], sems.at[2], p.partner())
        came = both.at[p.c, 1 - p.x]
        self.hand = remote(came, came, sems.at[3], sems.at[4], p.sibling())

    def start(self):
        self.cross.start()
        self.keep.start()

    def forward(self):
        self.cross.wait_recv()
        self.hand.start()

    def finish(self):
        self.keep.wait()
        self.cross.wait_send()
        self.hand.wait()


def gather_kernel(size, plan, swaps, *refs):
    p = Place(size)
    shards = sum(len(columns) for _, _, columns in plan)
    fulls = max(i for i, _, _ in plan) + 1
    ins, refs = take(refs, shards + swaps)
    outs, refs = take(refs, fulls + swaps)
    greet(p, sibling=True)
    work = gathers_of(p, plan, ins, outs, refs)
    moves = [Swap(p, ins[shards + n], outs[fulls + n], refs[4 * len(plan) + n]) for n in range(swaps)]
    for gathered in work:
        gathered.start_x()
    weave = Weave(gather_ops(work, 1))
    weave.run(4)
    for move in moves:
        move.start()
    weave.run(len(weave.steps) - len(work) - 4)
    for move in moves:
        move.forward()
    weave.rest()
    for move in moves:
        move.finish()


def gather(size, number, plan, shards, fulls, tokens):
    line = size // 4
    scratch = []
    for _, _, columns in plan:
        scratch += gather_sems(line, len(columns))
    shapes = [jax.ShapeDtypeStruct(shape, BF16) for shape in fulls]
    for array in tokens:
        shapes.append(jax.ShapeDtypeStruct((array.shape[0], 2) + array.shape[1:], BF16))
        scratch.append(pltpu.SemaphoreType.DMA((5,)))
    return pl.pallas_call(
        functools.partial(gather_kernel, size, plan, len(tokens)),
        out_shape=shapes,
        in_specs=[ANY] * (len(shards) + len(tokens)),
        out_specs=[ANY] * len(shapes),
        scratch_shapes=scratch,
        compiler_params=remote_params(number, 60),
        name="gather",
    )(*shards, *tokens)


def dot(left, right, dims, dtype=F32):
    return lax.dot_general(left, right, dims, preferred_element_type=F32).astype(dtype)


def lanes(row):
    return jnp.pad(row.reshape(-1), (0, 128 - row.size))


def shards(
    tokens, grad_out, query_weight, key_weight, value_weight, forget_weight, forget_bias, outgate_weight, output_weight,
    slot_gain, first_gain, second_gain, gate_weight, up_weight, down_weight,
):
    size = lax.axis_size("seq")
    x = lax.rem(lax.axis_index("seq"), 2)
    c = lax.axis_index("head")
    seqs, block, width = tokens.shape
    heads_here, slot_part = forget_bias.shape
    slots = slot_part * size
    head = slot_gain.shape[0] * size
    unit = first_gain.shape[0]
    hidden = gate_weight.shape[1] // 2
    rows = seqs * 2 * block
    pack = jnp.stack([lanes(first_gain), lanes(second_gain), lanes(slot_gain), lanes(forget_bias)] + [jnp.zeros(128, BF16)] * 12)
    plan = [
        (0, unit, [(0, head), (head, head), (2 * head, head)]), (1, unit, [(0, head), (head, 2 * slots)]), (2, unit, [(0, head)]),
        (3, 16, [(0, 128)]),
    ]
    fulls = [(width, 3 * head), (width, head + 2 * slots), (width, head), (16 * size, 128)]
    qkv_full, gate_full, out_full, small_full, tok = gather(
        size, 0, plan,
        (query_weight, key_weight, value_weight, outgate_weight, forget_weight, output_weight.T, pack),
        fulls, (tokens,),
    )
    small = small_full.reshape(size, 16, 128).astype(F32)
    first_full = small[:, 0, :unit].reshape(1, width)
    second_full = small[:, 1, :unit].reshape(1, width)
    slot_full = small[:, 2, : head // size].reshape(1, head)
    bias_full = small[:, 3, : heads_here * slot_part].reshape(size, heads_here, slot_part)
    bias_full = jnp.moveaxis(bias_full, 1, 0).reshape(heads_here, slots)

    def own_head(array, axis):
        return jnp.where(x == 0, *jnp.split(array, 2, axis=axis))

    inputs = tok.reshape(rows, width).astype(F32)
    normed_one = (inputs * inverse_rms(inputs) * first_full).astype(BF16)
    qkv = dot(normed_one, qkv_full, NN, BF16)
    gates = dot(normed_one, gate_full, NN)
    logit = own_head(gates[:, head:], 1) + own_head(bias_full, 0)
    decay = -jax.nn.softplus(-logit) / TAU
    keep = -jnp.expm1(decay)
    slot = Slots(seqs, 2 * block, head, slots, block)
    ff_plan = [(0, unit, [(0, hidden)]), (0, unit, [(hidden, hidden)]), (1, unit, [(0, hidden)])]
    (gated, attended, probs, scores, weights, states, decs, end_decs, residual, normed_two, gout, ff_full, down_full) = forward(
        size, 1, slot, ff_plan, [(width, 2 * hidden), (width, hidden)], qkv, gates, decay, keep, slot_full, out_full, tokens,
        second_full, grad_out, (gate_weight, up_weight, down_weight.T),
    )
    shape = (seqs, 2, block, width)
    normed_two = normed_two.reshape(rows, width)
    ff = dot(normed_two, ff_full, NN)
    ff_gate, ff_up = ff[:, :hidden], ff[:, hidden:]
    sig = jax.nn.sigmoid(ff_gate)
    activated = (ff_gate * sig * ff_up).astype(BF16)
    gout = gout.reshape(rows, width)
    act_grad = dot(gout, down_full, NN)
    ff_term = jnp.concatenate(
        [act_grad * ff_up * (sig + ff_gate * sig * (1.0 - sig)), act_grad * ff_gate * sig], axis=1
    ).astype(BF16)
    down_grad = dot(gout, activated, TN, BF16)
    ff_grad = dot(normed_two, ff_term, TN, BF16)
    normed_two_grad = dot(ff_term, ff_full, NT, BF16).reshape(shape)
    ff_plan = [(0, unit, 0, hidden, False), (0, unit, hidden, hidden, False), (1, unit, 0, hidden, False)]
    residual_grad, low, second_part, gate_term, slot_part_grad, qkv_term, decay_term, gate_grad, up_grad, down_grad = backward(
        size, 2, slot, ff_plan,
        (grad_out, gates, attended, normed_two_grad),
        (residual, second_full, out_full, qkv, decay, keep, slot_full, probs, scores, weights, states, decs,
         end_decs),
        (ff_grad, down_grad),
    )
    low = low.reshape(rows, width)
    out_grad = dot(low, gated, TN, BF16)
    forget_term = (decay_term * jax.nn.sigmoid(-logit) / TAU).astype(BF16)
    none = jnp.zeros_like(forget_term)
    gates_term = jnp.concatenate(
        [gate_term, jnp.where(x == 0, forget_term, none), jnp.where(x == 0, none, forget_term)], axis=1
    )
    qkv_grad = dot(normed_one, qkv_term, TN, BF16)
    gates_grad = dot(normed_one, gates_term, TN, BF16)
    bias_part = jnp.sum(forget_term.astype(F32), axis=0)
    which = jnp.arange(2 * heads_here) == heads_here * c + x
    bias_part = jnp.where(which[:, None], bias_part[None, :], 0.0).reshape(2 * heads_here, size, slot_part)

    def rows_of(array):
        array = array.reshape(size, -1)
        return jnp.pad(array, ((0, 0), (0, 128 - array.shape[1])))

    zero = jnp.zeros((size, 128), F32)
    packed = jnp.stack(
        [zero, rows_of(second_part), rows_of(slot_part_grad), rows_of(jnp.moveaxis(bias_part, 1, 0))] + [zero] * 4, axis=1
    )
    plan = [
        (0, unit, 0, head, False), (1, unit, 0, head, False), (1, unit, head, head, False), (1, unit, 2 * head, head, False),
        (2, unit, 0, head, False), (2, unit, head, 2 * slots, True),
    ]
    input_grad, output, sums, output_grad, query_grad, key_grad, value_grad, outgate_grad, forget_grad = last(
        size, 3, plan, (qkv_full, gate_full, down_full),
        (qkv_term, gates_term, activated, tokens, residual, residual_grad, first_full, packed),
        (out_grad, qkv_grad, gates_grad),
    )
    bias_grad = sums[3, : 2 * heads_here * slot_part].reshape(2, heads_here, slot_part)
    bias_grad = jnp.where(c == 0, bias_grad[0], bias_grad[1])
    return (
        output, input_grad, query_grad, key_grad, value_grad, forget_grad[0], bias_grad, outgate_grad, output_grad.T,
        sums[2, : head // size], sums[0, :unit], sums[1, :unit], gate_grad, up_grad, down_grad.T,
    )


def solution(mesh):
    row, column, vector, token = P("seq", "head"), P("head", "seq"), P("seq"), P(None, "seq", None)
    return jax.shard_map(
        shards,
        mesh=mesh,
        in_specs=(token, token, row, row, row, row, column, row, column, vector, vector, vector, row, row, column),
        out_specs=(token, token, row, row, row, row, column, row, column, vector, vector, vector, row, row, column),
        check_vma=False,
    )
```

```python
import functools

import jax
import jax.numpy as jnp
import numpy as np
from jax import lax
from jax.experimental import pallas as pl
from jax.experimental.pallas import tpu as pltpu
from jax.sharding import PartitionSpec as P

F32, BF16 = jnp.float32, jnp.bfloat16
MESH = pl.DeviceIdType.MESH
HBM = pltpu.HBM
EPS = 1e-06
TAU = 8.0


CHUNK = 256
NT = (((1,), (1,)), ((), ()))
NN = (((1,), (0,)), ((), ()))
TN = (((0,), (0,)), ((), ()))


def decay_tables(count):
    at = np.arange(count)
    paths, masks = [], []
    half = count // 2
    while half >= 1:
        block, second = at // (2 * half), (at // half) % 2 == 1
        edge = block * 2 * half + half - 1
        r, t = at[None, :], at[:, None]
        fore = second[:, None] & (r > edge[:, None]) & (r <= t)
        back = ~second[:, None] & (r > t) & (r <= edge[:, None])
        paths.append(fore | back)
        masks.append((block[:, None] == block[None, :]) & second[:, None] & ~second[None, :])
        half //= 2
    paths.append(at[None, :] <= at[:, None])
    paths.append(at[None, :] > at[:, None])
    return np.concatenate(paths, 0), np.stack(masks)


def bf(x):
    return x.astype(BF16)


def halves(x):
    hi = bf(x)
    return hi, bf(x - hi.astype(F32))


def mm(a, b, dims):
    return lax.dot_general(a, b, dims, preferred_element_type=F32)


def dot3(a, b, dims):
    return mm(a[0], b[0], dims) + (mm(a[0], b[1], dims) + mm(a[1], b[0], dims))


def exact_sums(table, x):
    hi, mid = halves(x)
    low = bf(x - hi.astype(F32) - mid.astype(F32))
    n = x.shape[1]
    both = mm(table, jnp.concatenate([hi, mid, low, jnp.zeros_like(low)], axis=1), NN)
    return both[:, :n] + (both[:, n : 2 * n] + both[:, 2 * n : 3 * n])


def silu(v):
    return v / (1.0 + jnp.exp(-v))


def sigmoid(v):
    return 1.0 / (1.0 + jnp.exp(-v))


def silu_slope(v):
    s = sigmoid(v)
    return s + v * s * (1.0 - s)


def columns_total(x):
    ones = jnp.ones((x.shape[0], 128), BF16)
    hi, mid = halves(x)
    low = bf(x - hi.astype(F32) - mid.astype(F32))
    return mm(hi, ones, TN) + (mm(mid, ones, TN) + mm(low, ones, TN))


def spread(column, width):
    return jnp.concatenate([column] * (width // 128), axis=1)


def mix(pair, ratios, keep, masks_ref, own):
    out = own * keep
    for l, ratio in enumerate(ratios):
        left = pair * masks_ref[l].astype(F32)
        out += ratio * dot3(halves(left), halves(ratio * keep), NN)
    return out


def unmix(probs, ratios, keep, masks_ref, diag):
    out = diag * jnp.sum(probs * keep, axis=1, keepdims=True)
    for l, ratio in enumerate(ratios):
        part = dot3(halves(probs * ratio), halves(ratio * keep), NT)
        out += masks_ref[l].astype(F32) * part
    return out


def on_diagonal(count):
    return (
        lax.broadcasted_iota(jnp.int32, (count, count), 0) == lax.broadcasted_iota(jnp.int32, (count, count), 1)
    ).astype(F32)


class Slots:
    def __init__(self, seqs, rows, head, slots, chunk):
        self.seqs, self.rows, self.head, self.slots, self.chunk = seqs, rows, head, slots, chunk
        self.chunks = rows // chunk
        paths, masks = decay_tables(chunk)
        self.levels = masks.shape[0]
        self.paths = jnp.asarray(paths, BF16)
        self.masks = jnp.asarray(masks, BF16)

class Place:
    def __init__(self, size):
        self.size = size
        self.line = size // 4
        s = lax.axis_index("seq")
        self.c = lax.axis_index("head")
        self.s = s
        self.x = lax.rem(s, 2)
        self.b = lax.rem(s // 2, 2)
        self.a = s // 4

    def at(self, a, b, x):
        return (a * 2 + b) * 2 + x

    def partner(self):
        return (self.at(self.a, self.b, 1 - self.x), self.c)

    def across(self):
        return (self.at(self.a, 1 - self.b, self.x), self.c)

    def up(self):
        return (self.at(jnp.minimum(self.a + 1, self.line - 1), self.b, self.x), self.c)

    def down(self):
        return (self.at(jnp.maximum(self.a - 1, 0), self.b, self.x), self.c)

    def sibling(self):
        return (self.s, 1 - self.c)

    def has_up(self):
        return self.a < self.line - 1

    def has_down(self):
        return self.a > 0


def signal(sem, device):
    pl.semaphore_signal(sem, inc=1, device_id=device, device_id_type=MESH)


def greet(place, partner=True, across=True, line=True, sibling=False):
    barrier = pltpu.get_barrier_semaphore()
    count = jnp.int32(0)
    if partner:
        signal(barrier, place.partner())
        count = count + 1
    if sibling:
        signal(barrier, place.sibling())
        count = count + 1
    if across:
        signal(barrier, place.across())
        count = count + 1
    if line:
        pl.when(place.has_up())(lambda: signal(barrier, place.up()))
        pl.when(place.has_down())(lambda: signal(barrier, place.down()))
        count = count + place.has_up().astype(jnp.int32) + place.has_down().astype(jnp.int32)
    pl.semaphore_wait(barrier, count)


def remote(src, dst, send, recv, device):
    return pltpu.make_async_remote_copy(
        src_ref=src, dst_ref=dst, send_sem=send, recv_sem=recv, device_id=device, device_id_type=MESH
    )


class Gather:
    def __init__(self, place, full, unit, pieces, sems, late=False):
        self.pl, self.full, self.unit, self.pieces, self.late = place, full, unit, pieces, late
        self.offset = min(offset for _, offset, _ in pieces)
        self.width = sum(width for _, _, width in pieces)
        self.x_sem, self.b_sem, self.up_sem, self.down_sem = sems

    def part(self, start, count, offset=None, width=None):
        offset, width = (self.offset, self.width) if width is None else (offset, width)
        rows = pl.ds(start * self.unit, count * self.unit)
        if width == self.full.shape[1]:
            return self.full.at[rows]
        return self.full.at[rows, pl.ds(offset, width)]

    def mine(self, i, x):
        shard, _, width = self.pieces[i]
        if shard.shape[1] == width:
            return shard
        return shard.at[:, pl.ds(x * width, width)]

    def x_copy(self, i):
        p = self.pl
        _, offset, width = self.pieces[i]
        here = self.part(p.s, 1, offset, width)
        return remote(self.mine(i, 1 - p.x), here, self.x_sem.at[0, i], self.x_sem.at[1, i], p.partner())

    def own_copy(self, i):
        _, offset, width = self.pieces[i]
        return pltpu.make_async_copy(self.mine(i, self.pl.x), self.part(self.pl.s, 1, offset, width), self.x_sem.at[2, i])

    def block(self, a):
        p = self.pl
        if self.late:
            return self.part(4 * a, 4)
        return self.part(4 * a + 2 * p.b, 2)

    def b_copy(self, i, a):
        p = self.pl
        return remote(
            self.part(4 * a + 2 * p.b, 2), self.part(4 * a + 2 * p.b, 2),
            self.b_sem.at[0, i], self.b_sem.at[1, i], p.across(),
        )

    def line_copy(self, way, h):
        p = self.pl
        if way == "up":
            blk = self.block(jnp.maximum(p.a - (h - 1), 0))
            return remote(blk, blk, self.up_sem.at[0, h - 1], self.up_sem.at[1, h - 1], p.up())
        blk = self.block(jnp.minimum(p.a + (h - 1), p.line - 1))
        return remote(blk, blk, self.down_sem.at[0, h - 1], self.down_sem.at[1, h - 1], p.down())

    def sends(self, way, h):
        p = self.pl
        if way == "up":
            return jnp.logical_and(p.has_up(), p.a - (h - 1) >= 0)
        return jnp.logical_and(p.has_down(), p.a + (h - 1) <= p.line - 1)

    def gets(self, way, h):
        p = self.pl
        if way == "up":
            return p.a - h >= 0
        return p.a + h <= p.line - 1

    def got(self, way, h):
        p = self.pl
        if way == "up":
            return jnp.maximum(p.a - h, 0)
        return jnp.minimum(p.a + h, p.line - 1)

    def slot(self, way, h):
        return h if way == "up" else self.pl.line - 1 + h

    def start_x(self):
        for i in range(len(self.pieces)):
            self.x_copy(i).start()
            self.own_copy(i).start()

    def stage(self, h):
        p = self.pl
        if h == 0:
            for i in range(len(self.pieces)):
                self.own_copy(i).wait()
                self.x_copy(i).wait_recv()
            if self.late:
                self.b_copy(0, p.a).start()
            else:
                for way in ("up", "down"):
                    pl.when(self.sends(way, 1))(lambda way=way: self.line_copy(way, 1).start())
                self.b_copy(0, p.a).start()
            return
        if self.late:
            if h == 1:
                self.b_copy(0, p.a).wait_recv()
                for way in ("up", "down"):
                    pl.when(self.sends(way, 1))(lambda way=way: self.line_copy(way, 1).start())
                return
            h = h - 1
        for way in ("up", "down"):

            def go(way=way):
                self.line_copy(way, h).wait_recv()
                if not self.late:
                    self.b_copy(self.slot(way, h), self.got(way, h)).start()

            def on(way=way):
                self.line_copy(way, h + 1).start()

            pl.when(self.gets(way, h))(go)
            if h + 1 <= p.line - 1:
                pl.when(self.sends(way, h + 1))(on)

    def stages(self):
        return self.pl.line + (1 if self.late else 0)

    def finish(self):
        p = self.pl
        for i in range(len(self.pieces)):
            self.x_copy(i).wait_send()
        self.b_copy(0, p.a).wait_send()
        if not self.late:
            self.b_copy(0, p.a).wait_recv()
        for way in ("up", "down"):
            for h in range(1, p.line):
                pl.when(self.sends(way, h))(lambda way=way, h=h: self.line_copy(way, h).wait_send())
                if not self.late:

                    def both(way=way, h=h):
                        cp = self.b_copy(self.slot(way, h), self.got(way, h))
                        cp.wait_send()
                        cp.wait_recv()

                    pl.when(self.gets(way, h))(both)


def gather_sems(line, pieces):
    return [
        pltpu.SemaphoreType.DMA((3, pieces)),
        pltpu.SemaphoreType.DMA((2, 2 * line - 1)),
        pltpu.SemaphoreType.DMA((2, line - 1)),
        pltpu.SemaphoreType.DMA((2, line - 1)),
    ]


def gathers_of(place, plan, shards, fulls, sems):
    work, at = [], 0
    for n, (i, unit, columns) in enumerate(plan):
        pieces = [(shards[at + m], offset, width) for m, (offset, width) in enumerate(columns)]
        at += len(columns)
        work.append(Gather(place, fulls[i], unit, pieces, sems[4 * n : 4 * n + 4]))
    return work


def gather_ops(gathers, pace):
    order = sorted((k * pace + h, k, h) for k, g in enumerate(gathers) for h in range(g.stages()))
    steps = [functools.partial(gathers[k].stage, h) for _, k, h in order]
    return steps + [g.finish for g in gathers]

VM = pl.BlockSpec(memory_space=pltpu.VMEM)
ANY = pl.BlockSpec(memory_space=HBM)


def remote_params(number, mib=56):
    return pltpu.CompilerParams(collective_id=number, has_side_effects=True, vmem_limit_bytes=mib * 2**20)


STRIPS = 4


class Fold:
    def __init__(self, place, part, sib, sent, came, sems, own=None):
        self.p, self.part, self.sib, self.sent, self.came = place, part, sib, sent, came
        self.own = part.at[place.c] if own is None else own
        self.s_sem, self.x_sem = sems
        self.rows = part.shape[2] // STRIPS

    def strip(self, r):
        return pl.ds(r * self.rows, self.rows)

    def sib_copy(self, far, r):
        p = self.p
        x = 1 - p.x if far else p.x
        i = (0 if far else STRIPS) + r
        return remote(
            self.part.at[1 - p.c, x, self.strip(r)], self.sib.at[1 if far else 0, self.strip(r)],
            self.s_sem.at[0, i], self.s_sem.at[1, i], p.sibling(),
        )

    def x_copy(self, r):
        return remote(
            self.sent.at[self.strip(r)], self.came.at[self.strip(r)], self.x_sem.at[0, r], self.x_sem.at[1, r], self.p.partner()
        )

    def start(self):
        for r in range(STRIPS):
            self.sib_copy(True, r).start()
        for r in range(STRIPS):
            self.sib_copy(False, r).start()

    def sib_all(self, far):
        for r in range(STRIPS):
            self.sib_copy(far, r).start()

    def cross(self, r):
        p = self.p
        self.sib_copy(True, r).wait_recv()
        own = self.own[1 - p.x, self.strip(r)].astype(F32)
        self.sent[self.strip(r)] = bf(own + self.sib[1, self.strip(r)].astype(F32))
        self.x_copy(r).start()

    def total(self, r):
        p = self.p
        self.sib_copy(False, r).wait_recv()
        self.x_copy(r).wait_recv()
        own = self.own[p.x, self.strip(r)].astype(F32) + self.sib[0, self.strip(r)].astype(F32)
        return own + self.came[self.strip(r)].astype(F32)

    def finish(self):
        for r in range(STRIPS):
            self.sib_copy(True, r).wait_send()
            self.sib_copy(False, r).wait_send()
            self.x_copy(r).wait_send()


def fold_scratch(rows, width):
    return [
        pltpu.VMEM((2, rows, width), BF16), pltpu.VMEM((rows, width), BF16), pltpu.VMEM((rows, width), BF16),
        pltpu.SemaphoreType.DMA((2, 2 * STRIPS)), pltpu.SemaphoreType.DMA((2, STRIPS)),
    ]


class Share:
    def __init__(self, place, out, sems):
        self.p, self.out = place, out
        self.x_sem, self.s_sem = sems
        self.rows = out.shape[2] // STRIPS

    def strip(self, r):
        return pl.ds(r * self.rows, self.rows)

    def x_copy(self, r):
        p = self.p
        block = self.out.at[p.c, p.x, self.strip(r)]
        return remote(block, block, self.x_sem.at[0, r], self.x_sem.at[1, r], p.partner())

    def s_copy(self, far, r):
        p = self.p
        block = self.out.at[p.c, 1 - p.x if far else p.x, self.strip(r)]
        i = (0 if far else STRIPS) + r
        return remote(block, block, self.s_sem.at[0, i], self.s_sem.at[1, i], p.sibling())

    def put(self, r, value):
        self.out[self.p.c, self.p.x, self.strip(r)] = value
        self.x_copy(r).start()
        self.s_copy(False, r).start()

    def forward(self, r):
        self.x_copy(r).wait_recv()
        self.s_copy(True, r).start()

    def wait_sibling(self, far):
        for r in range(STRIPS):
            self.s_copy(far, r).wait_recv()

    def finish(self, receive=True):
        for r in range(STRIPS):
            self.x_copy(r).wait_send()
            for far in (False, True):
                self.s_copy(far, r).wait_send()
                if receive:
                    self.s_copy(far, r).wait_recv()


SHARE_SEMS = [pltpu.SemaphoreType.DMA((2, STRIPS)), pltpu.SemaphoreType.DMA((2, 2 * STRIPS))]


def inverse_rms(values):
    return lax.rsqrt(jnp.mean(values * values, axis=-1, keepdims=True) + EPS)


def norm_back(grad, values, gain):
    scale = inverse_rms(values)
    u = grad * gain
    down = scale * u - values * (scale * scale * scale) * jnp.mean(u * values, axis=-1, keepdims=True)
    return down, jnp.sum(grad * values * scale, axis=0, keepdims=True)


def ends_chunk(k, v, decay, keep, tail):
    weight = halves(jnp.exp(exact_sums(tail, decay)) * keep)
    unit_k = dot3(weight, halves(silu(k.astype(F32))), TN)
    unit_v = mm(weight[0], v, TN) + mm(weight[1], v, TN)
    return jnp.concatenate([unit_k, unit_v], axis=1), jnp.exp(columns_total(decay))


def powers_of(table, count, levels, decay):
    powers = jnp.exp(exact_sums(table, decay))
    return [powers[l * count : (l + 1) * count] for l in range(levels)], [
        powers[l * count : (l + 1) * count] for l in range(levels, table.shape[0] // count)
    ]


class Prefix:
    def __init__(self, place, back, own, dec, start, peer, peer_dec, line, out, sems):
        p = self.p = place
        self.own, self.dec, self.start_ref, self.peer, self.peer_dec = own, dec, start, peer, peer_dec
        self.line, self.out = line, out
        self.p_sem, self.d_sem, self.l_sem = sems
        seqs, slots, width = own.shape
        self.half = width // 2
        self.pieces = [(b, h) for b in range(seqs) for h in range(2)]
        if back:
            self.has_prev, self.has_next, self.after = p.has_up(), p.has_down(), p.down()
        else:
            self.has_prev, self.has_next, self.after = p.has_down(), p.has_up(), p.up()
        self.first = ((p.b == 1) if back else (p.b == 0)).astype(F32)

    def cut(self, ref, i):
        b, h = self.pieces[i]
        return ref.at[b, :, pl.ds(h * self.half, self.half)]

    def peer_copy(self, i):
        return remote(self.cut(self.own, i), self.cut(self.peer, i), self.p_sem.at[0, i], self.p_sem.at[1, i], self.p.across())

    def line_copy(self, i):
        return remote(self.cut(self.out, i), self.cut(self.line, i), self.l_sem.at[0, i], self.l_sem.at[1, i], self.after)

    def dec_copy(self):
        return remote(self.dec, self.peer_dec, self.d_sem.at[0], self.d_sem.at[1], self.p.across())

    def start(self):
        self.dec_copy().start()
        for i in range(len(self.pieces)):
            self.peer_copy(i).start()

    def run(self):
        self.dec_copy().wait_recv()
        for i, (b, _) in enumerate(self.pieces):
            self.peer_copy(i).wait_recv()
            dec_own = spread(self.dec[b], self.half)
            dec_peer = spread(self.peer_dec[b], self.half)
            own, other = self.cut(self.own, i)[...], self.cut(self.peer, i)[...]
            first = self.first
            both = first * (dec_peer * own + other) + (1.0 - first) * (dec_own * other + own)
            here, result = self.cut(self.out, i), self.cut(self.start_ref, i)

            def go_on(i=i):
                self.line_copy(i).wait_recv()
                came = self.cut(self.line, i)[...]
                here[...] = dec_own * dec_peer * came + both
                result[...] = first * came + (1.0 - first) * (dec_peer * came + other)

            def begin():
                here[...] = both
                result[...] = (1.0 - first) * other

            pl.when(self.has_prev)(go_on)
            pl.when(jnp.logical_not(self.has_prev))(begin)
            pl.when(self.has_next)(lambda i=i: self.line_copy(i).start())

    def finish(self):
        self.dec_copy().wait_send()
        for i in range(len(self.pieces)):
            self.peer_copy(i).wait_send()
            pl.when(self.has_next)(lambda i=i: self.line_copy(i).wait_send())


def prefix_scratch(seqs, slots, width):
    count = 2 * seqs
    return [
        pltpu.VMEM((seqs, slots, width), F32), pltpu.VMEM((seqs, slots, width), F32), pltpu.VMEM((seqs, slots, 128), F32),
        pltpu.VMEM((seqs, slots, width), F32), pltpu.VMEM((seqs, slots, width), F32),
        pltpu.SemaphoreType.DMA((2, count)), pltpu.SemaphoreType.DMA((2,)), pltpu.SemaphoreType.DMA((2, count)),
    ]


def take(refs, count):
    return refs[:count], refs[count:]


class Weave:
    def __init__(self, steps):
        self.steps = list(steps)

    def run(self, count):
        for step in self.steps[:count]:
            step()
        self.steps = self.steps[count:]

    def rest(self):
        self.run(len(self.steps))


def blocks_in_order(p, seqs):
    def block(i):
        b = jnp.where(i < 2, 1 - p.c, p.c)
        x = jnp.where(lax.rem(i, 2) == 0, 1 - p.x, p.x)
        return b, x

    return block


PACE = 1.5
FORE_STEPS = (0, 6, 0, 4, 0, 2, 0, 0)


def forward_kernel(size, plan, levels, *refs):
    p = Place(size)
    (qkv, gates, decay, keep, gain, out_w, tokens, gain2, paths, masks, grad_out), refs = take(refs, 11)
    shard_refs, refs = take(refs, sum(len(columns) for _, _, columns in plan))
    (gated, attended, probs, scores, weights, states, decs, end_dec, residual, normed, grads), refs = take(refs, 11)
    fulls, refs = take(refs, max(i for i, _, _ in plan) + 1)
    (units, part, total), refs = take(refs, 3)
    (start, *prefix_refs), refs = take(refs, 8)
    fold_refs, refs = take(refs, 5)
    share_sems, refs = take(refs, 2)
    (swap_sem,), refs = take(refs, 1)
    count = paths.shape[1]
    head = gated.shape[1]
    seqs = tokens.shape[0]
    slots = keep.shape[1]
    greet(p, sibling=True)
    work = gathers_of(p, plan, shard_refs, fulls, refs)
    for gathered in work:
        gathered.start_x()
    weave = Weave(gather_ops(work, PACE))
    weave.run(FORE_STEPS[0])
    tail = paths[(levels + 1) * count :, :]

    def ends(b):
        for j in range(2):
            rows = pl.ds((b * 2 + j) * count, count)
            unit, dec = ends_chunk(
                qkv[rows, head : 2 * head], qkv[rows, 2 * head :], decay[rows, :], keep[rows, :], tail
            )
            units[b, j] = unit
            decs[b, j] = dec
        total[b] = spread(dec, 2 * head) * units[b, 0] + unit
        end_dec[b] = decs[b, 0] * dec

    for b in range(seqs):
        ends(b)
    carry = Prefix(p, False, total, end_dec, start, *prefix_refs[:4], prefix_refs[4:])
    carry.start()
    weave.run(FORE_STEPS[1])
    move = Swap(p, grad_out, grads, swap_sem)
    move.start()
    carry.run()
    for b in range(seqs):
        states[3 * b] = start[b]
        for j in range(2):
            states[3 * b + j + 1] = spread(decs[b, j], 2 * head) * states[3 * b + j] + units[b, j]
    weave.run(FORE_STEPS[2])
    diag = on_diagonal(count)
    order = blocks_in_order(p, seqs)
    fold = Fold(p, part, *fold_refs[:3], fold_refs[3:])
    share = Share(p, normed, share_sems)

    def attend(i, nothing):
        b, j = order(i)
        rows = pl.ds(pl.multiple_of((b * 2 + j) * count, count), count)
        here = keep[rows, :]
        ratios, (growth,) = powers_of(paths[: (levels + 1) * count, :], count, levels, decay[rows, :])
        query = halves(silu(qkv[rows, :head].astype(F32)) * head ** (-0.5))
        keys = halves(silu(qkv[rows, head : 2 * head].astype(F32)))
        state = states[3 * b + j]
        pair = dot3(query, keys, NT)
        score = mix(pair, ratios, here, masks, jnp.sum(pair * diag, axis=1, keepdims=True))
        score += growth * dot3(query, halves(state[:, :head]), NT)
        raised = jnp.exp(score - jnp.max(score, axis=1, keepdims=True))
        prob = raised / jnp.sum(raised, axis=1, keepdims=True)
        weight = unmix(prob, ratios, here, masks, diag)
        values = qkv[rows, 2 * head :]
        whi, wlo = halves(weight)
        result = mm(whi, values, NN) + mm(wlo, values, NN)
        result += dot3(halves(prob * growth), halves(state[:, head:]), NN)
        scale = lax.rsqrt(jnp.mean(result * result, axis=1, keepdims=True) + EPS)
        low = bf(result * scale * gain[...] * silu(gates[rows, :head]))
        gated[rows, :] = low
        attended[rows, :] = result
        probs[rows, :] = prob
        scores[rows, :] = score
        weights[rows, :] = weight
        part[b, j] = bf(mm(low, out_w[...], NT))
        pl.when(i == 0)(lambda: fold.sib_all(True))
        pl.when(i == 1)(lambda: fold.sib_all(False))
        return nothing

    lax.fori_loop(0, 2, attend, 0)
    weave.run(FORE_STEPS[3])
    lax.fori_loop(2, 3, attend, 0)
    for r in range(STRIPS):
        fold.cross(r)
    weave.run(FORE_STEPS[4])
    move.forward()
    lax.fori_loop(3, 4, attend, 0)
    weave.run(FORE_STEPS[5])
    for r in range(STRIPS):
        value = tokens[p.c, fold.strip(r)].astype(F32) + fold.total(r)
        residual[fold.strip(r)] = value
        share.put(r, bf(value * inverse_rms(value) * gain2[...]))
        if r == 1:
            weave.run(FORE_STEPS[6])
    weave.run(FORE_STEPS[7])
    for r in range(STRIPS):
        share.forward(r)
    weave.rest()
    share.finish()
    fold.finish()
    carry.finish()
    move.finish()


def forward(size, number, slot, plan, fulls, qkv, gates, decay, keep, gain, out_w, tokens, gain2, grad_out, shards):
    seqs, block, width = tokens.shape
    h, m, n, rows = slot.head, slot.slots, slot.chunks, slot.seqs * slot.rows
    shape = jax.ShapeDtypeStruct
    outs = [
        shape((rows, h), BF16), shape((rows, h), F32), shape((rows, m), F32), shape((rows, m), F32), shape((rows, slot.chunk), F32),
        shape((seqs * (n + 1), m, 2 * h), F32), shape((seqs, n, m, 128), F32), shape((seqs, m, 128), F32),
        shape((block, width), F32), shape((seqs, 2, block, width), BF16), shape((seqs, 2, block, width), BF16),
    ]
    scratch = [
        pltpu.VMEM((seqs, n, m, 2 * h), F32), pltpu.VMEM((seqs, 2, block, width), BF16), pltpu.VMEM((seqs, m, 2 * h), F32),
    ]
    scratch += prefix_scratch(seqs, m, 2 * h) + fold_scratch(block, width) + SHARE_SEMS + [pltpu.SemaphoreType.DMA((5,))]
    for _, _, columns in plan:
        scratch += gather_sems(size // 4, len(columns))
    return pl.pallas_call(
        functools.partial(forward_kernel, size, plan, slot.levels),
        out_shape=outs + [shape(full, BF16) for full in fulls],
        in_specs=[VM] * 10 + [ANY] * (1 + len(shards)),
        out_specs=[VM] * 10 + [ANY] * (1 + len(fulls)),
        scratch_shapes=scratch,
        compiler_params=remote_params(number, 60),
        name="attend_forward",
    )(qkv, gates, decay, keep, gain, out_w, tokens, gain2, slot.paths, slot.masks, grad_out, *shards)

class Pool:
    def __init__(self, refs):
        self.loads, self.extra, self.sends, self.totals, self.sems = refs

    def slot(self, which, slot):
        return self.extra if slot == 3 else self.loads.at[which, slot]


POOL_SENDS = 2
AHEAD = 3
LAG = 3


def pool_scratch(rows, width):
    return [
        pltpu.VMEM((2, 3, rows, width), BF16), pltpu.VMEM((rows, width), BF16), pltpu.VMEM((POOL_SENDS, rows, width), BF16),
        pltpu.VMEM((rows, width), F32),
        pltpu.SemaphoreType.DMA((2, 4)),
    ]


class Scatter:
    def __init__(self, place, grad, out, peer, line, unit, offset, width, sems):
        self.p, self.grad, self.out, self.peer, self.line = place, grad, out, peer, line
        self.unit, self.offset, self.width = unit, offset, width
        self.whole = out.shape[-1] == width
        self.b_sem, self.l_sem, self.x_sem = sems

    def goal(self, n):
        p = self.p
        low, high = p.a, p.line - 1 - p.a
        more, less = jnp.maximum(low, high), jnp.minimum(low, high)
        alone = more - less
        up_more = jnp.where(high >= low, 1, -1)
        m = n - alone
        early = n < alone
        reach = jnp.where(early, more - n, less - m // 2)
        side = jnp.where(early, up_more, jnp.where(lax.rem(jnp.maximum(m, 0), 2) == 0, 1, -1))
        return p.a + side * reach

    def block(self, a, b):
        rows = pl.ds((4 * a + 2 * b) * self.unit, 2 * self.unit)
        if self.width == self.grad.shape[1]:
            return self.grad.at[rows]
        return self.grad.at[rows, pl.ds(self.offset, self.width)]

    def b_copy(self, a):
        return remote(self.block(a, 1 - self.p.b), self.peer.at[a], self.b_sem.at[0, a], self.b_sem.at[1, a], self.p.across())

    def start(self, n):
        self.b_copy(self.goal(n)).start()

    def cut(self, ref):
        return ref if self.width == ref.shape[1] else ref.at[:, pl.ds(0, self.width)]

    def load(self, pool, which, slot, source):
        return pltpu.make_async_copy(source, self.cut(pool.slot(which, slot)), pool.sems.at[which, slot])

    def prepare(self, pool, which, n):
        d = self.goal(n)
        self.b_copy(d).wait_recv()
        self.load(pool, which, 0, self.block(d, self.p.b)).start()
        self.load(pool, which, 1, self.peer.at[d]).start()

    def loaded(self, pool, which, n):
        d = self.goal(n)
        self.load(pool, which, 0, self.block(d, self.p.b)).wait()
        self.load(pool, which, 1, self.peer.at[d]).wait()

    def strips(self, do):
        rows = 2 * self.unit
        step = max(r for r in (16, 32, 64, 128) if rows % r == 0 and (r == 16 or r * self.width <= 64 * 1024))

        def one(i, carry):
            do(pl.ds(pl.multiple_of(i * step, step), step))
            return carry

        lax.fori_loop(0, rows // step, one, 0)

    def bring(self, pool, which, slot, place):
        remote(self.line.at[place], self.line.at[place], self.l_sem.at[0, 0], self.l_sem.at[1, place], self.p.across()).wait_recv()
        self.load(pool, which, slot, self.line.at[place]).start()

    def send(self, pool, out, n):
        p = self.p
        d = self.goal(n)
        up = d > p.a
        to = jnp.clip(p.a + jnp.where(up, 1, -1), 0, p.line - 1)
        slot = jnp.where(jnp.logical_and(jnp.logical_not(up), d == p.a - 1), p.line, d)
        return remote(
            self.cut(pool.sends.at[out]), self.line.at[slot], self.l_sem.at[0, n], self.l_sem.at[1, slot], (p.at(to, p.b, p.x), p.c)
        )

    def hop(self, pool, which, n, out):
        p = self.p
        d = self.goal(n)
        behind = jnp.logical_or(jnp.logical_and(d > p.a, p.has_down()), jnp.logical_and(d < p.a, p.has_up()))
        pl.when(behind)(lambda: self.bring(pool, which, 2, d))
        self.loaded(pool, which, n)
        a, b, c = (self.cut(pool.slot(which, i)) for i in range(3))
        to = self.cut(pool.sends.at[out])

        def with_line():
            self.load(pool, which, 2, self.line.at[d]).wait()

            def do(rows):
                to[rows] = bf(a[rows].astype(F32) + b[rows].astype(F32) + c[rows].astype(F32))

            self.strips(do)

        def without():
            def do(rows):
                to[rows] = bf(a[rows].astype(F32) + b[rows].astype(F32))

            self.strips(do)

        pl.when(behind)(with_line)
        pl.when(jnp.logical_not(behind))(without)
        self.send(pool, out, n).start()

    def last(self, pool, which):
        p = self.p
        n = p.line - 1
        pl.when(p.has_down())(lambda: self.bring(pool, which, 2, p.a))
        pl.when(p.has_up())(lambda: self.bring(pool, which, 3, p.line))
        self.loaded(pool, which, n)
        a, b, c, d = (self.cut(pool.slot(which, i)) for i in range(4))
        to = self.total = self.cut(pool.totals)

        def first(rows):
            to[rows] = a[rows].astype(F32) + b[rows].astype(F32)

        self.strips(first)

        def more(slot, place, ref):
            def go():
                self.load(pool, which, slot, self.line.at[place]).wait()

                def do(rows):
                    to[rows] = to[rows] + ref[rows].astype(F32)

                self.strips(do)

            return go

        pl.when(p.has_down())(more(2, p.a, c))
        pl.when(p.has_up())(more(3, p.line, d))
        self.x_copy().start()
        if not self.whole:
            self.out_copy().start()

    def half(self, x):
        return self.total.at[pl.ds(x * self.unit, self.unit)]

    def place(self):
        return self.out.at[:, pl.ds(self.p.x * self.width, self.width)]

    def x_copy(self):
        p = self.p
        where = self.out.at[1] if self.whole else self.place()
        return remote(self.half(1 - p.x), where, self.x_sem.at[0], self.x_sem.at[1], p.partner())

    def out_copy(self):
        return pltpu.make_async_copy(self.half(self.p.x), self.place(), self.x_sem.at[2])

    def sent(self):
        self.x_copy().wait_send()
        if not self.whole:
            self.out_copy().wait()

    def finish(self):
        p = self.p
        self.x_copy().wait_recv()
        if self.whole:
            self.out[0] = self.out[1] + self.half(p.x)[...]
        for n in range(p.line):
            self.b_copy(self.goal(n)).wait_send()


def scatter_sems(line):
    return [pltpu.SemaphoreType.DMA((2, line)), pltpu.SemaphoreType.DMA((2, line + 1)), pltpu.SemaphoreType.DMA((3,))]


def scatter_ops(work, pool):
    lines = work[0].p.line
    jobs = [(k * (lines - 1) + n, k, n) for k in range(len(work)) for n in range(lines - 1)]
    jobs += [((k + 1) * (lines - 1) - 0.5 + LAG, k, lines - 1) for k in range(len(work))]
    jobs = [(k, n) for _, k, n in sorted(jobs)]
    sends, totals = [], []

    def begin():
        for k, n in jobs[:AHEAD]:
            work[k].start(n)


    def job(i):
        k, n = jobs[i]

        def step():
            work[k].prepare(pool, i % 2, n)
            if i + AHEAD < len(jobs):
                work[jobs[i + AHEAD][0]].start(jobs[i + AHEAD][1])
            if n < lines - 1:
                out = len(sends) % POOL_SENDS
                if len(sends) >= POOL_SENDS:
                    ok, on, oo = sends[-POOL_SENDS]
                    work[ok].send(pool, oo, on).wait_send()
                work[k].hop(pool, i % 2, n, out)
                sends.append((k, n, out))
            else:
                if totals:
                    work[totals[-1]].sent()
                work[k].last(pool, i % 2)
                totals.append(k)

        return step

    steps = [begin] + [job(i) for i in range(len(jobs))]

    def finish():
        for ok, on, oo in sends[-POOL_SENDS:]:
            work[ok].send(pool, oo, on).wait_send()
        work[totals[-1]].sent()
        for chunk in work:
            chunk.finish()

    steps.append(finish)
    return steps

BACK_STEPS = (0, 0, 1, 0, 2, 0, 0, 2, 2, 1, 4, 0)


def backward_kernel(size, plan, levels, *refs):
    p = Place(size)
    (grad_out_all, gates_all, attended, grad_part), refs = take(refs, 4)
    (residual, gain2, out_w, qkv, decay, keep, gain, probs, scores, weights, states, decs,
     end_dec, paths, later, masks), refs = take(refs, 16)
    grads = max(i for i, _, _, _, _ in plan) + 1
    grad_refs, refs = take(refs, grads)
    (residual_grad, low, second_part, gate_term, gain_part, term, decay_term), refs = take(refs, 7)
    outs, refs = take(refs, len(plan))
    spaces, refs = take(refs, 2 * len(plan))
    (grad_out, gates, own_part, own_sem, att_grad, dprobs, dscores, units, adjoints, total), refs = take(refs, 10)
    (ending, *prefix_refs), refs = take(refs, 8)
    fold_refs, refs = take(refs, 5)
    share_sems, refs = take(refs, 2)
    pool_refs, refs = take(refs, 5)
    count = paths.shape[1]
    head = gate_term.shape[1]
    seqs = grad_out_all.shape[0]
    own = [
        pltpu.make_async_copy(grad_out_all.at[p.c], grad_out, own_sem.at[0]),
        pltpu.make_async_copy(gates_all.at[:, pl.ds(0, head)], gates, own_sem.at[1]),
        pltpu.make_async_copy(attended, att_grad, own_sem.at[2]),
        pltpu.make_async_copy(grad_part.at[p.c], own_part, own_sem.at[3]),
    ]
    for copy in own:
        copy.start()
    greet(p, sibling=True)
    pool = Pool(pool_refs)
    work = []
    for n, (i, unit, offset, width, _) in enumerate(plan):
        work.append(
            Scatter(p, grad_refs[i], outs[n], spaces[2 * n], spaces[2 * n + 1], unit, offset, width, refs[3 * n : 3 * n + 3])
        )
    weave = Weave(scatter_ops(work, pool))
    fold = Fold(p, grad_part, *fold_refs[:3], fold_refs[3:], own_part)
    share = Share(p, low, share_sems)
    fold.start()
    weave.run(1 + BACK_STEPS[0])
    own[3].wait()
    for r in range(STRIPS):
        fold.cross(r)
    weave.run(BACK_STEPS[1])
    own[0].wait()
    gains = jnp.zeros((1, grad_part.shape[3]), F32)
    for r in range(STRIPS):
        down, more = norm_back(fold.total(r), residual[fold.strip(r)], gain2[...])
        value = grad_out[fold.strip(r)].astype(F32) + down
        gains += more
        residual_grad[fold.strip(r)] = value
        share.put(r, bf(value))
        if r == 1:
            weave.run(BACK_STEPS[2])
    second_part[...] = gains
    weave.run(BACK_STEPS[3])
    diag = on_diagonal(count)
    gain_part[...] = jnp.zeros_like(gain_part)

    def place(i):
        b = jnp.where(lax.rem(i, 2) == 0, p.c, 1 - p.c)
        x = jnp.where(i < 2, p.x, 1 - p.x)
        return b, x

    def first(i, nothing):
        b, j = place(i)
        rows = pl.ds(pl.multiple_of((b * 2 + j) * count, count), count)
        grad = mm(low[b, j], out_w[...], NN)
        gate = gates[rows, :]
        value = att_grad[rows, :]
        scale = lax.rsqrt(jnp.mean(value * value, axis=1, keepdims=True) + EPS)
        normed = value * scale
        weighted = grad * silu(gate)
        gate_term[rows, :] = bf(grad * normed * gain[...] * silu_slope(gate))
        gain_part[...] += jnp.sum(weighted * normed, axis=0, keepdims=True)
        c = weighted * gain[...]
        agrad = scale * c - value * (scale * scale * scale) * jnp.mean(c * value, axis=1, keepdims=True)
        att_grad[rows, :] = agrad
        here = keep[rows, :]
        ratios, (growth,) = powers_of(paths[: (levels + 1) * count, :], count, levels, decay[rows, :])
        ahalf = halves(agrad)
        values = qkv[rows, 2 * head :]
        pair = mm(ahalf[0], values, NT) + mm(ahalf[1], values, NT)
        state = states[3 * b + j]
        dprob = mix(pair, ratios, here, masks, jnp.sum(pair * diag, axis=1, keepdims=True))
        dprob += growth * dot3(ahalf, halves(state[:, head:]), NT)
        prob = probs[rows, :]
        dscore = prob * (dprob - jnp.sum(prob * dprob, axis=1, keepdims=True))
        query = halves(silu(qkv[rows, :head].astype(F32)) * head ** (-0.5))
        dprobs[rows, :] = dprob
        dscores[rows, :] = dscore
        unit_k = dot3(halves(growth * dscore), query, TN)
        unit_v = dot3(halves(growth * prob), ahalf, TN)
        units[b, j] = jnp.concatenate([unit_k, unit_v], axis=1)
        return nothing

    own[1].wait()
    own[2].wait()
    lax.fori_loop(0, 1, first, 0)
    weave.run(BACK_STEPS[4])
    for r in range(STRIPS):
        share.forward(r)
    share.wait_sibling(False)
    lax.fori_loop(1, 3, first, 0)
    weave.run(BACK_STEPS[5])
    share.wait_sibling(True)
    lax.fori_loop(3, 4, first, 0)
    weave.run(BACK_STEPS[6])
    for b in range(seqs):
        total[b] = spread(decs[b, 0], 2 * head) * units[b, 1] + units[b, 0]
    carry = Prefix(p, True, total, end_dec, ending, *prefix_refs[:4], prefix_refs[4:])
    carry.start()
    weave.run(BACK_STEPS[7])
    carry.run()
    for b in range(seqs):
        adjoints[b, 1] = ending[b]
        adjoints[b, 0] = spread(decs[b, 1], 2 * head) * ending[b] + units[b, 1]
    is_last = (lax.broadcasted_iota(jnp.int32, (count, 1), 0) == count - 1).astype(F32)

    def second(i, nothing):
        for k in range(4):
            pl.when(i == k)(functools.partial(weave.run, BACK_STEPS[8 + k]))
        b, j = place(i)
        rows = pl.ds(pl.multiple_of((b * 2 + j) * count, count), count)
        here = keep[rows, :]
        ratios, (growth, rest) = powers_of(paths[...], count, levels, decay[rows, :])
        qraw = qkv[rows, :head].astype(F32)
        kraw = qkv[rows, head : 2 * head].astype(F32)
        query = halves(silu(qraw) * head ** (-0.5))
        keys = halves(silu(kraw))
        values = qkv[rows, 2 * head :]
        agrad = halves(att_grad[rows, :])
        prob, dscore = probs[rows, :], dscores[rows, :]
        state = halves(states[3 * b + j][:, :head])
        adj = adjoints[b, j]
        ahalf = halves(adj)
        adj_k, adj_v = (ahalf[0][:, :head], ahalf[1][:, :head]), (ahalf[0][:, head:], ahalf[1][:, head:])
        dweights = halves(unmix(dscore, ratios, here, masks, diag))
        dquery = dot3(dweights, keys, NN) + dot3(halves(dscore * growth), state, NN)
        term[rows, :head] = bf(silu_slope(qraw) * dquery * head ** (-0.5))
        left = halves(rest * here)
        dkey = dot3(dweights, query, TN) + dot3(left, adj_k, NN)
        term[rows, head : 2 * head] = bf(silu_slope(kraw) * dkey)
        dvalue = dot3(halves(weights[rows, :]), agrad, TN) + dot3(left, adj_v, NN)
        term[rows, 2 * head :] = bf(dvalue)
        pair_k = dot3(query, keys, NT)
        pair_v = mm(agrad[0], values, NT) + mm(agrad[1], values, NT)
        dkeep = jnp.sum(pair_k * diag, axis=1, keepdims=True) * dscore
        dkeep += jnp.sum(pair_v * diag, axis=1, keepdims=True) * prob
        dkeep += rest * (dot3(keys, adj_k, NT) + mm(values, adj_v[0], NT) + mm(values, adj_v[1], NT))
        for l, ratio in enumerate(ratios):
            mask = masks[l].astype(F32)
            more = dot3(halves(pair_k * mask), halves(dscore * ratio), TN)
            more += dot3(halves(pair_v * mask), halves(prob * ratio), TN)
            dkeep += ratio * more
        dsum = dscore * scores[rows, :] + prob * dprobs[rows, :] - here * dkeep
        at_end = jnp.sum(adj * states[3 * b + j + 1], axis=1, keepdims=True)
        at_end = jnp.sum(at_end * on_diagonal(adj.shape[0]), axis=0, keepdims=True)
        dsum += is_last * at_end
        decay_term[rows, :] = exact_sums(later[...], dsum) - (1.0 - here) * dkeep
        return nothing

    lax.fori_loop(0, 4, second, 0)
    weave.rest()
    share.finish(False)
    fold.finish()
    carry.finish()


def backward(size, number, slot, plan, hbm_ins, vmem_ins, grads):
    seqs, block, width = hbm_ins[0].shape
    h, m, n, rows = slot.head, slot.slots, slot.chunks, slot.seqs * slot.rows
    line = size // 4
    shape = jax.ShapeDtypeStruct
    outs = [
        shape((block, width), F32), shape((seqs, 2, block, width), BF16), shape((1, width), F32), shape((rows, h), BF16),
        shape((1, h), F32), shape((rows, 3 * h), BF16), shape((rows, m), F32),
    ]
    results, spaces, sems = [], [], []
    for i, unit, offset, columns, whole in plan:
        results.append(shape((2, unit, columns) if whole else (unit, 2 * columns), F32))
        spaces += [shape((line, 2 * unit, columns), BF16), shape((line + 1, 2 * unit, columns), BF16)]
        sems += scatter_sems(line)
    widest = max(entry[3] for entry in plan)
    scratch = [
        pltpu.VMEM((block, width), BF16), pltpu.VMEM((rows, h), F32),
        pltpu.VMEM((2, block, width), BF16), pltpu.SemaphoreType.DMA((4,)),
        pltpu.VMEM((rows, h), F32), pltpu.VMEM((rows, m), F32), pltpu.VMEM((rows, m), F32), pltpu.VMEM((seqs, n, m, 2 * h), F32),
        pltpu.VMEM((seqs, n, m, 2 * h), F32), pltpu.VMEM((seqs, m, 2 * h), F32),
    ]
    scratch += prefix_scratch(seqs, m, 2 * h) + fold_scratch(block, width) + SHARE_SEMS
    scratch += pool_scratch(2 * plan[0][1], widest) + sems
    later = slot.paths[-2 * slot.chunk : -slot.chunk].T
    result = pl.pallas_call(
        functools.partial(backward_kernel, size, plan, slot.levels),
        out_shape=outs + results + spaces,
        in_specs=[ANY] * 4 + [VM] * 16 + [ANY] * len(grads),
        out_specs=[VM] * 7 + [ANY] * (len(results) + len(spaces)),
        scratch_shapes=scratch,
        compiler_params=remote_params(number, 62),
        name="attend_backward",
    )(*hbm_ins, *vmem_ins, slot.paths, later, slot.masks, *grads)
    return result[: 7 + len(results)]


def products(p, part, fold, terms, i):
    count, width = part.shape[2], part.shape[3]
    stripe = min(512, width)
    b, x = blocks_in_order(p, part.shape[0])(i)
    rows = pl.ds(pl.multiple_of((b * 2 + x) * count, count), count)

    def one(t, nothing):
        columns = pl.ds(pl.multiple_of(t * stripe, stripe), stripe)
        value = None
        for left, right in terms:
            more = mm(left[rows, :], right[columns, :], NT)
            value = more if value is None else value + more
        part[b, x, :, columns] = bf(value)
        return nothing

    lax.fori_loop(0, width // stripe, one, 0)
    if i < 2:
        fold.sib_all(i == 0)


LAST_STEPS = (0, 1, 1, 1, 1, 1, 1, 2, 1)


def last_kernel(size, plan, *refs):
    p = Place(size)
    (qkv_full, gate_full, down_full), refs = take(refs, 3)
    (qkv_term, gates_term, activated, tokens, residual, residual_grad, gain, pack), refs = take(refs, 8)
    grads = max(i for i, _, _, _, _ in plan) + 1
    grad_refs, refs = take(refs, grads)
    (input_grad, output, sums), refs = take(refs, 3)
    outs, refs = take(refs, len(plan))
    spaces, refs = take(refs, 2 * len(plan))
    (part, ff_part, qkv_w, gate_w, down_w, load_sem), refs = take(refs, 6)
    fold_refs, refs = take(refs, 5)
    ff_refs, refs = take(refs, 5)
    (out_sem, mine, came, s_sem), refs = take(refs, 4)
    pool_refs, refs = take(refs, 5)
    loads = [
        pltpu.make_async_copy(source, to, load_sem.at[n])
        for n, (source, to) in enumerate(((qkv_full, qkv_w), (gate_full, gate_w), (down_full, down_w)))
    ]
    for load in loads:
        load.start()
    greet_all(p)
    pool = Pool(pool_refs)
    work = []
    for n, (i, unit, offset, width, _) in enumerate(plan):
        work.append(
            Scatter(p, grad_refs[i], outs[n], spaces[2 * n], spaces[2 * n + 1], unit, offset, width, refs[3 * n : 3 * n + 3])
        )
    weave = Weave(scatter_ops(work, pool))
    fold = Fold(p, part, *fold_refs[:3], fold_refs[3:])
    ff = Fold(p, ff_part, *ff_refs[:3], ff_refs[3:])
    weave.run(1 + LAST_STEPS[0])
    loads[0].wait()
    loads[1].wait()
    terms = [(qkv_term, qkv_w), (gates_term, gate_w)]
    for i in range(3):
        products(p, part, fold, terms, i)
    for r in range(STRIPS):
        fold.cross(r)
    weave.run(LAST_STEPS[1])
    products(p, part, fold, terms, 3)
    loads[2].wait()
    products(p, ff_part, ff, [(activated, down_w)], 0)
    weave.run(LAST_STEPS[2])
    products(p, ff_part, ff, [(activated, down_w)], 1)
    products(p, ff_part, ff, [(activated, down_w)], 2)
    weave.run(LAST_STEPS[3])
    for r in range(STRIPS):
        ff.cross(r)
    products(p, ff_part, ff, [(activated, down_w)], 3)
    weave.run(LAST_STEPS[4])
    gains = jnp.zeros((1, part.shape[3]), F32)

    def out_copy(ref, k, r):
        block = ref.at[p.c, fold.strip(r)]
        return remote(block, block, out_sem.at[0, k * STRIPS + r], out_sem.at[1, k * STRIPS + r], p.sibling())

    for r in range(STRIPS):
        down, more = norm_back(fold.total(r), tokens[p.c, fold.strip(r)].astype(F32), gain[...])
        gains += more
        input_grad[p.c, fold.strip(r)] = residual_grad[fold.strip(r)] + down
        out_copy(input_grad, 1, r).start()
        if r % 2 == 1:
            weave.run(LAST_STEPS[5 + r // 2])
    unit = plan[0][1]
    mine[...] = pack[...]
    for s in range(size):
        mine[s, 0:1, pl.ds(0, unit)] = gains[:, s * unit : (s + 1) * unit]
    smalls = Smalls(p, mine, sums, came, s_sem)
    smalls.start()
    weave.run(LAST_STEPS[7])
    for r in range(STRIPS):
        output[p.c, fold.strip(r)] = bf(residual[fold.strip(r)] + ff.total(r))
        out_copy(output, 0, r).start()
        if r % 2 == 1:
            weave.run(LAST_STEPS[8])
    weave.rest()
    smalls.finish()
    for r in range(STRIPS):
        out_copy(output, 0, r).wait()
        out_copy(input_grad, 1, r).wait()
    ff.finish()
    fold.finish()


def last(size, number, plan, hbm_ins, vmem_ins, grads):
    qkv_term, _, _, tokens = vmem_ins[:4]
    seqs, block, width = tokens.shape
    pack = vmem_ins[-1]
    line = size // 4
    shape = jax.ShapeDtypeStruct
    outs = [shape((seqs, block, width), F32), shape((seqs, block, width), BF16), shape(pack.shape[1:], F32)]
    results, specs, spaces, sems = [], [], [], []
    for i, unit, offset, columns, whole in plan:
        results.append(shape((2, unit, columns) if whole else (unit, 2 * columns), F32))
        specs.append(VM if whole else ANY)
        spaces += [shape((line, 2 * unit, columns), BF16), shape((line + 1, 2 * unit, columns), BF16)]
        sems += scatter_sems(line)
    widest = max(entry[3] for entry in plan)
    scratch = [pltpu.VMEM((seqs, 2, block, width), BF16)] * 2 + [pltpu.VMEM(w.shape, BF16) for w in hbm_ins]
    scratch += [pltpu.SemaphoreType.DMA((3,))] + fold_scratch(block, width) * 2 + [
        pltpu.SemaphoreType.DMA((2, 2 * STRIPS)), pltpu.VMEM(pack.shape, F32), pltpu.VMEM((2 * size,) + pack.shape[1:], F32),
        pltpu.SemaphoreType.DMA((2, 2 * size)),
    ]
    scratch += pool_scratch(2 * plan[0][1], widest) + sems
    result = pl.pallas_call(
        functools.partial(last_kernel, size, plan),
        out_shape=outs + results + spaces,
        in_specs=[ANY] * 3 + [VM] * 8 + [ANY] * len(grads),
        out_specs=[VM] * 3 + specs + [ANY] * len(spaces),
        scratch_shapes=scratch,
        compiler_params=remote_params(number, 62),
        name="last",
    )(*hbm_ins, *vmem_ins, *grads)
    return result[: 3 + len(results)]

def greet_all(place):
    barrier = pltpu.get_barrier_semaphore()

    def one(i, carry):
        signal(barrier, (lax.rem(place.s + i // 2, place.size), lax.rem(place.c + lax.rem(i, 2), 2)))
        return carry

    lax.fori_loop(1, 2 * place.size, one, 0)
    pl.semaphore_wait(barrier, 2 * place.size - 1)


class Smalls:
    def __init__(self, place, pack, out, came, sems):
        self.p, self.pack, self.out, self.came, self.sems = place, pack, out, came, sems

    def copy(self, i):
        p = self.p
        s = lax.rem(p.s + i // 2, p.size)
        return remote(
            self.pack.at[s], self.came.at[i], self.sems.at[0, i], self.sems.at[1, i], (s, lax.rem(p.c + lax.rem(i, 2), 2))
        )

    def start(self):
        lax.fori_loop(1, 2 * self.p.size, lambda i, c: (self.copy(i).start(), c)[1], 0)

    def finish(self):
        def one(i, total):
            self.copy(i).wait()
            return total + self.came[i]

        self.out[...] = lax.fori_loop(1, 2 * self.p.size, one, self.pack[self.p.s])


class Swap:
    def __init__(self, place, own, both, sems):
        p = self.p = place
        self.keep = pltpu.make_async_copy(own, both.at[:, p.x], sems.at[0])
        self.cross = remote(own.at[p.c], both.at[p.c, p.x], sems.at[1], sems.at[2], p.partner())
        came = both.at[p.c, 1 - p.x]
        self.hand = remote(came, came, sems.at[3], sems.at[4], p.sibling())

    def start(self):
        self.cross.start()
        self.keep.start()

    def forward(self):
        self.cross.wait_recv()
        self.hand.start()

    def finish(self):
        self.keep.wait()
        self.cross.wait_send()
        self.hand.wait()


def gather_kernel(size, plan, *refs):
    p = Place(size)
    shards = sum(len(columns) for _, _, columns in plan)
    fulls = max(i for i, _, _ in plan) + 1
    ins, refs = take(refs, shards)
    (own_tokens,), refs = take(refs, 1)
    outs, refs = take(refs, fulls)
    (tokens, normed, qkv, gates), refs = take(refs, 4)
    (swap_sem, tok, qkv_w, gate_w, small, load_sem), refs = take(refs, 6)
    greet(p, sibling=True)
    work = gathers_of(p, plan, ins, outs, refs)
    smalls, qkv_gather, gate_gather, out_gather = work
    move = Swap(p, own_tokens, tokens, swap_sem)
    for gathered in work:
        gathered.start_x()
    weave = Weave(gather_ops(work, 1)[: -len(work)])
    weave.run(6)
    move.start()
    weave.run(4)
    move.forward()
    weave.run(2)
    move.finish()
    smalls.finish()
    loads = [
        pltpu.make_async_copy(source, to, load_sem.at[n])
        for n, (source, to) in enumerate(((tokens, tok), (outs[3], small), (outs[0], qkv_w), (outs[1], gate_w)))
    ]
    loads[0].start()
    loads[1].start()
    loads[0].wait()
    loads[1].wait()
    seqs, pair, block, width = tok.shape
    unit = plan[1][1]
    gain = jnp.concatenate([small[16 * s : 16 * s + 1, :unit].astype(F32) for s in range(size)], axis=1)
    step = 32

    def norm(i, nothing):
        b, x, r = i // (pair * (block // step)), lax.rem(i // (block // step), pair), lax.rem(i, block // step)
        rows = pl.ds(pl.multiple_of(r * step, step), step)
        value = tok[b, x, rows, :].astype(F32)
        where = pl.ds(pl.multiple_of(i * step, step), step)
        normed[where, :] = bf(value * inverse_rms(value) * gain)
        return nothing

    lax.fori_loop(0, seqs * pair * (block // step), norm, 0)
    weave.rest()
    qkv_gather.finish()
    loads[2].start()
    gate_gather.finish()
    loads[3].start()
    loads[2].wait()

    def rows_of(i):
        return pl.ds(pl.multiple_of(i * block, block), block)

    third = qkv.shape[1] // 3

    def project(i, nothing):
        for t in range(3):
            columns = pl.ds(t * third, third)
            qkv[rows_of(i), columns] = bf(mm(normed[rows_of(i), :], qkv_w[:, columns], NN))
        return nothing

    lax.fori_loop(0, seqs * pair, project, 0)
    loads[3].wait()

    def gate(i, nothing):
        gates[rows_of(i), :] = mm(normed[rows_of(i), :], gate_w[...], NN)
        return nothing

    lax.fori_loop(0, seqs * pair, gate, 0)
    out_gather.finish()


def gather(size, number, plan, shards, fulls, tokens):
    line = size // 4
    seqs, block, width = tokens.shape
    rows = 2 * seqs * block
    shape = jax.ShapeDtypeStruct
    sems = []
    for _, _, columns in plan:
        sems += gather_sems(line, len(columns))
    return pl.pallas_call(
        functools.partial(gather_kernel, size, plan),
        out_shape=[shape(full, BF16) for full in fulls] + [
            shape((seqs, 2, block, width), BF16), shape((rows, width), BF16), shape((rows, fulls[0][1]), BF16),
            shape((rows, fulls[1][1]), F32),
        ],
        in_specs=[ANY] * (len(shards) + 1),
        out_specs=[ANY] * (len(fulls) + 1) + [VM] * 3,
        scratch_shapes=[
            pltpu.SemaphoreType.DMA((5,)), pltpu.VMEM((seqs, 2, block, width), BF16), pltpu.VMEM(fulls[0], BF16),
            pltpu.VMEM(fulls[1], BF16), pltpu.VMEM(fulls[3], BF16), pltpu.SemaphoreType.DMA((4,)),
        ] + sems,
        compiler_params=remote_params(number, 60),
        name="gather",
    )(*shards, tokens)


def dot(left, right, dims, dtype=F32):
    return lax.dot_general(left, right, dims, preferred_element_type=F32).astype(dtype)


def lanes(row):
    return jnp.pad(row.reshape(-1), (0, 128 - row.size))


def shards(
    tokens, grad_out, query_weight, key_weight, value_weight, forget_weight, forget_bias, outgate_weight, output_weight,
    slot_gain, first_gain, second_gain, gate_weight, up_weight, down_weight,
):
    size = lax.axis_size("seq")
    x = lax.rem(lax.axis_index("seq"), 2)
    c = lax.axis_index("head")
    seqs, block, width = tokens.shape
    heads_here, slot_part = forget_bias.shape
    slots = slot_part * size
    head = slot_gain.shape[0] * size
    unit = first_gain.shape[0]
    hidden = gate_weight.shape[1] // 2
    rows = seqs * 2 * block
    pack = jnp.stack([lanes(first_gain), lanes(second_gain), lanes(slot_gain), lanes(forget_bias)] + [jnp.zeros(128, BF16)] * 12)
    plan = [
        (3, 16, [(0, 128)]), (0, unit, [(0, head), (head, head), (2 * head, head)]), (1, unit, [(0, head), (head, 2 * slots)]),
        (2, unit, [(0, head)]),
    ]
    fulls = [(width, 3 * head), (width, head + 2 * slots), (width, head), (16 * size, 128)]
    qkv_full, gate_full, out_full, small_full, _, normed_one, qkv, gates = gather(
        size, 0, plan,
        (pack, query_weight, key_weight, value_weight, outgate_weight, forget_weight, output_weight.T), fulls, tokens,
    )
    small = small_full.reshape(size, 16, 128).astype(F32)
    first_full = small[:, 0, :unit].reshape(1, width)
    second_full = small[:, 1, :unit].reshape(1, width)
    slot_full = small[:, 2, : head // size].reshape(1, head)
    bias_full = small[:, 3, : heads_here * slot_part].reshape(size, heads_here, slot_part)
    bias_full = jnp.moveaxis(bias_full, 1, 0).reshape(heads_here, slots)

    def own_head(array, axis):
        return jnp.where(x == 0, *jnp.split(array, 2, axis=axis))

    logit = own_head(gates[:, head:], 1) + own_head(bias_full, 0)
    decay = -jax.nn.softplus(-logit) / TAU
    keep = -jnp.expm1(decay)
    slot = Slots(seqs, 2 * block, head, slots, block)
    ff_plan = [(0, unit, [(0, hidden)]), (0, unit, [(hidden, hidden)]), (1, unit, [(0, hidden)])]
    (gated, attended, probs, scores, weights, states, decs, end_decs, residual, normed_two, gout, ff_full, down_full) = forward(
        size, 1, slot, ff_plan, [(width, 2 * hidden), (width, hidden)], qkv, gates, decay, keep, slot_full, out_full, tokens,
        second_full, grad_out, (gate_weight, up_weight, down_weight.T),
    )
    shape = (seqs, 2, block, width)
    normed_two = normed_two.reshape(rows, width)
    ff = dot(normed_two, ff_full, NN)
    ff_gate, ff_up = ff[:, :hidden], ff[:, hidden:]
    sig = jax.nn.sigmoid(ff_gate)
    activated = (ff_gate * sig * ff_up).astype(BF16)
    gout = gout.reshape(rows, width)
    act_grad = dot(gout, down_full, NN)
    ff_term = jnp.concatenate(
        [act_grad * ff_up * (sig + ff_gate * sig * (1.0 - sig)), act_grad * ff_gate * sig], axis=1
    ).astype(BF16)
    down_grad = dot(gout, activated, TN, BF16)
    ff_grad = dot(normed_two, ff_term, TN, BF16)
    normed_two_grad = dot(ff_term, ff_full, NT, BF16).reshape(shape)
    front = (hidden // 128 + 1) // 2 * 128
    back = hidden - front
    ff_plan = [
        (0, unit, 0, hidden, False), (0, unit, hidden, hidden, False), (1, unit, 0, front, False), (1, unit, front, back, False),
    ]
    residual_grad, low, second_part, gate_term, slot_part_grad, qkv_term, decay_term, gate_grad, up_grad, down_front, down_back = backward(
        size, 2, slot, ff_plan,
        (grad_out, gates, attended, normed_two_grad),
        (residual, second_full, out_full, qkv, decay, keep, slot_full, probs, scores, weights, states, decs,
         end_decs),
        (ff_grad, down_grad),
    )
    down_grad = jnp.concatenate([down_front[:, :front], down_back[:, :back], down_front[:, front:], down_back[:, back:]], axis=1)
    low = low.reshape(rows, width)
    out_grad = dot(low, gated, TN, BF16)
    forget_term = (decay_term * jax.nn.sigmoid(-logit) / TAU).astype(BF16)
    none = jnp.zeros_like(forget_term)
    gates_term = jnp.concatenate(
        [gate_term, jnp.where(x == 0, forget_term, none), jnp.where(x == 0, none, forget_term)], axis=1
    )
    qkv_grad = dot(normed_one, qkv_term, TN, BF16)
    gates_grad = dot(normed_one, gates_term, TN, BF16)
    bias_part = jnp.sum(forget_term.astype(F32), axis=0)
    which = jnp.arange(2 * heads_here) == heads_here * c + x
    bias_part = jnp.where(which[:, None], bias_part[None, :], 0.0).reshape(2 * heads_here, size, slot_part)

    def rows_of(array):
        array = array.reshape(size, -1)
        return jnp.pad(array, ((0, 0), (0, 128 - array.shape[1])))

    zero = jnp.zeros((size, 128), F32)
    packed = jnp.stack(
        [zero, rows_of(second_part), rows_of(slot_part_grad), rows_of(jnp.moveaxis(bias_part, 1, 0))] + [zero] * 4, axis=1
    )
    plan = [
        (0, unit, 0, head, False), (1, unit, 0, head, False), (1, unit, head, head, False), (1, unit, 2 * head, head, False),
        (2, unit, 0, head, False), (2, unit, head, 2 * slots, True),
    ]
    input_grad, output, sums, output_grad, query_grad, key_grad, value_grad, outgate_grad, forget_grad = last(
        size, 3, plan, (qkv_full, gate_full, down_full),
        (qkv_term, gates_term, activated, tokens, residual, residual_grad, first_full, packed),
        (out_grad, qkv_grad, gates_grad),
    )
    bias_grad = sums[3, : 2 * heads_here * slot_part].reshape(2, heads_here, slot_part)
    bias_grad = jnp.where(c == 0, bias_grad[0], bias_grad[1])
    return (
        output, input_grad, query_grad, key_grad, value_grad, forget_grad[0], bias_grad, outgate_grad, output_grad.T,
        sums[2, : head // size], sums[0, :unit], sums[1, :unit], gate_grad, up_grad, down_grad.T,
    )


def solution(mesh):
    row, column, vector, token = P("seq", "head"), P("head", "seq"), P("seq"), P(None, "seq", None)
    return jax.shard_map(
        shards,
        mesh=mesh,
        in_specs=(token, token, row, row, row, row, column, row, column, vector, vector, vector, row, row, column),
        out_specs=(token, token, row, row, row, row, column, row, column, vector, vector, vector, row, row, column),
        check_vma=False,
    )
```

```python
import functools

import jax
import jax.numpy as jnp
import numpy as np
from jax import lax
from jax.experimental import pallas as pl
from jax.experimental.pallas import tpu as pltpu
from jax.sharding import PartitionSpec as P

F32, BF16 = jnp.float32, jnp.bfloat16
MESH = pl.DeviceIdType.MESH
HBM = pltpu.HBM
EPS = 1e-06
TAU = 8.0


CHUNK = 256
NT = (((1,), (1,)), ((), ()))
NN = (((1,), (0,)), ((), ()))
TN = (((0,), (0,)), ((), ()))


def decay_tables(count):
    at = np.arange(count)
    paths, masks = [], []
    half = count // 2
    while half >= 1:
        block, second = at // (2 * half), (at // half) % 2 == 1
        edge = block * 2 * half + half - 1
        r, t = at[None, :], at[:, None]
        fore = second[:, None] & (r > edge[:, None]) & (r <= t)
        back = ~second[:, None] & (r > t) & (r <= edge[:, None])
        paths.append(fore | back)
        masks.append((block[:, None] == block[None, :]) & second[:, None] & ~second[None, :])
        half //= 2
    paths.append(at[None, :] <= at[:, None])
    paths.append(at[None, :] > at[:, None])
    return np.concatenate(paths, 0), np.stack(masks)


def bf(x):
    return x.astype(BF16)


def halves(x):
    hi = bf(x)
    return hi, bf(x - hi.astype(F32))


def mm(a, b, dims):
    return lax.dot_general(a, b, dims, preferred_element_type=F32)


def dot3(a, b, dims):
    return mm(a[0], b[0], dims) + (mm(a[0], b[1], dims) + mm(a[1], b[0], dims))


def exact_sums(table, x):
    hi, mid = halves(x)
    low = bf(x - hi.astype(F32) - mid.astype(F32))
    n = x.shape[1]
    both = mm(table, jnp.concatenate([hi, mid, low, jnp.zeros_like(low)], axis=1), NN)
    return both[:, :n] + (both[:, n : 2 * n] + both[:, 2 * n : 3 * n])


def silu(v):
    return v / (1.0 + jnp.exp(-v))


def sigmoid(v):
    return 1.0 / (1.0 + jnp.exp(-v))


def silu_slope(v):
    s = sigmoid(v)
    return s + v * s * (1.0 - s)


def columns_total(x):
    ones = jnp.ones((x.shape[0], 128), BF16)
    hi, mid = halves(x)
    low = bf(x - hi.astype(F32) - mid.astype(F32))
    return mm(hi, ones, TN) + (mm(mid, ones, TN) + mm(low, ones, TN))


def spread(column, width):
    return jnp.concatenate([column] * (width // 128), axis=1)


def mix(pair, ratios, keep, masks_ref, own):
    out = own * keep
    for l, ratio in enumerate(ratios):
        left = pair * masks_ref[l].astype(F32)
        out += ratio * dot3(halves(left), halves(ratio * keep), NN)
    return out


def unmix(probs, ratios, keep, masks_ref, diag):
    out = diag * jnp.sum(probs * keep, axis=1, keepdims=True)
    for l, ratio in enumerate(ratios):
        part = dot3(halves(probs * ratio), halves(ratio * keep), NT)
        out += masks_ref[l].astype(F32) * part
    return out


def on_diagonal(count):
    return (
        lax.broadcasted_iota(jnp.int32, (count, count), 0) == lax.broadcasted_iota(jnp.int32, (count, count), 1)
    ).astype(F32)


class Slots:
    def __init__(self, seqs, rows, head, slots, chunk):
        self.seqs, self.rows, self.head, self.slots, self.chunk = seqs, rows, head, slots, chunk
        self.chunks = rows // chunk
        paths, masks = decay_tables(chunk)
        self.levels = masks.shape[0]
        self.paths = jnp.asarray(paths, BF16)
        self.masks = jnp.asarray(masks, BF16)

class Place:
    def __init__(self, size):
        self.size = size
        self.line = size // 4
        s = lax.axis_index("seq")
        self.c = lax.axis_index("head")
        self.s = s
        self.x = lax.rem(s, 2)
        self.b = lax.rem(s // 2, 2)
        self.a = s // 4

    def at(self, a, b, x):
        return (a * 2 + b) * 2 + x

    def partner(self):
        return (self.at(self.a, self.b, 1 - self.x), self.c)

    def across(self):
        return (self.at(self.a, 1 - self.b, self.x), self.c)

    def up(self):
        return (self.at(jnp.minimum(self.a + 1, self.line - 1), self.b, self.x), self.c)

    def down(self):
        return (self.at(jnp.maximum(self.a - 1, 0), self.b, self.x), self.c)

    def sibling(self):
        return (self.s, 1 - self.c)

    def has_up(self):
        return self.a < self.line - 1

    def has_down(self):
        return self.a > 0


def signal(sem, device):
    pl.semaphore_signal(sem, inc=1, device_id=device, device_id_type=MESH)


def greet(place, partner=True, across=True, line=True, sibling=False):
    barrier = pltpu.get_barrier_semaphore()
    count = jnp.int32(0)
    if partner:
        signal(barrier, place.partner())
        count = count + 1
    if sibling:
        signal(barrier, place.sibling())
        count = count + 1
    if across:
        signal(barrier, place.across())
        count = count + 1
    if line:
        pl.when(place.has_up())(lambda: signal(barrier, place.up()))
        pl.when(place.has_down())(lambda: signal(barrier, place.down()))
        count = count + place.has_up().astype(jnp.int32) + place.has_down().astype(jnp.int32)
    pl.semaphore_wait(barrier, count)


def remote(src, dst, send, recv, device):
    return pltpu.make_async_remote_copy(
        src_ref=src, dst_ref=dst, send_sem=send, recv_sem=recv, device_id=device, device_id_type=MESH
    )


class Gather:
    def __init__(self, place, full, unit, pieces, sems, late=False):
        self.pl, self.full, self.unit, self.pieces, self.late = place, full, unit, pieces, late
        self.offset = min(offset for _, offset, _ in pieces)
        self.width = sum(width for _, _, width in pieces)
        self.x_sem, self.b_sem, self.up_sem, self.down_sem = sems

    def part(self, start, count, offset=None, width=None):
        offset, width = (self.offset, self.width) if width is None else (offset, width)
        rows = pl.ds(start * self.unit, count * self.unit)
        if width == self.full.shape[1]:
            return self.full.at[rows]
        return self.full.at[rows, pl.ds(offset, width)]

    def mine(self, i, x):
        shard, _, width = self.pieces[i]
        if shard.shape[1] == width:
            return shard
        return shard.at[:, pl.ds(x * width, width)]

    def x_copy(self, i):
        p = self.pl
        _, offset, width = self.pieces[i]
        here = self.part(p.s, 1, offset, width)
        return remote(self.mine(i, 1 - p.x), here, self.x_sem.at[0, i], self.x_sem.at[1, i], p.partner())

    def own_copy(self, i):
        _, offset, width = self.pieces[i]
        return pltpu.make_async_copy(self.mine(i, self.pl.x), self.part(self.pl.s, 1, offset, width), self.x_sem.at[2, i])

    def block(self, a):
        p = self.pl
        if self.late:
            return self.part(4 * a, 4)
        return self.part(4 * a + 2 * p.b, 2)

    def b_copy(self, i, a):
        p = self.pl
        return remote(
            self.part(4 * a + 2 * p.b, 2), self.part(4 * a + 2 * p.b, 2),
            self.b_sem.at[0, i], self.b_sem.at[1, i], p.across(),
        )

    def line_copy(self, way, h):
        p = self.pl
        if way == "up":
            blk = self.block(jnp.maximum(p.a - (h - 1), 0))
            return remote(blk, blk, self.up_sem.at[0, h - 1], self.up_sem.at[1, h - 1], p.up())
        blk = self.block(jnp.minimum(p.a + (h - 1), p.line - 1))
        return remote(blk, blk, self.down_sem.at[0, h - 1], self.down_sem.at[1, h - 1], p.down())

    def sends(self, way, h):
        p = self.pl
        if way == "up":
            return jnp.logical_and(p.has_up(), p.a - (h - 1) >= 0)
        return jnp.logical_and(p.has_down(), p.a + (h - 1) <= p.line - 1)

    def gets(self, way, h):
        p = self.pl
        if way == "up":
            return p.a - h >= 0
        return p.a + h <= p.line - 1

    def got(self, way, h):
        p = self.pl
        if way == "up":
            return jnp.maximum(p.a - h, 0)
        return jnp.minimum(p.a + h, p.line - 1)

    def slot(self, way, h):
        return h if way == "up" else self.pl.line - 1 + h

    def start_x(self):
        for i in range(len(self.pieces)):
            self.x_copy(i).start()
            self.own_copy(i).start()

    def stage(self, h):
        p = self.pl
        if h == 0:
            for i in range(len(self.pieces)):
                self.own_copy(i).wait()
                self.x_copy(i).wait_recv()
            if self.late:
                self.b_copy(0, p.a).start()
            else:
                for way in ("up", "down"):
                    pl.when(self.sends(way, 1))(lambda way=way: self.line_copy(way, 1).start())
                self.b_copy(0, p.a).start()
            return
        if self.late:
            if h == 1:
                self.b_copy(0, p.a).wait_recv()
                for way in ("up", "down"):
                    pl.when(self.sends(way, 1))(lambda way=way: self.line_copy(way, 1).start())
                return
            h = h - 1
        for way in ("up", "down"):

            def go(way=way):
                self.line_copy(way, h).wait_recv()
                if not self.late:
                    self.b_copy(self.slot(way, h), self.got(way, h)).start()

            def on(way=way):
                self.line_copy(way, h + 1).start()

            pl.when(self.gets(way, h))(go)
            if h + 1 <= p.line - 1:
                pl.when(self.sends(way, h + 1))(on)

    def stages(self):
        return self.pl.line + (1 if self.late else 0)

    def finish(self):
        p = self.pl
        for i in range(len(self.pieces)):
            self.x_copy(i).wait_send()
        self.b_copy(0, p.a).wait_send()
        if not self.late:
            self.b_copy(0, p.a).wait_recv()
        for way in ("up", "down"):
            for h in range(1, p.line):
                pl.when(self.sends(way, h))(lambda way=way, h=h: self.line_copy(way, h).wait_send())
                if not self.late:

                    def both(way=way, h=h):
                        cp = self.b_copy(self.slot(way, h), self.got(way, h))
                        cp.wait_send()
                        cp.wait_recv()

                    pl.when(self.gets(way, h))(both)


def gather_sems(line, pieces):
    return [
        pltpu.SemaphoreType.DMA((3, pieces)),
        pltpu.SemaphoreType.DMA((2, 2 * line - 1)),
        pltpu.SemaphoreType.DMA((2, line - 1)),
        pltpu.SemaphoreType.DMA((2, line - 1)),
    ]


def gathers_of(place, plan, shards, fulls, sems):
    work, at = [], 0
    for n, (i, unit, columns) in enumerate(plan):
        pieces = [(shards[at + m], offset, width) for m, (offset, width) in enumerate(columns)]
        at += len(columns)
        work.append(Gather(place, fulls[i], unit, pieces, sems[4 * n : 4 * n + 4]))
    return work


def gather_ops(gathers, pace):
    order = sorted((k * pace + h, k, h) for k, g in enumerate(gathers) for h in range(g.stages()))
    steps = [functools.partial(gathers[k].stage, h) for _, k, h in order]
    return steps + [g.finish for g in gathers]

VM = pl.BlockSpec(memory_space=pltpu.VMEM)
ANY = pl.BlockSpec(memory_space=HBM)


def remote_params(number, mib=56):
    return pltpu.CompilerParams(collective_id=number, has_side_effects=True, vmem_limit_bytes=mib * 2**20)


STRIPS = 4


class Fold:
    def __init__(self, place, part, sib, sent, came, sems, own=None):
        self.p, self.part, self.sib, self.sent, self.came = place, part, sib, sent, came
        self.own = part.at[place.c] if own is None else own
        self.s_sem, self.x_sem = sems
        self.rows = part.shape[2] // STRIPS

    def strip(self, r):
        return pl.ds(r * self.rows, self.rows)

    def sib_copy(self, far, r):
        p = self.p
        x = 1 - p.x if far else p.x
        i = (0 if far else STRIPS) + r
        return remote(
            self.part.at[1 - p.c, x, self.strip(r)], self.sib.at[1 if far else 0, self.strip(r)],
            self.s_sem.at[0, i], self.s_sem.at[1, i], p.sibling(),
        )

    def x_copy(self, r):
        return remote(
            self.sent.at[self.strip(r)], self.came.at[self.strip(r)], self.x_sem.at[0, r], self.x_sem.at[1, r], self.p.partner()
        )

    def start(self):
        for r in range(STRIPS):
            self.sib_copy(True, r).start()
        for r in range(STRIPS):
            self.sib_copy(False, r).start()

    def sib_all(self, far):
        for r in range(STRIPS):
            self.sib_copy(far, r).start()

    def cross(self, r):
        p = self.p
        self.sib_copy(True, r).wait_recv()
        own = self.own[1 - p.x, self.strip(r)].astype(F32)
        self.sent[self.strip(r)] = bf(own + self.sib[1, self.strip(r)].astype(F32))
        self.x_copy(r).start()

    def total(self, r):
        p = self.p
        self.sib_copy(False, r).wait_recv()
        self.x_copy(r).wait_recv()
        own = self.own[p.x, self.strip(r)].astype(F32) + self.sib[0, self.strip(r)].astype(F32)
        return own + self.came[self.strip(r)].astype(F32)

    def finish(self):
        for r in range(STRIPS):
            self.sib_copy(True, r).wait_send()
            self.sib_copy(False, r).wait_send()
            self.x_copy(r).wait_send()


def fold_scratch(rows, width):
    return [
        pltpu.VMEM((2, rows, width), BF16), pltpu.VMEM((rows, width), BF16), pltpu.VMEM((rows, width), BF16),
        pltpu.SemaphoreType.DMA((2, 2 * STRIPS)), pltpu.SemaphoreType.DMA((2, STRIPS)),
    ]


class Share:
    def __init__(self, place, out, sems):
        self.p, self.out = place, out
        self.x_sem, self.s_sem = sems
        self.rows = out.shape[2] // STRIPS

    def strip(self, r):
        return pl.ds(r * self.rows, self.rows)

    def x_copy(self, r):
        p = self.p
        block = self.out.at[p.c, p.x, self.strip(r)]
        return remote(block, block, self.x_sem.at[0, r], self.x_sem.at[1, r], p.partner())

    def s_copy(self, far, r):
        p = self.p
        block = self.out.at[p.c, 1 - p.x if far else p.x, self.strip(r)]
        i = (0 if far else STRIPS) + r
        return remote(block, block, self.s_sem.at[0, i], self.s_sem.at[1, i], p.sibling())

    def put(self, r, value):
        self.out[self.p.c, self.p.x, self.strip(r)] = value
        self.x_copy(r).start()
        self.s_copy(False, r).start()

    def forward(self, r):
        self.x_copy(r).wait_recv()
        self.s_copy(True, r).start()

    def wait_sibling(self, far):
        for r in range(STRIPS):
            self.s_copy(far, r).wait_recv()

    def finish(self, receive=True):
        for r in range(STRIPS):
            self.x_copy(r).wait_send()
            for far in (False, True):
                self.s_copy(far, r).wait_send()
                if receive:
                    self.s_copy(far, r).wait_recv()


SHARE_SEMS = [pltpu.SemaphoreType.DMA((2, STRIPS)), pltpu.SemaphoreType.DMA((2, 2 * STRIPS))]


def inverse_rms(values):
    return lax.rsqrt(jnp.mean(values * values, axis=-1, keepdims=True) + EPS)


def norm_back(grad, values, gain):
    scale = inverse_rms(values)
    u = grad * gain
    down = scale * u - values * (scale * scale * scale) * jnp.mean(u * values, axis=-1, keepdims=True)
    return down, jnp.sum(grad * values * scale, axis=0, keepdims=True)


def ends_chunk(k, v, decay, keep, tail):
    weight = halves(jnp.exp(exact_sums(tail, decay)) * keep)
    unit_k = dot3(weight, halves(silu(k.astype(F32))), TN)
    unit_v = mm(weight[0], v, TN) + mm(weight[1], v, TN)
    return jnp.concatenate([unit_k, unit_v], axis=1), jnp.exp(columns_total(decay))


def powers_of(table, count, levels, decay):
    powers = jnp.exp(exact_sums(table, decay))
    return [powers[l * count : (l + 1) * count] for l in range(levels)], [
        powers[l * count : (l + 1) * count] for l in range(levels, table.shape[0] // count)
    ]


class Prefix:
    def __init__(self, place, back, own, dec, start, peer, peer_dec, line, out, sems):
        p = self.p = place
        self.own, self.dec, self.start_ref, self.peer, self.peer_dec = own, dec, start, peer, peer_dec
        self.line, self.out = line, out
        self.p_sem, self.d_sem, self.l_sem = sems
        seqs, slots, width = own.shape
        self.half = width // 2
        self.pieces = [(b, h) for b in range(seqs) for h in range(2)]
        if back:
            self.has_prev, self.has_next, self.after = p.has_up(), p.has_down(), p.down()
        else:
            self.has_prev, self.has_next, self.after = p.has_down(), p.has_up(), p.up()
        self.first = ((p.b == 1) if back else (p.b == 0)).astype(F32)

    def cut(self, ref, i):
        b, h = self.pieces[i]
        return ref.at[b, :, pl.ds(h * self.half, self.half)]

    def peer_copy(self, i):
        return remote(self.cut(self.own, i), self.cut(self.peer, i), self.p_sem.at[0, i], self.p_sem.at[1, i], self.p.across())

    def line_copy(self, i):
        return remote(self.cut(self.out, i), self.cut(self.line, i), self.l_sem.at[0, i], self.l_sem.at[1, i], self.after)

    def dec_copy(self):
        return remote(self.dec, self.peer_dec, self.d_sem.at[0], self.d_sem.at[1], self.p.across())

    def start(self):
        self.dec_copy().start()
        for i in range(len(self.pieces)):
            self.peer_copy(i).start()

    def run(self):
        self.dec_copy().wait_recv()
        for i, (b, _) in enumerate(self.pieces):
            self.peer_copy(i).wait_recv()
            dec_own = spread(self.dec[b], self.half)
            dec_peer = spread(self.peer_dec[b], self.half)
            own, other = self.cut(self.own, i)[...], self.cut(self.peer, i)[...]
            first = self.first
            both = first * (dec_peer * own + other) + (1.0 - first) * (dec_own * other + own)
            here, result = self.cut(self.out, i), self.cut(self.start_ref, i)

            def go_on(i=i):
                self.line_copy(i).wait_recv()
                came = self.cut(self.line, i)[...]
                here[...] = dec_own * dec_peer * came + both
                result[...] = first * came + (1.0 - first) * (dec_peer * came + other)

            def begin():
                here[...] = both
                result[...] = (1.0 - first) * other

            pl.when(self.has_prev)(go_on)
            pl.when(jnp.logical_not(self.has_prev))(begin)
            pl.when(self.has_next)(lambda i=i: self.line_copy(i).start())

    def finish(self):
        self.dec_copy().wait_send()
        for i in range(len(self.pieces)):
            self.peer_copy(i).wait_send()
            pl.when(self.has_next)(lambda i=i: self.line_copy(i).wait_send())


def prefix_scratch(seqs, slots, width):
    count = 2 * seqs
    return [
        pltpu.VMEM((seqs, slots, width), F32), pltpu.VMEM((seqs, slots, width), F32), pltpu.VMEM((seqs, slots, 128), F32),
        pltpu.VMEM((seqs, slots, width), F32), pltpu.VMEM((seqs, slots, width), F32),
        pltpu.SemaphoreType.DMA((2, count)), pltpu.SemaphoreType.DMA((2,)), pltpu.SemaphoreType.DMA((2, count)),
    ]


def take(refs, count):
    return refs[:count], refs[count:]


class Weave:
    def __init__(self, steps):
        self.steps = list(steps)

    def run(self, count):
        for step in self.steps[:count]:
            step()
        self.steps = self.steps[count:]

    def rest(self):
        self.run(len(self.steps))


def blocks_in_order(p, seqs):
    def block(i):
        b = jnp.where(i < 2, 1 - p.c, p.c)
        x = jnp.where(lax.rem(i, 2) == 0, 1 - p.x, p.x)
        return b, x

    return block


PACE = 1.5
FORE_STEPS = (0, 6, 1, 1, 0, 2, 0, 2)


def forward_kernel(size, plan, levels, *refs):
    p = Place(size)
    (qkv, gates, decay, keep, gain, out_w, tokens, gain2, paths, masks, grad_out), refs = take(refs, 11)
    shard_refs, refs = take(refs, sum(len(columns) for _, _, columns in plan))
    (gated, attended, probs, scores, weights, states, decs, end_dec, residual, normed, grads, ff), refs = take(refs, 12)
    fulls, refs = take(refs, max(i for i, _, _ in plan) + 1)
    (units, part, total), refs = take(refs, 3)
    (start, *prefix_refs), refs = take(refs, 8)
    fold_refs, refs = take(refs, 5)
    share_sems, refs = take(refs, 2)
    (swap_sem, ff_w, ff_tile, ff_sem), refs = take(refs, 4)
    count = paths.shape[1]
    head = gated.shape[1]
    seqs = tokens.shape[0]
    slots = keep.shape[1]
    greet(p, sibling=True)
    work = gathers_of(p, plan, shard_refs, fulls, refs)
    for gathered in work:
        gathered.start_x()
    weave = Weave(gather_ops(work, PACE)[: -len(work)])
    weave.run(FORE_STEPS[0])
    tail = paths[(levels + 1) * count :, :]

    def ends(b):
        for j in range(2):
            rows = pl.ds((b * 2 + j) * count, count)
            unit, dec = ends_chunk(
                qkv[rows, head : 2 * head], qkv[rows, 2 * head :], decay[rows, :], keep[rows, :], tail
            )
            units[b, j] = unit
            decs[b, j] = dec
        total[b] = spread(dec, 2 * head) * units[b, 0] + unit
        end_dec[b] = decs[b, 0] * dec

    for b in range(seqs):
        ends(b)
    carry = Prefix(p, False, total, end_dec, start, *prefix_refs[:4], prefix_refs[4:])
    carry.start()
    weave.run(FORE_STEPS[1])
    move = Swap(p, grad_out, grads, swap_sem)
    move.start()
    carry.run()
    for b in range(seqs):
        states[3 * b] = start[b]
        for j in range(2):
            states[3 * b + j + 1] = spread(decs[b, j], 2 * head) * states[3 * b + j] + units[b, j]
    weave.run(FORE_STEPS[2])
    diag = on_diagonal(count)
    order = blocks_in_order(p, seqs)
    fold = Fold(p, part, *fold_refs[:3], fold_refs[3:])
    share = Share(p, normed, share_sems)

    def attend(i, nothing):
        b, j = order(i)
        rows = pl.ds(pl.multiple_of((b * 2 + j) * count, count), count)
        here = keep[rows, :]
        ratios, (growth,) = powers_of(paths[: (levels + 1) * count, :], count, levels, decay[rows, :])
        query = halves(silu(qkv[rows, :head].astype(F32)) * head ** (-0.5))
        keys = halves(silu(qkv[rows, head : 2 * head].astype(F32)))
        state = states[3 * b + j]
        pair = dot3(query, keys, NT)
        score = mix(pair, ratios, here, masks, jnp.sum(pair * diag, axis=1, keepdims=True))
        score += growth * dot3(query, halves(state[:, :head]), NT)
        raised = jnp.exp(score - jnp.max(score, axis=1, keepdims=True))
        prob = raised / jnp.sum(raised, axis=1, keepdims=True)
        weight = unmix(prob, ratios, here, masks, diag)
        values = qkv[rows, 2 * head :]
        whi, wlo = halves(weight)
        result = mm(whi, values, NN) + mm(wlo, values, NN)
        result += dot3(halves(prob * growth), halves(state[:, head:]), NN)
        scale = lax.rsqrt(jnp.mean(result * result, axis=1, keepdims=True) + EPS)
        low = bf(result * scale * gain[...] * silu(gates[rows, :head]))
        gated[rows, :] = low
        attended[rows, :] = result
        probs[rows, :] = prob
        scores[rows, :] = score
        weights[rows, :] = weight
        part[b, j] = bf(mm(low, out_w[...], NT))
        pl.when(i == 0)(lambda: fold.sib_all(True))
        pl.when(i == 1)(lambda: fold.sib_all(False))
        return nothing

    lax.fori_loop(0, 2, attend, 0)
    weave.run(FORE_STEPS[3])
    lax.fori_loop(2, 3, attend, 0)
    for r in range(STRIPS):
        fold.cross(r)
    weave.run(FORE_STEPS[4])
    move.forward()
    lax.fori_loop(3, 4, attend, 0)
    weave.run(FORE_STEPS[5])
    for r in range(STRIPS):
        value = tokens[p.c, fold.strip(r)].astype(F32) + fold.total(r)
        residual[fold.strip(r)] = value
        share.put(r, bf(value * inverse_rms(value) * gain2[...]))
        if r == 1:
            weave.run(FORE_STEPS[6])
    weave.run(FORE_STEPS[7])
    for r in range(STRIPS):
        share.forward(r)
    share.finish()

    def complete(gathered):
        while any(step.func.__self__ is gathered for step in weave.steps):
            weave.run(1)
        gathered.finish()

    columns = ff_w.shape[2]
    tiles = ff.shape[1] // columns
    up_from = (ff.shape[1] // 2) // columns

    def load(t):
        return pltpu.make_async_copy(fulls[0].at[:, pl.ds(t * columns, columns)], ff_w.at[t % 2], ff_sem.at[0, t % 2])

    def store(t):
        return pltpu.make_async_copy(ff_tile.at[t % 2], ff.at[:, pl.ds(t * columns, columns)], ff_sem.at[1, t % 2])

    complete(work[0])
    load(0).start()
    for t in range(tiles):
        load(t).wait()
        if t + 1 == up_from:
            complete(work[1])
        if t + 1 < tiles:
            load(t + 1).start()
        if t >= 2:
            store(t - 2).wait()

        def product(i, nothing, t=t):
            b, x = i // 2, lax.rem(i, 2)
            rows = pl.ds(pl.multiple_of(i * count, count), count)
            ff_tile[t % 2, rows, :] = mm(normed[b, x], ff_w[t % 2], NN)
            return nothing

        lax.fori_loop(0, 2 * seqs, product, 0)
        store(t).start()
    weave.rest()
    work[2].finish()
    store(tiles - 2).wait()
    store(tiles - 1).wait()
    fold.finish()
    carry.finish()
    move.finish()


def forward(size, number, slot, plan, fulls, qkv, gates, decay, keep, gain, out_w, tokens, gain2, grad_out, shards):
    seqs, block, width = tokens.shape
    h, m, n, rows = slot.head, slot.slots, slot.chunks, slot.seqs * slot.rows
    shape = jax.ShapeDtypeStruct
    outs = [
        shape((rows, h), BF16), shape((rows, h), F32), shape((rows, m), F32), shape((rows, m), F32), shape((rows, slot.chunk), F32),
        shape((seqs * (n + 1), m, 2 * h), F32), shape((seqs, n, m, 128), F32), shape((seqs, m, 128), F32),
        shape((block, width), F32), shape((seqs, 2, block, width), BF16), shape((seqs, 2, block, width), BF16),
        shape((rows, fulls[0][1]), F32),
    ]
    tile = 256
    scratch = [
        pltpu.VMEM((seqs, n, m, 2 * h), F32), pltpu.VMEM((seqs, 2, block, width), BF16), pltpu.VMEM((seqs, m, 2 * h), F32),
    ]
    scratch += prefix_scratch(seqs, m, 2 * h) + fold_scratch(block, width) + SHARE_SEMS + [pltpu.SemaphoreType.DMA((5,))]
    scratch += [pltpu.VMEM((2, width, tile), BF16), pltpu.VMEM((2, rows, tile), F32), pltpu.SemaphoreType.DMA((2, 2))]
    for _, _, columns in plan:
        scratch += gather_sems(size // 4, len(columns))
    return pl.pallas_call(
        functools.partial(forward_kernel, size, plan, slot.levels),
        out_shape=outs + [shape(full, BF16) for full in fulls],
        in_specs=[VM] * 10 + [ANY] * (1 + len(shards)),
        out_specs=[VM] * 10 + [ANY] * (2 + len(fulls)),
        scratch_shapes=scratch,
        compiler_params=remote_params(number, 60),
        name="attend_forward",
    )(qkv, gates, decay, keep, gain, out_w, tokens, gain2, slot.paths, slot.masks, grad_out, *shards)

class Pool:
    def __init__(self, refs):
        self.loads, self.extra, self.sends, self.totals, self.sems = refs

    def slot(self, which, slot):
        return self.extra if slot == 3 else self.loads.at[which, slot]


POOL_SENDS = 2
AHEAD = 3
LAG = 3


def pool_scratch(rows, width):
    return [
        pltpu.VMEM((2, 3, rows, width), BF16), pltpu.VMEM((rows, width), BF16), pltpu.VMEM((POOL_SENDS, rows, width), BF16),
        pltpu.VMEM((rows, width), F32),
        pltpu.SemaphoreType.DMA((2, 4)),
    ]


class Scatter:
    def __init__(self, place, grad, out, peer, line, unit, offset, width, sems):
        self.p, self.grad, self.out, self.peer, self.line = place, grad, out, peer, line
        self.unit, self.offset, self.width = unit, offset, width
        self.whole = out.shape[-1] == width
        self.b_sem, self.l_sem, self.x_sem = sems

    def goal(self, n):
        p = self.p
        low, high = p.a, p.line - 1 - p.a
        more, less = jnp.maximum(low, high), jnp.minimum(low, high)
        alone = more - less
        up_more = jnp.where(high >= low, 1, -1)
        m = n - alone
        early = n < alone
        reach = jnp.where(early, more - n, less - m // 2)
        side = jnp.where(early, up_more, jnp.where(lax.rem(jnp.maximum(m, 0), 2) == 0, 1, -1))
        return p.a + side * reach

    def block(self, a, b):
        rows = pl.ds((4 * a + 2 * b) * self.unit, 2 * self.unit)
        if self.width == self.grad.shape[1]:
            return self.grad.at[rows]
        return self.grad.at[rows, pl.ds(self.offset, self.width)]

    def b_copy(self, a):
        return remote(self.block(a, 1 - self.p.b), self.peer.at[a], self.b_sem.at[0, a], self.b_sem.at[1, a], self.p.across())

    def start(self, n):
        self.b_copy(self.goal(n)).start()

    def cut(self, ref):
        return ref if self.width == ref.shape[1] else ref.at[:, pl.ds(0, self.width)]

    def load(self, pool, which, slot, source):
        return pltpu.make_async_copy(source, self.cut(pool.slot(which, slot)), pool.sems.at[which, slot])

    def prepare(self, pool, which, n):
        d = self.goal(n)
        self.b_copy(d).wait_recv()
        self.load(pool, which, 0, self.block(d, self.p.b)).start()
        self.load(pool, which, 1, self.peer.at[d]).start()

    def loaded(self, pool, which, n):
        d = self.goal(n)
        self.load(pool, which, 0, self.block(d, self.p.b)).wait()
        self.load(pool, which, 1, self.peer.at[d]).wait()

    def strips(self, do):
        rows = 2 * self.unit
        step = max(r for r in (16, 32, 64, 128) if rows % r == 0 and (r == 16 or r * self.width <= 64 * 1024))

        def one(i, carry):
            do(pl.ds(pl.multiple_of(i * step, step), step))
            return carry

        lax.fori_loop(0, rows // step, one, 0)

    def bring(self, pool, which, slot, place):
        remote(self.line.at[place], self.line.at[place], self.l_sem.at[0, 0], self.l_sem.at[1, place], self.p.across()).wait_recv()
        self.load(pool, which, slot, self.line.at[place]).start()

    def send(self, pool, out, n):
        p = self.p
        d = self.goal(n)
        up = d > p.a
        to = jnp.clip(p.a + jnp.where(up, 1, -1), 0, p.line - 1)
        slot = jnp.where(jnp.logical_and(jnp.logical_not(up), d == p.a - 1), p.line, d)
        return remote(
            self.cut(pool.sends.at[out]), self.line.at[slot], self.l_sem.at[0, n], self.l_sem.at[1, slot], (p.at(to, p.b, p.x), p.c)
        )

    def hop(self, pool, which, n, out):
        p = self.p
        d = self.goal(n)
        behind = jnp.logical_or(jnp.logical_and(d > p.a, p.has_down()), jnp.logical_and(d < p.a, p.has_up()))
        pl.when(behind)(lambda: self.bring(pool, which, 2, d))
        self.loaded(pool, which, n)
        a, b, c = (self.cut(pool.slot(which, i)) for i in range(3))
        to = self.cut(pool.sends.at[out])

        def with_line():
            self.load(pool, which, 2, self.line.at[d]).wait()

            def do(rows):
                to[rows] = bf(a[rows].astype(F32) + b[rows].astype(F32) + c[rows].astype(F32))

            self.strips(do)

        def without():
            def do(rows):
                to[rows] = bf(a[rows].astype(F32) + b[rows].astype(F32))

            self.strips(do)

        pl.when(behind)(with_line)
        pl.when(jnp.logical_not(behind))(without)
        self.send(pool, out, n).start()

    def last(self, pool, which):
        p = self.p
        n = p.line - 1
        pl.when(p.has_down())(lambda: self.bring(pool, which, 2, p.a))
        pl.when(p.has_up())(lambda: self.bring(pool, which, 3, p.line))
        self.loaded(pool, which, n)
        a, b, c, d = (self.cut(pool.slot(which, i)) for i in range(4))
        to = self.total = self.cut(pool.totals)

        def first(rows):
            to[rows] = a[rows].astype(F32) + b[rows].astype(F32)

        self.strips(first)

        def more(slot, place, ref):
            def go():
                self.load(pool, which, slot, self.line.at[place]).wait()

                def do(rows):
                    to[rows] = to[rows] + ref[rows].astype(F32)

                self.strips(do)

            return go

        pl.when(p.has_down())(more(2, p.a, c))
        pl.when(p.has_up())(more(3, p.line, d))
        self.x_copy().start()
        if not self.whole:
            self.out_copy().start()

    def half(self, x):
        return self.total.at[pl.ds(x * self.unit, self.unit)]

    def place(self):
        return self.out.at[:, pl.ds(self.p.x * self.width, self.width)]

    def x_copy(self):
        p = self.p
        where = self.out.at[1] if self.whole else self.place()
        return remote(self.half(1 - p.x), where, self.x_sem.at[0], self.x_sem.at[1], p.partner())

    def out_copy(self):
        return pltpu.make_async_copy(self.half(self.p.x), self.place(), self.x_sem.at[2])

    def sent(self):
        self.x_copy().wait_send()
        if not self.whole:
            self.out_copy().wait()

    def finish(self):
        p = self.p
        self.x_copy().wait_recv()
        if self.whole:
            self.out[0] = self.out[1] + self.half(p.x)[...]
        for n in range(p.line):
            self.b_copy(self.goal(n)).wait_send()


def scatter_sems(line):
    return [pltpu.SemaphoreType.DMA((2, line)), pltpu.SemaphoreType.DMA((2, line + 1)), pltpu.SemaphoreType.DMA((3,))]


def scatter_ops(work, pool):
    lines = work[0].p.line
    jobs = [(k * (lines - 1) + n, k, n) for k in range(len(work)) for n in range(lines - 1)]
    jobs += [((k + 1) * (lines - 1) - 0.5 + LAG, k, lines - 1) for k in range(len(work))]
    jobs = [(k, n) for _, k, n in sorted(jobs)]
    sends, totals = [], []

    def begin():
        for k, n in jobs[:AHEAD]:
            work[k].start(n)


    def job(i):
        k, n = jobs[i]

        def step():
            work[k].prepare(pool, i % 2, n)
            if i + AHEAD < len(jobs):
                work[jobs[i + AHEAD][0]].start(jobs[i + AHEAD][1])
            if n < lines - 1:
                out = len(sends) % POOL_SENDS
                if len(sends) >= POOL_SENDS:
                    ok, on, oo = sends[-POOL_SENDS]
                    work[ok].send(pool, oo, on).wait_send()
                work[k].hop(pool, i % 2, n, out)
                sends.append((k, n, out))
            else:
                if totals:
                    work[totals[-1]].sent()
                work[k].last(pool, i % 2)
                totals.append(k)

        return step

    steps = [begin] + [job(i) for i in range(len(jobs))]

    def finish():
        for ok, on, oo in sends[-POOL_SENDS:]:
            work[ok].send(pool, oo, on).wait_send()
        work[totals[-1]].sent()
        for chunk in work:
            chunk.finish()

    steps.append(finish)
    return steps

BACK_STEPS = (0, 0, 1, 0, 2, 0, 0, 2, 2, 1, 4, 0)


def backward_kernel(size, plan, levels, *refs):
    p = Place(size)
    (grad_out_all, gates_all, attended, grad_part), refs = take(refs, 4)
    (residual, gain2, out_w, qkv, decay, keep, gain, probs, scores, weights, states, decs,
     end_dec, paths, later, masks), refs = take(refs, 16)
    grads = max(i for i, _, _, _, _ in plan) + 1
    grad_refs, refs = take(refs, grads)
    (residual_grad, low, second_part, gate_term, gain_part, term, decay_term), refs = take(refs, 7)
    outs, refs = take(refs, len(plan))
    spaces, refs = take(refs, 2 * len(plan))
    (grad_out, gates, own_part, own_sem, att_grad, dprobs, dscores, units, adjoints, total), refs = take(refs, 10)
    (ending, *prefix_refs), refs = take(refs, 8)
    fold_refs, refs = take(refs, 5)
    share_sems, refs = take(refs, 2)
    pool_refs, refs = take(refs, 5)
    count = paths.shape[1]
    head = gate_term.shape[1]
    seqs = grad_out_all.shape[0]
    own = [
        pltpu.make_async_copy(grad_out_all.at[p.c], grad_out, own_sem.at[0]),
        pltpu.make_async_copy(gates_all.at[:, pl.ds(0, head)], gates, own_sem.at[1]),
        pltpu.make_async_copy(attended, att_grad, own_sem.at[2]),
        pltpu.make_async_copy(grad_part.at[p.c], own_part, own_sem.at[3]),
    ]
    for copy in own:
        copy.start()
    greet(p, sibling=True)
    pool = Pool(pool_refs)
    work = []
    for n, (i, unit, offset, width, _) in enumerate(plan):
        work.append(
            Scatter(p, grad_refs[i], outs[n], spaces[2 * n], spaces[2 * n + 1], unit, offset, width, refs[3 * n : 3 * n + 3])
        )
    weave = Weave(scatter_ops(work, pool))
    fold = Fold(p, grad_part, *fold_refs[:3], fold_refs[3:], own_part)
    share = Share(p, low, share_sems)
    fold.start()
    weave.run(1 + BACK_STEPS[0])
    own[3].wait()
    for r in range(STRIPS):
        fold.cross(r)
    weave.run(BACK_STEPS[1])
    own[0].wait()
    gains = jnp.zeros((1, grad_part.shape[3]), F32)
    for r in range(STRIPS):
        down, more = norm_back(fold.total(r), residual[fold.strip(r)], gain2[...])
        value = grad_out[fold.strip(r)].astype(F32) + down
        gains += more
        residual_grad[fold.strip(r)] = value
        share.put(r, bf(value))
        if r == 1:
            weave.run(BACK_STEPS[2])
    second_part[...] = gains
    weave.run(BACK_STEPS[3])
    diag = on_diagonal(count)
    gain_part[...] = jnp.zeros_like(gain_part)

    def place(i):
        b = jnp.where(lax.rem(i, 2) == 0, p.c, 1 - p.c)
        x = jnp.where(i < 2, p.x, 1 - p.x)
        return b, x

    def first(i, nothing):
        b, j = place(i)
        rows = pl.ds(pl.multiple_of((b * 2 + j) * count, count), count)
        grad = mm(low[b, j], out_w[...], NN)
        gate = gates[rows, :]
        value = att_grad[rows, :]
        scale = lax.rsqrt(jnp.mean(value * value, axis=1, keepdims=True) + EPS)
        normed = value * scale
        weighted = grad * silu(gate)
        gate_term[rows, :] = bf(grad * normed * gain[...] * silu_slope(gate))
        gain_part[...] += jnp.sum(weighted * normed, axis=0, keepdims=True)
        c = weighted * gain[...]
        agrad = scale * c - value * (scale * scale * scale) * jnp.mean(c * value, axis=1, keepdims=True)
        att_grad[rows, :] = agrad
        here = keep[rows, :]
        ratios, (growth,) = powers_of(paths[: (levels + 1) * count, :], count, levels, decay[rows, :])
        ahalf = halves(agrad)
        values = qkv[rows, 2 * head :]
        pair = mm(ahalf[0], values, NT) + mm(ahalf[1], values, NT)
        state = states[3 * b + j]
        dprob = mix(pair, ratios, here, masks, jnp.sum(pair * diag, axis=1, keepdims=True))
        dprob += growth * dot3(ahalf, halves(state[:, head:]), NT)
        prob = probs[rows, :]
        dscore = prob * (dprob - jnp.sum(prob * dprob, axis=1, keepdims=True))
        query = halves(silu(qkv[rows, :head].astype(F32)) * head ** (-0.5))
        dprobs[rows, :] = dprob
        dscores[rows, :] = dscore
        unit_k = dot3(halves(growth * dscore), query, TN)
        unit_v = dot3(halves(growth * prob), ahalf, TN)
        units[b, j] = jnp.concatenate([unit_k, unit_v], axis=1)
        return nothing

    own[1].wait()
    own[2].wait()
    lax.fori_loop(0, 1, first, 0)
    weave.run(BACK_STEPS[4])
    for r in range(STRIPS):
        share.forward(r)
    share.wait_sibling(False)
    lax.fori_loop(1, 3, first, 0)
    weave.run(BACK_STEPS[5])
    share.wait_sibling(True)
    lax.fori_loop(3, 4, first, 0)
    weave.run(BACK_STEPS[6])
    for b in range(seqs):
        total[b] = spread(decs[b, 0], 2 * head) * units[b, 1] + units[b, 0]
    carry = Prefix(p, True, total, end_dec, ending, *prefix_refs[:4], prefix_refs[4:])
    carry.start()
    weave.run(BACK_STEPS[7])
    carry.run()
    for b in range(seqs):
        adjoints[b, 1] = ending[b]
        adjoints[b, 0] = spread(decs[b, 1], 2 * head) * ending[b] + units[b, 1]
    is_last = (lax.broadcasted_iota(jnp.int32, (count, 1), 0) == count - 1).astype(F32)

    def second(i, nothing):
        for k in range(4):
            pl.when(i == k)(functools.partial(weave.run, BACK_STEPS[8 + k]))
        b, j = place(i)
        rows = pl.ds(pl.multiple_of((b * 2 + j) * count, count), count)
        here = keep[rows, :]
        ratios, (growth, rest) = powers_of(paths[...], count, levels, decay[rows, :])
        qraw = qkv[rows, :head].astype(F32)
        kraw = qkv[rows, head : 2 * head].astype(F32)
        query = halves(silu(qraw) * head ** (-0.5))
        keys = halves(silu(kraw))
        values = qkv[rows, 2 * head :]
        agrad = halves(att_grad[rows, :])
        prob, dscore = probs[rows, :], dscores[rows, :]
        state = halves(states[3 * b + j][:, :head])
        adj = adjoints[b, j]
        ahalf = halves(adj)
        adj_k, adj_v = (ahalf[0][:, :head], ahalf[1][:, :head]), (ahalf[0][:, head:], ahalf[1][:, head:])
        dweights = halves(unmix(dscore, ratios, here, masks, diag))
        dquery = dot3(dweights, keys, NN) + dot3(halves(dscore * growth), state, NN)
        term[rows, :head] = bf(silu_slope(qraw) * dquery * head ** (-0.5))
        left = halves(rest * here)
        dkey = dot3(dweights, query, TN) + dot3(left, adj_k, NN)
        term[rows, head : 2 * head] = bf(silu_slope(kraw) * dkey)
        dvalue = dot3(halves(weights[rows, :]), agrad, TN) + dot3(left, adj_v, NN)
        term[rows, 2 * head :] = bf(dvalue)
        pair_k = dot3(query, keys, NT)
        pair_v = mm(agrad[0], values, NT) + mm(agrad[1], values, NT)
        dkeep = jnp.sum(pair_k * diag, axis=1, keepdims=True) * dscore
        dkeep += jnp.sum(pair_v * diag, axis=1, keepdims=True) * prob
        dkeep += rest * (dot3(keys, adj_k, NT) + mm(values, adj_v[0], NT) + mm(values, adj_v[1], NT))
        for l, ratio in enumerate(ratios):
            mask = masks[l].astype(F32)
            more = dot3(halves(pair_k * mask), halves(dscore * ratio), TN)
            more += dot3(halves(pair_v * mask), halves(prob * ratio), TN)
            dkeep += ratio * more
        dsum = dscore * scores[rows, :] + prob * dprobs[rows, :] - here * dkeep
        at_end = jnp.sum(adj * states[3 * b + j + 1], axis=1, keepdims=True)
        at_end = jnp.sum(at_end * on_diagonal(adj.shape[0]), axis=0, keepdims=True)
        dsum += is_last * at_end
        decay_term[rows, :] = exact_sums(later[...], dsum) - (1.0 - here) * dkeep
        return nothing

    lax.fori_loop(0, 4, second, 0)
    weave.rest()
    share.finish(False)
    fold.finish()
    carry.finish()


def backward(size, number, slot, plan, hbm_ins, vmem_ins, grads):
    seqs, block, width = hbm_ins[0].shape
    h, m, n, rows = slot.head, slot.slots, slot.chunks, slot.seqs * slot.rows
    line = size // 4
    shape = jax.ShapeDtypeStruct
    outs = [
        shape((block, width), F32), shape((seqs, 2, block, width), BF16), shape((1, width), F32), shape((rows, h), BF16),
        shape((1, h), F32), shape((rows, 3 * h), BF16), shape((rows, m), F32),
    ]
    results, spaces, sems = [], [], []
    for i, unit, offset, columns, whole in plan:
        results.append(shape((2, unit, columns) if whole else (unit, 2 * columns), F32))
        spaces += [shape((line, 2 * unit, columns), BF16), shape((line + 1, 2 * unit, columns), BF16)]
        sems += scatter_sems(line)
    widest = max(entry[3] for entry in plan)
    scratch = [
        pltpu.VMEM((block, width), BF16), pltpu.VMEM((rows, h), F32),
        pltpu.VMEM((2, block, width), BF16), pltpu.SemaphoreType.DMA((4,)),
        pltpu.VMEM((rows, h), F32), pltpu.VMEM((rows, m), F32), pltpu.VMEM((rows, m), F32), pltpu.VMEM((seqs, n, m, 2 * h), F32),
        pltpu.VMEM((seqs, n, m, 2 * h), F32), pltpu.VMEM((seqs, m, 2 * h), F32),
    ]
    scratch += prefix_scratch(seqs, m, 2 * h) + fold_scratch(block, width) + SHARE_SEMS
    scratch += pool_scratch(2 * plan[0][1], widest) + sems
    later = slot.paths[-2 * slot.chunk : -slot.chunk].T
    result = pl.pallas_call(
        functools.partial(backward_kernel, size, plan, slot.levels),
        out_shape=outs + results + spaces,
        in_specs=[ANY] * 4 + [VM] * 16 + [ANY] * len(grads),
        out_specs=[VM] * 7 + [ANY] * (len(results) + len(spaces)),
        scratch_shapes=scratch,
        compiler_params=remote_params(number, 62),
        name="attend_backward",
    )(*hbm_ins, *vmem_ins, slot.paths, later, slot.masks, *grads)
    return result[: 7 + len(results)]


def products(p, part, fold, terms, i):
    count, width = part.shape[2], part.shape[3]
    stripe = min(512, width)
    b, x = blocks_in_order(p, part.shape[0])(i)
    rows = pl.ds(pl.multiple_of((b * 2 + x) * count, count), count)

    def one(t, nothing):
        columns = pl.ds(pl.multiple_of(t * stripe, stripe), stripe)
        value = None
        for left, right in terms:
            more = mm(left[rows, :], right[columns, :], NT)
            value = more if value is None else value + more
        part[b, x, :, columns] = bf(value)
        return nothing

    lax.fori_loop(0, width // stripe, one, 0)
    if i < 2:
        fold.sib_all(i == 0)


LAST_STEPS = (0, 1, 1, 1, 1, 1, 1, 2, 1)


def last_kernel(size, plan, *refs):
    p = Place(size)
    (qkv_full, gate_full, down_full), refs = take(refs, 3)
    (qkv_term, gates_term, activated, tokens, residual, residual_grad, gain, pack), refs = take(refs, 8)
    grads = max(i for i, _, _, _, _ in plan) + 1
    grad_refs, refs = take(refs, grads)
    (input_grad, output, sums), refs = take(refs, 3)
    outs, refs = take(refs, len(plan))
    spaces, refs = take(refs, 2 * len(plan))
    (part, ff_part, qkv_w, gate_w, down_w, load_sem), refs = take(refs, 6)
    fold_refs, refs = take(refs, 5)
    ff_refs, refs = take(refs, 5)
    (out_sem, mine, came, s_sem), refs = take(refs, 4)
    pool_refs, refs = take(refs, 5)
    loads = [
        pltpu.make_async_copy(source, to, load_sem.at[n])
        for n, (source, to) in enumerate(((qkv_full, qkv_w), (gate_full, gate_w), (down_full, down_w)))
    ]
    for load in loads:
        load.start()
    greet_all(p)
    pool = Pool(pool_refs)
    work = []
    for n, (i, unit, offset, width, _) in enumerate(plan):
        work.append(
            Scatter(p, grad_refs[i], outs[n], spaces[2 * n], spaces[2 * n + 1], unit, offset, width, refs[3 * n : 3 * n + 3])
        )
    weave = Weave(scatter_ops(work, pool))
    fold = Fold(p, part, *fold_refs[:3], fold_refs[3:])
    ff = Fold(p, ff_part, *ff_refs[:3], ff_refs[3:])
    weave.run(1 + LAST_STEPS[0])
    loads[0].wait()
    loads[1].wait()
    terms = [(qkv_term, qkv_w), (gates_term, gate_w)]
    for i in range(3):
        products(p, part, fold, terms, i)
    for r in range(STRIPS):
        fold.cross(r)
    weave.run(LAST_STEPS[1])
    products(p, part, fold, terms, 3)
    loads[2].wait()
    products(p, ff_part, ff, [(activated, down_w)], 0)
    weave.run(LAST_STEPS[2])
    products(p, ff_part, ff, [(activated, down_w)], 1)
    products(p, ff_part, ff, [(activated, down_w)], 2)
    weave.run(LAST_STEPS[3])
    for r in range(STRIPS):
        ff.cross(r)
    products(p, ff_part, ff, [(activated, down_w)], 3)
    weave.run(LAST_STEPS[4])
    gains = jnp.zeros((1, part.shape[3]), F32)

    def out_copy(ref, k, r):
        block = ref.at[p.c, fold.strip(r)]
        return remote(block, block, out_sem.at[0, k * STRIPS + r], out_sem.at[1, k * STRIPS + r], p.sibling())

    for r in range(STRIPS):
        down, more = norm_back(fold.total(r), tokens[p.c, fold.strip(r)].astype(F32), gain[...])
        gains += more
        input_grad[p.c, fold.strip(r)] = residual_grad[fold.strip(r)] + down
        out_copy(input_grad, 1, r).start()
        if r % 2 == 1:
            weave.run(LAST_STEPS[5 + r // 2])
    unit = plan[0][1]
    mine[...] = pack[...]
    for s in range(size):
        mine[s, 0:1, pl.ds(0, unit)] = gains[:, s * unit : (s + 1) * unit]
    smalls = Smalls(p, mine, sums, came, s_sem)
    smalls.start()
    weave.run(LAST_STEPS[7])
    for r in range(STRIPS):
        output[p.c, fold.strip(r)] = bf(residual[fold.strip(r)] + ff.total(r))
        out_copy(output, 0, r).start()
        if r % 2 == 1:
            weave.run(LAST_STEPS[8])
    weave.rest()
    smalls.finish()
    for r in range(STRIPS):
        out_copy(output, 0, r).wait()
        out_copy(input_grad, 1, r).wait()
    ff.finish()
    fold.finish()


def last(size, number, plan, hbm_ins, vmem_ins, grads):
    qkv_term, _, _, tokens = vmem_ins[:4]
    seqs, block, width = tokens.shape
    pack = vmem_ins[-1]
    line = size // 4
    shape = jax.ShapeDtypeStruct
    outs = [shape((seqs, block, width), F32), shape((seqs, block, width), BF16), shape(pack.shape[1:], F32)]
    results, specs, spaces, sems = [], [], [], []
    for i, unit, offset, columns, whole in plan:
        results.append(shape((2, unit, columns) if whole else (unit, 2 * columns), F32))
        specs.append(VM if whole else ANY)
        spaces += [shape((line, 2 * unit, columns), BF16), shape((line + 1, 2 * unit, columns), BF16)]
        sems += scatter_sems(line)
    widest = max(entry[3] for entry in plan)
    scratch = [pltpu.VMEM((seqs, 2, block, width), BF16)] * 2 + [pltpu.VMEM(w.shape, BF16) for w in hbm_ins]
    scratch += [pltpu.SemaphoreType.DMA((3,))] + fold_scratch(block, width) * 2 + [
        pltpu.SemaphoreType.DMA((2, 2 * STRIPS)), pltpu.VMEM(pack.shape, F32), pltpu.VMEM((2 * size,) + pack.shape[1:], F32),
        pltpu.SemaphoreType.DMA((2, 2 * size)),
    ]
    scratch += pool_scratch(2 * plan[0][1], widest) + sems
    result = pl.pallas_call(
        functools.partial(last_kernel, size, plan),
        out_shape=outs + results + spaces,
        in_specs=[ANY] * 3 + [VM] * 8 + [ANY] * len(grads),
        out_specs=[VM] * 3 + specs + [ANY] * len(spaces),
        scratch_shapes=scratch,
        compiler_params=remote_params(number, 62),
        name="last",
    )(*hbm_ins, *vmem_ins, *grads)
    return result[: 3 + len(results)]

def greet_all(place):
    barrier = pltpu.get_barrier_semaphore()

    def one(i, carry):
        signal(barrier, (lax.rem(place.s + i // 2, place.size), lax.rem(place.c + lax.rem(i, 2), 2)))
        return carry

    lax.fori_loop(1, 2 * place.size, one, 0)
    pl.semaphore_wait(barrier, 2 * place.size - 1)


class Smalls:
    def __init__(self, place, pack, out, came, sems):
        self.p, self.pack, self.out, self.came, self.sems = place, pack, out, came, sems

    def copy(self, i):
        p = self.p
        s = lax.rem(p.s + i // 2, p.size)
        return remote(
            self.pack.at[s], self.came.at[i], self.sems.at[0, i], self.sems.at[1, i], (s, lax.rem(p.c + lax.rem(i, 2), 2))
        )

    def start(self):
        lax.fori_loop(1, 2 * self.p.size, lambda i, c: (self.copy(i).start(), c)[1], 0)

    def finish(self):
        def one(i, total):
            self.copy(i).wait()
            return total + self.came[i]

        self.out[...] = lax.fori_loop(1, 2 * self.p.size, one, self.pack[self.p.s])


class Swap:
    def __init__(self, place, own, both, sems):
        p = self.p = place
        self.keep = pltpu.make_async_copy(own, both.at[:, p.x], sems.at[0])
        self.cross = remote(own.at[p.c], both.at[p.c, p.x], sems.at[1], sems.at[2], p.partner())
        came = both.at[p.c, 1 - p.x]
        self.hand = remote(came, came, sems.at[3], sems.at[4], p.sibling())

    def start(self):
        self.cross.start()
        self.keep.start()

    def forward(self):
        self.cross.wait_recv()
        self.hand.start()

    def finish(self):
        self.keep.wait()
        self.cross.wait_send()
        self.hand.wait()


def gather_kernel(size, plan, *refs):
    p = Place(size)
    shards = sum(len(columns) for _, _, columns in plan)
    fulls = max(i for i, _, _ in plan) + 1
    ins, refs = take(refs, shards)
    (own_tokens,), refs = take(refs, 1)
    outs, refs = take(refs, fulls)
    (tokens, normed, qkv, gates), refs = take(refs, 4)
    (swap_sem, tok, qkv_w, gate_w, small, load_sem), refs = take(refs, 6)
    greet(p, sibling=True)
    work = gathers_of(p, plan, ins, outs, refs)
    smalls, qkv_gather, gate_gather, out_gather = work
    move = Swap(p, own_tokens, tokens, swap_sem)
    for gathered in work:
        gathered.start_x()
    weave = Weave(gather_ops(work, 1)[: -len(work)])
    weave.run(6)
    move.start()
    weave.run(4)
    move.forward()
    weave.run(2)
    move.finish()
    smalls.finish()
    loads = [
        pltpu.make_async_copy(source, to, load_sem.at[n])
        for n, (source, to) in enumerate(((tokens, tok), (outs[3], small), (outs[0], qkv_w), (outs[1], gate_w)))
    ]
    loads[0].start()
    loads[1].start()
    loads[0].wait()
    loads[1].wait()
    seqs, pair, block, width = tok.shape
    unit = plan[1][1]
    gain = jnp.concatenate([small[16 * s : 16 * s + 1, :unit].astype(F32) for s in range(size)], axis=1)
    step = 32

    def norm(i, nothing):
        b, x, r = i // (pair * (block // step)), lax.rem(i // (block // step), pair), lax.rem(i, block // step)
        rows = pl.ds(pl.multiple_of(r * step, step), step)
        value = tok[b, x, rows, :].astype(F32)
        where = pl.ds(pl.multiple_of(i * step, step), step)
        normed[where, :] = bf(value * inverse_rms(value) * gain)
        return nothing

    lax.fori_loop(0, seqs * pair * (block // step), norm, 0)
    weave.rest()
    qkv_gather.finish()
    loads[2].start()
    gate_gather.finish()
    loads[3].start()
    loads[2].wait()

    def rows_of(i):
        return pl.ds(pl.multiple_of(i * block, block), block)

    third = qkv.shape[1] // 3

    def project(i, nothing):
        for t in range(3):
            columns = pl.ds(t * third, third)
            qkv[rows_of(i), columns] = bf(mm(normed[rows_of(i), :], qkv_w[:, columns], NN))
        return nothing

    lax.fori_loop(0, seqs * pair, project, 0)
    loads[3].wait()

    def gate(i, nothing):
        gates[rows_of(i), :] = mm(normed[rows_of(i), :], gate_w[...], NN)
        return nothing

    lax.fori_loop(0, seqs * pair, gate, 0)
    out_gather.finish()


def gather(size, number, plan, shards, fulls, tokens):
    line = size // 4
    seqs, block, width = tokens.shape
    rows = 2 * seqs * block
    shape = jax.ShapeDtypeStruct
    sems = []
    for _, _, columns in plan:
        sems += gather_sems(line, len(columns))
    return pl.pallas_call(
        functools.partial(gather_kernel, size, plan),
        out_shape=[shape(full, BF16) for full in fulls] + [
            shape((seqs, 2, block, width), BF16), shape((rows, width), BF16), shape((rows, fulls[0][1]), BF16),
            shape((rows, fulls[1][1]), F32),
        ],
        in_specs=[ANY] * (len(shards) + 1),
        out_specs=[ANY] * (len(fulls) + 1) + [VM] * 3,
        scratch_shapes=[
            pltpu.SemaphoreType.DMA((5,)), pltpu.VMEM((seqs, 2, block, width), BF16), pltpu.VMEM(fulls[0], BF16),
            pltpu.VMEM(fulls[1], BF16), pltpu.VMEM(fulls[3], BF16), pltpu.SemaphoreType.DMA((4,)),
        ] + sems,
        compiler_params=remote_params(number, 60),
        name="gather",
    )(*shards, tokens)


def dot(left, right, dims, dtype=F32):
    return lax.dot_general(left, right, dims, preferred_element_type=F32).astype(dtype)


def lanes(row):
    return jnp.pad(row.reshape(-1), (0, 128 - row.size))


def shards(
    tokens, grad_out, query_weight, key_weight, value_weight, forget_weight, forget_bias, outgate_weight, output_weight,
    slot_gain, first_gain, second_gain, gate_weight, up_weight, down_weight,
):
    size = lax.axis_size("seq")
    x = lax.rem(lax.axis_index("seq"), 2)
    c = lax.axis_index("head")
    seqs, block, width = tokens.shape
    heads_here, slot_part = forget_bias.shape
    slots = slot_part * size
    head = slot_gain.shape[0] * size
    unit = first_gain.shape[0]
    hidden = gate_weight.shape[1] // 2
    rows = seqs * 2 * block
    pack = jnp.stack([lanes(first_gain), lanes(second_gain), lanes(slot_gain), lanes(forget_bias)] + [jnp.zeros(128, BF16)] * 12)
    plan = [
        (3, 16, [(0, 128)]), (0, unit, [(0, head), (head, head), (2 * head, head)]), (1, unit, [(0, head), (head, 2 * slots)]),
        (2, unit, [(0, head)]),
    ]
    fulls = [(width, 3 * head), (width, head + 2 * slots), (width, head), (16 * size, 128)]
    qkv_full, gate_full, out_full, small_full, _, normed_one, qkv, gates = gather(
        size, 0, plan,
        (pack, query_weight, key_weight, value_weight, outgate_weight, forget_weight, output_weight.T), fulls, tokens,
    )
    small = small_full.reshape(size, 16, 128).astype(F32)
    first_full = small[:, 0, :unit].reshape(1, width)
    second_full = small[:, 1, :unit].reshape(1, width)
    slot_full = small[:, 2, : head // size].reshape(1, head)
    bias_full = small[:, 3, : heads_here * slot_part].reshape(size, heads_here, slot_part)
    bias_full = jnp.moveaxis(bias_full, 1, 0).reshape(heads_here, slots)

    def own_head(array, axis):
        return jnp.where(x == 0, *jnp.split(array, 2, axis=axis))

    logit = own_head(gates[:, head:], 1) + own_head(bias_full, 0)
    decay = -jax.nn.softplus(-logit) / TAU
    keep = -jnp.expm1(decay)
    slot = Slots(seqs, 2 * block, head, slots, block)
    ff_plan = [(0, unit, [(0, hidden)]), (0, unit, [(hidden, hidden)]), (1, unit, [(0, hidden)])]
    (gated, attended, probs, scores, weights, states, decs, end_decs, residual, normed_two, gout, ff, ff_full, down_full) = forward(
        size, 1, slot, ff_plan, [(width, 2 * hidden), (width, hidden)], qkv, gates, decay, keep, slot_full, out_full, tokens,
        second_full, grad_out, (gate_weight, up_weight, down_weight.T),
    )
    shape = (seqs, 2, block, width)
    normed_two = normed_two.reshape(rows, width)
    ff_gate, ff_up = ff[:, :hidden], ff[:, hidden:]
    sig = jax.nn.sigmoid(ff_gate)
    activated = (ff_gate * sig * ff_up).astype(BF16)
    gout = gout.reshape(rows, width)
    act_grad = dot(gout, down_full, NN)
    ff_term = jnp.concatenate(
        [act_grad * ff_up * (sig + ff_gate * sig * (1.0 - sig)), act_grad * ff_gate * sig], axis=1
    ).astype(BF16)
    down_grad = dot(gout, activated, TN, BF16)
    ff_grad = dot(normed_two, ff_term, TN, BF16)
    normed_two_grad = dot(ff_term, ff_full, NT, BF16).reshape(shape)
    front = (hidden // 128 + 1) // 2 * 128
    back = hidden - front
    ff_plan = [
        (0, unit, 0, hidden, False), (0, unit, hidden, hidden, False), (1, unit, 0, front, False), (1, unit, front, back, False),
    ]
    residual_grad, low, second_part, gate_term, slot_part_grad, qkv_term, decay_term, gate_grad, up_grad, down_front, down_back = backward(
        size, 2, slot, ff_plan,
        (grad_out, gates, attended, normed_two_grad),
        (residual, second_full, out_full, qkv, decay, keep, slot_full, probs, scores, weights, states, decs,
         end_decs),
        (ff_grad, down_grad),
    )
    down_grad = jnp.concatenate([down_front[:, :front], down_back[:, :back], down_front[:, front:], down_back[:, back:]], axis=1)
    low = low.reshape(rows, width)
    out_grad = dot(low, gated, TN, BF16)
    forget_term = (decay_term * jax.nn.sigmoid(-logit) / TAU).astype(BF16)
    none = jnp.zeros_like(forget_term)
    gates_term = jnp.concatenate(
        [gate_term, jnp.where(x == 0, forget_term, none), jnp.where(x == 0, none, forget_term)], axis=1
    )
    qkv_grad = dot(normed_one, qkv_term, TN, BF16)
    gates_grad = dot(normed_one, gates_term, TN, BF16)
    bias_part = jnp.sum(forget_term.astype(F32), axis=0)
    which = jnp.arange(2 * heads_here) == heads_here * c + x
    bias_part = jnp.where(which[:, None], bias_part[None, :], 0.0).reshape(2 * heads_here, size, slot_part)

    def rows_of(array):
        array = array.reshape(size, -1)
        return jnp.pad(array, ((0, 0), (0, 128 - array.shape[1])))

    zero = jnp.zeros((size, 128), F32)
    packed = jnp.stack(
        [zero, rows_of(second_part), rows_of(slot_part_grad), rows_of(jnp.moveaxis(bias_part, 1, 0))] + [zero] * 4, axis=1
    )
    plan = [
        (0, unit, 0, head, False), (1, unit, 0, head, False), (1, unit, head, head, False), (1, unit, 2 * head, head, False),
        (2, unit, 0, head, False), (2, unit, head, 2 * slots, True),
    ]
    input_grad, output, sums, output_grad, query_grad, key_grad, value_grad, outgate_grad, forget_grad = last(
        size, 3, plan, (qkv_full, gate_full, down_full),
        (qkv_term, gates_term, activated, tokens, residual, residual_grad, first_full, packed),
        (out_grad, qkv_grad, gates_grad),
    )
    bias_grad = sums[3, : 2 * heads_here * slot_part].reshape(2, heads_here, slot_part)
    bias_grad = jnp.where(c == 0, bias_grad[0], bias_grad[1])
    return (
        output, input_grad, query_grad, key_grad, value_grad, forget_grad[0], bias_grad, outgate_grad, output_grad.T,
        sums[2, : head // size], sums[0, :unit], sums[1, :unit], gate_grad, up_grad, down_grad.T,
    )


def solution(mesh):
    row, column, vector, token = P("seq", "head"), P("head", "seq"), P("seq"), P(None, "seq", None)
    return jax.shard_map(
        shards,
        mesh=mesh,
        in_specs=(token, token, row, row, row, row, column, row, column, vector, vector, vector, row, row, column),
        out_specs=(token, token, row, row, row, row, column, row, column, vector, vector, vector, row, row, column),
        check_vma=False,
    )
```
